128 devices in a mesh: req: 16 (over x, y), head: 8 (over z, core).
Axes of the slice: x: 4, y: 4, z: 4, core: 2. Of those that a mesh axis runs over, the one named last changes fastest.
Arguments:
- streams: bfloat16 [12288, 4, 2048], P('req', None, 'head'), may hold values from -6 to 6
- hc_in: float32 [2, 4], replicated, may hold values from 0.2 to 1
- hc_mix: float32 [2, 4, 4], replicated, may hold values from -0.4 to 0.4
- hc_out: float32 [2, 4], replicated, may hold values from 0.5 to 1.5
- qkv_weight: bfloat16 [2048, 3, 2048], P(None, None, 'head'), may hold values from -0.125 to 0.125
- out_weight: bfloat16 [2048, 2048], P('head'), may hold values from -0.125 to 0.125
- up_gate: bfloat16 [2048, 2, 8192], P(None, None, 'head'), may hold values from -0.125 to 0.125
- down_weight: bfloat16 [8192, 2048], P('head'), may hold values from -0.0625 to 0.0625
- draft_weight: bfloat16 [2, 2048, 2048], P(None, None, 'head'), may hold values from -0.125 to 0.125
- lm_head: bfloat16 [2048, 50304], P(None, ('req', 'head')), may hold values from -0.125 to 0.125
- k_pages: bfloat16 [768, 128, 16, 128], P('req', None, 'head'), may hold values from -45 to 45
- v_pages: bfloat16 [768, 128, 16, 128], P('req', None, 'head'), may hold values from -6 to 6
- page_owner: int32 [768], P('req'), may hold values from -1 to 255, as said below
- page_fill: int32 [768], P('req'), may hold values from 0 to 128, as said below
- cache_len: int32 [256], P('req'), may hold values from 1 to 16384, as said below
- tree_parent: int32 [256, 48], P('req'), may hold values from 0 to 46, as said below
- accepted_index: int32 [256], P('req'), may hold values from 0 to 47
Outputs:
- new_streams: bfloat16 [12288, 4, 2048], P('req', None, 'head')
- logits: float32 [256, 2, 50304], P(('req', 'head'))
The draws below stay inside these ranges and needn't reach their ends.
Inputs may be any that keep to these rules, and one draw needn't show every extreme that they name: `page_owner`: each page slot holds one page of the request it names, or -1 where it is empty. Every request owns at least one page and one request owns 128 pages; the live pages of a device's slots vary widely from device to device. `page_fill`: 0 for an empty slot; every page of a request is full except at most one. `cache_len`: equals the valid entries of the pages the request owns; one request has exactly 16384. `tree_parent`: entry i names a smaller position, the parent of position i; position 0 is the root and names itself.
All inputs are finite; a program needn't handle non-finite values.
Results may differ from the reference program's by a relative error of at most 0.027.
Values may be sent and summed in bfloat16 or wider, within the bound.
A program may use at most 512 MiB of HBM per device.

```python
import math
import jax
import jax.numpy as jnp
from jax import lax

D = 2048
HEADS = 16
HD = 128
FF = 8192
VOCAB = 50304
NS = 4
TREE = 48
PAGE = 128
LONG_PAGES = 128
NDRAFT = 2
LEAVES_EACH_PART = 48
REQUESTS = 256
TOKENS = 12288
LEAF_PLACES_SUM = 768


def page_layout(key):
    sampler_seeds = jax.random.split(jax.random.fold_in(key, 5), 6)
    order_req = jnp.arange(REQUESTS, dtype=jnp.int32)
    power = jax.random.randint(sampler_seeds[0], (REQUESTS,), 0, 6)
    extra = jax.random.randint(sampler_seeds[1], (REQUESTS,), 0, jnp.left_shift(1, power))
    extra = jnp.minimum(extra, LONG_PAGES - 2)
    longest = jax.random.randint(sampler_seeds[2], (), 0, REQUESTS)
    is_long = order_req == longest
    extra = jnp.where(is_long, 0, extra)
    before = jnp.cumsum(extra) - extra
    room = 2 * LEAF_PLACES_SUM // 3 - REQUESTS - (LONG_PAGES - 1)
    extra = jnp.clip(room - before, 0, extra)
    extra = jnp.where(is_long, LONG_PAGES - 1, extra)
    count = 1 + extra
    last_fill = jax.random.randint(sampler_seeds[3], (REQUESTS,), 1, PAGE + 1)
    last_fill = jnp.where(is_long, PAGE, last_fill)
    lengths = (count - 1) * PAGE + last_fill
    starts = jnp.cumsum(count) - count
    total = jnp.sum(count)
    current_position = jnp.arange(LEAF_PLACES_SUM, dtype=jnp.int32)
    owner_of = jnp.sum((starts[None, :] <= current_position[:, None]).astype(jnp.int32), axis=1) - 1
    within = current_position - starts[owner_of]
    fill_of = jnp.where(within == count[owner_of] - 1, last_fill[owner_of], PAGE)
    is_live = current_position < total
    owner_of = jnp.where(is_live, owner_of, -1)
    fill_of = jnp.where(is_live, fill_of, 0)
    partition_number = LEAF_PLACES_SUM // LEAVES_EACH_PART
    appended_symbol = jnp.left_shift(1, jax.random.randint(sampler_seeds[4], (partition_number,), 0, 12))
    extreme_perturbation = jax.random.randint(sampler_seeds[5], (LEAF_PLACES_SUM,), 0, 1024)
    proposal_rating = (appended_symbol[current_position // LEAVES_EACH_PART] + extreme_perturbation) * LEAF_PLACES_SUM + current_position
    slot_of = jnp.argsort(-proposal_rating, stable=True)
    owner = jnp.zeros((LEAF_PLACES_SUM,), jnp.int32).at[slot_of].set(owner_of.astype(jnp.int32))
    fill = jnp.zeros((LEAF_PLACES_SUM,), jnp.int32).at[slot_of].set(fill_of.astype(jnp.int32))
    return (owner, fill, lengths.astype(jnp.int32))


def draw_page_owner(key, part):
    return page_layout(key)[0]


def draw_page_fill(key, part):
    return page_layout(key)[1]


def draw_cache_len(key, part):
    return page_layout(key)[2]


def draw_tree_parent(key, part):
    places = jnp.arange(TREE, dtype=jnp.int32)
    raw = jax.random.randint(jax.random.fold_in(key, 3), (REQUESTS, TREE), 0, jnp.maximum(places, 1)[None, :])
    return jnp.where(places[None, :] == 0, 0, raw).astype(jnp.int32)


def draw_k_pages(key, part):
    shape = (LEAF_PLACES_SUM, PAGE, HEADS, HD)
    base = jnp.clip(jax.random.normal(key, shape, jnp.float32), -6.0, 6.0)
    return base.astype(jnp.bfloat16)


def plant(result, own_key, least, largest):
    longest = result.shape.index(max(result.shape))
    spots = []
    for shift in (0, 1):
        where = [jax.random.randint(jax.random.fold_in(own_key, axis), (), 0, length) for axis, length in enumerate(result.shape)]
        where[longest] = (where[longest] + shift) % result.shape[longest]
        spots.append(tuple(where))
    return result.at[spots[0]].set(least).at[spots[1]].set(largest)


def level_of(rng, extent, cuts, low, high):
    def one(position, shards_of):
        draws = jax.random.uniform(jax.random.fold_in(jax.random.fold_in(rng, 6), position), (shards_of,), jnp.float32, low / len(cuts), high / len(cuts))
        return jnp.repeat(jnp.exp(draws), extent[position] // shards_of).reshape((-1,) + (1,) * (len(extent) - position - 1))

    gain = one(*cuts[0])
    for cut in cuts[1:]:
        gain = gain * one(*cut)
    return gain


def scatter_about(stream_key, shape, scale, limit, pieces=(), kind=jnp.bfloat16):
    result = jax.random.normal(stream_key, shape, jnp.float32) * scale
    if len(pieces) > 0:
        result = level_of(stream_key, shape, pieces, -0.22, 0.18) * result
    return jnp.clip(result, min=-limit, max=limit).astype(kind)


def setup_inputs(seed: int = 0) -> dict:
    keys = jax.random.split(jax.random.key(seed), 18)
    streams = scatter_about(keys[0], (TOKENS, NS, D), 1.0, 6.0, ((0, 16), (2, 8)))
    hc_in = jnp.clip(jax.random.uniform(keys[1], (2, NS), jnp.float32, 0.2, 1.0), 0.2, 1.0)
    hc_mix = jnp.clip(jax.random.uniform(keys[2], (2, NS, NS), jnp.float32, -0.4, 0.4), -0.4, 0.4)
    hc_out = jnp.clip(jax.random.uniform(keys[3], (2, NS), jnp.float32, 0.5, 1.5), 0.5, 1.5)
    qkv_weight = scatter_about(keys[4], (D, 3, HEADS * HD), D ** -0.5, 0.125, ((2, 8),))
    out_weight = scatter_about(keys[5], (HEADS * HD, D), (HEADS * HD) ** -0.5, 0.125, ((0, 8),))
    up_gate = scatter_about(keys[6], (D, 2, FF), D ** -0.5, 0.125, ((2, 8),))
    down_weight = scatter_about(keys[7], (FF, D), FF ** -0.5, 0.0625, ((0, 8),))
    draft_weight = scatter_about(keys[8], (NDRAFT, D, D), D ** -0.5, 0.125, ((2, 8),))
    lm_head = scatter_about(keys[9], (D, VOCAB), D ** -0.5, 0.125, ((1, 128),))
    k_pages = draw_k_pages(jax.random.fold_in(keys[17], 71), 0)
    v_pages = scatter_about(keys[11], (LEAF_PLACES_SUM, PAGE, HEADS, HD), 1.0, 6.0, ((0, 16), (2, 8)))
    page_owner = draw_page_owner(jax.random.fold_in(keys[17], 71), 0)
    page_fill = draw_page_fill(jax.random.fold_in(keys[17], 71), 0)
    cache_len = draw_cache_len(jax.random.fold_in(keys[17], 71), 0)
    tree_parent = draw_tree_parent(jax.random.fold_in(keys[17], 71), 0)
    accepted_index = plant(jax.random.randint(keys[16], (REQUESTS,), 0, TREE), jax.random.fold_in(keys[16], 1), 0, TREE - 1).astype(jnp.int32)
    return dict(streams=streams, hc_in=hc_in, hc_mix=hc_mix, hc_out=hc_out, qkv_weight=qkv_weight, out_weight=out_weight, up_gate=up_gate, down_weight=down_weight, draft_weight=draft_weight, lm_head=lm_head, k_pages=k_pages, v_pages=v_pages, page_owner=page_owner, page_fill=page_fill, cache_len=cache_len, tree_parent=tree_parent, accepted_index=accepted_index)


NEG_FILL = -1e+30
PRECISE = lax.Precision.HIGHEST

def layer_norm(values):
    center = lax.optimization_barrier(jnp.mean(values, axis=-1, keepdims=True))
    square = lax.optimization_barrier(jnp.mean(values * values, axis=-1, keepdims=True))
    return (values - center) * lax.rsqrt(square - center * center + 1e-05)

def ancestors(parents):
    length = parents.shape[1]
    places = jnp.arange(length, dtype=jnp.int32)
    linked = (parents[:, :, None] == places[None, None, :]) | (places[:, None] == places[None, :])[None]
    reach = linked.astype(jnp.float32)
    for repeat in range(max(1, (length - 1).bit_length())):
        reach = jnp.minimum(jnp.einsum('jik,jkl->jil', reach, reach, precision=PRECISE), 1.0)
    return reach

def rotate(values, positions):
    half = values.shape[-1] // 2
    freqs = jnp.exp(jnp.arange(half, dtype=jnp.float32) * (-2.0 * math.log(10000.0) / values.shape[-1]))
    angles = positions.astype(jnp.float32)[:, None] * freqs[None, :]
    cosine = jnp.cos(angles)[:, None, :]
    sine = jnp.sin(angles)[:, None, :]
    first = values[..., :half]
    second = values[..., half:]
    return jnp.concatenate([first * cosine - second * sine, second * cosine + first * sine], axis=-1)

def blend(stream_vals, weights):
    total = weights[0] * stream_vals[:, 0]
    for index in range(1, stream_vals.shape[1]):
        total = total + weights[index] * stream_vals[:, index]
    return total

def remix(stream_vals, mixing, out_scale, delta):
    count = stream_vals.shape[1]
    matrix = jnp.eye(count, dtype=jnp.float32) + mixing
    rows = [blend(stream_vals, matrix[:, target]) + out_scale[target] * delta for target in range(count)]
    return jnp.stack(rows, axis=1)

def stream_total(stream_vals):
    total = stream_vals[:, 0]
    for index in range(1, stream_vals.shape[1]):
        total = total + stream_vals[:, index]
    return total

def rounded(values):
    return lax.optimization_barrier(values.astype(jnp.bfloat16)).astype(jnp.float32)

def reference(streams, hc_in, hc_mix, hc_out, qkv_weight, out_weight, up_gate, down_weight, draft_weight, lm_head, k_pages, v_pages, page_owner, page_fill, cache_len, tree_parent, accepted_index):
    reach = ancestors(tree_parent)
    depth = (lax.optimization_barrier(jnp.sum(reach, axis=2)) - 1.0).astype(jnp.int32)
    positions = (cache_len[:, None] + depth).reshape(TOKENS)
    stream_vals = streams.astype(jnp.float32)
    normed = layer_norm(blend(stream_vals, hc_in[0])).astype(jnp.bfloat16)
    projected = jnp.dot(normed, qkv_weight.reshape(D, 3 * HEADS * HD), preferred_element_type=jnp.float32)
    projected = projected.reshape(TOKENS, 3, HEADS, HD)
    queries = (rotate(projected[:, 0], positions) * HD ** (-0.5)).astype(jnp.bfloat16)
    keys_new = rotate(projected[:, 1], positions).astype(jnp.bfloat16)
    values_new = projected[:, 2].astype(jnp.bfloat16)
    query_all = queries.reshape(REQUESTS, TREE, HEADS, HD)
    key_all = keys_new.reshape(REQUESTS, TREE, HEADS, HD)
    value_all = values_new.reshape(REQUESTS, TREE, HEADS, HD)
    safe_owner = jnp.maximum(page_owner, 0)
    live = (page_owner >= 0)[:, None] & (jnp.arange(PAGE, dtype=jnp.int32)[None, :] < page_fill[:, None])
    owned = (page_owner[:, None] == jnp.arange(REQUESTS, dtype=jnp.int32)[None, :]).astype(jnp.float32)

    def one_head(head):
        query = lax.dynamic_index_in_dim(query_all, head, 2, keepdims=False).astype(jnp.float32)
        key_new = lax.dynamic_index_in_dim(key_all, head, 2, keepdims=False).astype(jnp.float32)
        value_new = lax.dynamic_index_in_dim(value_all, head, 2, keepdims=False).astype(jnp.float32)
        key_old = lax.dynamic_index_in_dim(k_pages, head, 2, keepdims=False).astype(jnp.float32)
        value_old = lax.dynamic_index_in_dim(v_pages, head, 2, keepdims=False).astype(jnp.float32)
        cache_scores = jnp.einsum('sqd,spd->sqp', query[safe_owner], key_old, precision=PRECISE)
        cache_scores = jnp.where(live[:, None, :], cache_scores, NEG_FILL)
        tree_scores = jnp.einsum('jqd,jkd->jqk', query, key_new, precision=PRECISE)
        tree_scores = jnp.where(reach > 0, tree_scores, NEG_FILL)
        page_top = lax.optimization_barrier(jnp.max(cache_scores, axis=2))
        owned_top = lax.optimization_barrier(jnp.max(jnp.where(owned[:, :, None] > 0, page_top[:, None, :], NEG_FILL), axis=0))
        top = jnp.maximum(owned_top, lax.optimization_barrier(jnp.max(tree_scores, axis=2)))
        cache_weights = jnp.where(live[:, None, :], jnp.exp(cache_scores - top[safe_owner][:, :, None]), 0.0)
        tree_weights = jnp.where(reach > 0, jnp.exp(tree_scores - top[:, :, None]), 0.0)
        total = jnp.dot(owned.T, lax.optimization_barrier(jnp.sum(cache_weights, axis=2)), precision=PRECISE) + lax.optimization_barrier(jnp.sum(tree_weights, axis=2))
        page_sums = jnp.einsum('sqp,spd->sqd', rounded(cache_weights), value_old, precision=PRECISE)
        summed = jnp.dot(owned.T, page_sums.reshape(LEAF_PLACES_SUM, TREE * HD), precision=PRECISE).reshape(REQUESTS, TREE, HD)
        summed = summed + jnp.einsum('jqk,jkd->jqd', rounded(tree_weights), value_new, precision=PRECISE)
        return summed / total[:, :, None]
    per_head = lax.map(one_head, jnp.arange(HEADS, dtype=jnp.int32))
    attended = jnp.transpose(per_head, (1, 2, 0, 3)).reshape(TOKENS, HEADS * HD).astype(jnp.bfloat16)
    attn_delta = jnp.dot(attended, out_weight, preferred_element_type=jnp.float32)
    first_streams = remix(stream_vals, hc_mix[0], hc_out[0], attn_delta)
    normed_mid = layer_norm(blend(first_streams, hc_in[1])).astype(jnp.bfloat16)
    gate_up = jnp.dot(normed_mid, up_gate.reshape(D, 2 * FF), preferred_element_type=jnp.float32)
    hidden = (jax.nn.silu(gate_up[:, :FF]) * gate_up[:, FF:]).astype(jnp.bfloat16)
    mlp_delta = jnp.dot(hidden, down_weight, preferred_element_type=jnp.float32)
    second_streams = remix(first_streams, hc_mix[1], hc_out[1], mlp_delta)
    new_streams = second_streams.astype(jnp.bfloat16)
    rows_taken = jnp.arange(REQUESTS, dtype=jnp.int32) * TREE + accepted_index
    final_norm = layer_norm(stream_total(second_streams[rows_taken]))
    branch = jnp.einsum('jd,kde->jke', rounded(final_norm), draft_weight.astype(jnp.float32), precision=PRECISE)
    drafts = (final_norm[:, None, :] + jax.nn.silu(branch)).astype(jnp.bfloat16)
    logits = jnp.dot(drafts.reshape(REQUESTS * NDRAFT, D), lm_head, preferred_element_type=jnp.float32)
    return (new_streams, logits.reshape(REQUESTS, NDRAFT, VOCAB))
```

```python
import functools
import math

import jax
import jax.numpy as jnp
from jax import lax
from jax.experimental import pallas as pl
from jax.experimental.pallas import tpu as pltpu
from jax.sharding import PartitionSpec as P

NEG_FILL = -1e30
PRECISE = lax.Precision.HIGHEST


def layer_norm(values):
    center = jnp.mean(values, axis=-1, keepdims=True)
    square = jnp.mean(values * values, axis=-1, keepdims=True)
    return (values - center) * lax.rsqrt(square - center * center + 1e-05)


def normalize(values, sums, squares, width):
    center = sums / width
    return (values - center) * lax.rsqrt(squares / width - center * center + 1e-05)


def ancestors(parents):
    length = parents.shape[1]
    places = jnp.arange(length, dtype=jnp.int32)
    linked = (parents[:, :, None] == places[None, None, :]) | (places[:, None] == places[None, :])[
        None
    ]
    reach = linked.astype(jnp.float32)
    for repeat in range(max(1, (length - 1).bit_length())):
        reach = jnp.minimum(jnp.einsum("jik,jkl->jil", reach, reach, precision=PRECISE), 1.0)
    return reach


def rotate(values, positions):
    half = values.shape[-1] // 2
    freqs = jnp.exp(
        jnp.arange(half, dtype=jnp.float32) * (-2.0 * math.log(10000.0) / values.shape[-1])
    )
    angles = positions.astype(jnp.float32)[:, None] * freqs[None, :]
    cosine = jnp.cos(angles)[:, None, :]
    sine = jnp.sin(angles)[:, None, :]
    first = values[..., :half]
    second = values[..., half:]
    return jnp.concatenate(
        [first * cosine - second * sine, second * cosine + first * sine], axis=-1
    )


def blend(stream_vals, weights):
    total = weights[0] * stream_vals[:, 0]
    for index in range(1, stream_vals.shape[1]):
        total = total + weights[index] * stream_vals[:, index]
    return total


def remix(stream_vals, mixing, out_scale, delta):
    count = stream_vals.shape[1]
    matrix = jnp.eye(count, dtype=jnp.float32) + mixing
    rows = [
        blend(stream_vals, matrix[:, target]) + out_scale[target] * delta for target in range(count)
    ]
    return jnp.stack(rows, axis=1)


def stream_total(stream_vals):
    total = stream_vals[:, 0]
    for index in range(1, stream_vals.shape[1]):
        total = total + stream_vals[:, index]
    return total


def fold_rows(weight, piece):
    return jnp.dot(piece, weight, preferred_element_type=jnp.float32)


MESH = pl.DeviceIdType.MESH
SLOT_BITS = 6
FILL_BITS = 8


def remote(source, target, send_sem, recv_sem, req):
    return pltpu.make_async_remote_copy(
        src_ref=source,
        dst_ref=target,
        send_sem=send_sem,
        recv_sem=recv_sem,
        device_id={"req": req},
        device_id_type=MESH,
    )


def weigh(tops, totals):
    top = functools.reduce(jnp.maximum, tops)
    factors = [jnp.exp(value - top) for value in tops]
    total = functools.reduce(lambda a, b: a + b, [f * t for f, t in zip(factors, totals)])
    return top, total, factors


def cache_kernel(
    side,
    table,
    last,
    q_ref,
    k_hbm,
    v_hbm,
    num_ref,
    top_ref,
    den_ref,
    q_all,
    k_buf,
    v_buf,
    scores,
    seg_acc,
    seg_top,
    seg_den,
    parts,
    stats,
    relay,
    merged,
    single,
    relay_s,
    merged_s,
    single_s,
    outgoing_s,
    factors,
    small,
    small_s,
    hop,
    hop_s,
    gather_send,
    gather_recv,
    spread_send,
    spread_recv,
    load_sem,
    far_send,
    far_recv,
    near_send,
    near_recv,
    join_send,
    join_recv,
    stat_send,
    stat_recv,
    last_send,
    last_recv,
    last_stat_send,
    last_stat_recv,
):
    block = q_ref.shape[0] // 2
    rows = q_ref.shape[1]
    slots = k_buf.shape[0]
    half_rows = rows // 2
    me = lax.axis_index("req")
    place = (me // side, lax.rem(me, side))
    turn = 1 - 2 * lax.rem(lax.axis_index("head"), 2)

    def shifted(axis, delta):
        moved = lax.rem(place[axis] + side + delta, side)
        return moved * side + place[1] if axis == 0 else place[0] * side + moved

    def at(axis, delta):
        return lax.rem(place[axis] + side + delta, side)

    first = (0, 1)
    second = (1, 0)

    def spot(half, p2, p1):
        return pl.ds(((half * side + p2) * side + p1) * block, block)

    loads = [
        pltpu.make_async_copy(k_hbm, k_buf, load_sem.at[0]),
        pltpu.make_async_copy(v_hbm, v_buf, load_sem.at[1]),
    ]
    for load in loads:
        load.start()
    barrier = pltpu.get_barrier_semaphore()
    for axis in (0, 1):
        for delta in (1, -1):
            pl.semaphore_signal(
                barrier, inc=1, device_id={"req": shifted(axis, delta)}, device_id_type=MESH
            )
    pl.semaphore_wait(barrier, 4)

    sends = []

    def go(copy):
        copy.start()
        sends.append(copy)
        return copy

    def pass_block(half, axis, delta, p2, p1, send, recv, own=False):
        view = q_all.at[spot(half, p2, p1)]
        source = q_ref.at[pl.ds(half * block, block)] if own else view
        return go(remote(source, view, send, recv, shifted(axis, delta)))

    lines = {}
    crosses = {}

    def line(half, index, delta, p1, own=False):
        lines[half, index] = pass_block(
            half, first[half], delta, at(second[half], 0), p1,
            gather_send.at[half, index], gather_recv.at[half, index], own,
        )

    def cross(half, piece, index, delta, p2, p1, own=False):
        crosses[half, piece, index] = pass_block(
            half, second[half], delta, p2, p1,
            spread_send.at[half, piece, index], spread_recv.at[half, piece, index], own,
        )

    halves = (0, 1)
    for half in halves:
        line(half, 0, turn, at(first[half], 0), True)
        line(half, 1, -turn, at(first[half], 0), True)
    for half in halves:
        cross(half, 0, 0, turn, at(second[half], 0), at(first[half], 0), True)
        cross(half, 0, 1, -turn, at(second[half], 0), at(first[half], 0), True)
    for half in halves:
        q_all[spot(half, at(second[half], 0), at(first[half], 0))] = q_ref[
            half * block : (half + 1) * block
        ]
    seg_top[...] = jnp.full(seg_top.shape, NEG_FILL, jnp.float32)
    seg_den[...] = jnp.zeros(seg_den.shape, jnp.float32)
    seg_acc[slots] = jnp.zeros(seg_acc.shape[1:], seg_acc.dtype)
    for half in halves:
        lines[half, 0].wait_recv()
        line(half, 2, turn, at(first[half], -turn))
        cross(half, 1, 0, turn, at(second[half], 0), at(first[half], -turn))
        cross(half, 1, 1, -turn, at(second[half], 0), at(first[half], -turn))
    for half in halves:
        lines[half, 1].wait_recv()
        cross(half, 2, 0, turn, at(second[half], 0), at(first[half], turn))
        cross(half, 2, 1, -turn, at(second[half], 0), at(first[half], turn))
    for half in halves:
        crosses[half, 0, 0].wait_recv()
        cross(half, 0, 2, turn, at(second[half], -turn), at(first[half], 0))
    for half in halves:
        lines[half, 2].wait_recv()
        cross(half, 3, 0, turn, at(second[half], 0), at(first[half], 2))
        cross(half, 3, 1, -turn, at(second[half], 0), at(first[half], 2))
    for piece, delta in ((1, -turn), (2, turn), (3, 2)):
        for half in halves:
            crosses[half, piece, 0].wait_recv()
            cross(half, piece, 2, turn, at(second[half], -turn), at(first[half], delta))
    for piece in range(4):
        for half in halves:
            crosses[half, piece, 1].wait_recv()
            crosses[half, piece, 2].wait_recv()
    for load in loads:
        load.wait()

    slot_mask = (1 << SLOT_BITS) - 1
    fill_mask = (1 << FILL_BITS) - 1
    requests = 2 * block * side * side

    def owner_at(index):
        return table[index] >> (SLOT_BITS + FILL_BITS)

    def starts_new(index):
        before = owner_at(jnp.maximum(index - 1, 0))
        return jnp.logical_or(index == 0, before != owner_at(index))

    shape = (k_buf.shape[1], rows)
    row_ids = lax.broadcasted_iota(jnp.int32, shape, 0)
    col_head = (lax.broadcasted_iota(jnp.int32, shape, 1) >= half_rows).astype(jnp.int32)
    matched = (row_ids & 1) == col_head
    key_ids = row_ids >> 1
    unroll = 4

    def score_step(group, carry):
        for offset in range(unroll):
            index = group * unroll + offset
            entry = table[index]
            fill = (entry >> SLOT_BITS) & fill_mask
            owner = jnp.minimum(entry >> (SLOT_BITS + FILL_BITS), requests - 1)
            home = owner // (2 * block)
            within = lax.rem(owner, 2 * block)
            half = within // block
            hx = home // side
            hy = lax.rem(home, side)
            outer = jnp.where(half == 0, hy, hx)
            inner = jnp.where(half == 0, hx, hy)
            row = ((half * side + outer) * side + inner) * block + lax.rem(within, block)
            found = lax.dot_general(
                k_buf[entry & slot_mask],
                q_all[row],
                (((1,), (1,)), ((), ())),
                preferred_element_type=jnp.float32,
            )
            found = jnp.where(jnp.logical_and(matched, key_ids < fill), found, NEG_FILL)
            scores[index] = found
            seg_top[index, :, 0:rows] = jnp.max(found, axis=0, keepdims=True)
        return carry

    lax.fori_loop(0, slots // unroll, score_step, 0)

    def forward(index, run):
        here = seg_top[index]
        run = jnp.where(starts_new(index), here, jnp.maximum(run, here))
        seg_top[index] = run
        return run

    lax.fori_loop(0, slots, forward, jnp.full(seg_top.shape[1:], NEG_FILL, jnp.float32))

    def backward(step, run):
        index = slots - 1 - step
        follow = jnp.minimum(index + 1, slots - 1)
        ends = jnp.logical_or(step == 0, owner_at(follow) != owner_at(index))
        run = jnp.where(ends, seg_top[index], run)
        seg_top[index] = run
        return run

    lax.fori_loop(0, slots, backward, jnp.full(seg_top.shape[1:], NEG_FILL, jnp.float32))

    def value_step(group, carry):
        acc_run, den_run = carry
        for offset in range(unroll):
            index = group * unroll + offset
            fresh = starts_new(index)
            top = seg_top[index][:, 0:rows]
            top = jnp.where(top < 0.5 * NEG_FILL, 0.0, top)
            weight = jnp.exp(scores[index] - top)
            den = jnp.sum(weight, axis=0, keepdims=True)
            acc = lax.dot_general(
                weight.astype(jnp.bfloat16),
                v_buf[table[index] & slot_mask],
                (((0,), (0,)), ((), ())),
                preferred_element_type=jnp.float32,
            )
            acc_run = acc + jnp.where(fresh, 0.0, acc_run)
            den_run = den + jnp.where(fresh, 0.0, den_run)
            seg_acc[index] = acc_run.astype(seg_acc.dtype)
            seg_den[index, :, 0:rows] = den_run
        return acc_run, den_run

    lax.fori_loop(
        0,
        slots // unroll,
        value_step,
        (jnp.zeros(seg_acc.shape[1:], jnp.float32), jnp.zeros((1, rows), jnp.float32)),
    )

    def place_step(group, carry):
        for piece in range(side):
            tops, dens = [], []
            for offset in range(block):
                spot_index = (group * side + piece) * block + offset
                found = last[spot_index]
                parts[spot_index] = seg_acc[found]
                tops.append(seg_top[found])
                dens.append(seg_den[found])
            stats[group, 0, piece * block : (piece + 1) * block] = jnp.concatenate(tops, axis=0)
            stats[group, 1, piece * block : (piece + 1) * block] = jnp.concatenate(dens, axis=0)
        return carry

    lax.fori_loop(0, 2 * side, place_step, 0)

    def part(half, p2, p1):
        return parts.at[spot(half, p2, p1)]

    def stat(half, p2):
        return stats.at[half * side + p2]

    def combine(put, terms, weights):
        columns = [jnp.transpose(weight) for weight in weights]
        for item in range(block):
            total = None
            for term, column in zip(terms, columns):
                value = term[item].astype(jnp.float32) * column[0:rows, item : item + 1]
                total = value if total is None else total + value
            put(item, total)

    stat_copies = {}
    far, near = {}, {}
    for half in halves:
        up, down = shifted(second[half], turn), shifted(second[half], -turn)
        stat_copies[half, 0] = go(
            remote(stat(half, at(second[half], 2)), relay_s.at[half],
                   stat_send.at[half, 0], stat_recv.at[half, 0], up))
        stat_copies[half, 1] = go(
            remote(stat(half, at(second[half], -turn)), single_s.at[half],
                   stat_send.at[half, 1], stat_recv.at[half, 1], down))
    for order in range(4):
        for half in halves:
            up, down = shifted(second[half], turn), shifted(second[half], -turn)
            p1 = at(first[half], 2 - turn * order)
            far[half, order] = go(
                remote(part(half, at(second[half], 2), p1), relay.at[half, p1],
                       far_send.at[half, order], far_recv.at[half, order], up))
            near[half, order] = go(
                remote(part(half, at(second[half], -turn), p1), single.at[half, p1],
                       near_send.at[half, order], near_recv.at[half, order], down))

    for half in halves:
        stat_copies[half, 0].wait_recv()
        mine = stat(half, at(second[half], turn))
        top, den, weights = weigh([mine[0], relay_s[half, 0]], [mine[1], relay_s[half, 1]])
        outgoing_s[half, 0] = top
        outgoing_s[half, 1] = den
        factors[half, 0] = weights[0]
        factors[half, 1] = weights[1]
        stat_copies[half, 2] = go(
            remote(outgoing_s.at[half], merged_s.at[half],
                   stat_send.at[half, 2], stat_recv.at[half, 2], shifted(second[half], turn)))

    def join_copy(half, order):
        p1 = at(first[half], 2 - turn * order)
        return remote(relay.at[half, p1], merged.at[half, p1],
                      join_send.at[half, order], join_recv.at[half, order],
                      shifted(second[half], turn))

    def far_copy(half, order):
        p1 = at(first[half], 2 - turn * order)
        return remote(part(half, at(second[half], 2), p1), relay.at[half, p1],
                      far_send.at[half, order], far_recv.at[half, order],
                      shifted(second[half], turn))

    def near_copy(half, order):
        p1 = at(first[half], 2 - turn * order)
        return remote(part(half, at(second[half], -turn), p1), single.at[half, p1],
                      near_send.at[half, order], near_recv.at[half, order],
                      shifted(second[half], -turn))

    def relay_step(order, carry):
        for half in halves:
            p1 = at(first[half], 2 + side - turn * order)
            far_copy(half, order).wait_recv()
            lanes = pl.ds(p1 * block, block)
            target = relay.at[half, p1]

            def put(item, value):
                target[item] = value.astype(target.dtype)

            combine(
                put,
                [part(half, at(second[half], turn), p1), target],
                [factors[half, 0, lanes], factors[half, 1, lanes]],
            )
            join_copy(half, order).start()
        return carry

    lax.fori_loop(0, 4, relay_step, 0)

    for half in halves:
        stat_copies[half, 1].wait_recv()
        stat_copies[half, 2].wait_recv()
        mine = stat(half, at(second[half], 0))
        top, den, weights = weigh(
            [mine[0], merged_s[half, 0], single_s[half, 0]],
            [mine[1], merged_s[half, 1], single_s[half, 1]],
        )
        for index in range(3):
            factors[half, index] = weights[index]
        for p1 in range(side):
            small_s[half, p1, 0] = top[p1 * block : (p1 + 1) * block]
            small_s[half, p1, 1] = den[p1 * block : (p1 + 1) * block]

    def gather_piece(half, order):
        p1 = at(first[half], 2 + side - turn * order)
        near_copy(half, order).wait_recv()
        join_copy(half, order).wait_recv()
        lanes = pl.ds(p1 * block, block)
        target = small.at[half, p1]

        def put(item, value):
            target[item] = value.astype(target.dtype)

        combine(
            put,
            [part(half, at(second[half], 0), p1), merged.at[half, p1], single.at[half, p1]],
            [factors[half, index, lanes] for index in range(3)],
        )

    def piece_step(order, carry):
        for half in halves:
            gather_piece(half, order)
        return carry

    tails = {}

    def tail(half, index, source, source_s, delta):
        peer = shifted(first[half], delta)
        tails[half, index] = (
            go(remote(source_s, hop_s.at[half, index],
                      last_stat_send.at[half, index], last_stat_recv.at[half, index], peer)),
            go(remote(source, hop.at[half, index],
                      last_send.at[half, index], last_recv.at[half, index], peer)),
        )

    lax.fori_loop(0, 1, piece_step, 0)
    for half in halves:
        p1 = at(first[half], 2)
        tail(half, 0, small.at[half, p1], small_s.at[half, p1], turn)
    lax.fori_loop(1, 2, piece_step, 0)
    for half in halves:
        p1 = at(first[half], -turn + 2 + 2)
    lax.fori_loop(2, 4, piece_step, 0)
    for half in halves:
        p1 = at(first[half], -turn)
        tail(half, 1, small.at[half, p1], small_s.at[half, p1], -turn)
    for half in halves:
        p1 = at(first[half], turn)
        for copy in tails[half, 0]:
            copy.wait_recv()
        target = small.at[half, p1]
        top, den, weights = weigh(
            [small_s[half, p1, 0], hop_s[half, 0, 0]], [small_s[half, p1, 1], hop_s[half, 0, 1]]
        )
        small_s[half, p1, 0] = top
        small_s[half, p1, 1] = den

        def put(item, value, target=target):
            target[item] = value.astype(target.dtype)

        combine(put, [target, hop.at[half, 0]], weights)
        tail(half, 2, target, small_s.at[half, p1], turn)
    for half in halves:
        p1 = at(first[half], 0)
        for index in (1, 2):
            for copy in tails[half, index]:
                copy.wait_recv()
        top, den, weights = weigh(
            [small_s[half, p1, 0], hop_s[half, 1, 0], hop_s[half, 2, 0]],
            [small_s[half, p1, 1], hop_s[half, 1, 1], hop_s[half, 2, 1]],
        )
        top_ref[half * block : (half + 1) * block] = top
        den_ref[half * block : (half + 1) * block] = den

        def put(item, value, half=half):
            num_ref[half * block + item] = value

        combine(put, [small.at[half, p1], hop.at[half, 1], hop.at[half, 2]], weights)
    for copy in sends:
        copy.wait_send()
    for half in halves:
        for order in range(4):
            join_copy(half, order).wait_send()


def cache_attention(queries, k_pages, v_pages, page_owner, page_fill):
    req_local, rows, head_dim = queries.shape
    slots, keys = k_pages.shape[0], k_pages.shape[1] * k_pages.shape[2]
    devices = lax.axis_size("req")
    side = math.isqrt(devices)
    block = req_local // 2
    requests = req_local * devices
    owner_key = jnp.where(page_owner < 0, requests, page_owner)
    packed = (
        (owner_key << (SLOT_BITS + FILL_BITS))
        | (jnp.where(page_owner < 0, 0, page_fill) << SLOT_BITS)
        | jnp.arange(slots, dtype=jnp.int32)
    )
    rank = jnp.sum((packed[None, :] < packed[:, None]).astype(jnp.int32), axis=1)
    places = jnp.arange(slots, dtype=jnp.int32)
    table = jnp.sum(jnp.where(rank[None, :] == places[:, None], packed[None, :], 0), axis=1)
    spots = jnp.arange(requests, dtype=jnp.int32)
    half = spots // (requests // 2)
    outer = (spots // (block * side)) % side
    inner = (spots // block) % side
    home = jnp.where(half == 0, inner * side + outer, outer * side + inner)
    request = home * req_local + half * block + spots % block
    below = jnp.sum((owner_key[None, :] <= request[:, None]).astype(jnp.int32), axis=1)
    exact = jnp.sum((owner_key[None, :] == request[:, None]).astype(jnp.int32), axis=1)
    last = jnp.where(exact > 0, below - 1, slots)
    bf16, f32 = jnp.bfloat16, jnp.float32
    unit = (2, side, block, rows, head_dim)
    dma = pltpu.SemaphoreType.DMA
    scratch = [
        pltpu.VMEM((requests, rows, head_dim), bf16),
        pltpu.VMEM((slots, keys, head_dim), bf16),
        pltpu.VMEM((slots, keys, head_dim), bf16),
        pltpu.VMEM((slots, keys, rows), f32),
        pltpu.VMEM((slots + 1, rows, head_dim), bf16),
        pltpu.VMEM((slots + 1, 1, 128), f32),
        pltpu.VMEM((slots + 1, 1, 128), f32),
        pltpu.VMEM((requests, rows, head_dim), bf16),
        pltpu.VMEM((2 * side, 2, side * block, 128), f32),
        pltpu.VMEM(unit, bf16),
        pltpu.VMEM(unit, bf16),
        pltpu.VMEM(unit, bf16),
        pltpu.VMEM((2, 2, side * block, 128), f32),
        pltpu.VMEM((2, 2, side * block, 128), f32),
        pltpu.VMEM((2, 2, side * block, 128), f32),
        pltpu.VMEM((2, 2, side * block, 128), f32),
        pltpu.VMEM((2, 3, side * block, 128), f32),
        pltpu.VMEM(unit, bf16),
        pltpu.VMEM((2, side, 2, block, 128), f32),
        pltpu.VMEM((2, 3, block, rows, head_dim), bf16),
        pltpu.VMEM((2, 3, 2, block, 128), f32),
        dma((2, 3)), dma((2, 3)),
        dma((2, 4, 3)), dma((2, 4, 3)),
        dma((2,)),
        dma((2, 4)), dma((2, 4)),
        dma((2, 4)), dma((2, 4)),
        dma((2, 4)), dma((2, 4)),
        dma((2, 3)), dma((2, 3)),
        dma((2, 3)), dma((2, 3)),
        dma((2, 3)), dma((2, 3)),
    ]
    vmem = pl.BlockSpec(memory_space=pltpu.VMEM)
    smem = pl.BlockSpec(memory_space=pltpu.SMEM)
    anywhere = pl.BlockSpec(memory_space=pl.ANY)
    return pl.pallas_call(
        functools.partial(cache_kernel, side),
        out_shape=(
            jax.ShapeDtypeStruct((req_local, rows, head_dim), f32),
            jax.ShapeDtypeStruct((req_local, 128), f32),
            jax.ShapeDtypeStruct((req_local, 128), f32),
        ),
        in_specs=[smem, smem, vmem, anywhere, anywhere],
        out_specs=(vmem, vmem, vmem),
        scratch_shapes=scratch,
        compiler_params=pltpu.CompilerParams(
            collective_id=0, has_side_effects=True, vmem_limit_bytes=56 << 20
        ),
    )(
        table,
        last,
        queries,
        k_pages.reshape(slots, keys, head_dim),
        v_pages.reshape(slots, keys, head_dim),
    )


def on_device(
    streams,
    hc_in,
    hc_mix,
    hc_out,
    qkv_weight,
    out_weight,
    up_gate,
    down_weight,
    draft_weight,
    lm_head,
    k_pages,
    v_pages,
    page_owner,
    page_fill,
    cache_len,
    tree_parent,
    accepted_index,
):
    tokens_local = streams.shape[0]
    feature_local = streams.shape[2]
    width = qkv_weight.shape[0]
    req_local = cache_len.shape[0]
    tree_size = tree_parent.shape[1]
    slot_count = k_pages.shape[0]
    page_size = k_pages.shape[1]
    heads_local = k_pages.shape[2]
    head_dim = k_pages.shape[3]
    draft_count = draft_weight.shape[0]
    all_requests = req_local * lax.axis_size("req")
    reach = ancestors(tree_parent)
    depth = (jnp.sum(reach, axis=2) - 1.0).astype(jnp.int32)
    positions = (cache_len[:, None] + depth).reshape(tokens_local)
    stream_vals = streams.astype(jnp.float32)
    mixed_in = blend(stream_vals, hc_in[0])
    stat_sum, stat_square = lax.psum(
        (jnp.sum(mixed_in, axis=1), jnp.sum(mixed_in * mixed_in, axis=1)), "head"
    )
    normed = normalize(mixed_in, stat_sum[:, None], stat_square[:, None], width).astype(
        jnp.bfloat16
    )
    qkv_flat = qkv_weight.reshape(width, -1)
    projected = fold_rows(qkv_flat, lax.all_gather(normed, "head", axis=1, tiled=True))
    projected = projected.reshape(tokens_local, 3, heads_local, head_dim)
    queries = (rotate(projected[:, 0], positions) * head_dim ** (-0.5)).astype(jnp.bfloat16)
    keys_new = rotate(projected[:, 1], positions).astype(jnp.bfloat16)
    values_new = projected[:, 2].astype(jnp.bfloat16)
    query_rows = (
        queries.reshape(req_local, tree_size, heads_local, head_dim)
        .transpose(0, 2, 1, 3)
        .reshape(req_local, heads_local * tree_size, head_dim)
    )
    own_sum, own_top, own_den = cache_attention(
        query_rows, k_pages, v_pages, page_owner, page_fill
    )
    own_sum = own_sum.reshape(req_local, heads_local, tree_size, head_dim).transpose(0, 2, 1, 3)
    used = heads_local * tree_size
    own_top = own_top[:, :used].reshape(req_local, heads_local, tree_size).transpose(0, 2, 1)
    own_den = own_den[:, :used].reshape(req_local, heads_local, tree_size).transpose(0, 2, 1)
    query_own = queries.reshape(req_local, tree_size, heads_local, head_dim)
    keys_own = keys_new.reshape(req_local, tree_size, heads_local, head_dim)
    values_own = values_new.reshape(req_local, tree_size, heads_local, head_dim)
    tree_scores = jnp.einsum(
        "jqhd,jkhd->jqhk", query_own, keys_own, preferred_element_type=jnp.float32
    )
    tree_mask = (reach > 0)[:, :, None, :]
    tree_scores = jnp.where(tree_mask, tree_scores, NEG_FILL)
    top = jnp.maximum(own_top, jnp.max(tree_scores, axis=3))
    carried = jnp.exp(own_top - top)
    tree_weights = jnp.where(tree_mask, jnp.exp(tree_scores - top[..., None]), 0.0)
    denominator = own_den * carried + jnp.sum(tree_weights, axis=3)
    numerator = own_sum * carried[..., None] + jnp.einsum(
        "jqhk,jkhd->jqhd",
        tree_weights.astype(jnp.bfloat16),
        values_own,
        preferred_element_type=jnp.float32,
    )
    attended = (
        (numerator / denominator[..., None])
        .astype(jnp.bfloat16)
        .reshape(tokens_local, heads_local * head_dim)
    )
    attn_delta = lax.psum_scatter(
        jnp.dot(attended, out_weight, preferred_element_type=jnp.float32).astype(jnp.bfloat16),
        "head",
        scatter_dimension=1,
        tiled=True,
    ).astype(jnp.float32)
    first_streams = remix(stream_vals, hc_mix[0], hc_out[0], attn_delta)
    mixed_mid = blend(first_streams, hc_in[1])
    mid_sum, mid_square = lax.psum(
        (jnp.sum(mixed_mid, axis=1), jnp.sum(mixed_mid * mixed_mid, axis=1)), "head"
    )
    normed_mid = normalize(mixed_mid, mid_sum[:, None], mid_square[:, None], width).astype(
        jnp.bfloat16
    )
    gate_up_flat = up_gate.reshape(width, -1)
    hidden_local = gate_up_flat.shape[1] // 2
    gate_up = fold_rows(gate_up_flat, lax.all_gather(normed_mid, "head", axis=1, tiled=True))
    hidden = (jax.nn.silu(gate_up[:, :hidden_local]) * gate_up[:, hidden_local:]).astype(
        jnp.bfloat16
    )
    mlp_delta = lax.psum_scatter(
        jnp.dot(hidden, down_weight, preferred_element_type=jnp.float32).astype(jnp.bfloat16),
        "head",
        scatter_dimension=1,
        tiled=True,
    ).astype(jnp.float32)
    second_streams = remix(first_streams, hc_mix[1], hc_out[1], mlp_delta)
    new_streams = second_streams.astype(jnp.bfloat16)
    rows_taken = jnp.arange(req_local, dtype=jnp.int32) * tree_size + accepted_index
    final_local = stream_total(second_streams[rows_taken])
    final_full = lax.all_gather(final_local, "head", axis=1, tiled=True)
    final_norm = layer_norm(final_full)
    own_columns = lax.dynamic_slice_in_dim(
        final_norm, lax.axis_index("head") * feature_local, feature_local, 1
    )
    branch = jnp.einsum(
        "jd,kde->jke",
        final_norm.astype(jnp.bfloat16),
        draft_weight,
        preferred_element_type=jnp.float32,
    )
    drafted = (own_columns[:, None, :] + jax.nn.silu(branch)).astype(jnp.bfloat16)
    draft_full = lax.all_gather(drafted, "head", axis=2, tiled=True)
    draft_all = lax.all_gather(draft_full, "req", axis=0, tiled=True)
    logits_local = jnp.dot(
        draft_all.reshape(-1, width), lm_head, preferred_element_type=jnp.float32
    )
    logits_local = logits_local.reshape(all_requests, draft_count, -1)
    logits = lax.all_to_all(
        logits_local.astype(jnp.bfloat16), ("req", "head"), split_axis=0, concat_axis=2, tiled=True
    ).astype(logits_local.dtype)
    return (new_streams, logits)


def solution(mesh):
    in_specs = (
        P("req", None, "head"),
        P(),
        P(),
        P(),
        P(None, None, "head"),
        P("head", None),
        P(None, None, "head"),
        P("head", None),
        P(None, None, "head"),
        P(None, ("req", "head")),
        P("req", None, "head", None),
        P("req", None, "head", None),
        P("req"),
        P("req"),
        P("req"),
        P("req", None),
        P("req"),
    )
    out_specs = (P("req", None, "head"), P(("req", "head"), None, None))
    return jax.shard_map(
        on_device, mesh=mesh, in_specs=in_specs, out_specs=out_specs, check_vma=False
    )
```

```python
import functools
import math

import jax
import jax.numpy as jnp
from jax import lax
from jax.experimental import pallas as pl
from jax.experimental.pallas import tpu as pltpu
from jax.sharding import PartitionSpec as P

NEG_FILL = -1e30
PRECISE = lax.Precision.HIGHEST


def layer_norm(values):
    center = jnp.mean(values, axis=-1, keepdims=True)
    square = jnp.mean(values * values, axis=-1, keepdims=True)
    return (values - center) * lax.rsqrt(square - center * center + 1e-05)


def normalize(values, sums, squares, width):
    center = sums / width
    return (values - center) * lax.rsqrt(squares / width - center * center + 1e-05)


def ancestors(parents):
    length = parents.shape[1]
    places = jnp.arange(length, dtype=jnp.int32)
    linked = (parents[:, :, None] == places[None, None, :]) | (places[:, None] == places[None, :])[
        None
    ]
    reach = linked.astype(jnp.float32)
    for repeat in range(max(1, (length - 1).bit_length())):
        reach = jnp.minimum(jnp.einsum("jik,jkl->jil", reach, reach, precision=PRECISE), 1.0)
    return reach


def rotate(values, positions):
    half = values.shape[-1] // 2
    freqs = jnp.exp(
        jnp.arange(half, dtype=jnp.float32) * (-2.0 * math.log(10000.0) / values.shape[-1])
    )
    angles = positions.astype(jnp.float32)[:, None] * freqs[None, :]
    cosine = jnp.cos(angles)[:, None, :]
    sine = jnp.sin(angles)[:, None, :]
    first = values[..., :half]
    second = values[..., half:]
    return jnp.concatenate(
        [first * cosine - second * sine, second * cosine + first * sine], axis=-1
    )


def blend(stream_vals, weights):
    total = weights[0] * stream_vals[:, 0]
    for index in range(1, stream_vals.shape[1]):
        total = total + weights[index] * stream_vals[:, index]
    return total


def remix(stream_vals, mixing, out_scale, delta):
    count = stream_vals.shape[1]
    matrix = jnp.eye(count, dtype=jnp.float32) + mixing
    rows = [
        blend(stream_vals, matrix[:, target]) + out_scale[target] * delta for target in range(count)
    ]
    return jnp.stack(rows, axis=1)


def stream_total(stream_vals):
    total = stream_vals[:, 0]
    for index in range(1, stream_vals.shape[1]):
        total = total + stream_vals[:, index]
    return total


def fold_rows(weight, piece):
    return jnp.dot(piece, weight, preferred_element_type=jnp.float32)


MESH = pl.DeviceIdType.MESH
SLOT_BITS = 6
FILL_BITS = 8


def remote(source, target, send_sem, recv_sem, req):
    return pltpu.make_async_remote_copy(
        src_ref=source,
        dst_ref=target,
        send_sem=send_sem,
        recv_sem=recv_sem,
        device_id={"req": req},
        device_id_type=MESH,
    )


def weigh(tops, totals):
    top = functools.reduce(jnp.maximum, tops)
    factors = [jnp.exp(value - top) for value in tops]
    total = functools.reduce(lambda a, b: a + b, [f * t for f, t in zip(factors, totals)])
    return top, total, factors


def cache_kernel(
    side,
    table,
    last,
    q_ref,
    k_hbm,
    v_hbm,
    num_ref,
    top_ref,
    den_ref,
    q_all,
    k_buf,
    v_buf,
    scores,
    seg_acc,
    seg_top,
    seg_den,
    parts,
    stats,
    relay,
    merged,
    single,
    relay_s,
    merged_s,
    single_s,
    outgoing_s,
    factors,
    small,
    small_s,
    hop,
    hop_s,
    gather_send,
    gather_recv,
    spread_send,
    spread_recv,
    load_sem,
    far_send,
    far_recv,
    near_send,
    near_recv,
    join_send,
    join_recv,
    stat_send,
    stat_recv,
    last_send,
    last_recv,
    last_stat_send,
    last_stat_recv,
):
    block = q_ref.shape[0] // 2
    rows = q_ref.shape[1]
    slots = k_buf.shape[0]
    half_rows = rows // 2
    me = lax.axis_index("req")
    place = (me // side, lax.rem(me, side))
    turn = 1 - 2 * lax.rem(lax.axis_index("head"), 2)

    def shifted(axis, delta):
        moved = lax.rem(place[axis] + side + delta, side)
        return moved * side + place[1] if axis == 0 else place[0] * side + moved

    def at(axis, delta):
        return lax.rem(place[axis] + side + delta, side)

    first = (0, 1)
    second = (1, 0)

    def spot(half, p2, p1):
        return pl.ds(((half * side + p2) * side + p1) * block, block)

    loads = [
        pltpu.make_async_copy(k_hbm, k_buf, load_sem.at[0]),
        pltpu.make_async_copy(v_hbm, v_buf, load_sem.at[1]),
    ]
    for load in loads:
        load.start()
    barrier = pltpu.get_barrier_semaphore()
    for axis in (0, 1):
        for delta in (1, -1):
            pl.semaphore_signal(
                barrier, inc=1, device_id={"req": shifted(axis, delta)}, device_id_type=MESH
            )
    pl.semaphore_wait(barrier, 4)

    sends = []

    def go(copy):
        copy.start()
        sends.append(copy)
        return copy

    def pass_block(half, axis, delta, p2, p1, send, recv, own=False):
        view = q_all.at[spot(half, p2, p1)]
        source = q_ref.at[pl.ds(half * block, block)] if own else view
        return go(remote(source, view, send, recv, shifted(axis, delta)))

    lines = {}
    crosses = {}

    def line(half, index, delta, p1, own=False):
        lines[half, index] = pass_block(
            half, first[half], delta, at(second[half], 0), p1,
            gather_send.at[half, index], gather_recv.at[half, index], own,
        )

    def cross(half, piece, index, delta, p2, p1, own=False):
        crosses[half, piece, index] = pass_block(
            half, second[half], delta, p2, p1,
            spread_send.at[half, piece, index], spread_recv.at[half, piece, index], own,
        )

    halves = (0, 1)
    for half in halves:
        line(half, 0, turn, at(first[half], 0), True)
        line(half, 1, -turn, at(first[half], 0), True)
    for half in halves:
        cross(half, 0, 0, turn, at(second[half], 0), at(first[half], 0), True)
        cross(half, 0, 1, -turn, at(second[half], 0), at(first[half], 0), True)
    for half in halves:
        q_all[spot(half, at(second[half], 0), at(first[half], 0))] = q_ref[
            half * block : (half + 1) * block
        ]
    seg_top[...] = jnp.full(seg_top.shape, NEG_FILL, jnp.float32)
    seg_den[...] = jnp.zeros(seg_den.shape, jnp.float32)
    seg_acc[slots] = jnp.zeros(seg_acc.shape[1:], seg_acc.dtype)
    for half in halves:
        lines[half, 0].wait_recv()
        line(half, 2, turn, at(first[half], -turn))
        cross(half, 1, 0, turn, at(second[half], 0), at(first[half], -turn))
        cross(half, 1, 1, -turn, at(second[half], 0), at(first[half], -turn))
    for half in halves:
        lines[half, 1].wait_recv()
        cross(half, 2, 0, turn, at(second[half], 0), at(first[half], turn))
        cross(half, 2, 1, -turn, at(second[half], 0), at(first[half], turn))
    for half in halves:
        crosses[half, 0, 0].wait_recv()
        cross(half, 0, 2, turn, at(second[half], -turn), at(first[half], 0))
    for half in halves:
        lines[half, 2].wait_recv()
        cross(half, 3, 0, turn, at(second[half], 0), at(first[half], 2))
        cross(half, 3, 1, -turn, at(second[half], 0), at(first[half], 2))
    for piece, delta in ((1, -turn), (2, turn), (3, 2)):
        for half in halves:
            crosses[half, piece, 0].wait_recv()
            cross(half, piece, 2, turn, at(second[half], -turn), at(first[half], delta))
    for piece in range(4):
        for half in halves:
            crosses[half, piece, 1].wait_recv()
            crosses[half, piece, 2].wait_recv()
    for load in loads:
        load.wait()

    slot_mask = (1 << SLOT_BITS) - 1
    fill_mask = (1 << FILL_BITS) - 1
    requests = 2 * block * side * side

    def owner_at(index):
        return table[index] >> (SLOT_BITS + FILL_BITS)

    def starts_new(index):
        before = owner_at(jnp.maximum(index - 1, 0))
        return jnp.logical_or(index == 0, before != owner_at(index))

    shape = (k_buf.shape[1], rows)
    row_ids = lax.broadcasted_iota(jnp.int32, shape, 0)
    col_head = (lax.broadcasted_iota(jnp.int32, shape, 1) >= half_rows).astype(jnp.int32)
    matched = (row_ids & 1) == col_head
    key_ids = row_ids >> 1
    unroll = 4

    def score_step(group, carry):
        for offset in range(unroll):
            index = group * unroll + offset
            entry = table[index]
            fill = (entry >> SLOT_BITS) & fill_mask
            owner = jnp.minimum(entry >> (SLOT_BITS + FILL_BITS), requests - 1)
            home = owner // (2 * block)
            within = lax.rem(owner, 2 * block)
            half = within // block
            hx = home // side
            hy = lax.rem(home, side)
            outer = jnp.where(half == 0, hy, hx)
            inner = jnp.where(half == 0, hx, hy)
            row = ((half * side + outer) * side + inner) * block + lax.rem(within, block)
            found = lax.dot_general(
                k_buf[entry & slot_mask],
                q_all[row],
                (((1,), (1,)), ((), ())),
                preferred_element_type=jnp.float32,
            )
            found = jnp.where(jnp.logical_and(matched, key_ids < fill), found, NEG_FILL)
            scores[index] = found
            seg_top[index, :, 0:rows] = jnp.max(found, axis=0, keepdims=True)
        return carry

    lax.fori_loop(0, slots // unroll, score_step, 0)

    def forward(index, run):
        here = seg_top[index]
        run = jnp.where(starts_new(index), here, jnp.maximum(run, here))
        seg_top[index] = run
        return run

    lax.fori_loop(0, slots, forward, jnp.full(seg_top.shape[1:], NEG_FILL, jnp.float32))

    def backward(step, run):
        index = slots - 1 - step
        follow = jnp.minimum(index + 1, slots - 1)
        ends = jnp.logical_or(step == 0, owner_at(follow) != owner_at(index))
        run = jnp.where(ends, seg_top[index], run)
        seg_top[index] = run
        return run

    lax.fori_loop(0, slots, backward, jnp.full(seg_top.shape[1:], NEG_FILL, jnp.float32))

    def value_step(group, carry):
        acc_run, den_run = carry
        for offset in range(unroll):
            index = group * unroll + offset
            fresh = starts_new(index)
            top = seg_top[index][:, 0:rows]
            top = jnp.where(top < 0.5 * NEG_FILL, 0.0, top)
            weight = jnp.exp(scores[index] - top)
            den = jnp.sum(weight, axis=0, keepdims=True)
            acc = lax.dot_general(
                weight.astype(jnp.bfloat16),
                v_buf[table[index] & slot_mask],
                (((0,), (0,)), ((), ())),
                preferred_element_type=jnp.float32,
            )
            acc_run = acc + jnp.where(fresh, 0.0, acc_run)
            den_run = den + jnp.where(fresh, 0.0, den_run)
            seg_acc[index] = acc_run.astype(seg_acc.dtype)
            seg_den[index, :, 0:rows] = den_run
        return acc_run, den_run

    lax.fori_loop(
        0,
        slots // unroll,
        value_step,
        (jnp.zeros(seg_acc.shape[1:], jnp.float32), jnp.zeros((1, rows), jnp.float32)),
    )

    def place_step(group, carry):
        for piece in range(side):
            tops, dens = [], []
            for offset in range(block):
                spot_index = (group * side + piece) * block + offset
                found = last[spot_index]
                parts[spot_index] = seg_acc[found]
                tops.append(seg_top[found])
                dens.append(seg_den[found])
            stats[group, 0, piece * block : (piece + 1) * block] = jnp.concatenate(tops, axis=0)
            stats[group, 1, piece * block : (piece + 1) * block] = jnp.concatenate(dens, axis=0)
        return carry

    lax.fori_loop(0, 2 * side, place_step, 0)

    def part(half, p2, p1):
        return parts.at[spot(half, p2, p1)]

    def stat(half, p2):
        return stats.at[half * side + p2]

    def combine(put, terms, weights):
        columns = [jnp.transpose(weight) for weight in weights]
        for item in range(block):
            total = None
            for term, column in zip(terms, columns):
                value = term[item].astype(jnp.float32) * column[0:rows, item : item + 1]
                total = value if total is None else total + value
            put(item, total)

    stat_copies = {}
    far, near = {}, {}
    for half in halves:
        up, down = shifted(second[half], turn), shifted(second[half], -turn)
        stat_copies[half, 0] = go(
            remote(stat(half, at(second[half], 2)), relay_s.at[half],
                   stat_send.at[half, 0], stat_recv.at[half, 0], up))
        stat_copies[half, 1] = go(
            remote(stat(half, at(second[half], -turn)), single_s.at[half],
                   stat_send.at[half, 1], stat_recv.at[half, 1], down))
    for order in range(4):
        for half in halves:
            up, down = shifted(second[half], turn), shifted(second[half], -turn)
            p1 = at(first[half], 2 - turn * order)
            far[half, order] = go(
                remote(part(half, at(second[half], 2), p1), relay.at[half, p1],
                       far_send.at[half, order], far_recv.at[half, order], up))
            near[half, order] = go(
                remote(part(half, at(second[half], -turn), p1), single.at[half, p1],
                       near_send.at[half, order], near_recv.at[half, order], down))

    for half in halves:
        stat_copies[half, 0].wait_recv()
        mine = stat(half, at(second[half], turn))
        top, den, weights = weigh([mine[0], relay_s[half, 0]], [mine[1], relay_s[half, 1]])
        outgoing_s[half, 0] = top
        outgoing_s[half, 1] = den
        factors[half, 0] = weights[0]
        factors[half, 1] = weights[1]
        stat_copies[half, 2] = go(
            remote(outgoing_s.at[half], merged_s.at[half],
                   stat_send.at[half, 2], stat_recv.at[half, 2], shifted(second[half], turn)))

    def join_copy(half, order):
        p1 = at(first[half], 2 - turn * order)
        return remote(relay.at[half, p1], merged.at[half, p1],
                      join_send.at[half, order], join_recv.at[half, order],
                      shifted(second[half], turn))

    def far_copy(half, order):
        p1 = at(first[half], 2 - turn * order)
        return remote(part(half, at(second[half], 2), p1), relay.at[half, p1],
                      far_send.at[half, order], far_recv.at[half, order],
                      shifted(second[half], turn))

    def near_copy(half, order):
        p1 = at(first[half], 2 - turn * order)
        return remote(part(half, at(second[half], -turn), p1), single.at[half, p1],
                      near_send.at[half, order], near_recv.at[half, order],
                      shifted(second[half], -turn))

    def relay_step(order, carry):
        for half in halves:
            p1 = at(first[half], 2 + side - turn * order)
            far_copy(half, order).wait_recv()
            lanes = pl.ds(p1 * block, block)
            target = relay.at[half, p1]

            def put(item, value):
                target[item] = value.astype(target.dtype)

            combine(
                put,
                [part(half, at(second[half], turn), p1), target],
                [factors[half, 0, lanes], factors[half, 1, lanes]],
            )
            join_copy(half, order).start()
        return carry

    lax.fori_loop(0, 4, relay_step, 0)

    for half in halves:
        stat_copies[half, 1].wait_recv()
        stat_copies[half, 2].wait_recv()
        mine = stat(half, at(second[half], 0))
        top, den, weights = weigh(
            [mine[0], merged_s[half, 0], single_s[half, 0]],
            [mine[1], merged_s[half, 1], single_s[half, 1]],
        )
        for index in range(3):
            factors[half, index] = weights[index]
        for p1 in range(side):
            small_s[half, p1, 0] = top[p1 * block : (p1 + 1) * block]
            small_s[half, p1, 1] = den[p1 * block : (p1 + 1) * block]

    def gather_piece(half, order):
        p1 = at(first[half], 2 + side - turn * order)
        near_copy(half, order).wait_recv()
        join_copy(half, order).wait_recv()
        lanes = pl.ds(p1 * block, block)
        target = small.at[half, p1]

        def put(item, value):
            target[item] = value.astype(target.dtype)

        combine(
            put,
            [part(half, at(second[half], 0), p1), merged.at[half, p1], single.at[half, p1]],
            [factors[half, index, lanes] for index in range(3)],
        )

    def piece_step(order, carry):
        for half in halves:
            gather_piece(half, order)
        return carry

    tails = {}

    def tail(half, index, source, source_s, delta):
        peer = shifted(first[half], delta)
        tails[half, index] = (
            go(remote(source_s, hop_s.at[half, index],
                      last_stat_send.at[half, index], last_stat_recv.at[half, index], peer)),
            go(remote(source, hop.at[half, index],
                      last_send.at[half, index], last_recv.at[half, index], peer)),
        )

    lax.fori_loop(0, 1, piece_step, 0)
    for half in halves:
        p1 = at(first[half], 2)
        tail(half, 0, small.at[half, p1], small_s.at[half, p1], turn)
    lax.fori_loop(1, 2, piece_step, 0)
    for half in halves:
        p1 = at(first[half], -turn + 2 + 2)
    lax.fori_loop(2, 4, piece_step, 0)
    for half in halves:
        p1 = at(first[half], -turn)
        tail(half, 1, small.at[half, p1], small_s.at[half, p1], -turn)
    for half in halves:
        p1 = at(first[half], turn)
        for copy in tails[half, 0]:
            copy.wait_recv()
        target = small.at[half, p1]
        top, den, weights = weigh(
            [small_s[half, p1, 0], hop_s[half, 0, 0]], [small_s[half, p1, 1], hop_s[half, 0, 1]]
        )
        small_s[half, p1, 0] = top
        small_s[half, p1, 1] = den

        def put(item, value, target=target):
            target[item] = value.astype(target.dtype)

        combine(put, [target, hop.at[half, 0]], weights)
        tail(half, 2, target, small_s.at[half, p1], turn)
    for half in halves:
        p1 = at(first[half], 0)
        for index in (1, 2):
            for copy in tails[half, index]:
                copy.wait_recv()
        top, den, weights = weigh(
            [small_s[half, p1, 0], hop_s[half, 1, 0], hop_s[half, 2, 0]],
            [small_s[half, p1, 1], hop_s[half, 1, 1], hop_s[half, 2, 1]],
        )
        top_ref[half * block : (half + 1) * block] = top
        den_ref[half * block : (half + 1) * block] = den

        def put(item, value, half=half):
            num_ref[half * block + item] = value

        combine(put, [small.at[half, p1], hop.at[half, 1], hop.at[half, 2]], weights)
    for copy in sends:
        copy.wait_send()
    for half in halves:
        for order in range(4):
            join_copy(half, order).wait_send()


def cache_attention(queries, k_pages, v_pages, page_owner, page_fill):
    req_local, rows, head_dim = queries.shape
    slots, keys = k_pages.shape[0], k_pages.shape[1] * k_pages.shape[2]
    devices = lax.axis_size("req")
    side = math.isqrt(devices)
    block = req_local // 2
    requests = req_local * devices
    owner_key = jnp.where(page_owner < 0, requests, page_owner)
    packed = (
        (owner_key << (SLOT_BITS + FILL_BITS))
        | (jnp.where(page_owner < 0, 0, page_fill) << SLOT_BITS)
        | jnp.arange(slots, dtype=jnp.int32)
    )
    rank = jnp.sum((packed[None, :] < packed[:, None]).astype(jnp.int32), axis=1)
    places = jnp.arange(slots, dtype=jnp.int32)
    table = jnp.sum(jnp.where(rank[None, :] == places[:, None], packed[None, :], 0), axis=1)
    spots = jnp.arange(requests, dtype=jnp.int32)
    half = spots // (requests // 2)
    outer = (spots // (block * side)) % side
    inner = (spots // block) % side
    home = jnp.where(half == 0, inner * side + outer, outer * side + inner)
    request = home * req_local + half * block + spots % block
    below = jnp.sum((owner_key[None, :] <= request[:, None]).astype(jnp.int32), axis=1)
    exact = jnp.sum((owner_key[None, :] == request[:, None]).astype(jnp.int32), axis=1)
    last = jnp.where(exact > 0, below - 1, slots)
    bf16, f32 = jnp.bfloat16, jnp.float32
    unit = (2, side, block, rows, head_dim)
    dma = pltpu.SemaphoreType.DMA
    scratch = [
        pltpu.VMEM((requests, rows, head_dim), bf16),
        pltpu.VMEM((slots, keys, head_dim), bf16),
        pltpu.VMEM((slots, keys, head_dim), bf16),
        pltpu.VMEM((slots, keys, rows), f32),
        pltpu.VMEM((slots + 1, rows, head_dim), bf16),
        pltpu.VMEM((slots + 1, 1, 128), f32),
        pltpu.VMEM((slots + 1, 1, 128), f32),
        pltpu.VMEM((requests, rows, head_dim), bf16),
        pltpu.VMEM((2 * side, 2, side * block, 128), f32),
        pltpu.VMEM(unit, bf16),
        pltpu.VMEM(unit, bf16),
        pltpu.VMEM(unit, bf16),
        pltpu.VMEM((2, 2, side * block, 128), f32),
        pltpu.VMEM((2, 2, side * block, 128), f32),
        pltpu.VMEM((2, 2, side * block, 128), f32),
        pltpu.VMEM((2, 2, side * block, 128), f32),
        pltpu.VMEM((2, 3, side * block, 128), f32),
        pltpu.VMEM(unit, bf16),
        pltpu.VMEM((2, side, 2, block, 128), f32),
        pltpu.VMEM((2, 3, block, rows, head_dim), bf16),
        pltpu.VMEM((2, 3, 2, block, 128), f32),
        dma((2, 3)), dma((2, 3)),
        dma((2, 4, 3)), dma((2, 4, 3)),
        dma((2,)),
        dma((2, 4)), dma((2, 4)),
        dma((2, 4)), dma((2, 4)),
        dma((2, 4)), dma((2, 4)),
        dma((2, 3)), dma((2, 3)),
        dma((2, 3)), dma((2, 3)),
        dma((2, 3)), dma((2, 3)),
    ]
    vmem = pl.BlockSpec(memory_space=pltpu.VMEM)
    smem = pl.BlockSpec(memory_space=pltpu.SMEM)
    anywhere = pl.BlockSpec(memory_space=pl.ANY)
    return pl.pallas_call(
        functools.partial(cache_kernel, side),
        out_shape=(
            jax.ShapeDtypeStruct((req_local, rows, head_dim), f32),
            jax.ShapeDtypeStruct((req_local, 128), f32),
            jax.ShapeDtypeStruct((req_local, 128), f32),
        ),
        in_specs=[smem, smem, vmem, anywhere, anywhere],
        out_specs=(vmem, vmem, vmem),
        scratch_shapes=scratch,
        compiler_params=pltpu.CompilerParams(
            collective_id=0, has_side_effects=True, vmem_limit_bytes=56 << 20
        ),
    )(
        table,
        last,
        queries,
        k_pages.reshape(slots, keys, head_dim),
        v_pages.reshape(slots, keys, head_dim),
    )


def transpose_sum(values):
    half = values.shape[1] // 2
    return jnp.sum(jnp.transpose(values[:, 0:half] + values[:, half:]), axis=0, keepdims=True)


def layer_kernel(
    chips,
    chunks,
    hc_in,
    hc_mix,
    hc_out,
    accepted,
    attended,
    streams,
    out_hbm,
    gate_hbm,
    down_hbm,
    fresh_ref,
    final_ref,
    out_buf,
    gate_buf,
    down_buf,
    first_buf,
    mixed_buf,
    total_buf,
    share,
    twin,
    relay,
    joined,
    single,
    stat_all,
    columns,
    normed,
    gathered,
    hidden,
    load_sem,
    own_sem,
    twin_send,
    twin_recv,
    ring_send,
    ring_recv,
    stat_send,
    stat_recv,
    copy_send,
    copy_recv,
    pass_send,
    pass_recv,
):
    tokens, feature = attended.shape
    size = tokens // chunks
    group = 2 * chips
    width = group * feature
    count = streams.shape[0]
    inner = hidden.shape[1]
    strips = inner // feature
    me = lax.axis_index("head")
    chip = me // 2
    core = lax.rem(me, 2)
    turn = 1 - 2 * core

    def at(delta):
        return lax.rem(chip + chips + delta, chips)

    def peer(delta):
        return at(delta) * 2 + core

    sibling = chip * 2 + 1 - core

    def send_to(source, target, send_sem, recv_sem, head):
        return pltpu.make_async_remote_copy(
            src_ref=source,
            dst_ref=target,
            send_sem=send_sem,
            recv_sem=recv_sem,
            device_id={"head": head},
            device_id_type=MESH,
        )

    loads = []
    for index in range(group):
        loads.append(
            pltpu.make_async_copy(
                out_hbm.at[:, pl.ds(index * feature, feature)], out_buf.at[index], load_sem.at[0, index]
            )
        )
    for index in range(2 * strips):
        kind, strip = index // strips, index % strips
        loads.append(
            pltpu.make_async_copy(
                gate_hbm.at[kind, :, pl.ds(strip * feature, feature)],
                gate_buf.at[index],
                load_sem.at[1, index],
            )
        )
    for index in range(group):
        loads.append(
            pltpu.make_async_copy(
                down_hbm.at[:, pl.ds(index * feature, feature)], down_buf.at[index], load_sem.at[2, index]
            )
        )
    for load in loads:
        load.start()
    barrier = pltpu.get_barrier_semaphore()
    for step in range(1, group):
        pl.semaphore_signal(
            barrier, inc=1, device_id={"head": lax.rem(me + step, group)}, device_id_type=MESH
        )
    pl.semaphore_wait(barrier, group - 1)

    sends = []

    def go(copy):
        copy.start()
        sends.append(copy)
        return copy

    offsets = (2, 1, 3, 0)
    waits = {}

    def chunk_rows(t):
        return pl.ds(t * size, size)

    def lanes(head):
        return pl.ds(pl.multiple_of(head * feature, feature), feature)

    def scatter(which, t, product):
        for k, offset in enumerate(offsets):
            target = at(offset)
            piece = share.at[which, t, 1 - core, target]
            piece[...] = product(target * 2 + 1 - core).astype(piece.dtype)
            waits["twin", which, t, k] = go(
                send_to(piece, twin.at[which, t, target], twin_send.at[which, t, k],
                        twin_recv.at[which, t, k], sibling))
        for offset in offsets:
            target = at(offset)
            piece = share.at[which, t, core, target]
            piece[...] = product(target * 2 + core).astype(piece.dtype)

    def widen(ref):
        return ref[...].astype(jnp.float32)

    def chip_sum(which, t):
        def fold(k):
            waits["twin", which, t, k].wait_recv()
            target = at(offsets[k])
            piece = share.at[which, t, core, target]
            piece[...] = (widen(piece) + widen(twin.at[which, t, target])).astype(piece.dtype)

        fold(0)
        waits["far", which, t] = go(
            send_to(share.at[which, t, core, at(2)], relay.at[which, t],
                    ring_send.at[which, t, 0], ring_recv.at[which, t, 0], peer(turn)))
        fold(1)
        fold(2)
        waits["near", which, t] = go(
            send_to(share.at[which, t, core, at(-turn)], single.at[which, t],
                    ring_send.at[which, t, 1], ring_recv.at[which, t, 1], peer(-turn)))
        fold(3)

    def chip_relay(which, t):
        waits["far", which, t].wait_recv()
        piece = relay.at[which, t]
        piece[...] = (widen(piece) + widen(share.at[which, t, core, at(turn)])).astype(piece.dtype)
        waits["join", which, t] = go(
            send_to(piece, joined.at[which, t],
                    ring_send.at[which, t, 2], ring_recv.at[which, t, 2], peer(turn)))

    def finish(which, t):
        waits["near", which, t].wait_recv()
        waits["join", which, t].wait_recv()

    block = 32

    def delta_of(which, t, rows):
        return (
            share[which, t, core, at(0), rows].astype(jnp.float32)
            + joined[which, t, rows].astype(jnp.float32)
            + single[which, t, rows].astype(jnp.float32)
        )

    def remixed(layer, values, delta):
        result = []
        for target in range(count):
            total = hc_out[layer * count + target] * delta
            for source in range(count):
                weight = hc_mix[(layer * count + source) * count + target]
                if source == target:
                    weight = weight + 1.0
                total = total + weight * values[source]
            result.append(total)
        return result

    def project(t):
        if t == 0:
            for load in loads[:group]:
                load.wait()
        values = attended[t * size : (t + 1) * size]
        scatter(0, t, lambda head: jnp.dot(
            values, out_buf[head], preferred_element_type=jnp.float32))

    def middle(t):
        finish(0, t)

        def step(index, carry):
            inside = pl.ds(index * block, block)
            rows = pl.ds(t * size + index * block, block)
            values = [streams[s, rows].astype(jnp.float32) for s in range(count)]
            result = remixed(0, values, delta_of(0, t, inside))
            mixed = None
            for s in range(count):
                first_buf[s, rows] = result[s]
                term = hc_in[count + s] * result[s]
                mixed = term if mixed is None else mixed + term
            mixed_buf[rows] = mixed
            return carry

        lax.fori_loop(0, size // block, step, 0)
        mixed = mixed_buf[t * size : (t + 1) * size]
        stat_all[t, me, 0:1] = transpose_sum(mixed)
        stat_all[t, me, 1:2] = transpose_sum(mixed * mixed)
        stat_all[t, me, 2:8] = jnp.zeros((6, size), jnp.float32)
        for step in range(1, group):
            waits["stat", t, step] = go(
                send_to(stat_all.at[t, me], stat_all.at[t, me], stat_send.at[t, step],
                        stat_recv.at[t, step], lax.rem(me + step, group)))

    def normalized(t):
        for step in range(1, group):
            waits["stat", t, step].wait_recv()
        total = stat_all[t, 0]
        for index in range(1, group):
            total = total + stat_all[t, index]
        center = total[0:1] / width
        scale = lax.rsqrt(total[1:2] / width - center * center + 1e-05)
        row = lax.broadcasted_iota(jnp.int32, total.shape, 0)
        packed = jnp.where(row == 0, center, jnp.where(row == 1, scale, 0.0))
        columns[t] = jnp.transpose(packed)

        def step(index, carry):
            inside = pl.ds(index * block, block)
            rows = pl.ds(t * size + index * block, block)
            column = columns[t, inside]
            value = (mixed_buf[rows] - column[:, 0:1]) * column[:, 1:2]
            normed[rows] = value.astype(normed.dtype)
            return carry

        lax.fori_loop(0, size // block, step, 0)
        mine = normed.at[chunk_rows(t)]
        view = gathered.at[chunk_rows(t), lanes(me)]
        waits["fwd", t] = go(send_to(mine, view, pass_send.at[t, 0], pass_recv.at[t, 0], peer(turn)))
        waits["bwd", t] = go(send_to(mine, view, pass_send.at[t, 1], pass_recv.at[t, 1], peer(-turn)))
        waits["own", t] = go(send_to(mine, view, copy_send.at[t, 0], copy_recv.at[t, 0], sibling))
        local = pltpu.make_async_copy(mine, view, own_sem.at[t])
        local.start()
        waits["local", t] = local

    def hand_over(t, index, delta):
        view = gathered.at[chunk_rows(t), lanes(peer(delta))]
        waits["copy", t, index] = go(
            send_to(view, view, copy_send.at[t, index], copy_recv.at[t, index], sibling))

    def pass_on(t):
        waits["fwd", t].wait_recv()
        view = gathered.at[chunk_rows(t), lanes(peer(-turn))]
        waits["opp", t] = go(send_to(view, view, pass_send.at[t, 2], pass_recv.at[t, 2], peer(turn)))
        hand_over(t, 1, -turn)
        waits["bwd", t].wait_recv()
        hand_over(t, 2, turn)

    def pass_last(t):
        waits["opp", t].wait_recv()
        hand_over(t, 3, 2)

    def feed_forward(t):
        if t == 0:
            for load in loads[group:]:
                load.wait()
        waits["own", t].wait_recv()
        waits["local", t].wait()
        for index in (1, 2, 3):
            waits["copy", t, index].wait_recv()
        values = gathered.at[chunk_rows(t)]
        for strip in range(strips):
            gate = jnp.dot(values[...], gate_buf[strip], preferred_element_type=jnp.float32)
            up = jnp.dot(values[...], gate_buf[strips + strip], preferred_element_type=jnp.float32)
            hidden[:, strip * feature : (strip + 1) * feature] = (
                gate * lax.logistic(gate) * up
            ).astype(hidden.dtype)
        scatter(1, t, lambda head: jnp.dot(
            hidden[...], down_buf[head], preferred_element_type=jnp.float32))

    def last(t):
        finish(1, t)

        def step(index, carry):
            inside = pl.ds(index * block, block)
            rows = pl.ds(t * size + index * block, block)
            values = [first_buf[s, rows] for s in range(count)]
            result = remixed(1, values, delta_of(1, t, inside))
            total = result[0]
            for s in range(count):
                fresh_ref[s, rows] = result[s].astype(fresh_ref.dtype)
                if s > 0:
                    total = total + result[s]
            total_buf[rows] = total
            return carry

        lax.fori_loop(0, size // block, step, 0)

    phases = (
        project,
        lambda t: chip_sum(0, t),
        lambda t: chip_relay(0, t),
        middle,
        normalized,
        pass_on,
        pass_last,
        feed_forward,
        lambda t: chip_sum(1, t),
        lambda t: chip_relay(1, t),
        last,
    )
    for step in range(len(phases) + chunks - 1):
        for t in range(chunks):
            if 0 <= step - t < len(phases):
                phases[step - t](t)
    requests = final_ref.shape[0]
    tree = tokens // requests
    for item in range(requests):
        final_ref[item : item + 1] = total_buf[pl.ds(item * tree + accepted[item], 1)]
    for copy in sends:
        copy.wait_send()


def layer(attended, streams, hc_in, hc_mix, hc_out, out_weight, gate_up, down_weight, accepted):
    tokens, feature = attended.shape
    count = streams.shape[0]
    group = lax.axis_size("head")
    chips = group // 2
    width = out_weight.shape[1]
    inner = down_weight.shape[0]
    strips = inner // feature
    chunks = 3
    size = tokens // chunks
    bf16, f32 = jnp.bfloat16, jnp.float32
    dma = pltpu.SemaphoreType.DMA
    vmem = pl.BlockSpec(memory_space=pltpu.VMEM)
    smem = pl.BlockSpec(memory_space=pltpu.SMEM)
    anywhere = pl.BlockSpec(memory_space=pl.ANY)
    scratch = [
        pltpu.VMEM((group, feature, feature), bf16),
        pltpu.VMEM((2 * strips, width, feature), bf16),
        pltpu.VMEM((group, inner, feature), bf16),
        pltpu.VMEM((count, tokens, feature), f32),
        pltpu.VMEM((tokens, feature), f32),
        pltpu.VMEM((tokens, feature), f32),
        pltpu.VMEM((2, chunks, 2, chips, size, feature), bf16),
        pltpu.VMEM((2, chunks, chips, size, feature), bf16),
        pltpu.VMEM((2, chunks, size, feature), bf16),
        pltpu.VMEM((2, chunks, size, feature), bf16),
        pltpu.VMEM((2, chunks, size, feature), bf16),
        pltpu.VMEM((chunks, group, 8, size), f32),
        pltpu.VMEM((chunks, size, 8), f32),
        pltpu.VMEM((tokens, feature), bf16),
        pltpu.VMEM((tokens, width), bf16),
        pltpu.VMEM((size, inner), bf16),
        dma((3, max(group, 2 * strips))),
        dma((chunks,)),
        dma((2, chunks, 4)), dma((2, chunks, 4)),
        dma((2, chunks, 3)), dma((2, chunks, 3)),
        dma((chunks, group)), dma((chunks, group)),
        dma((chunks, 4)), dma((chunks, 4)),
        dma((chunks, 3)), dma((chunks, 3)),
    ]
    return pl.pallas_call(
        functools.partial(layer_kernel, chips, chunks),
        out_shape=(
            jax.ShapeDtypeStruct((count, tokens, feature), bf16),
            jax.ShapeDtypeStruct((accepted.shape[0], feature), f32),
        ),
        in_specs=[smem] * 4 + [vmem, vmem, anywhere, anywhere, anywhere],
        out_specs=(vmem, vmem),
        scratch_shapes=scratch,
        compiler_params=pltpu.CompilerParams(
            collective_id=1, has_side_effects=True, vmem_limit_bytes=60 << 20
        ),
    )(
        hc_in.reshape(-1),
        hc_mix.reshape(-1),
        hc_out.reshape(-1),
        accepted,
        attended,
        streams,
        out_weight,
        gate_up,
        down_weight,
    )


def on_device(
    streams,
    hc_in,
    hc_mix,
    hc_out,
    qkv_weight,
    out_weight,
    up_gate,
    down_weight,
    draft_weight,
    lm_head,
    k_pages,
    v_pages,
    page_owner,
    page_fill,
    cache_len,
    tree_parent,
    accepted_index,
):
    tokens_local = streams.shape[0]
    feature_local = streams.shape[2]
    width = qkv_weight.shape[0]
    req_local = cache_len.shape[0]
    tree_size = tree_parent.shape[1]
    slot_count = k_pages.shape[0]
    page_size = k_pages.shape[1]
    heads_local = k_pages.shape[2]
    head_dim = k_pages.shape[3]
    draft_count = draft_weight.shape[0]
    all_requests = req_local * lax.axis_size("req")
    reach = ancestors(tree_parent)
    depth = (jnp.sum(reach, axis=2) - 1.0).astype(jnp.int32)
    positions = (cache_len[:, None] + depth).reshape(tokens_local)
    stream_vals = streams.astype(jnp.float32)
    mixed_in = blend(stream_vals, hc_in[0])
    stat_sum, stat_square = lax.psum(
        (jnp.sum(mixed_in, axis=1), jnp.sum(mixed_in * mixed_in, axis=1)), "head"
    )
    normed = normalize(mixed_in, stat_sum[:, None], stat_square[:, None], width).astype(
        jnp.bfloat16
    )
    qkv_flat = qkv_weight.reshape(width, -1)
    normed_full = lax.all_gather(normed, "head", axis=1, tiled=True)
    gate_up = jnp.transpose(up_gate, (1, 0, 2))
    normed_full, gate_up = lax.optimization_barrier((normed_full, gate_up))
    projected = fold_rows(qkv_flat, normed_full)
    projected = projected.reshape(tokens_local, 3, heads_local, head_dim)
    queries = (rotate(projected[:, 0], positions) * head_dim ** (-0.5)).astype(jnp.bfloat16)
    keys_new = rotate(projected[:, 1], positions).astype(jnp.bfloat16)
    values_new = projected[:, 2].astype(jnp.bfloat16)
    query_rows = (
        queries.reshape(req_local, tree_size, heads_local, head_dim)
        .transpose(0, 2, 1, 3)
        .reshape(req_local, heads_local * tree_size, head_dim)
    )
    own_sum, own_top, own_den = cache_attention(
        query_rows, k_pages, v_pages, page_owner, page_fill
    )
    own_sum = own_sum.reshape(req_local, heads_local, tree_size, head_dim).transpose(0, 2, 1, 3)
    used = heads_local * tree_size
    own_top = own_top[:, :used].reshape(req_local, heads_local, tree_size).transpose(0, 2, 1)
    own_den = own_den[:, :used].reshape(req_local, heads_local, tree_size).transpose(0, 2, 1)
    query_own = queries.reshape(req_local, tree_size, heads_local, head_dim)
    keys_own = keys_new.reshape(req_local, tree_size, heads_local, head_dim)
    values_own = values_new.reshape(req_local, tree_size, heads_local, head_dim)
    tree_scores = jnp.einsum(
        "jqhd,jkhd->jqhk", query_own, keys_own, preferred_element_type=jnp.float32
    )
    tree_mask = (reach > 0)[:, :, None, :]
    tree_scores = jnp.where(tree_mask, tree_scores, NEG_FILL)
    top = jnp.maximum(own_top, jnp.max(tree_scores, axis=3))
    carried = jnp.exp(own_top - top)
    tree_weights = jnp.where(tree_mask, jnp.exp(tree_scores - top[..., None]), 0.0)
    denominator = own_den * carried + jnp.sum(tree_weights, axis=3)
    numerator = own_sum * carried[..., None] + jnp.einsum(
        "jqhk,jkhd->jqhd",
        tree_weights.astype(jnp.bfloat16),
        values_own,
        preferred_element_type=jnp.float32,
    )
    attended = (
        (numerator / denominator[..., None])
        .astype(jnp.bfloat16)
        .reshape(tokens_local, heads_local * head_dim)
    )
    fresh, final_local = layer(
        attended,
        jnp.transpose(streams, (1, 0, 2)),
        hc_in,
        hc_mix,
        hc_out,
        out_weight,
        gate_up,
        down_weight,
        accepted_index,
    )
    new_streams = jnp.transpose(fresh, (1, 0, 2))
    final_full = lax.all_gather(final_local, "head", axis=1, tiled=True)
    final_norm = layer_norm(final_full)
    own_columns = lax.dynamic_slice_in_dim(
        final_norm, lax.axis_index("head") * feature_local, feature_local, 1
    )
    branch = jnp.einsum(
        "jd,kde->jke",
        final_norm.astype(jnp.bfloat16),
        draft_weight,
        preferred_element_type=jnp.float32,
    )
    drafted = (own_columns[:, None, :] + jax.nn.silu(branch)).astype(jnp.bfloat16)
    draft_full = lax.all_gather(drafted, "head", axis=2, tiled=True)
    draft_all = lax.all_gather(draft_full, "req", axis=0, tiled=True)
    logits_local = jnp.dot(
        draft_all.reshape(-1, width), lm_head, preferred_element_type=jnp.float32
    )
    logits_local = logits_local.reshape(all_requests, draft_count, -1)
    logits = lax.all_to_all(
        logits_local.astype(jnp.bfloat16), ("req", "head"), split_axis=0, concat_axis=2, tiled=True
    ).astype(logits_local.dtype)
    return (new_streams, logits)


def solution(mesh):
    in_specs = (
        P("req", None, "head"),
        P(),
        P(),
        P(),
        P(None, None, "head"),
        P("head", None),
        P(None, None, "head"),
        P("head", None),
        P(None, None, "head"),
        P(None, ("req", "head")),
        P("req", None, "head", None),
        P("req", None, "head", None),
        P("req"),
        P("req"),
        P("req"),
        P("req", None),
        P("req"),
    )
    out_specs = (P("req", None, "head"), P(("req", "head"), None, None))
    return jax.shard_map(
        on_device, mesh=mesh, in_specs=in_specs, out_specs=out_specs, check_vma=False
    )
```

```python
import functools
import math

import jax
import jax.numpy as jnp
from jax import lax
from jax.experimental import pallas as pl
from jax.experimental.pallas import tpu as pltpu
from jax.sharding import PartitionSpec as P

NEG_FILL = -1e30
PRECISE = lax.Precision.HIGHEST


def layer_norm(values):
    center = jnp.mean(values, axis=-1, keepdims=True)
    square = jnp.mean(values * values, axis=-1, keepdims=True)
    return (values - center) * lax.rsqrt(square - center * center + 1e-05)


def normalize(values, sums, squares, width):
    center = sums / width
    return (values - center) * lax.rsqrt(squares / width - center * center + 1e-05)


def ancestors(parents):
    length = parents.shape[1]
    places = jnp.arange(length, dtype=jnp.int32)
    linked = (parents[:, :, None] == places[None, None, :]) | (places[:, None] == places[None, :])[
        None
    ]
    reach = linked.astype(jnp.float32)
    for repeat in range(max(1, (length - 1).bit_length())):
        reach = jnp.minimum(jnp.einsum("jik,jkl->jil", reach, reach, precision=PRECISE), 1.0)
    return reach


def rotate(values, positions):
    half = values.shape[-1] // 2
    freqs = jnp.exp(
        jnp.arange(half, dtype=jnp.float32) * (-2.0 * math.log(10000.0) / values.shape[-1])
    )
    angles = positions.astype(jnp.float32)[:, None] * freqs[None, :]
    cosine = jnp.cos(angles)[:, None, :]
    sine = jnp.sin(angles)[:, None, :]
    first = values[..., :half]
    second = values[..., half:]
    return jnp.concatenate(
        [first * cosine - second * sine, second * cosine + first * sine], axis=-1
    )


def blend(stream_vals, weights):
    total = weights[0] * stream_vals[:, 0]
    for index in range(1, stream_vals.shape[1]):
        total = total + weights[index] * stream_vals[:, index]
    return total


def remix(stream_vals, mixing, out_scale, delta):
    count = stream_vals.shape[1]
    matrix = jnp.eye(count, dtype=jnp.float32) + mixing
    rows = [
        blend(stream_vals, matrix[:, target]) + out_scale[target] * delta for target in range(count)
    ]
    return jnp.stack(rows, axis=1)


def stream_total(stream_vals):
    total = stream_vals[:, 0]
    for index in range(1, stream_vals.shape[1]):
        total = total + stream_vals[:, index]
    return total


def fold_rows(weight, piece):
    return jnp.dot(piece, weight, preferred_element_type=jnp.float32)


MESH = pl.DeviceIdType.MESH
SLOT_BITS = 6
FILL_BITS = 8


def remote(source, target, send_sem, recv_sem, req):
    return pltpu.make_async_remote_copy(
        src_ref=source,
        dst_ref=target,
        send_sem=send_sem,
        recv_sem=recv_sem,
        device_id={"req": req},
        device_id_type=MESH,
    )


def weigh(tops, totals):
    top = functools.reduce(jnp.maximum, tops)
    factors = [jnp.exp(value - top) for value in tops]
    total = functools.reduce(lambda a, b: a + b, [f * t for f, t in zip(factors, totals)])
    return top, total, factors


def cache_kernel(
    side,
    table,
    last,
    q_ref,
    k_hbm,
    v_hbm,
    num_ref,
    top_ref,
    den_ref,
    q_all,
    k_buf,
    v_buf,
    scores,
    seg_acc,
    seg_top,
    seg_den,
    parts,
    stats,
    relay,
    merged,
    single,
    relay_s,
    merged_s,
    single_s,
    outgoing_s,
    factors,
    small,
    small_s,
    hop,
    hop_s,
    gather_send,
    gather_recv,
    spread_send,
    spread_recv,
    load_sem,
    far_send,
    far_recv,
    near_send,
    near_recv,
    join_send,
    join_recv,
    stat_send,
    stat_recv,
    last_send,
    last_recv,
    last_stat_send,
    last_stat_recv,
):
    block = q_ref.shape[0] // 2
    rows = q_ref.shape[1]
    slots = k_buf.shape[0]
    half_rows = rows // 2
    me = lax.axis_index("req")
    place = (me // side, lax.rem(me, side))
    turn = 1 - 2 * lax.rem(lax.axis_index("head"), 2)

    def shifted(axis, delta):
        moved = lax.rem(place[axis] + side + delta, side)
        return moved * side + place[1] if axis == 0 else place[0] * side + moved

    def at(axis, delta):
        return lax.rem(place[axis] + side + delta, side)

    first = (0, 1)
    second = (1, 0)

    def spot(half, p2, p1):
        return pl.ds(((half * side + p2) * side + p1) * block, block)

    loads = [
        pltpu.make_async_copy(k_hbm, k_buf, load_sem.at[0]),
        pltpu.make_async_copy(v_hbm, v_buf, load_sem.at[1]),
    ]
    for load in loads:
        load.start()
    barrier = pltpu.get_barrier_semaphore()
    for axis in (0, 1):
        for delta in (1, -1):
            pl.semaphore_signal(
                barrier, inc=1, device_id={"req": shifted(axis, delta)}, device_id_type=MESH
            )
    pl.semaphore_wait(barrier, 4)

    sends = []

    def go(copy):
        copy.start()
        sends.append(copy)
        return copy

    def pass_block(half, axis, delta, p2, p1, send, recv, own=False):
        view = q_all.at[spot(half, p2, p1)]
        source = q_ref.at[pl.ds(half * block, block)] if own else view
        return go(remote(source, view, send, recv, shifted(axis, delta)))

    lines = {}
    crosses = {}

    def line(half, index, delta, p1, own=False):
        lines[half, index] = pass_block(
            half, first[half], delta, at(second[half], 0), p1,
            gather_send.at[half, index], gather_recv.at[half, index], own,
        )

    def cross(half, piece, index, delta, p2, p1, own=False):
        crosses[half, piece, index] = pass_block(
            half, second[half], delta, p2, p1,
            spread_send.at[half, piece, index], spread_recv.at[half, piece, index], own,
        )

    halves = (0, 1)
    for half in halves:
        line(half, 0, turn, at(first[half], 0), True)
        line(half, 1, -turn, at(first[half], 0), True)
    for half in halves:
        cross(half, 0, 0, turn, at(second[half], 0), at(first[half], 0), True)
        cross(half, 0, 1, -turn, at(second[half], 0), at(first[half], 0), True)
    for half in halves:
        q_all[spot(half, at(second[half], 0), at(first[half], 0))] = q_ref[
            half * block : (half + 1) * block
        ]
    seg_top[...] = jnp.full(seg_top.shape, NEG_FILL, jnp.float32)
    seg_den[...] = jnp.zeros(seg_den.shape, jnp.float32)
    seg_acc[slots] = jnp.zeros(seg_acc.shape[1:], seg_acc.dtype)
    for half in halves:
        lines[half, 0].wait_recv()
        line(half, 2, turn, at(first[half], -turn))
        cross(half, 1, 0, turn, at(second[half], 0), at(first[half], -turn))
        cross(half, 1, 1, -turn, at(second[half], 0), at(first[half], -turn))
    for half in halves:
        lines[half, 1].wait_recv()
        cross(half, 2, 0, turn, at(second[half], 0), at(first[half], turn))
        cross(half, 2, 1, -turn, at(second[half], 0), at(first[half], turn))
    for half in halves:
        crosses[half, 0, 0].wait_recv()
        cross(half, 0, 2, turn, at(second[half], -turn), at(first[half], 0))
    for half in halves:
        lines[half, 2].wait_recv()
        cross(half, 3, 0, turn, at(second[half], 0), at(first[half], 2))
        cross(half, 3, 1, -turn, at(second[half], 0), at(first[half], 2))
    for piece, delta in ((1, -turn), (2, turn), (3, 2)):
        for half in halves:
            crosses[half, piece, 0].wait_recv()
            cross(half, piece, 2, turn, at(second[half], -turn), at(first[half], delta))
    for piece in range(4):
        for half in halves:
            crosses[half, piece, 1].wait_recv()
            crosses[half, piece, 2].wait_recv()
    for load in loads:
        load.wait()

    slot_mask = (1 << SLOT_BITS) - 1
    fill_mask = (1 << FILL_BITS) - 1
    requests = 2 * block * side * side

    def owner_at(index):
        return table[index] >> (SLOT_BITS + FILL_BITS)

    def starts_new(index):
        before = owner_at(jnp.maximum(index - 1, 0))
        return jnp.logical_or(index == 0, before != owner_at(index))

    shape = (k_buf.shape[1], rows)
    row_ids = lax.broadcasted_iota(jnp.int32, shape, 0)
    col_head = (lax.broadcasted_iota(jnp.int32, shape, 1) >= half_rows).astype(jnp.int32)
    matched = (row_ids & 1) == col_head
    key_ids = row_ids >> 1
    unroll = 4

    def score_step(group, carry):
        for offset in range(unroll):
            index = group * unroll + offset
            entry = table[index]
            fill = (entry >> SLOT_BITS) & fill_mask
            owner = jnp.minimum(entry >> (SLOT_BITS + FILL_BITS), requests - 1)
            home = owner // (2 * block)
            within = lax.rem(owner, 2 * block)
            half = within // block
            hx = home // side
            hy = lax.rem(home, side)
            outer = jnp.where(half == 0, hy, hx)
            inner = jnp.where(half == 0, hx, hy)
            row = ((half * side + outer) * side + inner) * block + lax.rem(within, block)
            found = lax.dot_general(
                k_buf[entry & slot_mask],
                q_all[row],
                (((1,), (1,)), ((), ())),
                preferred_element_type=jnp.float32,
            )
            found = jnp.where(jnp.logical_and(matched, key_ids < fill), found, NEG_FILL)
            scores[index] = found
            seg_top[index, :, 0:rows] = jnp.max(found, axis=0, keepdims=True)
        return carry

    lax.fori_loop(0, slots // unroll, score_step, 0)

    def forward(index, run):
        here = seg_top[index]
        run = jnp.where(starts_new(index), here, jnp.maximum(run, here))
        seg_top[index] = run
        return run

    lax.fori_loop(0, slots, forward, jnp.full(seg_top.shape[1:], NEG_FILL, jnp.float32))

    def backward(step, run):
        index = slots - 1 - step
        follow = jnp.minimum(index + 1, slots - 1)
        ends = jnp.logical_or(step == 0, owner_at(follow) != owner_at(index))
        run = jnp.where(ends, seg_top[index], run)
        seg_top[index] = run
        return run

    lax.fori_loop(0, slots, backward, jnp.full(seg_top.shape[1:], NEG_FILL, jnp.float32))

    def value_step(group, carry):
        acc_run, den_run = carry
        for offset in range(unroll):
            index = group * unroll + offset
            fresh = starts_new(index)
            top = seg_top[index][:, 0:rows]
            top = jnp.where(top < 0.5 * NEG_FILL, 0.0, top)
            weight = jnp.exp(scores[index] - top)
            den = jnp.sum(weight, axis=0, keepdims=True)
            acc = lax.dot_general(
                weight.astype(jnp.bfloat16),
                v_buf[table[index] & slot_mask],
                (((0,), (0,)), ((), ())),
                preferred_element_type=jnp.float32,
            )
            acc_run = acc + jnp.where(fresh, 0.0, acc_run)
            den_run = den + jnp.where(fresh, 0.0, den_run)
            seg_acc[index] = acc_run.astype(seg_acc.dtype)
            seg_den[index, :, 0:rows] = den_run
        return acc_run, den_run

    lax.fori_loop(
        0,
        slots // unroll,
        value_step,
        (jnp.zeros(seg_acc.shape[1:], jnp.float32), jnp.zeros((1, rows), jnp.float32)),
    )

    def place_step(group, carry):
        for piece in range(side):
            tops, dens = [], []
            for offset in range(block):
                spot_index = (group * side + piece) * block + offset
                found = last[spot_index]
                parts[spot_index] = seg_acc[found]
                tops.append(seg_top[found])
                dens.append(seg_den[found])
            stats[group, 0, piece * block : (piece + 1) * block] = jnp.concatenate(tops, axis=0)
            stats[group, 1, piece * block : (piece + 1) * block] = jnp.concatenate(dens, axis=0)
        return carry

    lax.fori_loop(0, 2 * side, place_step, 0)

    def part(half, p2, p1):
        return parts.at[spot(half, p2, p1)]

    def stat(half, p2):
        return stats.at[half * side + p2]

    def combine(put, terms, weights):
        columns = [jnp.transpose(weight) for weight in weights]
        for item in range(block):
            total = None
            for term, column in zip(terms, columns):
                value = term[item].astype(jnp.float32) * column[0:rows, item : item + 1]
                total = value if total is None else total + value
            put(item, total)

    stat_copies = {}
    far, near = {}, {}
    for half in halves:
        up, down = shifted(second[half], turn), shifted(second[half], -turn)
        stat_copies[half, 0] = go(
            remote(stat(half, at(second[half], 2)), relay_s.at[half],
                   stat_send.at[half, 0], stat_recv.at[half, 0], up))
        stat_copies[half, 1] = go(
            remote(stat(half, at(second[half], -turn)), single_s.at[half],
                   stat_send.at[half, 1], stat_recv.at[half, 1], down))
    for order in range(4):
        for half in halves:
            up, down = shifted(second[half], turn), shifted(second[half], -turn)
            p1 = at(first[half], 2 - turn * order)
            far[half, order] = go(
                remote(part(half, at(second[half], 2), p1), relay.at[half, p1],
                       far_send.at[half, order], far_recv.at[half, order], up))
            near[half, order] = go(
                remote(part(half, at(second[half], -turn), p1), single.at[half, p1],
                       near_send.at[half, order], near_recv.at[half, order], down))

    for half in halves:
        stat_copies[half, 0].wait_recv()
        mine = stat(half, at(second[half], turn))
        top, den, weights = weigh([mine[0], relay_s[half, 0]], [mine[1], relay_s[half, 1]])
        outgoing_s[half, 0] = top
        outgoing_s[half, 1] = den
        factors[half, 0] = weights[0]
        factors[half, 1] = weights[1]
        stat_copies[half, 2] = go(
            remote(outgoing_s.at[half], merged_s.at[half],
                   stat_send.at[half, 2], stat_recv.at[half, 2], shifted(second[half], turn)))

    def join_copy(half, order):
        p1 = at(first[half], 2 - turn * order)
        return remote(relay.at[half, p1], merged.at[half, p1],
                      join_send.at[half, order], join_recv.at[half, order],
                      shifted(second[half], turn))

    def far_copy(half, order):
        p1 = at(first[half], 2 - turn * order)
        return remote(part(half, at(second[half], 2), p1), relay.at[half, p1],
                      far_send.at[half, order], far_recv.at[half, order],
                      shifted(second[half], turn))

    def near_copy(half, order):
        p1 = at(first[half], 2 - turn * order)
        return remote(part(half, at(second[half], -turn), p1), single.at[half, p1],
                      near_send.at[half, order], near_recv.at[half, order],
                      shifted(second[half], -turn))

    def relay_step(order, carry):
        for half in halves:
            p1 = at(first[half], 2 + side - turn * order)
            far_copy(half, order).wait_recv()
            lanes = pl.ds(p1 * block, block)
            target = relay.at[half, p1]

            def put(item, value):
                target[item] = value.astype(target.dtype)

            combine(
                put,
                [part(half, at(second[half], turn), p1), target],
                [factors[half, 0, lanes], factors[half, 1, lanes]],
            )
            join_copy(half, order).start()
        return carry

    lax.fori_loop(0, 4, relay_step, 0)

    for half in halves:
        stat_copies[half, 1].wait_recv()
        stat_copies[half, 2].wait_recv()
        mine = stat(half, at(second[half], 0))
        top, den, weights = weigh(
            [mine[0], merged_s[half, 0], single_s[half, 0]],
            [mine[1], merged_s[half, 1], single_s[half, 1]],
        )
        for index in range(3):
            factors[half, index] = weights[index]
        for p1 in range(side):
            small_s[half, p1, 0] = top[p1 * block : (p1 + 1) * block]
            small_s[half, p1, 1] = den[p1 * block : (p1 + 1) * block]

    def gather_piece(half, order):
        p1 = at(first[half], 2 + side - turn * order)
        near_copy(half, order).wait_recv()
        join_copy(half, order).wait_recv()
        lanes = pl.ds(p1 * block, block)
        target = small.at[half, p1]

        def put(item, value):
            target[item] = value.astype(target.dtype)

        combine(
            put,
            [part(half, at(second[half], 0), p1), merged.at[half, p1], single.at[half, p1]],
            [factors[half, index, lanes] for index in range(3)],
        )

    def piece_step(order, carry):
        for half in halves:
            gather_piece(half, order)
        return carry

    tails = {}

    def tail(half, index, source, source_s, delta):
        peer = shifted(first[half], delta)
        tails[half, index] = (
            go(remote(source_s, hop_s.at[half, index],
                      last_stat_send.at[half, index], last_stat_recv.at[half, index], peer)),
            go(remote(source, hop.at[half, index],
                      last_send.at[half, index], last_recv.at[half, index], peer)),
        )

    lax.fori_loop(0, 1, piece_step, 0)
    for half in halves:
        p1 = at(first[half], 2)
        tail(half, 0, small.at[half, p1], small_s.at[half, p1], turn)
    lax.fori_loop(1, 2, piece_step, 0)
    for half in halves:
        p1 = at(first[half], -turn + 2 + 2)
    lax.fori_loop(2, 4, piece_step, 0)
    for half in halves:
        p1 = at(first[half], -turn)
        tail(half, 1, small.at[half, p1], small_s.at[half, p1], -turn)
    for half in halves:
        p1 = at(first[half], turn)
        for copy in tails[half, 0]:
            copy.wait_recv()
        target = small.at[half, p1]
        top, den, weights = weigh(
            [small_s[half, p1, 0], hop_s[half, 0, 0]], [small_s[half, p1, 1], hop_s[half, 0, 1]]
        )
        small_s[half, p1, 0] = top
        small_s[half, p1, 1] = den

        def put(item, value, target=target):
            target[item] = value.astype(target.dtype)

        combine(put, [target, hop.at[half, 0]], weights)
        tail(half, 2, target, small_s.at[half, p1], turn)
    for half in halves:
        p1 = at(first[half], 0)
        for index in (1, 2):
            for copy in tails[half, index]:
                copy.wait_recv()
        top, den, weights = weigh(
            [small_s[half, p1, 0], hop_s[half, 1, 0], hop_s[half, 2, 0]],
            [small_s[half, p1, 1], hop_s[half, 1, 1], hop_s[half, 2, 1]],
        )
        top_ref[half * block : (half + 1) * block] = top
        den_ref[half * block : (half + 1) * block] = den

        def put(item, value, half=half):
            num_ref[half * block + item] = value

        combine(put, [small.at[half, p1], hop.at[half, 1], hop.at[half, 2]], weights)
    for copy in sends:
        copy.wait_send()
    for half in halves:
        for order in range(4):
            join_copy(half, order).wait_send()


def cache_attention(queries, k_pages, v_pages, page_owner, page_fill):
    req_local, rows, head_dim = queries.shape
    slots, keys = k_pages.shape[0], k_pages.shape[1] * k_pages.shape[2]
    devices = lax.axis_size("req")
    side = math.isqrt(devices)
    block = req_local // 2
    requests = req_local * devices
    owner_key = jnp.where(page_owner < 0, requests, page_owner)
    packed = (
        (owner_key << (SLOT_BITS + FILL_BITS))
        | (jnp.where(page_owner < 0, 0, page_fill) << SLOT_BITS)
        | jnp.arange(slots, dtype=jnp.int32)
    )
    rank = jnp.sum((packed[None, :] < packed[:, None]).astype(jnp.int32), axis=1)
    places = jnp.arange(slots, dtype=jnp.int32)
    table = jnp.sum(jnp.where(rank[None, :] == places[:, None], packed[None, :], 0), axis=1)
    spots = jnp.arange(requests, dtype=jnp.int32)
    half = spots // (requests // 2)
    outer = (spots // (block * side)) % side
    inner = (spots // block) % side
    home = jnp.where(half == 0, inner * side + outer, outer * side + inner)
    request = home * req_local + half * block + spots % block
    below = jnp.sum((owner_key[None, :] <= request[:, None]).astype(jnp.int32), axis=1)
    exact = jnp.sum((owner_key[None, :] == request[:, None]).astype(jnp.int32), axis=1)
    last = jnp.where(exact > 0, below - 1, slots)
    bf16, f32 = jnp.bfloat16, jnp.float32
    unit = (2, side, block, rows, head_dim)
    dma = pltpu.SemaphoreType.DMA
    scratch = [
        pltpu.VMEM((requests, rows, head_dim), bf16),
        pltpu.VMEM((slots, keys, head_dim), bf16),
        pltpu.VMEM((slots, keys, head_dim), bf16),
        pltpu.VMEM((slots, keys, rows), f32),
        pltpu.VMEM((slots + 1, rows, head_dim), bf16),
        pltpu.VMEM((slots + 1, 1, 128), f32),
        pltpu.VMEM((slots + 1, 1, 128), f32),
        pltpu.VMEM((requests, rows, head_dim), bf16),
        pltpu.VMEM((2 * side, 2, side * block, 128), f32),
        pltpu.VMEM(unit, bf16),
        pltpu.VMEM(unit, bf16),
        pltpu.VMEM(unit, bf16),
        pltpu.VMEM((2, 2, side * block, 128), f32),
        pltpu.VMEM((2, 2, side * block, 128), f32),
        pltpu.VMEM((2, 2, side * block, 128), f32),
        pltpu.VMEM((2, 2, side * block, 128), f32),
        pltpu.VMEM((2, 3, side * block, 128), f32),
        pltpu.VMEM(unit, bf16),
        pltpu.VMEM((2, side, 2, block, 128), f32),
        pltpu.VMEM((2, 3, block, rows, head_dim), bf16),
        pltpu.VMEM((2, 3, 2, block, 128), f32),
        dma((2, 3)), dma((2, 3)),
        dma((2, 4, 3)), dma((2, 4, 3)),
        dma((2,)),
        dma((2, 4)), dma((2, 4)),
        dma((2, 4)), dma((2, 4)),
        dma((2, 4)), dma((2, 4)),
        dma((2, 3)), dma((2, 3)),
        dma((2, 3)), dma((2, 3)),
        dma((2, 3)), dma((2, 3)),
    ]
    vmem = pl.BlockSpec(memory_space=pltpu.VMEM)
    smem = pl.BlockSpec(memory_space=pltpu.SMEM)
    anywhere = pl.BlockSpec(memory_space=pl.ANY)
    return pl.pallas_call(
        functools.partial(cache_kernel, side),
        out_shape=(
            jax.ShapeDtypeStruct((req_local, rows, head_dim), f32),
            jax.ShapeDtypeStruct((req_local, 128), f32),
            jax.ShapeDtypeStruct((req_local, 128), f32),
        ),
        in_specs=[smem, smem, vmem, anywhere, anywhere],
        out_specs=(vmem, vmem, vmem),
        scratch_shapes=scratch,
        compiler_params=pltpu.CompilerParams(
            collective_id=0, has_side_effects=True, vmem_limit_bytes=56 << 20
        ),
    )(
        table,
        last,
        queries,
        k_pages.reshape(slots, keys, head_dim),
        v_pages.reshape(slots, keys, head_dim),
    )


def transpose_sum(values):
    half = values.shape[1] // 2
    return jnp.sum(jnp.transpose(values[:, 0:half] + values[:, half:]), axis=0, keepdims=True)


def layer_kernel(
    chips,
    chunks,
    hc_in,
    hc_mix,
    hc_out,
    accepted,
    attended,
    streams,
    out_hbm,
    gate_hbm,
    down_hbm,
    fresh_ref,
    final_ref,
    out_buf,
    gate_buf,
    down_buf,
    first_buf,
    mixed_buf,
    total_buf,
    share,
    twin,
    relay,
    joined,
    single,
    stat_all,
    columns,
    normed,
    gathered,
    hidden,
    load_sem,
    own_sem,
    twin_send,
    twin_recv,
    ring_send,
    ring_recv,
    stat_send,
    stat_recv,
    copy_send,
    copy_recv,
    pass_send,
    pass_recv,
):
    tokens, feature = attended.shape
    size = tokens // chunks
    group = 2 * chips
    width = group * feature
    count = streams.shape[0]
    inner = hidden.shape[1]
    strips = inner // feature
    me = lax.axis_index("head")
    chip = me // 2
    core = lax.rem(me, 2)
    turn = 1 - 2 * core

    def at(delta):
        return lax.rem(chip + chips + delta, chips)

    def peer(delta):
        return at(delta) * 2 + core

    sibling = chip * 2 + 1 - core

    def send_to(source, target, send_sem, recv_sem, head):
        return pltpu.make_async_remote_copy(
            src_ref=source,
            dst_ref=target,
            send_sem=send_sem,
            recv_sem=recv_sem,
            device_id={"head": head},
            device_id_type=MESH,
        )

    loads = []
    for index in range(group):
        loads.append(
            pltpu.make_async_copy(
                out_hbm.at[:, pl.ds(index * feature, feature)], out_buf.at[index], load_sem.at[0, index]
            )
        )
    for index in range(2 * strips):
        kind, strip = index // strips, index % strips
        loads.append(
            pltpu.make_async_copy(
                gate_hbm.at[kind, :, pl.ds(strip * feature, feature)],
                gate_buf.at[index],
                load_sem.at[1, index],
            )
        )
    for index in range(group):
        loads.append(
            pltpu.make_async_copy(
                down_hbm.at[:, pl.ds(index * feature, feature)], down_buf.at[index], load_sem.at[2, index]
            )
        )
    for load in loads:
        load.start()
    barrier = pltpu.get_barrier_semaphore()
    for step in range(1, group):
        pl.semaphore_signal(
            barrier, inc=1, device_id={"head": lax.rem(me + step, group)}, device_id_type=MESH
        )
    pl.semaphore_wait(barrier, group - 1)

    sends = []

    def go(copy):
        copy.start()
        sends.append(copy)
        return copy

    offsets = (2, 1, 3, 0)
    waits = {}

    def chunk_rows(t):
        return pl.ds(t * size, size)

    def lanes(head):
        return pl.ds(pl.multiple_of(head * feature, feature), feature)

    def scatter(which, t, product):
        for k, offset in enumerate(offsets):
            target = at(offset)
            piece = share.at[which, t, 1 - core, target]
            piece[...] = product(target * 2 + 1 - core).astype(piece.dtype)
            waits["twin", which, t, k] = go(
                send_to(piece, twin.at[which, t, target], twin_send.at[which, t, k],
                        twin_recv.at[which, t, k], sibling))
        for offset in offsets:
            target = at(offset)
            piece = share.at[which, t, core, target]
            piece[...] = product(target * 2 + core).astype(piece.dtype)

    def widen(ref):
        return ref[...].astype(jnp.float32)

    def chip_sum(which, t):
        def fold(k):
            waits["twin", which, t, k].wait_recv()
            target = at(offsets[k])
            piece = share.at[which, t, core, target]
            piece[...] = (widen(piece) + widen(twin.at[which, t, target])).astype(piece.dtype)

        fold(0)
        waits["far", which, t] = go(
            send_to(share.at[which, t, core, at(2)], relay.at[which, t],
                    ring_send.at[which, t, 0], ring_recv.at[which, t, 0], peer(turn)))
        fold(1)
        fold(2)
        waits["near", which, t] = go(
            send_to(share.at[which, t, core, at(-turn)], single.at[which, t],
                    ring_send.at[which, t, 1], ring_recv.at[which, t, 1], peer(-turn)))
        fold(3)

    def chip_relay(which, t):
        waits["far", which, t].wait_recv()
        piece = relay.at[which, t]
        piece[...] = (widen(piece) + widen(share.at[which, t, core, at(turn)])).astype(piece.dtype)
        waits["join", which, t] = go(
            send_to(piece, joined.at[which, t],
                    ring_send.at[which, t, 2], ring_recv.at[which, t, 2], peer(turn)))

    def finish(which, t):
        waits["near", which, t].wait_recv()
        waits["join", which, t].wait_recv()

    block = 32

    def delta_of(which, t, rows):
        return (
            share[which, t, core, at(0), rows].astype(jnp.float32)
            + joined[which, t, rows].astype(jnp.float32)
            + single[which, t, rows].astype(jnp.float32)
        )

    def remixed(layer, values, delta):
        result = []
        for target in range(count):
            total = hc_out[layer * count + target] * delta
            for source in range(count):
                weight = hc_mix[(layer * count + source) * count + target]
                if source == target:
                    weight = weight + 1.0
                total = total + weight * values[source]
            result.append(total)
        return result

    def project(t):
        if t == 0:
            for load in loads[:group]:
                load.wait()
        values = attended[t * size : (t + 1) * size]
        scatter(0, t, lambda head: jnp.dot(
            values, out_buf[head], preferred_element_type=jnp.float32))

    def middle(t):
        finish(0, t)

        def step(index, carry):
            inside = pl.ds(index * block, block)
            rows = pl.ds(t * size + index * block, block)
            values = [streams[s, rows].astype(jnp.float32) for s in range(count)]
            result = remixed(0, values, delta_of(0, t, inside))
            mixed = None
            for s in range(count):
                first_buf[s, rows] = result[s]
                term = hc_in[count + s] * result[s]
                mixed = term if mixed is None else mixed + term
            mixed_buf[rows] = mixed
            return carry

        lax.fori_loop(0, size // block, step, 0)
        mixed = mixed_buf[t * size : (t + 1) * size]
        stat_all[t, me, 0:1] = transpose_sum(mixed)
        stat_all[t, me, 1:2] = transpose_sum(mixed * mixed)
        stat_all[t, me, 2:8] = jnp.zeros((6, size), jnp.float32)
        for step in range(1, group):
            waits["stat", t, step] = go(
                send_to(stat_all.at[t, me], stat_all.at[t, me], stat_send.at[t, step],
                        stat_recv.at[t, step], lax.rem(me + step, group)))

    def normalized(t):
        for step in range(1, group):
            waits["stat", t, step].wait_recv()
        total = stat_all[t, 0]
        for index in range(1, group):
            total = total + stat_all[t, index]
        center = total[0:1] / width
        scale = lax.rsqrt(total[1:2] / width - center * center + 1e-05)
        row = lax.broadcasted_iota(jnp.int32, total.shape, 0)
        packed = jnp.where(row == 0, center, jnp.where(row == 1, scale, 0.0))
        columns[t] = jnp.transpose(packed)

        def step(index, carry):
            inside = pl.ds(index * block, block)
            rows = pl.ds(t * size + index * block, block)
            column = columns[t, inside]
            value = (mixed_buf[rows] - column[:, 0:1]) * column[:, 1:2]
            normed[rows] = value.astype(normed.dtype)
            return carry

        lax.fori_loop(0, size // block, step, 0)
        mine = normed.at[chunk_rows(t)]
        view = gathered.at[chunk_rows(t), lanes(me)]
        waits["fwd", t] = go(send_to(mine, view, pass_send.at[t, 0], pass_recv.at[t, 0], peer(turn)))
        waits["bwd", t] = go(send_to(mine, view, pass_send.at[t, 1], pass_recv.at[t, 1], peer(-turn)))
        waits["own", t] = go(send_to(mine, view, copy_send.at[t, 0], copy_recv.at[t, 0], sibling))
        local = pltpu.make_async_copy(mine, view, own_sem.at[t])
        local.start()
        waits["local", t] = local

    def hand_over(t, index, delta):
        view = gathered.at[chunk_rows(t), lanes(peer(delta))]
        waits["copy", t, index] = go(
            send_to(view, view, copy_send.at[t, index], copy_recv.at[t, index], sibling))

    def pass_on(t):
        waits["fwd", t].wait_recv()
        view = gathered.at[chunk_rows(t), lanes(peer(-turn))]
        waits["opp", t] = go(send_to(view, view, pass_send.at[t, 2], pass_recv.at[t, 2], peer(turn)))
        hand_over(t, 1, -turn)
        waits["bwd", t].wait_recv()
        hand_over(t, 2, turn)

    def pass_last(t):
        waits["opp", t].wait_recv()
        hand_over(t, 3, 2)

    def feed_forward(t):
        if t == 0:
            for load in loads[group:]:
                load.wait()
        waits["own", t].wait_recv()
        waits["local", t].wait()
        for index in (1, 2, 3):
            waits["copy", t, index].wait_recv()
        values = gathered.at[chunk_rows(t)]
        for strip in range(strips):
            gate = jnp.dot(values[...], gate_buf[strip], preferred_element_type=jnp.float32)
            up = jnp.dot(values[...], gate_buf[strips + strip], preferred_element_type=jnp.float32)
            hidden[:, strip * feature : (strip + 1) * feature] = (
                gate * lax.logistic(gate) * up
            ).astype(hidden.dtype)
        scatter(1, t, lambda head: jnp.dot(
            hidden[...], down_buf[head], preferred_element_type=jnp.float32))

    def last(t):
        finish(1, t)

        def step(index, carry):
            inside = pl.ds(index * block, block)
            rows = pl.ds(t * size + index * block, block)
            values = [first_buf[s, rows] for s in range(count)]
            result = remixed(1, values, delta_of(1, t, inside))
            total = result[0]
            for s in range(count):
                fresh_ref[s, rows] = result[s].astype(fresh_ref.dtype)
                if s > 0:
                    total = total + result[s]
            total_buf[rows] = total
            return carry

        lax.fori_loop(0, size // block, step, 0)

    phases = (
        project,
        lambda t: chip_sum(0, t),
        lambda t: chip_relay(0, t),
        middle,
        normalized,
        pass_on,
        pass_last,
        feed_forward,
        lambda t: chip_sum(1, t),
        lambda t: chip_relay(1, t),
        last,
    )
    for step in range(len(phases) + chunks - 1):
        for t in range(chunks):
            if 0 <= step - t < len(phases):
                phases[step - t](t)
    requests = accepted.shape[0]
    repeats = final_ref.shape[0] // requests
    tree = tokens // requests
    for item in range(requests):
        row = total_buf[pl.ds(item * tree + accepted[item], 1)]
        for copy_index in range(repeats):
            place = item * repeats + copy_index
            final_ref[place : place + 1] = row
    for copy in sends:
        copy.wait_send()


def layer(
    attended, streams, hc_in, hc_mix, hc_out, out_weight, gate_up, down_weight, accepted, repeats
):
    tokens, feature = attended.shape
    count = streams.shape[0]
    group = lax.axis_size("head")
    chips = group // 2
    width = out_weight.shape[1]
    inner = down_weight.shape[0]
    strips = inner // feature
    chunks = 3
    size = tokens // chunks
    bf16, f32 = jnp.bfloat16, jnp.float32
    dma = pltpu.SemaphoreType.DMA
    vmem = pl.BlockSpec(memory_space=pltpu.VMEM)
    smem = pl.BlockSpec(memory_space=pltpu.SMEM)
    anywhere = pl.BlockSpec(memory_space=pl.ANY)
    scratch = [
        pltpu.VMEM((group, feature, feature), bf16),
        pltpu.VMEM((2 * strips, width, feature), bf16),
        pltpu.VMEM((group, inner, feature), bf16),
        pltpu.VMEM((count, tokens, feature), f32),
        pltpu.VMEM((tokens, feature), f32),
        pltpu.VMEM((tokens, feature), f32),
        pltpu.VMEM((2, chunks, 2, chips, size, feature), bf16),
        pltpu.VMEM((2, chunks, chips, size, feature), bf16),
        pltpu.VMEM((2, chunks, size, feature), bf16),
        pltpu.VMEM((2, chunks, size, feature), bf16),
        pltpu.VMEM((2, chunks, size, feature), bf16),
        pltpu.VMEM((chunks, group, 8, size), f32),
        pltpu.VMEM((chunks, size, 8), f32),
        pltpu.VMEM((tokens, feature), bf16),
        pltpu.VMEM((tokens, width), bf16),
        pltpu.VMEM((size, inner), bf16),
        dma((3, max(group, 2 * strips))),
        dma((chunks,)),
        dma((2, chunks, 4)), dma((2, chunks, 4)),
        dma((2, chunks, 3)), dma((2, chunks, 3)),
        dma((chunks, group)), dma((chunks, group)),
        dma((chunks, 4)), dma((chunks, 4)),
        dma((chunks, 3)), dma((chunks, 3)),
    ]
    return pl.pallas_call(
        functools.partial(layer_kernel, chips, chunks),
        out_shape=(
            jax.ShapeDtypeStruct((count, tokens, feature), bf16),
            jax.ShapeDtypeStruct((accepted.shape[0] * repeats, feature), f32),
        ),
        in_specs=[smem] * 4 + [vmem, vmem, anywhere, anywhere, anywhere],
        out_specs=(vmem, vmem),
        scratch_shapes=scratch,
        compiler_params=pltpu.CompilerParams(
            collective_id=1, has_side_effects=True, vmem_limit_bytes=60 << 20
        ),
    )(
        hc_in.reshape(-1),
        hc_mix.reshape(-1),
        hc_out.reshape(-1),
        accepted,
        attended,
        streams,
        out_weight,
        gate_up,
        down_weight,
    )


def draft_kernel(
    chips,
    final_ref,
    weight_hbm,
    vocab_hbm,
    logits_ref,
    final_all,
    weight_buf,
    vocab_buf,
    gathered,
    total,
    load_sem,
    sum_send,
    sum_recv,
    draft_send,
    draft_recv,
    copy_send,
    copy_recv,
    pass_send,
    pass_recv,
):
    rows, feature = final_ref.shape
    group = 2 * chips
    width = group * feature
    devices = gathered.shape[1] // rows
    me = lax.axis_index("head")
    home = lax.axis_index("req")
    chip = me // 2
    core = lax.rem(me, 2)
    turn = 1 - 2 * core
    sibling = chip * 2 + 1 - core

    def peer(delta):
        return lax.rem(chip + chips + delta, chips) * 2 + core

    def send_to(source, target, send_sem, recv_sem, device):
        return pltpu.make_async_remote_copy(
            src_ref=source,
            dst_ref=target,
            send_sem=send_sem,
            recv_sem=recv_sem,
            device_id=device,
            device_id_type=MESH,
        )

    loads = [pltpu.make_async_copy(weight_hbm, weight_buf, load_sem.at[0])]
    for index in range(group):
        loads.append(
            pltpu.make_async_copy(
                vocab_hbm.at[:, pl.ds(index * feature, feature)],
                vocab_buf.at[index],
                load_sem.at[1 + index],
            )
        )
    for load in loads:
        load.start()
    barrier = pltpu.get_barrier_semaphore()
    for step in range(1, group):
        pl.semaphore_signal(
            barrier, inc=1, device_id={"head": lax.rem(me + step, group)}, device_id_type=MESH
        )
    for step in range(1, devices):
        pl.semaphore_signal(
            barrier, inc=1, device_id={"req": lax.rem(home + step, devices)}, device_id_type=MESH
        )
    pl.semaphore_wait(barrier, group + devices - 2)

    sends = []

    def go(copy):
        copy.start()
        sends.append(copy)
        return copy

    sums = []
    for step in range(1, group):
        sums.append(
            go(send_to(final_ref, final_all.at[me], sum_send.at[step], sum_recv.at[step],
                       {"head": lax.rem(me + step, group)}))
        )
    final_all[me] = final_ref[...]
    loads[0].wait()
    for copy in sums:
        copy.wait_recv()
    center = jnp.zeros((rows, 1), jnp.float32)
    square = jnp.zeros((rows, 1), jnp.float32)
    for index in range(group):
        values = final_all[index]
        center = center + jnp.sum(values, axis=1, keepdims=True)
        square = square + jnp.sum(values * values, axis=1, keepdims=True)
    center = center / width
    scale = lax.rsqrt(square / width - center * center + 1e-05)
    branches = []
    for kind in range(2):
        branch = jnp.zeros((rows, feature), jnp.float32)
        for index in range(group):
            values = ((final_all[index] - center) * scale).astype(jnp.bfloat16)
            branch = branch + jnp.dot(
                values,
                weight_buf[kind, index * feature : (index + 1) * feature],
                preferred_element_type=jnp.float32,
            )
        branches.append(branch)
    odd = (lax.broadcasted_iota(jnp.int32, (rows, feature), 0) & 1) == 1
    branch = jnp.where(odd, branches[1], branches[0])
    drafted = (final_ref[...] - center) * scale + branch * lax.logistic(branch)
    mine = gathered.at[me, pl.ds(pl.multiple_of(home * rows, rows), rows)]
    mine[...] = drafted.astype(gathered.dtype)
    drafts = []
    for step in range(1, devices):
        drafts.append(
            go(send_to(mine, mine, draft_send.at[step], draft_recv.at[step],
                       {"req": lax.rem(home + step, devices)}))
        )
    for copy in drafts:
        copy.wait_recv()

    def shard(head):
        return gathered.at[head]

    def ring(index, delta, source):
        return go(send_to(shard(source), shard(source), pass_send.at[index], pass_recv.at[index],
                          {"head": peer(delta)}))

    def hand_over(index, source):
        return go(send_to(shard(source), shard(source), copy_send.at[index], copy_recv.at[index],
                          {"head": sibling}))

    fwd = ring(0, turn, me)
    bwd = ring(1, -turn, me)
    hands = [hand_over(0, me)]
    for load in loads[1:]:
        load.wait()

    def add(head, first=False):
        value = lax.dot_general(
            gathered[head],
            vocab_buf[head],
            (((1,), (1,)), ((), ())),
            preferred_element_type=jnp.float32,
        )
        total[...] = value if first else total[...] + value

    add(me, True)
    fwd.wait_recv()
    opp = ring(2, turn, peer(-turn))
    hands.append(hand_over(1, peer(-turn)))
    bwd.wait_recv()
    hands.append(hand_over(2, peer(turn)))
    add(peer(-turn))
    hands[0].wait_recv()
    add(sibling)
    add(peer(turn))
    opp.wait_recv()
    hands.append(hand_over(3, peer(2)))
    hands[1].wait_recv()

    def across(delta):
        return lax.rem(chip + chips + delta, chips) * 2 + 1 - core

    add(across(turn))
    hands[2].wait_recv()
    add(across(-turn))
    add(peer(2))
    hands[3].wait_recv()
    add(across(2))
    logits_ref[...] = total[...].astype(logits_ref.dtype)
    for copy in sends:
        copy.wait_send()


def draft_logits(final_rows, draft_weight, lm_head):
    rows, feature = final_rows.shape
    group = lax.axis_size("head")
    devices = lax.axis_size("req")
    width, vocab = lm_head.shape
    bf16, f32 = jnp.bfloat16, jnp.float32
    dma = pltpu.SemaphoreType.DMA
    vmem = pl.BlockSpec(memory_space=pltpu.VMEM)
    anywhere = pl.BlockSpec(memory_space=pl.ANY)
    return pl.pallas_call(
        functools.partial(draft_kernel, group // 2),
        out_shape=jax.ShapeDtypeStruct((devices * rows, vocab), bf16),
        in_specs=[vmem, anywhere, anywhere],
        out_specs=vmem,
        scratch_shapes=[
            pltpu.VMEM((group, rows, feature), f32),
            pltpu.VMEM(draft_weight.shape, bf16),
            pltpu.VMEM((group, vocab, feature), bf16),
            pltpu.VMEM((group, devices * rows, feature), bf16),
            pltpu.VMEM((devices * rows, vocab), f32),
            dma((1 + group,)),
            dma((group,)), dma((group,)),
            dma((devices,)), dma((devices,)),
            dma((4,)), dma((4,)),
            dma((3,)), dma((3,)),
        ],
        compiler_params=pltpu.CompilerParams(
            collective_id=2, has_side_effects=True, vmem_limit_bytes=40 << 20
        ),
    )(final_rows, draft_weight, jnp.transpose(lm_head))


def on_device(
    streams,
    hc_in,
    hc_mix,
    hc_out,
    qkv_weight,
    out_weight,
    up_gate,
    down_weight,
    draft_weight,
    lm_head,
    k_pages,
    v_pages,
    page_owner,
    page_fill,
    cache_len,
    tree_parent,
    accepted_index,
):
    tokens_local = streams.shape[0]
    feature_local = streams.shape[2]
    width = qkv_weight.shape[0]
    req_local = cache_len.shape[0]
    tree_size = tree_parent.shape[1]
    slot_count = k_pages.shape[0]
    page_size = k_pages.shape[1]
    heads_local = k_pages.shape[2]
    head_dim = k_pages.shape[3]
    draft_count = draft_weight.shape[0]
    all_requests = req_local * lax.axis_size("req")
    reach = ancestors(tree_parent)
    depth = (jnp.sum(reach, axis=2) - 1.0).astype(jnp.int32)
    positions = (cache_len[:, None] + depth).reshape(tokens_local)
    stream_vals = streams.astype(jnp.float32)
    mixed_in = blend(stream_vals, hc_in[0])
    stat_sum, stat_square = lax.psum(
        (jnp.sum(mixed_in, axis=1), jnp.sum(mixed_in * mixed_in, axis=1)), "head"
    )
    normed = normalize(mixed_in, stat_sum[:, None], stat_square[:, None], width).astype(
        jnp.bfloat16
    )
    qkv_flat = qkv_weight.reshape(width, -1)
    normed_full = lax.all_gather(normed, "head", axis=1, tiled=True)
    gate_up = jnp.transpose(up_gate, (1, 0, 2))
    normed_full, gate_up = lax.optimization_barrier((normed_full, gate_up))
    projected = fold_rows(qkv_flat, normed_full)
    projected = projected.reshape(tokens_local, 3, heads_local, head_dim)
    queries = (rotate(projected[:, 0], positions) * head_dim ** (-0.5)).astype(jnp.bfloat16)
    keys_new = rotate(projected[:, 1], positions).astype(jnp.bfloat16)
    values_new = projected[:, 2].astype(jnp.bfloat16)
    query_rows = (
        queries.reshape(req_local, tree_size, heads_local, head_dim)
        .transpose(0, 2, 1, 3)
        .reshape(req_local, heads_local * tree_size, head_dim)
    )
    own_sum, own_top, own_den = cache_attention(
        query_rows, k_pages, v_pages, page_owner, page_fill
    )
    own_sum = own_sum.reshape(req_local, heads_local, tree_size, head_dim).transpose(0, 2, 1, 3)
    used = heads_local * tree_size
    own_top = own_top[:, :used].reshape(req_local, heads_local, tree_size).transpose(0, 2, 1)
    own_den = own_den[:, :used].reshape(req_local, heads_local, tree_size).transpose(0, 2, 1)
    query_own = queries.reshape(req_local, tree_size, heads_local, head_dim)
    keys_own = keys_new.reshape(req_local, tree_size, heads_local, head_dim)
    values_own = values_new.reshape(req_local, tree_size, heads_local, head_dim)
    tree_scores = jnp.einsum(
        "jqhd,jkhd->jqhk", query_own, keys_own, preferred_element_type=jnp.float32
    )
    tree_mask = (reach > 0)[:, :, None, :]
    tree_scores = jnp.where(tree_mask, tree_scores, NEG_FILL)
    top = jnp.maximum(own_top, jnp.max(tree_scores, axis=3))
    carried = jnp.exp(own_top - top)
    tree_weights = jnp.where(tree_mask, jnp.exp(tree_scores - top[..., None]), 0.0)
    denominator = own_den * carried + jnp.sum(tree_weights, axis=3)
    numerator = own_sum * carried[..., None] + jnp.einsum(
        "jqhk,jkhd->jqhd",
        tree_weights.astype(jnp.bfloat16),
        values_own,
        preferred_element_type=jnp.float32,
    )
    attended = (
        (numerator / denominator[..., None])
        .astype(jnp.bfloat16)
        .reshape(tokens_local, heads_local * head_dim)
    )
    fresh, final_local = layer(
        attended,
        jnp.transpose(streams, (1, 0, 2)),
        hc_in,
        hc_mix,
        hc_out,
        out_weight,
        gate_up,
        down_weight,
        accepted_index,
        draft_count,
    )
    new_streams = jnp.transpose(fresh, (1, 0, 2))
    logits_local = draft_logits(final_local, draft_weight, lm_head)
    logits_local = logits_local.reshape(all_requests, draft_count, -1)
    logits = lax.all_to_all(
        logits_local, ("req", "head"), split_axis=0, concat_axis=2, tiled=True
    ).astype(jnp.float32)
    return (new_streams, logits)


def solution(mesh):
    in_specs = (
        P("req", None, "head"),
        P(),
        P(),
        P(),
        P(None, None, "head"),
        P("head", None),
        P(None, None, "head"),
        P("head", None),
        P(None, None, "head"),
        P(None, ("req", "head")),
        P("req", None, "head", None),
        P("req", None, "head", None),
        P("req"),
        P("req"),
        P("req"),
        P("req", None),
        P("req"),
    )
    out_specs = (P("req", None, "head"), P(("req", "head"), None, None))
    return jax.shard_map(
        on_device, mesh=mesh, in_specs=in_specs, out_specs=out_specs, check_vma=False
    )
```

```python
import functools
import math

import jax
import jax.numpy as jnp
from jax import lax
from jax.experimental import pallas as pl
from jax.experimental.pallas import tpu as pltpu
from jax.sharding import PartitionSpec as P

NEG_FILL = -1e30


def ancestors(parents):
    length = parents.shape[1]
    places = jnp.arange(length, dtype=jnp.int32)
    linked = (places[None, :, None] == parents[:, None, :]) | (places[:, None] == places[None, :])[
        None
    ]
    reach = linked.astype(jnp.bfloat16)
    for repeat in range(max(1, (length - 1).bit_length())):
        counts = jnp.einsum("jki,jil->jkl", reach, reach, preferred_element_type=jnp.float32)
        reach = jnp.minimum(counts, 1.0).astype(jnp.bfloat16)
    return reach


def turns(positions, head_dim):
    half = head_dim // 2
    freqs = jnp.exp(
        jnp.arange(half, dtype=jnp.float32) * (-2.0 * math.log(10000.0) / head_dim)
    )
    angles = positions.astype(jnp.float32)[:, None] * freqs[None, :]
    cosine = jnp.cos(angles)
    sine = jnp.sin(angles)
    return jnp.concatenate([cosine, cosine], axis=1), jnp.concatenate([-sine, sine], axis=1)


MESH = pl.DeviceIdType.MESH
SLOT_BITS = 6
FILL_BITS = 8


def remote(source, target, send_sem, recv_sem, req):
    return pltpu.make_async_remote_copy(
        src_ref=source,
        dst_ref=target,
        send_sem=send_sem,
        recv_sem=recv_sem,
        device_id={"req": req},
        device_id_type=MESH,
    )


def weigh(tops, totals):
    top = functools.reduce(jnp.maximum, tops)
    factors = [jnp.exp(value - top) for value in tops]
    total = functools.reduce(lambda a, b: a + b, [f * t for f, t in zip(factors, totals)])
    return top, total, factors


def cache_kernel(
    side,
    table,
    last,
    q_ref,
    key_ref,
    value_ref,
    mask_ref,
    k_hbm,
    v_hbm,
    out_ref,
    tree_acc,
    tree_stat,
    q_all,
    k_buf,
    v_buf,
    scores,
    seg_acc,
    seg_top,
    seg_den,
    parts,
    stats,
    relay,
    merged,
    single,
    relay_s,
    merged_s,
    single_s,
    outgoing_s,
    factors,
    small,
    small_s,
    hop,
    hop_s,
    gather_send,
    gather_recv,
    spread_send,
    spread_recv,
    load_sem,
    far_send,
    far_recv,
    near_send,
    near_recv,
    join_send,
    join_recv,
    stat_send,
    stat_recv,
    last_send,
    last_recv,
    last_stat_send,
    last_stat_recv,
):
    block = q_ref.shape[0] // 2
    rows = q_ref.shape[1]
    slots = k_buf.shape[0]
    half_rows = rows // 2
    me = lax.axis_index("req")
    place = (me // side, lax.rem(me, side))
    turn = 1 - 2 * lax.rem(lax.axis_index("head"), 2)

    def shifted(axis, delta):
        moved = lax.rem(place[axis] + side + delta, side)
        return moved * side + place[1] if axis == 0 else place[0] * side + moved

    def at(axis, delta):
        return lax.rem(place[axis] + side + delta, side)

    first = (0, 1)
    second = (1, 0)

    def spot(half, p2, p1):
        return pl.ds(((half * side + p2) * side + p1) * block, block)

    loads = [
        pltpu.make_async_copy(k_hbm, k_buf, load_sem.at[0]),
        pltpu.make_async_copy(v_hbm, v_buf, load_sem.at[1]),
    ]
    for load in loads:
        load.start()
    barrier = pltpu.get_barrier_semaphore()
    for axis in (0, 1):
        for delta in (1, -1):
            pl.semaphore_signal(
                barrier, inc=1, device_id={"req": shifted(axis, delta)}, device_id_type=MESH
            )
    pl.semaphore_wait(barrier, 4)

    sends = []

    def go(copy):
        copy.start()
        sends.append(copy)
        return copy

    def pass_block(half, axis, delta, p2, p1, send, recv, own=False):
        view = q_all.at[spot(half, p2, p1)]
        source = q_ref.at[pl.ds(half * block, block)] if own else view
        return go(remote(source, view, send, recv, shifted(axis, delta)))

    lines = {}
    crosses = {}

    def line(half, index, delta, p1, own=False):
        lines[half, index] = pass_block(
            half, first[half], delta, at(second[half], 0), p1,
            gather_send.at[half, index], gather_recv.at[half, index], own,
        )

    def cross(half, piece, index, delta, p2, p1, own=False):
        crosses[half, piece, index] = pass_block(
            half, second[half], delta, p2, p1,
            spread_send.at[half, piece, index], spread_recv.at[half, piece, index], own,
        )

    halves = (0, 1)
    for half in halves:
        line(half, 0, turn, at(first[half], 0), True)
        line(half, 1, -turn, at(first[half], 0), True)
    for half in halves:
        cross(half, 0, 0, turn, at(second[half], 0), at(first[half], 0), True)
        cross(half, 0, 1, -turn, at(second[half], 0), at(first[half], 0), True)
    for half in halves:
        q_all[spot(half, at(second[half], 0), at(first[half], 0))] = q_ref[
            half * block : (half + 1) * block
        ]
    seg_top[...] = jnp.full(seg_top.shape, NEG_FILL, jnp.float32)
    seg_den[...] = jnp.zeros(seg_den.shape, jnp.float32)
    seg_acc[slots] = jnp.zeros(seg_acc.shape[1:], seg_acc.dtype)
    tree_stat[...] = jnp.zeros(tree_stat.shape, jnp.float32)

    def tree_step(item, carry):
        found = lax.dot_general(
            key_ref[item],
            q_ref[item],
            (((1,), (1,)), ((), ())),
            preferred_element_type=jnp.float32,
        )
        found = jnp.where(mask_ref[item].astype(jnp.float32) > 0.0, found, NEG_FILL)
        top = jnp.max(found, axis=0, keepdims=True)
        weight = jnp.exp(found - top)
        tree_acc[item] = lax.dot_general(
            weight.astype(jnp.bfloat16),
            value_ref[item],
            (((0,), (0,)), ((), ())),
            preferred_element_type=jnp.float32,
        )
        tree_stat[0, item, :, 0:rows] = top
        tree_stat[1, item, :, 0:rows] = jnp.sum(weight, axis=0, keepdims=True)
        return carry

    lax.fori_loop(0, 2 * block, tree_step, 0)
    for half in halves:
        lines[half, 0].wait_recv()
        line(half, 2, turn, at(first[half], -turn))
        cross(half, 1, 0, turn, at(second[half], 0), at(first[half], -turn))
        cross(half, 1, 1, -turn, at(second[half], 0), at(first[half], -turn))
    for half in halves:
        lines[half, 1].wait_recv()
        cross(half, 2, 0, turn, at(second[half], 0), at(first[half], turn))
        cross(half, 2, 1, -turn, at(second[half], 0), at(first[half], turn))
    for half in halves:
        crosses[half, 0, 0].wait_recv()
        cross(half, 0, 2, turn, at(second[half], -turn), at(first[half], 0))
    for half in halves:
        lines[half, 2].wait_recv()
        cross(half, 3, 0, turn, at(second[half], 0), at(first[half], 2))
        cross(half, 3, 1, -turn, at(second[half], 0), at(first[half], 2))
    for piece, delta in ((1, -turn), (2, turn), (3, 2)):
        for half in halves:
            crosses[half, piece, 0].wait_recv()
            cross(half, piece, 2, turn, at(second[half], -turn), at(first[half], delta))
    for piece in range(4):
        for half in halves:
            crosses[half, piece, 1].wait_recv()
            crosses[half, piece, 2].wait_recv()
    for load in loads:
        load.wait()

    slot_mask = (1 << SLOT_BITS) - 1
    fill_mask = (1 << FILL_BITS) - 1
    requests = 2 * block * side * side

    def owner_at(index):
        return table[index] >> (SLOT_BITS + FILL_BITS)

    def starts_new(index):
        before = owner_at(jnp.maximum(index - 1, 0))
        return jnp.logical_or(index == 0, before != owner_at(index))

    shape = (k_buf.shape[1], rows)
    row_ids = lax.broadcasted_iota(jnp.int32, shape, 0)
    col_head = (lax.broadcasted_iota(jnp.int32, shape, 1) >= half_rows).astype(jnp.int32)
    matched = (row_ids & 1) == col_head
    key_ids = row_ids >> 1
    unroll = 4

    def score_step(group, carry):
        for offset in range(unroll):
            index = group * unroll + offset
            entry = table[index]
            fill = (entry >> SLOT_BITS) & fill_mask
            owner = jnp.minimum(entry >> (SLOT_BITS + FILL_BITS), requests - 1)
            home = owner // (2 * block)
            within = lax.rem(owner, 2 * block)
            half = within // block
            hx = home // side
            hy = lax.rem(home, side)
            outer = jnp.where(half == 0, hy, hx)
            inner = jnp.where(half == 0, hx, hy)
            row = ((half * side + outer) * side + inner) * block + lax.rem(within, block)
            found = lax.dot_general(
                k_buf[entry & slot_mask],
                q_all[row],
                (((1,), (1,)), ((), ())),
                preferred_element_type=jnp.float32,
            )
            found = jnp.where(jnp.logical_and(matched, key_ids < fill), found, NEG_FILL)
            scores[index] = found
            seg_top[index, :, 0:rows] = jnp.max(found, axis=0, keepdims=True)
        return carry

    lax.fori_loop(0, slots // unroll, score_step, 0)

    def forward(index, run):
        here = seg_top[index]
        run = jnp.where(starts_new(index), here, jnp.maximum(run, here))
        seg_top[index] = run
        return run

    lax.fori_loop(0, slots, forward, jnp.full(seg_top.shape[1:], NEG_FILL, jnp.float32))

    def backward(step, run):
        index = slots - 1 - step
        follow = jnp.minimum(index + 1, slots - 1)
        ends = jnp.logical_or(step == 0, owner_at(follow) != owner_at(index))
        run = jnp.where(ends, seg_top[index], run)
        seg_top[index] = run
        return run

    lax.fori_loop(0, slots, backward, jnp.full(seg_top.shape[1:], NEG_FILL, jnp.float32))

    def value_step(group, carry):
        acc_run, den_run = carry
        for offset in range(unroll):
            index = group * unroll + offset
            fresh = starts_new(index)
            top = seg_top[index][:, 0:rows]
            top = jnp.where(top < 0.5 * NEG_FILL, 0.0, top)
            weight = jnp.exp(scores[index] - top)
            den = jnp.sum(weight, axis=0, keepdims=True)
            acc = lax.dot_general(
                weight.astype(jnp.bfloat16),
                v_buf[table[index] & slot_mask],
                (((0,), (0,)), ((), ())),
                preferred_element_type=jnp.float32,
            )
            acc_run = acc + jnp.where(fresh, 0.0, acc_run)
            den_run = den + jnp.where(fresh, 0.0, den_run)
            seg_acc[index] = acc_run.astype(seg_acc.dtype)
            seg_den[index, :, 0:rows] = den_run
        return acc_run, den_run

    lax.fori_loop(
        0,
        slots // unroll,
        value_step,
        (jnp.zeros(seg_acc.shape[1:], jnp.float32), jnp.zeros((1, rows), jnp.float32)),
    )

    def place_step(group, carry):
        for piece in range(side):
            tops, dens = [], []
            for offset in range(block):
                spot_index = (group * side + piece) * block + offset
                found = last[spot_index]
                parts[spot_index] = seg_acc[found]
                tops.append(seg_top[found])
                dens.append(seg_den[found])
            stats[group, 0, piece * block : (piece + 1) * block] = jnp.concatenate(tops, axis=0)
            stats[group, 1, piece * block : (piece + 1) * block] = jnp.concatenate(dens, axis=0)
        return carry

    lax.fori_loop(0, 2 * side, place_step, 0)

    def part(half, p2, p1):
        return parts.at[spot(half, p2, p1)]

    def stat(half, p2):
        return stats.at[half * side + p2]

    def combine(put, terms, weights):
        columns = [jnp.transpose(weight) for weight in weights]
        for item in range(block):
            total = None
            for term, column in zip(terms, columns):
                value = term[item].astype(jnp.float32) * column[0:rows, item : item + 1]
                total = value if total is None else total + value
            put(item, total)

    stat_copies = {}
    far, near = {}, {}
    for half in halves:
        up, down = shifted(second[half], turn), shifted(second[half], -turn)
        stat_copies[half, 0] = go(
            remote(stat(half, at(second[half], 2)), relay_s.at[half],
                   stat_send.at[half, 0], stat_recv.at[half, 0], up))
        stat_copies[half, 1] = go(
            remote(stat(half, at(second[half], -turn)), single_s.at[half],
                   stat_send.at[half, 1], stat_recv.at[half, 1], down))
    for order in range(4):
        for half in halves:
            up, down = shifted(second[half], turn), shifted(second[half], -turn)
            p1 = at(first[half], 2 - turn * order)
            far[half, order] = go(
                remote(part(half, at(second[half], 2), p1), relay.at[half, p1],
                       far_send.at[half, order], far_recv.at[half, order], up))
            near[half, order] = go(
                remote(part(half, at(second[half], -turn), p1), single.at[half, p1],
                       near_send.at[half, order], near_recv.at[half, order], down))

    for half in halves:
        stat_copies[half, 0].wait_recv()
        mine = stat(half, at(second[half], turn))
        top, den, weights = weigh([mine[0], relay_s[half, 0]], [mine[1], relay_s[half, 1]])
        outgoing_s[half, 0] = top
        outgoing_s[half, 1] = den
        factors[half, 0] = weights[0]
        factors[half, 1] = weights[1]
        stat_copies[half, 2] = go(
            remote(outgoing_s.at[half], merged_s.at[half],
                   stat_send.at[half, 2], stat_recv.at[half, 2], shifted(second[half], turn)))

    def join_copy(half, order):
        p1 = at(first[half], 2 - turn * order)
        return remote(relay.at[half, p1], merged.at[half, p1],
                      join_send.at[half, order], join_recv.at[half, order],
                      shifted(second[half], turn))

    def far_copy(half, order):
        p1 = at(first[half], 2 - turn * order)
        return remote(part(half, at(second[half], 2), p1), relay.at[half, p1],
                      far_send.at[half, order], far_recv.at[half, order],
                      shifted(second[half], turn))

    def near_copy(half, order):
        p1 = at(first[half], 2 - turn * order)
        return remote(part(half, at(second[half], -turn), p1), single.at[half, p1],
                      near_send.at[half, order], near_recv.at[half, order],
                      shifted(second[half], -turn))

    def relay_step(order, carry):
        for half in halves:
            p1 = at(first[half], 2 + side - turn * order)
            far_copy(half, order).wait_recv()
            lanes = pl.ds(p1 * block, block)
            target = relay.at[half, p1]

            def put(item, value):
                target[item] = value.astype(target.dtype)

            combine(
                put,
                [part(half, at(second[half], turn), p1), target],
                [factors[half, 0, lanes], factors[half, 1, lanes]],
            )
            join_copy(half, order).start()
        return carry

    lax.fori_loop(0, 4, relay_step, 0)

    for half in halves:
        stat_copies[half, 1].wait_recv()
        stat_copies[half, 2].wait_recv()
        mine = stat(half, at(second[half], 0))
        top, den, weights = weigh(
            [mine[0], merged_s[half, 0], single_s[half, 0]],
            [mine[1], merged_s[half, 1], single_s[half, 1]],
        )
        for index in range(3):
            factors[half, index] = weights[index]
        for p1 in range(side):
            small_s[half, p1, 0] = top[p1 * block : (p1 + 1) * block]
            small_s[half, p1, 1] = den[p1 * block : (p1 + 1) * block]

    def gather_piece(half, order):
        p1 = at(first[half], 2 + side - turn * order)
        near_copy(half, order).wait_recv()
        join_copy(half, order).wait_recv()
        lanes = pl.ds(p1 * block, block)
        target = small.at[half, p1]

        def put(item, value):
            target[item] = value.astype(target.dtype)

        combine(
            put,
            [part(half, at(second[half], 0), p1), merged.at[half, p1], single.at[half, p1]],
            [factors[half, index, lanes] for index in range(3)],
        )

    def piece_step(order, carry):
        for half in halves:
            gather_piece(half, order)
        return carry

    tails = {}

    def tail(half, index, source, source_s, delta):
        peer = shifted(first[half], delta)
        tails[half, index] = (
            go(remote(source_s, hop_s.at[half, index],
                      last_stat_send.at[half, index], last_stat_recv.at[half, index], peer)),
            go(remote(source, hop.at[half, index],
                      last_send.at[half, index], last_recv.at[half, index], peer)),
        )

    lax.fori_loop(0, 1, piece_step, 0)
    for half in halves:
        p1 = at(first[half], 2)
        tail(half, 0, small.at[half, p1], small_s.at[half, p1], turn)
    lax.fori_loop(1, 2, piece_step, 0)
    lax.fori_loop(2, 4, piece_step, 0)
    for half in halves:
        p1 = at(first[half], -turn)
        tail(half, 1, small.at[half, p1], small_s.at[half, p1], -turn)
    for half in halves:
        p1 = at(first[half], turn)
        for copy in tails[half, 0]:
            copy.wait_recv()
        target = small.at[half, p1]
        top, den, weights = weigh(
            [small_s[half, p1, 0], hop_s[half, 0, 0]], [small_s[half, p1, 1], hop_s[half, 0, 1]]
        )
        small_s[half, p1, 0] = top
        small_s[half, p1, 1] = den

        def put(item, value, target=target):
            target[item] = value.astype(target.dtype)

        combine(put, [target, hop.at[half, 0]], weights)
        tail(half, 2, target, small_s.at[half, p1], turn)
    for half in halves:
        p1 = at(first[half], 0)
        for index in (1, 2):
            for copy in tails[half, index]:
                copy.wait_recv()
        tree = [
            jnp.concatenate(
                [tree_stat[kind, half * block + item] for item in range(block)], axis=0
            )
            for kind in (0, 1)
        ]
        top, den, weights = weigh(
            [small_s[half, p1, 0], hop_s[half, 1, 0], hop_s[half, 2, 0], tree[0]],
            [small_s[half, p1, 1], hop_s[half, 1, 1], hop_s[half, 2, 1], tree[1]],
        )
        lane = lax.broadcasted_iota(jnp.int32, den.shape, 1)
        inverse = 1.0 / jnp.where(lane < rows, den, 1.0)

        def put(item, value, half=half):
            start = (half * block + item) * half_rows
            value = value.astype(out_ref.dtype)
            width = value.shape[1]
            for head in (0, 1):
                out_ref[start : start + half_rows, head * width : (head + 1) * width] = value[
                    head * half_rows : (head + 1) * half_rows
                ]

        combine(
            put,
            [
                small.at[half, p1],
                hop.at[half, 1],
                hop.at[half, 2],
                tree_acc.at[pl.ds(half * block, block)],
            ],
            [weight * inverse for weight in weights],
        )
    for copy in sends:
        copy.wait_send()
    for half in halves:
        for order in range(4):
            join_copy(half, order).wait_send()


def cache_attention(
    queries, keys_new, values_new, tree_mask, k_pages, v_pages, page_owner, page_fill
):
    req_local, rows, head_dim = queries.shape
    slots, keys = k_pages.shape[0], k_pages.shape[1] * k_pages.shape[2]
    devices = lax.axis_size("req")
    side = math.isqrt(devices)
    block = req_local // 2
    requests = req_local * devices
    owner_key = jnp.where(page_owner < 0, requests, page_owner)
    packed = (
        (owner_key << (SLOT_BITS + FILL_BITS))
        | (jnp.where(page_owner < 0, 0, page_fill) << SLOT_BITS)
        | jnp.arange(slots, dtype=jnp.int32)
    )
    rank = jnp.sum((packed[None, :] < packed[:, None]).astype(jnp.int32), axis=1)
    places = jnp.arange(slots, dtype=jnp.int32)
    table = jnp.sum(jnp.where(rank[None, :] == places[:, None], packed[None, :], 0), axis=1)
    spots = jnp.arange(requests, dtype=jnp.int32)
    half = spots // (requests // 2)
    outer = (spots // (block * side)) % side
    inner = (spots // block) % side
    home = jnp.where(half == 0, inner * side + outer, outer * side + inner)
    request = home * req_local + half * block + spots % block
    below = jnp.sum((owner_key[None, :] <= request[:, None]).astype(jnp.int32), axis=1)
    exact = jnp.sum((owner_key[None, :] == request[:, None]).astype(jnp.int32), axis=1)
    last = jnp.where(exact > 0, below - 1, slots)
    bf16, f32 = jnp.bfloat16, jnp.float32
    unit = (2, side, block, rows, head_dim)
    dma = pltpu.SemaphoreType.DMA
    scratch = [
        pltpu.VMEM((req_local, rows, head_dim), f32),
        pltpu.VMEM((2, req_local, 1, 128), f32),
        pltpu.VMEM((requests, rows, head_dim), bf16),
        pltpu.VMEM((slots, keys, head_dim), bf16),
        pltpu.VMEM((slots, keys, head_dim), bf16),
        pltpu.VMEM((slots, keys, rows), f32),
        pltpu.VMEM((slots + 1, rows, head_dim), bf16),
        pltpu.VMEM((slots + 1, 1, 128), f32),
        pltpu.VMEM((slots + 1, 1, 128), f32),
        pltpu.VMEM((requests, rows, head_dim), bf16),
        pltpu.VMEM((2 * side, 2, side * block, 128), f32),
        pltpu.VMEM(unit, bf16),
        pltpu.VMEM(unit, bf16),
        pltpu.VMEM(unit, bf16),
        pltpu.VMEM((2, 2, side * block, 128), f32),
        pltpu.VMEM((2, 2, side * block, 128), f32),
        pltpu.VMEM((2, 2, side * block, 128), f32),
        pltpu.VMEM((2, 2, side * block, 128), f32),
        pltpu.VMEM((2, 3, side * block, 128), f32),
        pltpu.VMEM(unit, bf16),
        pltpu.VMEM((2, side, 2, block, 128), f32),
        pltpu.VMEM((2, 3, block, rows, head_dim), bf16),
        pltpu.VMEM((2, 3, 2, block, 128), f32),
        dma((2, 3)), dma((2, 3)),
        dma((2, 4, 3)), dma((2, 4, 3)),
        dma((2,)),
        dma((2, 4)), dma((2, 4)),
        dma((2, 4)), dma((2, 4)),
        dma((2, 4)), dma((2, 4)),
        dma((2, 3)), dma((2, 3)),
        dma((2, 3)), dma((2, 3)),
        dma((2, 3)), dma((2, 3)),
    ]
    vmem = pl.BlockSpec(memory_space=pltpu.VMEM)
    smem = pl.BlockSpec(memory_space=pltpu.SMEM)
    anywhere = pl.BlockSpec(memory_space=pl.ANY)
    return pl.pallas_call(
        functools.partial(cache_kernel, side),
        out_shape=jax.ShapeDtypeStruct((req_local * rows // 2, 2 * head_dim), bf16),
        in_specs=[smem, smem] + [vmem] * 4 + [anywhere, anywhere],
        out_specs=vmem,
        scratch_shapes=scratch,
        compiler_params=pltpu.CompilerParams(
            collective_id=0, has_side_effects=True, vmem_limit_bytes=56 << 20
        ),
    )(
        table,
        last,
        queries,
        keys_new,
        values_new,
        tree_mask,
        k_pages.reshape(slots, keys, head_dim),
        v_pages.reshape(slots, keys, head_dim),
    )


def transpose_sum(values):
    half = values.shape[1] // 2
    return jnp.sum(jnp.transpose(values[:, 0:half] + values[:, half:]), axis=0, keepdims=True)


def layer_kernel(
    chips,
    chunks,
    hc_in,
    hc_mix,
    hc_out,
    accepted,
    attended,
    streams,
    out_hbm,
    gate_hbm,
    down_hbm,
    fresh_ref,
    final_ref,
    out_buf,
    gate_buf,
    down_buf,
    first_buf,
    mixed_buf,
    total_buf,
    share,
    twin,
    relay,
    joined,
    single,
    stat_all,
    columns,
    normed,
    gathered,
    hidden,
    load_sem,
    own_sem,
    twin_send,
    twin_recv,
    ring_send,
    ring_recv,
    stat_send,
    stat_recv,
    copy_send,
    copy_recv,
    pass_send,
    pass_recv,
):
    tokens, feature = attended.shape
    size = tokens // chunks
    group = 2 * chips
    width = group * feature
    count = streams.shape[0]
    inner = hidden.shape[1]
    strips = inner // feature
    me = lax.axis_index("head")
    chip = me // 2
    core = lax.rem(me, 2)
    turn = 1 - 2 * core

    def at(delta):
        return lax.rem(chip + chips + delta, chips)

    def peer(delta):
        return at(delta) * 2 + core

    sibling = chip * 2 + 1 - core

    def send_to(source, target, send_sem, recv_sem, head):
        return pltpu.make_async_remote_copy(
            src_ref=source,
            dst_ref=target,
            send_sem=send_sem,
            recv_sem=recv_sem,
            device_id={"head": head},
            device_id_type=MESH,
        )

    loads = []
    for index in range(group):
        loads.append(
            pltpu.make_async_copy(
                out_hbm.at[:, pl.ds(index * feature, feature)], out_buf.at[index], load_sem.at[0, index]
            )
        )
    for index in range(2 * strips):
        kind, strip = index // strips, index % strips
        loads.append(
            pltpu.make_async_copy(
                gate_hbm.at[kind, :, pl.ds(strip * feature, feature)],
                gate_buf.at[index],
                load_sem.at[1, index],
            )
        )
    for index in range(group):
        loads.append(
            pltpu.make_async_copy(
                down_hbm.at[:, pl.ds(index * feature, feature)], down_buf.at[index], load_sem.at[2, index]
            )
        )
    for load in loads:
        load.start()
    barrier = pltpu.get_barrier_semaphore()
    for step in range(1, group):
        pl.semaphore_signal(
            barrier, inc=1, device_id={"head": lax.rem(me + step, group)}, device_id_type=MESH
        )
    pl.semaphore_wait(barrier, group - 1)

    sends = []

    def go(copy):
        copy.start()
        sends.append(copy)
        return copy

    offsets = (2, 1, 3, 0)
    waits = {}

    def chunk_rows(t):
        return pl.ds(t * size, size)

    def lanes(head):
        return pl.ds(pl.multiple_of(head * feature, feature), feature)

    def scatter(which, t, product):
        for k, offset in enumerate(offsets):
            target = at(offset)
            piece = share.at[which, t, 1 - core, target]
            piece[...] = product(target * 2 + 1 - core).astype(piece.dtype)
            waits["twin", which, t, k] = go(
                send_to(piece, twin.at[which, t, target], twin_send.at[which, t, k],
                        twin_recv.at[which, t, k], sibling))
        for offset in offsets:
            target = at(offset)
            piece = share.at[which, t, core, target]
            piece[...] = product(target * 2 + core).astype(piece.dtype)

    def widen(ref):
        return ref[...].astype(jnp.float32)

    def chip_sum(which, t):
        def fold(k):
            waits["twin", which, t, k].wait_recv()
            target = at(offsets[k])
            piece = share.at[which, t, core, target]
            piece[...] = (widen(piece) + widen(twin.at[which, t, target])).astype(piece.dtype)

        fold(0)
        waits["far", which, t] = go(
            send_to(share.at[which, t, core, at(2)], relay.at[which, t],
                    ring_send.at[which, t, 0], ring_recv.at[which, t, 0], peer(turn)))
        fold(1)
        fold(2)
        waits["near", which, t] = go(
            send_to(share.at[which, t, core, at(-turn)], single.at[which, t],
                    ring_send.at[which, t, 1], ring_recv.at[which, t, 1], peer(-turn)))
        fold(3)

    def chip_relay(which, t):
        waits["far", which, t].wait_recv()
        piece = relay.at[which, t]
        piece[...] = (widen(piece) + widen(share.at[which, t, core, at(turn)])).astype(piece.dtype)
        waits["join", which, t] = go(
            send_to(piece, joined.at[which, t],
                    ring_send.at[which, t, 2], ring_recv.at[which, t, 2], peer(turn)))

    def finish(which, t):
        waits["near", which, t].wait_recv()
        waits["join", which, t].wait_recv()

    block = 32

    def delta_of(which, t, rows):
        return (
            share[which, t, core, at(0), rows].astype(jnp.float32)
            + joined[which, t, rows].astype(jnp.float32)
            + single[which, t, rows].astype(jnp.float32)
        )

    def remixed(layer, values, delta):
        result = []
        for target in range(count):
            total = hc_out[layer * count + target] * delta
            for source in range(count):
                weight = hc_mix[(layer * count + source) * count + target]
                if source == target:
                    weight = weight + 1.0
                total = total + weight * values[source]
            result.append(total)
        return result

    def project(t):
        if t == 0:
            for load in loads[:group]:
                load.wait()
        values = attended[t * size : (t + 1) * size]
        scatter(0, t, lambda head: jnp.dot(
            values, out_buf[head], preferred_element_type=jnp.float32))

    def middle(t):
        finish(0, t)

        def step(index, carry):
            inside = pl.ds(index * block, block)
            rows = pl.ds(t * size + index * block, block)
            values = [streams[s, rows].astype(jnp.float32) for s in range(count)]
            result = remixed(0, values, delta_of(0, t, inside))
            mixed = None
            for s in range(count):
                first_buf[s, rows] = result[s]
                term = hc_in[count + s] * result[s]
                mixed = term if mixed is None else mixed + term
            mixed_buf[rows] = mixed
            return carry

        lax.fori_loop(0, size // block, step, 0)
        mixed = mixed_buf[t * size : (t + 1) * size]
        stat_all[t, me, 0:1] = transpose_sum(mixed)
        stat_all[t, me, 1:2] = transpose_sum(mixed * mixed)
        stat_all[t, me, 2:8] = jnp.zeros((6, size), jnp.float32)
        for step in range(1, group):
            waits["stat", t, step] = go(
                send_to(stat_all.at[t, me], stat_all.at[t, me], stat_send.at[t, step],
                        stat_recv.at[t, step], lax.rem(me + step, group)))

    def normalized(t):
        for step in range(1, group):
            waits["stat", t, step].wait_recv()
        total = stat_all[t, 0]
        for index in range(1, group):
            total = total + stat_all[t, index]
        center = total[0:1] / width
        scale = lax.rsqrt(total[1:2] / width - center * center + 1e-05)
        row = lax.broadcasted_iota(jnp.int32, total.shape, 0)
        packed = jnp.where(row == 0, center, jnp.where(row == 1, scale, 0.0))
        columns[t] = jnp.transpose(packed)

        def step(index, carry):
            inside = pl.ds(index * block, block)
            rows = pl.ds(t * size + index * block, block)
            column = columns[t, inside]
            value = (mixed_buf[rows] - column[:, 0:1]) * column[:, 1:2]
            normed[rows] = value.astype(normed.dtype)
            return carry

        lax.fori_loop(0, size // block, step, 0)
        mine = normed.at[chunk_rows(t)]
        view = gathered.at[chunk_rows(t), lanes(me)]
        waits["fwd", t] = go(send_to(mine, view, pass_send.at[t, 0], pass_recv.at[t, 0], peer(turn)))
        waits["bwd", t] = go(send_to(mine, view, pass_send.at[t, 1], pass_recv.at[t, 1], peer(-turn)))
        waits["own", t] = go(send_to(mine, view, copy_send.at[t, 0], copy_recv.at[t, 0], sibling))
        local = pltpu.make_async_copy(mine, view, own_sem.at[t])
        local.start()
        waits["local", t] = local

    def hand_over(t, index, delta):
        view = gathered.at[chunk_rows(t), lanes(peer(delta))]
        waits["copy", t, index] = go(
            send_to(view, view, copy_send.at[t, index], copy_recv.at[t, index], sibling))

    def pass_on(t):
        waits["fwd", t].wait_recv()
        view = gathered.at[chunk_rows(t), lanes(peer(-turn))]
        waits["opp", t] = go(send_to(view, view, pass_send.at[t, 2], pass_recv.at[t, 2], peer(turn)))
        hand_over(t, 1, -turn)
        waits["bwd", t].wait_recv()
        hand_over(t, 2, turn)

    def pass_last(t):
        waits["opp", t].wait_recv()
        hand_over(t, 3, 2)

    def feed_forward(t):
        if t == 0:
            for load in loads[group:]:
                load.wait()
        waits["own", t].wait_recv()
        waits["local", t].wait()
        for index in (1, 2, 3):
            waits["copy", t, index].wait_recv()
        values = gathered.at[chunk_rows(t)]
        for strip in range(strips):
            gate = jnp.dot(values[...], gate_buf[strip], preferred_element_type=jnp.float32)
            up = jnp.dot(values[...], gate_buf[strips + strip], preferred_element_type=jnp.float32)
            hidden[:, strip * feature : (strip + 1) * feature] = (
                gate * lax.logistic(gate) * up
            ).astype(hidden.dtype)
        scatter(1, t, lambda head: jnp.dot(
            hidden[...], down_buf[head], preferred_element_type=jnp.float32))

    def last(t):
        finish(1, t)

        def step(index, carry):
            inside = pl.ds(index * block, block)
            rows = pl.ds(t * size + index * block, block)
            values = [first_buf[s, rows] for s in range(count)]
            result = remixed(1, values, delta_of(1, t, inside))
            total = result[0]
            for s in range(count):
                fresh_ref[s, rows] = result[s].astype(fresh_ref.dtype)
                if s > 0:
                    total = total + result[s]
            total_buf[rows] = total
            return carry

        lax.fori_loop(0, size // block, step, 0)

    phases = (
        project,
        lambda t: chip_sum(0, t),
        lambda t: chip_relay(0, t),
        middle,
        normalized,
        pass_on,
        pass_last,
        feed_forward,
        lambda t: chip_sum(1, t),
        lambda t: chip_relay(1, t),
        last,
    )
    for step in range(len(phases) + chunks - 1):
        for t in range(chunks):
            if 0 <= step - t < len(phases):
                phases[step - t](t)
    requests = accepted.shape[0]
    repeats = final_ref.shape[0] // requests
    tree = tokens // requests
    for item in range(requests):
        row = total_buf[pl.ds(item * tree + accepted[item], 1)]
        for copy_index in range(repeats):
            place = item * repeats + copy_index
            final_ref[place : place + 1] = row
    for copy in sends:
        copy.wait_send()


def layer(
    attended, streams, hc_in, hc_mix, hc_out, out_weight, gate_up, down_weight, accepted, repeats
):
    tokens, feature = attended.shape
    count = streams.shape[0]
    group = lax.axis_size("head")
    chips = group // 2
    width = out_weight.shape[1]
    inner = down_weight.shape[0]
    strips = inner // feature
    chunks = 3
    size = tokens // chunks
    bf16, f32 = jnp.bfloat16, jnp.float32
    dma = pltpu.SemaphoreType.DMA
    vmem = pl.BlockSpec(memory_space=pltpu.VMEM)
    smem = pl.BlockSpec(memory_space=pltpu.SMEM)
    anywhere = pl.BlockSpec(memory_space=pl.ANY)
    scratch = [
        pltpu.VMEM((group, feature, feature), bf16),
        pltpu.VMEM((2 * strips, width, feature), bf16),
        pltpu.VMEM((group, inner, feature), bf16),
        pltpu.VMEM((count, tokens, feature), f32),
        pltpu.VMEM((tokens, feature), f32),
        pltpu.VMEM((tokens, feature), f32),
        pltpu.VMEM((2, chunks, 2, chips, size, feature), bf16),
        pltpu.VMEM((2, chunks, chips, size, feature), bf16),
        pltpu.VMEM((2, chunks, size, feature), bf16),
        pltpu.VMEM((2, chunks, size, feature), bf16),
        pltpu.VMEM((2, chunks, size, feature), bf16),
        pltpu.VMEM((chunks, group, 8, size), f32),
        pltpu.VMEM((chunks, size, 8), f32),
        pltpu.VMEM((tokens, feature), bf16),
        pltpu.VMEM((tokens, width), bf16),
        pltpu.VMEM((size, inner), bf16),
        dma((3, max(group, 2 * strips))),
        dma((chunks,)),
        dma((2, chunks, 4)), dma((2, chunks, 4)),
        dma((2, chunks, 3)), dma((2, chunks, 3)),
        dma((chunks, group)), dma((chunks, group)),
        dma((chunks, 4)), dma((chunks, 4)),
        dma((chunks, 3)), dma((chunks, 3)),
    ]
    return pl.pallas_call(
        functools.partial(layer_kernel, chips, chunks),
        out_shape=(
            jax.ShapeDtypeStruct((count, tokens, feature), bf16),
            jax.ShapeDtypeStruct((accepted.shape[0] * repeats, feature), f32),
        ),
        in_specs=[smem] * 4 + [vmem, vmem, anywhere, anywhere, anywhere],
        out_specs=(vmem, vmem),
        scratch_shapes=scratch,
        compiler_params=pltpu.CompilerParams(
            collective_id=1, has_side_effects=True, vmem_limit_bytes=60 << 20
        ),
    )(
        hc_in.reshape(-1),
        hc_mix.reshape(-1),
        hc_out.reshape(-1),
        accepted,
        attended,
        streams,
        out_weight,
        gate_up,
        down_weight,
    )


def draft_kernel(
    chips,
    final_ref,
    weight_hbm,
    vocab_hbm,
    logits_ref,
    final_all,
    weight_buf,
    vocab_buf,
    gathered,
    total,
    load_sem,
    sum_send,
    sum_recv,
    draft_send,
    draft_recv,
    copy_send,
    copy_recv,
    pass_send,
    pass_recv,
):
    rows, feature = final_ref.shape
    group = 2 * chips
    width = group * feature
    devices = gathered.shape[1] // rows
    me = lax.axis_index("head")
    home = lax.axis_index("req")
    chip = me // 2
    core = lax.rem(me, 2)
    turn = 1 - 2 * core
    sibling = chip * 2 + 1 - core

    def peer(delta):
        return lax.rem(chip + chips + delta, chips) * 2 + core

    def send_to(source, target, send_sem, recv_sem, device):
        return pltpu.make_async_remote_copy(
            src_ref=source,
            dst_ref=target,
            send_sem=send_sem,
            recv_sem=recv_sem,
            device_id=device,
            device_id_type=MESH,
        )

    loads = [pltpu.make_async_copy(weight_hbm, weight_buf, load_sem.at[0])]
    for index in range(group):
        loads.append(
            pltpu.make_async_copy(
                vocab_hbm.at[:, pl.ds(index * feature, feature)],
                vocab_buf.at[index],
                load_sem.at[1 + index],
            )
        )
    for load in loads:
        load.start()
    barrier = pltpu.get_barrier_semaphore()
    for step in range(1, group):
        pl.semaphore_signal(
            barrier, inc=1, device_id={"head": lax.rem(me + step, group)}, device_id_type=MESH
        )
    for step in range(1, devices):
        pl.semaphore_signal(
            barrier, inc=1, device_id={"req": lax.rem(home + step, devices)}, device_id_type=MESH
        )
    pl.semaphore_wait(barrier, group + devices - 2)

    sends = []

    def go(copy):
        copy.start()
        sends.append(copy)
        return copy

    sums = []
    for step in range(1, group):
        sums.append(
            go(send_to(final_ref, final_all.at[me], sum_send.at[step], sum_recv.at[step],
                       {"head": lax.rem(me + step, group)}))
        )
    final_all[me] = final_ref[...]
    loads[0].wait()
    for copy in sums:
        copy.wait_recv()
    center = jnp.zeros((rows, 1), jnp.float32)
    square = jnp.zeros((rows, 1), jnp.float32)
    for index in range(group):
        values = final_all[index]
        center = center + jnp.sum(values, axis=1, keepdims=True)
        square = square + jnp.sum(values * values, axis=1, keepdims=True)
    center = center / width
    scale = lax.rsqrt(square / width - center * center + 1e-05)
    branches = []
    for kind in range(2):
        branch = jnp.zeros((rows, feature), jnp.float32)
        for index in range(group):
            values = ((final_all[index] - center) * scale).astype(jnp.bfloat16)
            branch = branch + jnp.dot(
                values,
                weight_buf[kind, index * feature : (index + 1) * feature],
                preferred_element_type=jnp.float32,
            )
        branches.append(branch)
    odd = (lax.broadcasted_iota(jnp.int32, (rows, feature), 0) & 1) == 1
    branch = jnp.where(odd, branches[1], branches[0])
    drafted = (final_ref[...] - center) * scale + branch * lax.logistic(branch)
    mine = gathered.at[me, pl.ds(pl.multiple_of(home * rows, rows), rows)]
    mine[...] = drafted.astype(gathered.dtype)
    drafts = []
    for step in range(1, devices):
        drafts.append(
            go(send_to(mine, mine, draft_send.at[step], draft_recv.at[step],
                       {"req": lax.rem(home + step, devices)}))
        )
    for copy in drafts:
        copy.wait_recv()

    def shard(head):
        return gathered.at[head]

    def ring(index, delta, source):
        return go(send_to(shard(source), shard(source), pass_send.at[index], pass_recv.at[index],
                          {"head": peer(delta)}))

    def hand_over(index, source):
        return go(send_to(shard(source), shard(source), copy_send.at[index], copy_recv.at[index],
                          {"head": sibling}))

    fwd = ring(0, turn, me)
    bwd = ring(1, -turn, me)
    hands = [hand_over(0, me)]
    for load in loads[1:]:
        load.wait()

    def add(head, first=False):
        value = lax.dot_general(
            gathered[head],
            vocab_buf[head],
            (((1,), (1,)), ((), ())),
            preferred_element_type=jnp.float32,
        )
        total[...] = value if first else total[...] + value

    add(me, True)
    fwd.wait_recv()
    opp = ring(2, turn, peer(-turn))
    hands.append(hand_over(1, peer(-turn)))
    bwd.wait_recv()
    hands.append(hand_over(2, peer(turn)))
    add(peer(-turn))
    hands[0].wait_recv()
    add(sibling)
    add(peer(turn))
    opp.wait_recv()
    hands.append(hand_over(3, peer(2)))
    hands[1].wait_recv()

    def across(delta):
        return lax.rem(chip + chips + delta, chips) * 2 + 1 - core

    add(across(turn))
    hands[2].wait_recv()
    add(across(-turn))
    add(peer(2))
    hands[3].wait_recv()
    add(across(2))
    logits_ref[...] = total[...].astype(logits_ref.dtype)
    for copy in sends:
        copy.wait_send()


def draft_logits(final_rows, draft_weight, lm_head):
    rows, feature = final_rows.shape
    group = lax.axis_size("head")
    devices = lax.axis_size("req")
    width, vocab = lm_head.shape
    bf16, f32 = jnp.bfloat16, jnp.float32
    dma = pltpu.SemaphoreType.DMA
    vmem = pl.BlockSpec(memory_space=pltpu.VMEM)
    anywhere = pl.BlockSpec(memory_space=pl.ANY)
    return pl.pallas_call(
        functools.partial(draft_kernel, group // 2),
        out_shape=jax.ShapeDtypeStruct((devices * rows, vocab), bf16),
        in_specs=[vmem, anywhere, anywhere],
        out_specs=vmem,
        scratch_shapes=[
            pltpu.VMEM((group, rows, feature), f32),
            pltpu.VMEM(draft_weight.shape, bf16),
            pltpu.VMEM((group, vocab, feature), bf16),
            pltpu.VMEM((group, devices * rows, feature), bf16),
            pltpu.VMEM((devices * rows, vocab), f32),
            dma((1 + group,)),
            dma((group,)), dma((group,)),
            dma((devices,)), dma((devices,)),
            dma((4,)), dma((4,)),
            dma((3,)), dma((3,)),
        ],
        compiler_params=pltpu.CompilerParams(
            collective_id=2, has_side_effects=True, vmem_limit_bytes=40 << 20
        ),
    )(final_rows, draft_weight, jnp.transpose(lm_head))


def front_kernel(
    chips,
    chunks,
    hc_in,
    streams,
    cosine,
    sine,
    weight_hbm,
    query_ref,
    key_ref,
    value_ref,
    weight_buf,
    mixed_buf,
    stat_all,
    columns,
    normed,
    gathered,
    load_sem,
    own_sem,
    stat_send,
    stat_recv,
    copy_send,
    copy_recv,
    pass_send,
    pass_recv,
):
    count, tokens, feature = streams.shape
    size = tokens // chunks
    group = 2 * chips
    width = group * feature
    requests, rows, head_dim = query_ref.shape
    heads = feature // head_dim
    tree = rows // heads
    me = lax.axis_index("head")
    chip = me // 2
    core = lax.rem(me, 2)
    turn = 1 - 2 * core
    sibling = chip * 2 + 1 - core

    def peer(delta):
        return lax.rem(chip + chips + delta, chips) * 2 + core

    def send_to(source, target, send_sem, recv_sem, head):
        return pltpu.make_async_remote_copy(
            src_ref=source,
            dst_ref=target,
            send_sem=send_sem,
            recv_sem=recv_sem,
            device_id={"head": head},
            device_id_type=MESH,
        )

    load = pltpu.make_async_copy(weight_hbm, weight_buf, load_sem)
    load.start()
    barrier = pltpu.get_barrier_semaphore()
    for step in range(1, group):
        pl.semaphore_signal(
            barrier, inc=1, device_id={"head": lax.rem(me + step, group)}, device_id_type=MESH
        )
    block = 32
    for t in range(chunks):

        def mix(index, carry, t=t):
            here = pl.ds(t * size + index * block, block)
            mixed = None
            for s in range(count):
                term = hc_in[s] * streams[s, here].astype(jnp.float32)
                mixed = term if mixed is None else mixed + term
            mixed_buf[here] = mixed
            return carry

        lax.fori_loop(0, size // block, mix, 0)
        mixed = mixed_buf[t * size : (t + 1) * size]
        stat_all[t, me, 0:1] = transpose_sum(mixed)
        stat_all[t, me, 1:2] = transpose_sum(mixed * mixed)
        stat_all[t, me, 2:8] = jnp.zeros((6, size), jnp.float32)
    pl.semaphore_wait(barrier, group - 1)

    sends = []
    waits = {}

    def go(copy):
        copy.start()
        sends.append(copy)
        return copy

    def chunk_rows(t):
        return pl.ds(t * size, size)

    def lanes(head):
        return pl.ds(pl.multiple_of(head * feature, feature), feature)

    for t in range(chunks):
        for step in range(1, group):
            waits["stat", t, step] = go(
                send_to(stat_all.at[t, me], stat_all.at[t, me], stat_send.at[t, step],
                        stat_recv.at[t, step], lax.rem(me + step, group)))

    def normalized(t):
        for step in range(1, group):
            waits["stat", t, step].wait_recv()
        total = stat_all[t, 0]
        for index in range(1, group):
            total = total + stat_all[t, index]
        center = total[0:1] / width
        scale = lax.rsqrt(total[1:2] / width - center * center + 1e-05)
        row = lax.broadcasted_iota(jnp.int32, total.shape, 0)
        packed = jnp.where(row == 0, center, jnp.where(row == 1, scale, 0.0))
        columns[t] = jnp.transpose(packed)

        def step(index, carry):
            inside = pl.ds(index * block, block)
            here = pl.ds(t * size + index * block, block)
            column = columns[t, inside]
            value = (mixed_buf[here] - column[:, 0:1]) * column[:, 1:2]
            normed[here] = value.astype(normed.dtype)
            return carry

        lax.fori_loop(0, size // block, step, 0)
        mine = normed.at[chunk_rows(t)]
        view = gathered.at[chunk_rows(t), lanes(me)]
        waits["fwd", t] = go(send_to(mine, view, pass_send.at[t, 0], pass_recv.at[t, 0], peer(turn)))
        waits["bwd", t] = go(send_to(mine, view, pass_send.at[t, 1], pass_recv.at[t, 1], peer(-turn)))
        waits["own", t] = go(send_to(mine, view, copy_send.at[t, 0], copy_recv.at[t, 0], sibling))
        local = pltpu.make_async_copy(mine, view, own_sem.at[t])
        local.start()
        waits["local", t] = local

    def hand_over(t, index, delta):
        view = gathered.at[chunk_rows(t), lanes(peer(delta))]
        waits["copy", t, index] = go(
            send_to(view, view, copy_send.at[t, index], copy_recv.at[t, index], sibling))

    def pass_on(t):
        waits["fwd", t].wait_recv()
        view = gathered.at[chunk_rows(t), lanes(peer(-turn))]
        waits["opp", t] = go(send_to(view, view, pass_send.at[t, 2], pass_recv.at[t, 2], peer(turn)))
        hand_over(t, 1, -turn)
        waits["bwd", t].wait_recv()
        hand_over(t, 2, turn)

    def pass_last(t):
        waits["opp", t].wait_recv()
        hand_over(t, 3, 2)

    def project(t):
        if t == 0:
            load.wait()
        waits["own", t].wait_recv()
        waits["local", t].wait()
        for index in (1, 2, 3):
            waits["copy", t, index].wait_recv()
        here = slice(t * size, (t + 1) * size)
        for kind, target in enumerate((query_ref, key_ref, value_ref)):
            product = jnp.dot(gathered[here], weight_buf[kind], preferred_element_type=jnp.float32)
            for head in range(heads):
                value = product[:, head * head_dim : (head + 1) * head_dim]
                if kind < 2:
                    turned = pltpu.roll(value, head_dim // 2, 1)
                    value = value * cosine[here] + turned * sine[here]
                if kind == 0:
                    value = value * head_dim ** (-0.5)
                value = value.astype(target.dtype)
                for item in range(size // tree):
                    target[t * (size // tree) + item, head * tree : (head + 1) * tree] = value[
                        item * tree : (item + 1) * tree
                    ]

    phases = (normalized, pass_on, pass_last, project)
    for step in range(len(phases) + chunks - 1):
        for t in range(chunks):
            if 0 <= step - t < len(phases):
                phases[step - t](t)
    for copy in sends:
        copy.wait_send()


def front(streams, hc_in, qkv, cosine, sine, requests, heads):
    count, tokens, feature = streams.shape
    group = lax.axis_size("head")
    width = qkv.shape[1]
    chunks = 2
    size = tokens // chunks
    rows = heads * (tokens // requests)
    head_dim = feature // heads
    bf16, f32 = jnp.bfloat16, jnp.float32
    dma = pltpu.SemaphoreType.DMA
    vmem = pl.BlockSpec(memory_space=pltpu.VMEM)
    smem = pl.BlockSpec(memory_space=pltpu.SMEM)
    anywhere = pl.BlockSpec(memory_space=pl.ANY)
    return pl.pallas_call(
        functools.partial(front_kernel, group // 2, chunks),
        out_shape=(jax.ShapeDtypeStruct((requests, rows, head_dim), bf16),) * 3,
        in_specs=[smem, vmem, vmem, vmem, anywhere],
        out_specs=(vmem,) * 3,
        scratch_shapes=[
            pltpu.VMEM(qkv.shape, bf16),
            pltpu.VMEM((tokens, feature), f32),
            pltpu.VMEM((chunks, group, 8, size), f32),
            pltpu.VMEM((chunks, size, 8), f32),
            pltpu.VMEM((tokens, feature), bf16),
            pltpu.VMEM((tokens, width), bf16),
            dma,
            dma((chunks,)),
            dma((chunks, group)), dma((chunks, group)),
            dma((chunks, 4)), dma((chunks, 4)),
            dma((chunks, 3)), dma((chunks, 3)),
        ],
        compiler_params=pltpu.CompilerParams(
            collective_id=3, has_side_effects=True, vmem_limit_bytes=40 << 20
        ),
    )(hc_in.reshape(-1), streams, cosine, sine, qkv)


def on_device(
    streams,
    hc_in,
    hc_mix,
    hc_out,
    qkv_weight,
    out_weight,
    up_gate,
    down_weight,
    draft_weight,
    lm_head,
    k_pages,
    v_pages,
    page_owner,
    page_fill,
    cache_len,
    tree_parent,
    accepted_index,
):
    tokens_local = streams.shape[0]
    req_local = cache_len.shape[0]
    tree_size = tree_parent.shape[1]
    heads_local = k_pages.shape[2]
    head_dim = k_pages.shape[3]
    draft_count = draft_weight.shape[0]
    all_requests = req_local * lax.axis_size("req")
    reach = ancestors(tree_parent)
    depth = (jnp.sum(reach.astype(jnp.float32), axis=1) - 1.0).astype(jnp.int32)
    positions = (cache_len[:, None] + depth).reshape(tokens_local)
    cosine, sine = turns(positions, head_dim)
    same_head = jnp.eye(heads_local, dtype=jnp.bfloat16)
    tree_mask = (same_head[None, :, None, :, None] * reach[:, None, :, None, :]).reshape(
        req_local, heads_local * tree_size, heads_local * tree_size
    )
    gate_up = jnp.transpose(up_gate, (1, 0, 2))
    by_stream = jnp.transpose(streams, (1, 0, 2))
    queries, keys_new, values_new = front(
        by_stream,
        hc_in,
        jnp.transpose(qkv_weight, (1, 0, 2)),
        cosine,
        sine,
        req_local,
        heads_local,
    )
    attended = cache_attention(
        queries, keys_new, values_new, tree_mask, k_pages, v_pages, page_owner, page_fill
    )
    fresh, final_local = layer(
        attended,
        by_stream,
        hc_in,
        hc_mix,
        hc_out,
        out_weight,
        gate_up,
        down_weight,
        accepted_index,
        draft_count,
    )
    new_streams = jnp.transpose(fresh, (1, 0, 2))
    logits_local = draft_logits(final_local, draft_weight, lm_head)
    logits_local = logits_local.reshape(all_requests, draft_count, -1)
    logits = lax.all_to_all(
        logits_local, ("req", "head"), split_axis=0, concat_axis=2, tiled=True
    ).astype(jnp.float32)
    return (new_streams, logits)


def solution(mesh):
    in_specs = (
        P("req", None, "head"),
        P(),
        P(),
        P(),
        P(None, None, "head"),
        P("head", None),
        P(None, None, "head"),
        P("head", None),
        P(None, None, "head"),
        P(None, ("req", "head")),
        P("req", None, "head", None),
        P("req", None, "head", None),
        P("req"),
        P("req"),
        P("req"),
        P("req", None),
        P("req"),
    )
    out_specs = (P("req", None, "head"), P(("req", "head"), None, None))
    return jax.shard_map(
        on_device, mesh=mesh, in_specs=in_specs, out_specs=out_specs, check_vma=False
    )
```

```python
import functools
import math

import jax
import jax.numpy as jnp
from jax import lax
from jax.experimental import pallas as pl
from jax.experimental.pallas import tpu as pltpu
from jax.sharding import PartitionSpec as P

NEG_FILL = -1e30


def ancestors(parents):
    length = parents.shape[1]
    places = jnp.arange(length, dtype=jnp.int32)
    linked = (places[None, :, None] == parents[:, None, :]) | (places[:, None] == places[None, :])[
        None
    ]
    reach = linked.astype(jnp.bfloat16)
    for repeat in range(max(1, (length - 1).bit_length())):
        counts = jnp.einsum("jki,jil->jkl", reach, reach, preferred_element_type=jnp.float32)
        reach = jnp.minimum(counts, 1.0).astype(jnp.bfloat16)
    return reach


def turns(positions, head_dim):
    half = head_dim // 2
    freqs = jnp.exp(
        jnp.arange(half, dtype=jnp.float32) * (-2.0 * math.log(10000.0) / head_dim)
    )
    angles = positions.astype(jnp.float32)[:, None] * freqs[None, :]
    cosine = jnp.cos(angles)
    sine = jnp.sin(angles)
    return jnp.concatenate([cosine, cosine], axis=1), jnp.concatenate([-sine, sine], axis=1)


MESH = pl.DeviceIdType.MESH
SLOT_BITS = 6
FILL_BITS = 8


def remote(source, target, send_sem, recv_sem, req):
    return pltpu.make_async_remote_copy(
        src_ref=source,
        dst_ref=target,
        send_sem=send_sem,
        recv_sem=recv_sem,
        device_id={"req": req},
        device_id_type=MESH,
    )


def weigh(tops, totals):
    top = functools.reduce(jnp.maximum, tops)
    factors = [jnp.exp(value - top) for value in tops]
    total = functools.reduce(lambda a, b: a + b, [f * t for f, t in zip(factors, totals)])
    return top, total, factors


def cache_kernel(
    side,
    chips,
    table,
    last,
    hc_in,
    streams,
    cosine,
    sine,
    mask_ref,
    weight_hbm,
    up_hbm,
    k_hbm,
    v_hbm,
    out_ref,
    gate_ref,
    q_ref,
    key_ref,
    value_ref,
    weight_buf,
    mixed_buf,
    stat_all,
    columns,
    normed,
    gathered,
    up_in,
    up_out,
    front_sem,
    own_sem,
    front_send,
    front_recv,
    copy_send,
    copy_recv,
    pass_send,
    pass_recv,
    up_in_sem,
    up_out_sem,
    tree_acc,
    tree_stat,
    q_all,
    k_buf,
    v_buf,
    scores,
    seg_acc,
    seg_top,
    seg_den,
    parts,
    stats,
    relay,
    merged,
    single,
    relay_s,
    merged_s,
    single_s,
    outgoing_s,
    factors,
    small,
    small_s,
    hop,
    hop_s,
    gather_send,
    gather_recv,
    spread_send,
    spread_recv,
    load_sem,
    far_send,
    far_recv,
    near_send,
    near_recv,
    join_send,
    join_recv,
    stat_send,
    stat_recv,
    last_send,
    last_recv,
    last_stat_send,
    last_stat_recv,
):
    block = q_ref.shape[0] // 2
    rows = q_ref.shape[1]
    slots = k_buf.shape[0]
    half_rows = rows // 2
    me = lax.axis_index("req")
    place = (me // side, lax.rem(me, side))
    turn = 1 - 2 * lax.rem(lax.axis_index("head"), 2)

    def shifted(axis, delta):
        moved = lax.rem(place[axis] + side + delta, side)
        return moved * side + place[1] if axis == 0 else place[0] * side + moved

    def at(axis, delta):
        return lax.rem(place[axis] + side + delta, side)

    first = (0, 1)
    second = (1, 0)

    def spot(half, p2, p1):
        return pl.ds(((half * side + p2) * side + p1) * block, block)

    loads = [
        pltpu.make_async_copy(k_hbm, k_buf, load_sem.at[0]),
        pltpu.make_async_copy(v_hbm, v_buf, load_sem.at[1]),
    ]
    weight_load = pltpu.make_async_copy(weight_hbm, weight_buf, front_sem)
    weight_load.start()
    barrier = pltpu.get_barrier_semaphore()
    for axis in (0, 1):
        for delta in (1, -1):
            pl.semaphore_signal(
                barrier, inc=1, device_id={"req": shifted(axis, delta)}, device_id_type=MESH
            )
    head_index = lax.axis_index("head")
    for step in range(1, 2 * chips):
        pl.semaphore_signal(
            barrier,
            inc=1,
            device_id={"head": lax.rem(head_index + step, 2 * chips)},
            device_id_type=MESH,
        )

    def enter():
        pl.semaphore_wait(barrier, 4 + 2 * chips - 1)

    pieces = gate_ref.shape[1] // up_out.shape[2]
    span = up_out.shape[2]
    tall = up_in.shape[1]

    def up_load(c):
        return pltpu.make_async_copy(
            up_hbm.at[pl.ds(c * tall, tall)], up_in.at[c % 2], up_in_sem.at[c]
        )

    def up_store(c):
        return pltpu.make_async_copy(
            up_out.at[c % 2], gate_ref.at[:, pl.ds(c * span, span)], up_out_sem.at[c]
        )

    strips = gate_ref.shape[2] // 128
    unit = 2 * strips * 16

    def untangle(c):
        if c + 1 < pieces:
            up_load(c + 1).start()
        up_load(c).wait()
        if c >= 2:
            up_store(c - 2).wait()
        out_row = lax.broadcasted_iota(jnp.int32, (unit, unit), 0)
        in_row = lax.broadcasted_iota(jnp.int32, (unit, unit), 1)
        kind = out_row // (unit // 2)
        strip = (out_row // 16) & (strips - 1)
        pick = (out_row & 15) * (2 * strips) + strip * 2 + kind
        chosen = jnp.where(in_row == pick, 1.0, 0.0).astype(jnp.bfloat16)

        def step(index, carry):
            sorted_rows = jnp.dot(
                chosen,
                up_in[c % 2, pl.ds(index * unit, unit)],
                preferred_element_type=jnp.float32,
            ).astype(up_out.dtype)
            place = pl.ds(index * 16, 16)
            for kind in (0, 1):
                for strip in range(strips):
                    row = (kind * strips + strip) * 16
                    up_out[c % 2, kind, place, strip * 128 : (strip + 1) * 128] = sorted_rows[
                        row : row + 16
                    ]
            return carry

        lax.fori_loop(0, span // 16, step, 0)
        up_store(c).start()

    up_load(0).start()

    sends = []

    def go(copy):
        copy.start()
        sends.append(copy)
        return copy

    def pass_block(half, axis, delta, p2, p1, send, recv, own=False):
        view = q_all.at[spot(half, p2, p1)]
        source = q_ref.at[pl.ds(half * block, block)] if own else view
        return go(remote(source, view, send, recv, shifted(axis, delta)))

    lines = {}
    crosses = {}

    def line(half, index, delta, p1, own=False):
        lines[half, index] = pass_block(
            half, first[half], delta, at(second[half], 0), p1,
            gather_send.at[half, index], gather_recv.at[half, index], own,
        )

    def cross(half, piece, index, delta, p2, p1, own=False):
        crosses[half, piece, index] = pass_block(
            half, second[half], delta, p2, p1,
            spread_send.at[half, piece, index], spread_recv.at[half, piece, index], own,
        )

    chunks = 2

    def front_part():
        count, tokens, feature = streams.shape
        size = tokens // chunks
        group = 2 * chips
        width = group * feature
        head_dim = q_ref.shape[2]
        rows = q_ref.shape[1]
        heads = feature // head_dim
        tree = rows // heads
        me = lax.axis_index("head")
        chip = me // 2
        core = lax.rem(me, 2)
        turn = 1 - 2 * core
        sibling = chip * 2 + 1 - core

        def peer(delta):
            return lax.rem(chip + chips + delta, chips) * 2 + core

        def send_to(source, target, send_sem, recv_sem, head):
            return pltpu.make_async_remote_copy(
                src_ref=source,
                dst_ref=target,
                send_sem=send_sem,
                recv_sem=recv_sem,
                device_id={"head": head},
                device_id_type=MESH,
            )

        block = 32
        for t in range(chunks):

            def mix(index, carry, t=t):
                here = pl.ds(t * size + index * block, block)
                mixed = None
                for s in range(count):
                    term = hc_in[0, s] * streams[s, here].astype(jnp.float32)
                    mixed = term if mixed is None else mixed + term
                mixed_buf[here] = mixed
                return carry

            lax.fori_loop(0, size // block, mix, 0)
            mixed = mixed_buf[t * size : (t + 1) * size]
            stat_all[t, me, 0:1] = transpose_sum(mixed)
            stat_all[t, me, 1:2] = transpose_sum(mixed * mixed)
            stat_all[t, me, 2:8] = jnp.zeros((6, size), jnp.float32)
        enter()
        waits = {}

        def chunk_rows(t):
            return pl.ds(t * size, size)

        def lanes(head):
            return pl.ds(pl.multiple_of(head * feature, feature), feature)

        for t in range(chunks):
            for step in range(1, group):
                waits["stat", t, step] = go(
                    send_to(stat_all.at[t, me], stat_all.at[t, me], front_send.at[t, step],
                            front_recv.at[t, step], lax.rem(me + step, group)))

        def normalized(t):
            for step in range(1, group):
                waits["stat", t, step].wait_recv()
            total = stat_all[t, 0]
            for index in range(1, group):
                total = total + stat_all[t, index]
            center = total[0:1] / width
            scale = lax.rsqrt(total[1:2] / width - center * center + 1e-05)
            row = lax.broadcasted_iota(jnp.int32, total.shape, 0)
            packed = jnp.where(row == 0, center, jnp.where(row == 1, scale, 0.0))
            columns[t] = jnp.transpose(packed)

            def step(index, carry):
                inside = pl.ds(index * block, block)
                here = pl.ds(t * size + index * block, block)
                column = columns[t, inside]
                value = (mixed_buf[here] - column[:, 0:1]) * column[:, 1:2]
                normed[here] = value.astype(normed.dtype)
                return carry

            lax.fori_loop(0, size // block, step, 0)
            mine = normed.at[chunk_rows(t)]
            view = gathered.at[chunk_rows(t), lanes(me)]
            waits["fwd", t] = go(send_to(mine, view, pass_send.at[t, 0], pass_recv.at[t, 0], peer(turn)))
            waits["bwd", t] = go(send_to(mine, view, pass_send.at[t, 1], pass_recv.at[t, 1], peer(-turn)))
            waits["own", t] = go(send_to(mine, view, copy_send.at[t, 0], copy_recv.at[t, 0], sibling))
            local = pltpu.make_async_copy(mine, view, own_sem.at[t])
            local.start()
            waits["local", t] = local

        def hand_over(t, index, delta):
            view = gathered.at[chunk_rows(t), lanes(peer(delta))]
            waits["copy", t, index] = go(
                send_to(view, view, copy_send.at[t, index], copy_recv.at[t, index], sibling))

        def pass_on(t):
            waits["fwd", t].wait_recv()
            view = gathered.at[chunk_rows(t), lanes(peer(-turn))]
            waits["opp", t] = go(send_to(view, view, pass_send.at[t, 2], pass_recv.at[t, 2], peer(turn)))
            hand_over(t, 1, -turn)
            waits["bwd", t].wait_recv()
            hand_over(t, 2, turn)

        def pass_last(t):
            waits["opp", t].wait_recv()
            hand_over(t, 3, 2)

        def project(t):
            if t == 0:
                weight_load.wait()
            waits["own", t].wait_recv()
            waits["local", t].wait()
            for index in (1, 2, 3):
                waits["copy", t, index].wait_recv()
            here = slice(t * size, (t + 1) * size)
            for kind, target in enumerate((q_ref, key_ref, value_ref)):
                product = jnp.dot(gathered[here], weight_buf[kind], preferred_element_type=jnp.float32)
                for head in range(heads):
                    value = product[:, head * head_dim : (head + 1) * head_dim]
                    if kind < 2:
                        turned = pltpu.roll(value, head_dim // 2, 1)
                        value = value * cosine[here] + turned * sine[here]
                    if kind == 0:
                        value = value * head_dim ** (-0.5)
                    value = value.astype(target.dtype)
                    for item in range(size // tree):
                        target[t * (size // tree) + item, head * tree : (head + 1) * tree] = value[
                            item * tree : (item + 1) * tree
                        ]
            launch(t)

        phases = (normalized, pass_on, pass_last, project)
        for step in range(len(phases) + chunks - 1):
            for t in range(chunks):
                if 0 <= step - t < len(phases):
                    phases[step - t](t)

    halves = (0, 1)

    def launch(half):
        line(half, 0, turn, at(first[half], 0), True)
        line(half, 1, -turn, at(first[half], 0), True)
        cross(half, 0, 0, turn, at(second[half], 0), at(first[half], 0), True)
        cross(half, 0, 1, -turn, at(second[half], 0), at(first[half], 0), True)

    front_part()
    for load in loads:
        load.start()
    for half in halves:
        q_all[spot(half, at(second[half], 0), at(first[half], 0))] = q_ref[
            half * block : (half + 1) * block
        ]
    seg_top[...] = jnp.full(seg_top.shape, NEG_FILL, jnp.float32)
    seg_den[...] = jnp.zeros(seg_den.shape, jnp.float32)
    seg_acc[slots] = jnp.zeros(seg_acc.shape[1:], seg_acc.dtype)
    tree_stat[...] = jnp.zeros(tree_stat.shape, jnp.float32)

    def tree_step(item, carry):
        found = lax.dot_general(
            key_ref[item],
            q_ref[item],
            (((1,), (1,)), ((), ())),
            preferred_element_type=jnp.float32,
        )
        found = jnp.where(mask_ref[item].astype(jnp.float32) > 0.0, found, NEG_FILL)
        top = jnp.max(found, axis=0, keepdims=True)
        weight = jnp.exp(found - top)
        tree_acc[item] = lax.dot_general(
            weight.astype(jnp.bfloat16),
            value_ref[item],
            (((0,), (0,)), ((), ())),
            preferred_element_type=jnp.float32,
        )
        tree_stat[0, item, :, 0:rows] = top
        tree_stat[1, item, :, 0:rows] = jnp.sum(weight, axis=0, keepdims=True)
        return carry

    lax.fori_loop(0, 2 * block, tree_step, 0)
    for half in halves:
        lines[half, 0].wait_recv()
        line(half, 2, turn, at(first[half], -turn))
        cross(half, 1, 0, turn, at(second[half], 0), at(first[half], -turn))
        cross(half, 1, 1, -turn, at(second[half], 0), at(first[half], -turn))
    untangle(0)
    untangle(1)
    for half in halves:
        lines[half, 1].wait_recv()
        cross(half, 2, 0, turn, at(second[half], 0), at(first[half], turn))
        cross(half, 2, 1, -turn, at(second[half], 0), at(first[half], turn))
    untangle(2)
    for half in halves:
        crosses[half, 0, 0].wait_recv()
        cross(half, 0, 2, turn, at(second[half], -turn), at(first[half], 0))
    untangle(3)
    for half in halves:
        lines[half, 2].wait_recv()
        cross(half, 3, 0, turn, at(second[half], 0), at(first[half], 2))
        cross(half, 3, 1, -turn, at(second[half], 0), at(first[half], 2))
    for piece, delta in ((1, -turn), (2, turn), (3, 2)):
        untangle(3 + piece)
        for half in halves:
            crosses[half, piece, 0].wait_recv()
            cross(half, piece, 2, turn, at(second[half], -turn), at(first[half], delta))
    untangle(7)
    for piece in range(4):
        for half in halves:
            crosses[half, piece, 1].wait_recv()
            crosses[half, piece, 2].wait_recv()
    for load in loads:
        load.wait()

    slot_mask = (1 << SLOT_BITS) - 1
    fill_mask = (1 << FILL_BITS) - 1
    requests = 2 * block * side * side

    def owner_at(index):
        return table[index] >> (SLOT_BITS + FILL_BITS)

    def starts_new(index):
        before = owner_at(jnp.maximum(index - 1, 0))
        return jnp.logical_or(index == 0, before != owner_at(index))

    shape = (k_buf.shape[1], rows)
    row_ids = lax.broadcasted_iota(jnp.int32, shape, 0)
    col_head = (lax.broadcasted_iota(jnp.int32, shape, 1) >= half_rows).astype(jnp.int32)
    matched = (row_ids & 1) == col_head
    key_ids = row_ids >> 1
    unroll = 4

    def score_step(group, carry):
        for offset in range(unroll):
            index = group * unroll + offset
            entry = table[index]
            fill = (entry >> SLOT_BITS) & fill_mask
            owner = jnp.minimum(entry >> (SLOT_BITS + FILL_BITS), requests - 1)
            home = owner // (2 * block)
            within = lax.rem(owner, 2 * block)
            half = within // block
            hx = home // side
            hy = lax.rem(home, side)
            outer = jnp.where(half == 0, hy, hx)
            inner = jnp.where(half == 0, hx, hy)
            row = ((half * side + outer) * side + inner) * block + lax.rem(within, block)
            found = lax.dot_general(
                k_buf[entry & slot_mask],
                q_all[row],
                (((1,), (1,)), ((), ())),
                preferred_element_type=jnp.float32,
            )
            found = jnp.where(jnp.logical_and(matched, key_ids < fill), found, NEG_FILL)
            scores[index] = found
            seg_top[index, :, 0:rows] = jnp.max(found, axis=0, keepdims=True)
        return carry

    lax.fori_loop(0, slots // unroll, score_step, 0)

    def forward(index, run):
        here = seg_top[index]
        run = jnp.where(starts_new(index), here, jnp.maximum(run, here))
        seg_top[index] = run
        return run

    lax.fori_loop(0, slots, forward, jnp.full(seg_top.shape[1:], NEG_FILL, jnp.float32))

    def backward(step, run):
        index = slots - 1 - step
        follow = jnp.minimum(index + 1, slots - 1)
        ends = jnp.logical_or(step == 0, owner_at(follow) != owner_at(index))
        run = jnp.where(ends, seg_top[index], run)
        seg_top[index] = run
        return run

    lax.fori_loop(0, slots, backward, jnp.full(seg_top.shape[1:], NEG_FILL, jnp.float32))

    def value_step(group, carry):
        acc_run, den_run = carry
        for offset in range(unroll):
            index = group * unroll + offset
            fresh = starts_new(index)
            top = seg_top[index][:, 0:rows]
            top = jnp.where(top < 0.5 * NEG_FILL, 0.0, top)
            weight = jnp.exp(scores[index] - top)
            den = jnp.sum(weight, axis=0, keepdims=True)
            acc = lax.dot_general(
                weight.astype(jnp.bfloat16),
                v_buf[table[index] & slot_mask],
                (((0,), (0,)), ((), ())),
                preferred_element_type=jnp.float32,
            )
            acc_run = acc + jnp.where(fresh, 0.0, acc_run)
            den_run = den + jnp.where(fresh, 0.0, den_run)
            seg_acc[index] = acc_run.astype(seg_acc.dtype)
            seg_den[index, :, 0:rows] = den_run
        return acc_run, den_run

    lax.fori_loop(
        0,
        slots // unroll,
        value_step,
        (jnp.zeros(seg_acc.shape[1:], jnp.float32), jnp.zeros((1, rows), jnp.float32)),
    )

    def place_step(group, carry):
        for piece in range(side):
            tops, dens = [], []
            for offset in range(block):
                spot_index = (group * side + piece) * block + offset
                found = last[spot_index]
                parts[spot_index] = seg_acc[found]
                tops.append(seg_top[found])
                dens.append(seg_den[found])
            stats[group, 0, piece * block : (piece + 1) * block] = jnp.concatenate(tops, axis=0)
            stats[group, 1, piece * block : (piece + 1) * block] = jnp.concatenate(dens, axis=0)
        return carry

    lax.fori_loop(0, 2 * side, place_step, 0)

    def part(half, p2, p1):
        return parts.at[spot(half, p2, p1)]

    def stat(half, p2):
        return stats.at[half * side + p2]

    def combine(put, terms, weights):
        columns = [jnp.transpose(weight) for weight in weights]
        for item in range(block):
            total = None
            for term, column in zip(terms, columns):
                value = term[item].astype(jnp.float32) * column[0:rows, item : item + 1]
                total = value if total is None else total + value
            put(item, total)

    stat_copies = {}
    far, near = {}, {}
    for half in halves:
        up, down = shifted(second[half], turn), shifted(second[half], -turn)
        stat_copies[half, 0] = go(
            remote(stat(half, at(second[half], 2)), relay_s.at[half],
                   stat_send.at[half, 0], stat_recv.at[half, 0], up))
        stat_copies[half, 1] = go(
            remote(stat(half, at(second[half], -turn)), single_s.at[half],
                   stat_send.at[half, 1], stat_recv.at[half, 1], down))
    for order in range(4):
        for half in halves:
            up, down = shifted(second[half], turn), shifted(second[half], -turn)
            p1 = at(first[half], 2 - turn * order)
            far[half, order] = go(
                remote(part(half, at(second[half], 2), p1), relay.at[half, p1],
                       far_send.at[half, order], far_recv.at[half, order], up))
            near[half, order] = go(
                remote(part(half, at(second[half], -turn), p1), single.at[half, p1],
                       near_send.at[half, order], near_recv.at[half, order], down))

    for half in halves:
        stat_copies[half, 0].wait_recv()
        mine = stat(half, at(second[half], turn))
        top, den, weights = weigh([mine[0], relay_s[half, 0]], [mine[1], relay_s[half, 1]])
        outgoing_s[half, 0] = top
        outgoing_s[half, 1] = den
        factors[half, 0] = weights[0]
        factors[half, 1] = weights[1]
        stat_copies[half, 2] = go(
            remote(outgoing_s.at[half], merged_s.at[half],
                   stat_send.at[half, 2], stat_recv.at[half, 2], shifted(second[half], turn)))

    def join_copy(half, order):
        p1 = at(first[half], 2 - turn * order)
        return remote(relay.at[half, p1], merged.at[half, p1],
                      join_send.at[half, order], join_recv.at[half, order],
                      shifted(second[half], turn))

    def far_copy(half, order):
        p1 = at(first[half], 2 - turn * order)
        return remote(part(half, at(second[half], 2), p1), relay.at[half, p1],
                      far_send.at[half, order], far_recv.at[half, order],
                      shifted(second[half], turn))

    def near_copy(half, order):
        p1 = at(first[half], 2 - turn * order)
        return remote(part(half, at(second[half], -turn), p1), single.at[half, p1],
                      near_send.at[half, order], near_recv.at[half, order],
                      shifted(second[half], -turn))

    def relay_step(order, carry):
        for half in halves:
            p1 = at(first[half], 2 + side - turn * order)
            far_copy(half, order).wait_recv()
            lanes = pl.ds(p1 * block, block)
            target = relay.at[half, p1]

            def put(item, value):
                target[item] = value.astype(target.dtype)

            combine(
                put,
                [part(half, at(second[half], turn), p1), target],
                [factors[half, 0, lanes], factors[half, 1, lanes]],
            )
            join_copy(half, order).start()
        return carry

    lax.fori_loop(0, 4, relay_step, 0)

    for half in halves:
        stat_copies[half, 1].wait_recv()
        stat_copies[half, 2].wait_recv()
        mine = stat(half, at(second[half], 0))
        top, den, weights = weigh(
            [mine[0], merged_s[half, 0], single_s[half, 0]],
            [mine[1], merged_s[half, 1], single_s[half, 1]],
        )
        for index in range(3):
            factors[half, index] = weights[index]
        for p1 in range(side):
            small_s[half, p1, 0] = top[p1 * block : (p1 + 1) * block]
            small_s[half, p1, 1] = den[p1 * block : (p1 + 1) * block]

    def gather_piece(half, order):
        p1 = at(first[half], 2 + side - turn * order)
        near_copy(half, order).wait_recv()
        join_copy(half, order).wait_recv()
        lanes = pl.ds(p1 * block, block)
        target = small.at[half, p1]

        def put(item, value):
            target[item] = value.astype(target.dtype)

        combine(
            put,
            [part(half, at(second[half], 0), p1), merged.at[half, p1], single.at[half, p1]],
            [factors[half, index, lanes] for index in range(3)],
        )

    def piece_step(order, carry):
        for half in halves:
            gather_piece(half, order)
        return carry

    tails = {}

    def tail(half, index, source, source_s, delta):
        peer = shifted(first[half], delta)
        tails[half, index] = (
            go(remote(source_s, hop_s.at[half, index],
                      last_stat_send.at[half, index], last_stat_recv.at[half, index], peer)),
            go(remote(source, hop.at[half, index],
                      last_send.at[half, index], last_recv.at[half, index], peer)),
        )

    lax.fori_loop(0, 1, piece_step, 0)
    for half in halves:
        p1 = at(first[half], 2)
        tail(half, 0, small.at[half, p1], small_s.at[half, p1], turn)
    lax.fori_loop(1, 2, piece_step, 0)
    lax.fori_loop(2, 4, piece_step, 0)
    for half in halves:
        p1 = at(first[half], -turn)
        tail(half, 1, small.at[half, p1], small_s.at[half, p1], -turn)
    for half in halves:
        p1 = at(first[half], turn)
        for copy in tails[half, 0]:
            copy.wait_recv()
        target = small.at[half, p1]
        top, den, weights = weigh(
            [small_s[half, p1, 0], hop_s[half, 0, 0]], [small_s[half, p1, 1], hop_s[half, 0, 1]]
        )
        small_s[half, p1, 0] = top
        small_s[half, p1, 1] = den

        def put(item, value, target=target):
            target[item] = value.astype(target.dtype)

        combine(put, [target, hop.at[half, 0]], weights)
        tail(half, 2, target, small_s.at[half, p1], turn)
    for half in halves:
        p1 = at(first[half], 0)
        for index in (1, 2):
            for copy in tails[half, index]:
                copy.wait_recv()
        tree = [
            jnp.concatenate(
                [tree_stat[kind, half * block + item] for item in range(block)], axis=0
            )
            for kind in (0, 1)
        ]
        top, den, weights = weigh(
            [small_s[half, p1, 0], hop_s[half, 1, 0], hop_s[half, 2, 0], tree[0]],
            [small_s[half, p1, 1], hop_s[half, 1, 1], hop_s[half, 2, 1], tree[1]],
        )
        lane = lax.broadcasted_iota(jnp.int32, den.shape, 1)
        inverse = 1.0 / jnp.where(lane < rows, den, 1.0)

        def put(item, value, half=half):
            start = (half * block + item) * half_rows
            value = value.astype(out_ref.dtype)
            width = value.shape[1]
            for head in (0, 1):
                out_ref[start : start + half_rows, head * width : (head + 1) * width] = value[
                    head * half_rows : (head + 1) * half_rows
                ]

        combine(
            put,
            [
                small.at[half, p1],
                hop.at[half, 1],
                hop.at[half, 2],
                tree_acc.at[pl.ds(half * block, block)],
            ],
            [weight * inverse for weight in weights],
        )
    for copy in sends:
        copy.wait_send()
    for half in halves:
        for order in range(4):
            join_copy(half, order).wait_send()
    for c in (pieces - 2, pieces - 1):
        up_store(c).wait()


def cache_attention(
    streams, hc_in, qkv, up_rows, cosine, sine, tree_mask, k_pages, v_pages, page_owner, page_fill
):
    req_local, rows = tree_mask.shape[0:2]
    head_dim = k_pages.shape[3]
    tokens, feature = streams.shape[1:3]
    group = lax.axis_size("head")
    width = qkv.shape[1]
    hidden_units = up_rows.shape[0] * 128 // (2 * width)
    pieces = 8
    half_tokens = tokens // 2
    slots, keys = k_pages.shape[0], k_pages.shape[1] * k_pages.shape[2]
    devices = lax.axis_size("req")
    side = math.isqrt(devices)
    block = req_local // 2
    requests = req_local * devices
    owner_key = jnp.where(page_owner < 0, requests, page_owner)
    packed = (
        (owner_key << (SLOT_BITS + FILL_BITS))
        | (jnp.where(page_owner < 0, 0, page_fill) << SLOT_BITS)
        | jnp.arange(slots, dtype=jnp.int32)
    )
    rank = jnp.sum((packed[None, :] < packed[:, None]).astype(jnp.int32), axis=1)
    places = jnp.arange(slots, dtype=jnp.int32)
    table = jnp.sum(jnp.where(rank[None, :] == places[:, None], packed[None, :], 0), axis=1)
    spots = jnp.arange(requests, dtype=jnp.int32)
    half = spots // (requests // 2)
    outer = (spots // (block * side)) % side
    inner = (spots // block) % side
    home = jnp.where(half == 0, inner * side + outer, outer * side + inner)
    request = home * req_local + half * block + spots % block
    below = jnp.sum((owner_key[None, :] <= request[:, None]).astype(jnp.int32), axis=1)
    exact = jnp.sum((owner_key[None, :] == request[:, None]).astype(jnp.int32), axis=1)
    last = jnp.where(exact > 0, below - 1, slots)
    bf16, f32 = jnp.bfloat16, jnp.float32
    unit = (2, side, block, rows, head_dim)
    dma = pltpu.SemaphoreType.DMA
    scratch = [
        pltpu.VMEM((req_local, rows, head_dim), bf16),
        pltpu.VMEM((req_local, rows, head_dim), bf16),
        pltpu.VMEM((req_local, rows, head_dim), bf16),
        pltpu.VMEM(qkv.shape, bf16),
        pltpu.VMEM((tokens, feature), f32),
        pltpu.VMEM((2, group, 8, half_tokens), f32),
        pltpu.VMEM((2, half_tokens, 8), f32),
        pltpu.VMEM((tokens, feature), bf16),
        pltpu.VMEM((tokens, width), bf16),
        pltpu.VMEM((2, up_rows.shape[0] // pieces, 128), bf16),
        pltpu.VMEM((2, 2, width // pieces, hidden_units), bf16),
        dma,
        dma((2,)),
        dma((2, group)), dma((2, group)),
        dma((2, 4)), dma((2, 4)),
        dma((2, 3)), dma((2, 3)),
        dma((pieces,)), dma((pieces,)),
        pltpu.VMEM((req_local, rows, head_dim), f32),
        pltpu.VMEM((2, req_local, 1, 128), f32),
        pltpu.VMEM((requests, rows, head_dim), bf16),
        pltpu.VMEM((slots, keys, head_dim), bf16),
        pltpu.VMEM((slots, keys, head_dim), bf16),
        pltpu.VMEM((slots, keys, rows), f32),
        pltpu.VMEM((slots + 1, rows, head_dim), bf16),
        pltpu.VMEM((slots + 1, 1, 128), f32),
        pltpu.VMEM((slots + 1, 1, 128), f32),
        pltpu.VMEM((requests, rows, head_dim), bf16),
        pltpu.VMEM((2 * side, 2, side * block, 128), f32),
        pltpu.VMEM(unit, bf16),
        pltpu.VMEM(unit, bf16),
        pltpu.VMEM(unit, bf16),
        pltpu.VMEM((2, 2, side * block, 128), f32),
        pltpu.VMEM((2, 2, side * block, 128), f32),
        pltpu.VMEM((2, 2, side * block, 128), f32),
        pltpu.VMEM((2, 2, side * block, 128), f32),
        pltpu.VMEM((2, 3, side * block, 128), f32),
        pltpu.VMEM(unit, bf16),
        pltpu.VMEM((2, side, 2, block, 128), f32),
        pltpu.VMEM((2, 3, block, rows, head_dim), bf16),
        pltpu.VMEM((2, 3, 2, block, 128), f32),
        dma((2, 3)), dma((2, 3)),
        dma((2, 4, 3)), dma((2, 4, 3)),
        dma((2,)),
        dma((2, 4)), dma((2, 4)),
        dma((2, 4)), dma((2, 4)),
        dma((2, 4)), dma((2, 4)),
        dma((2, 3)), dma((2, 3)),
        dma((2, 3)), dma((2, 3)),
        dma((2, 3)), dma((2, 3)),
    ]
    vmem = pl.BlockSpec(memory_space=pltpu.VMEM)
    smem = pl.BlockSpec(memory_space=pltpu.SMEM)
    anywhere = pl.BlockSpec(memory_space=pl.ANY)
    return pl.pallas_call(
        functools.partial(cache_kernel, side, group // 2),
        out_shape=(
            jax.ShapeDtypeStruct((req_local * rows // 2, 2 * head_dim), bf16),
            jax.ShapeDtypeStruct((2, width, hidden_units), bf16),
        ),
        in_specs=[smem] * 3 + [vmem] * 4 + [anywhere] * 4,
        out_specs=(vmem, anywhere),
        scratch_shapes=scratch,
        compiler_params=pltpu.CompilerParams(
            collective_id=0, has_side_effects=True, vmem_limit_bytes=56 << 20
        ),
    )(
        table,
        last,
        hc_in,
        streams,
        cosine,
        sine,
        tree_mask,
        qkv,
        up_rows,
        k_pages.reshape(slots, keys, head_dim),
        v_pages.reshape(slots, keys, head_dim),
    )


def transpose_sum(values):
    half = values.shape[1] // 2
    return jnp.sum(jnp.transpose(values[:, 0:half] + values[:, half:]), axis=0, keepdims=True)


def layer_kernel(
    chips,
    chunks,
    hc_in,
    hc_mix,
    hc_out,
    accepted,
    attended,
    streams,
    out_hbm,
    gate_hbm,
    down_hbm,
    fresh_ref,
    final_ref,
    out_buf,
    gate_buf,
    down_buf,
    first_buf,
    mixed_buf,
    total_buf,
    share,
    twin,
    relay,
    joined,
    single,
    stat_all,
    columns,
    normed,
    gathered,
    hidden,
    load_sem,
    own_sem,
    twin_send,
    twin_recv,
    ring_send,
    ring_recv,
    stat_send,
    stat_recv,
    copy_send,
    copy_recv,
    pass_send,
    pass_recv,
):
    tokens, feature = attended.shape
    size = tokens // chunks
    group = 2 * chips
    width = group * feature
    count = streams.shape[0]
    inner = hidden.shape[1]
    strips = inner // feature
    me = lax.axis_index("head")
    chip = me // 2
    core = lax.rem(me, 2)
    turn = 1 - 2 * core

    def at(delta):
        return lax.rem(chip + chips + delta, chips)

    def peer(delta):
        return at(delta) * 2 + core

    sibling = chip * 2 + 1 - core

    def send_to(source, target, send_sem, recv_sem, head):
        return pltpu.make_async_remote_copy(
            src_ref=source,
            dst_ref=target,
            send_sem=send_sem,
            recv_sem=recv_sem,
            device_id={"head": head},
            device_id_type=MESH,
        )

    loads = []
    for index in range(group):
        loads.append(
            pltpu.make_async_copy(
                out_hbm.at[:, pl.ds(index * feature, feature)], out_buf.at[index], load_sem.at[0, index]
            )
        )
    for index in range(2 * strips):
        kind, strip = index // strips, index % strips
        loads.append(
            pltpu.make_async_copy(
                gate_hbm.at[kind, :, pl.ds(strip * feature, feature)],
                gate_buf.at[index],
                load_sem.at[1, index],
            )
        )
    for index in range(group):
        loads.append(
            pltpu.make_async_copy(
                down_hbm.at[:, pl.ds(index * feature, feature)], down_buf.at[index], load_sem.at[2, index]
            )
        )
    for load in loads:
        load.start()
    barrier = pltpu.get_barrier_semaphore()
    for step in range(1, group):
        pl.semaphore_signal(
            barrier, inc=1, device_id={"head": lax.rem(me + step, group)}, device_id_type=MESH
        )
    pl.semaphore_wait(barrier, group - 1)

    sends = []

    def go(copy):
        copy.start()
        sends.append(copy)
        return copy

    offsets = (2, 1, 3, 0)
    waits = {}

    def chunk_rows(t):
        return pl.ds(t * size, size)

    def lanes(head):
        return pl.ds(pl.multiple_of(head * feature, feature), feature)

    def scatter(which, t, product):
        for k, offset in enumerate(offsets):
            target = at(offset)
            piece = share.at[which, t, 1 - core, target]
            piece[...] = product(target * 2 + 1 - core).astype(piece.dtype)
            waits["twin", which, t, k] = go(
                send_to(piece, twin.at[which, t, target], twin_send.at[which, t, k],
                        twin_recv.at[which, t, k], sibling))
        for offset in offsets:
            target = at(offset)
            piece = share.at[which, t, core, target]
            piece[...] = product(target * 2 + core).astype(piece.dtype)

    def widen(ref):
        return ref[...].astype(jnp.float32)

    def chip_sum(which, t):
        def fold(k):
            waits["twin", which, t, k].wait_recv()
            target = at(offsets[k])
            piece = share.at[which, t, core, target]
            piece[...] = (widen(piece) + widen(twin.at[which, t, target])).astype(piece.dtype)

        fold(0)
        waits["far", which, t] = go(
            send_to(share.at[which, t, core, at(2)], relay.at[which, t],
                    ring_send.at[which, t, 0], ring_recv.at[which, t, 0], peer(turn)))
        fold(1)
        fold(2)
        waits["near", which, t] = go(
            send_to(share.at[which, t, core, at(-turn)], single.at[which, t],
                    ring_send.at[which, t, 1], ring_recv.at[which, t, 1], peer(-turn)))
        fold(3)

    def chip_relay(which, t):
        waits["far", which, t].wait_recv()
        piece = relay.at[which, t]
        piece[...] = (widen(piece) + widen(share.at[which, t, core, at(turn)])).astype(piece.dtype)
        waits["join", which, t] = go(
            send_to(piece, joined.at[which, t],
                    ring_send.at[which, t, 2], ring_recv.at[which, t, 2], peer(turn)))

    def finish(which, t):
        waits["near", which, t].wait_recv()
        waits["join", which, t].wait_recv()

    block = 32

    def delta_of(which, t, rows):
        return (
            share[which, t, core, at(0), rows].astype(jnp.float32)
            + joined[which, t, rows].astype(jnp.float32)
            + single[which, t, rows].astype(jnp.float32)
        )

    def remixed(layer, values, delta):
        result = []
        for target in range(count):
            total = hc_out[layer, target] * delta
            for source in range(count):
                weight = hc_mix[layer, source, target]
                if source == target:
                    weight = weight + 1.0
                total = total + weight * values[source]
            result.append(total)
        return result

    def project(t):
        if t == 0:
            for load in loads[:group]:
                load.wait()
        values = attended[t * size : (t + 1) * size]
        scatter(0, t, lambda head: jnp.dot(
            values, out_buf[head], preferred_element_type=jnp.float32))

    def middle(t):
        finish(0, t)

        def step(index, carry):
            inside = pl.ds(index * block, block)
            rows = pl.ds(t * size + index * block, block)
            values = [streams[s, rows].astype(jnp.float32) for s in range(count)]
            result = remixed(0, values, delta_of(0, t, inside))
            mixed = None
            for s in range(count):
                first_buf[s, rows] = result[s]
                term = hc_in[1, s] * result[s]
                mixed = term if mixed is None else mixed + term
            mixed_buf[rows] = mixed
            return carry

        lax.fori_loop(0, size // block, step, 0)
        mixed = mixed_buf[t * size : (t + 1) * size]
        stat_all[t, me, 0:1] = transpose_sum(mixed)
        stat_all[t, me, 1:2] = transpose_sum(mixed * mixed)
        stat_all[t, me, 2:8] = jnp.zeros((6, size), jnp.float32)
        for step in range(1, group):
            waits["stat", t, step] = go(
                send_to(stat_all.at[t, me], stat_all.at[t, me], stat_send.at[t, step],
                        stat_recv.at[t, step], lax.rem(me + step, group)))

    def normalized(t):
        for step in range(1, group):
            waits["stat", t, step].wait_recv()
        total = stat_all[t, 0]
        for index in range(1, group):
            total = total + stat_all[t, index]
        center = total[0:1] / width
        scale = lax.rsqrt(total[1:2] / width - center * center + 1e-05)
        row = lax.broadcasted_iota(jnp.int32, total.shape, 0)
        packed = jnp.where(row == 0, center, jnp.where(row == 1, scale, 0.0))
        columns[t] = jnp.transpose(packed)

        def step(index, carry):
            inside = pl.ds(index * block, block)
            rows = pl.ds(t * size + index * block, block)
            column = columns[t, inside]
            value = (mixed_buf[rows] - column[:, 0:1]) * column[:, 1:2]
            normed[rows] = value.astype(normed.dtype)
            return carry

        lax.fori_loop(0, size // block, step, 0)
        mine = normed.at[chunk_rows(t)]
        view = gathered.at[chunk_rows(t), lanes(me)]
        waits["fwd", t] = go(send_to(mine, view, pass_send.at[t, 0], pass_recv.at[t, 0], peer(turn)))
        waits["bwd", t] = go(send_to(mine, view, pass_send.at[t, 1], pass_recv.at[t, 1], peer(-turn)))
        waits["own", t] = go(send_to(mine, view, copy_send.at[t, 0], copy_recv.at[t, 0], sibling))
        local = pltpu.make_async_copy(mine, view, own_sem.at[t])
        local.start()
        waits["local", t] = local

    def hand_over(t, index, delta):
        view = gathered.at[chunk_rows(t), lanes(peer(delta))]
        waits["copy", t, index] = go(
            send_to(view, view, copy_send.at[t, index], copy_recv.at[t, index], sibling))

    def pass_on(t):
        waits["fwd", t].wait_recv()
        view = gathered.at[chunk_rows(t), lanes(peer(-turn))]
        waits["opp", t] = go(send_to(view, view, pass_send.at[t, 2], pass_recv.at[t, 2], peer(turn)))
        hand_over(t, 1, -turn)
        waits["bwd", t].wait_recv()
        hand_over(t, 2, turn)

    def pass_last(t):
        waits["opp", t].wait_recv()
        hand_over(t, 3, 2)

    def feed_forward(t):
        if t == 0:
            for load in loads[group:]:
                load.wait()
        waits["own", t].wait_recv()
        waits["local", t].wait()
        for index in (1, 2, 3):
            waits["copy", t, index].wait_recv()
        values = gathered.at[chunk_rows(t)]
        for strip in range(strips):
            gate = jnp.dot(values[...], gate_buf[strip], preferred_element_type=jnp.float32)
            up = jnp.dot(values[...], gate_buf[strips + strip], preferred_element_type=jnp.float32)
            hidden[:, strip * feature : (strip + 1) * feature] = (
                gate * lax.logistic(gate) * up
            ).astype(hidden.dtype)
        scatter(1, t, lambda head: jnp.dot(
            hidden[...], down_buf[head], preferred_element_type=jnp.float32))

    def last(t):
        finish(1, t)

        def step(index, carry):
            inside = pl.ds(index * block, block)
            rows = pl.ds(t * size + index * block, block)
            values = [first_buf[s, rows] for s in range(count)]
            result = remixed(1, values, delta_of(1, t, inside))
            total = result[0]
            for s in range(count):
                fresh_ref[s, rows] = result[s].astype(fresh_ref.dtype)
                if s > 0:
                    total = total + result[s]
            total_buf[rows] = total
            return carry

        lax.fori_loop(0, size // block, step, 0)

    phases = (
        project,
        lambda t: chip_sum(0, t),
        lambda t: chip_relay(0, t),
        middle,
        normalized,
        pass_on,
        pass_last,
        feed_forward,
        lambda t: chip_sum(1, t),
        lambda t: chip_relay(1, t),
        last,
    )
    for step in range(len(phases) + chunks - 1):
        for t in range(chunks):
            if 0 <= step - t < len(phases):
                phases[step - t](t)
    requests = accepted.shape[0]
    repeats = final_ref.shape[0] // requests
    tree = tokens // requests
    for item in range(requests):
        row = total_buf[pl.ds(item * tree + accepted[item], 1)]
        for copy_index in range(repeats):
            place = item * repeats + copy_index
            final_ref[place : place + 1] = row
    for copy in sends:
        copy.wait_send()


def layer(
    attended, streams, hc_in, hc_mix, hc_out, out_weight, gate_up, down_weight, accepted, repeats
):
    tokens, feature = attended.shape
    count = streams.shape[0]
    group = lax.axis_size("head")
    chips = group // 2
    width = out_weight.shape[1]
    inner = down_weight.shape[0]
    strips = inner // feature
    chunks = 3
    size = tokens // chunks
    bf16, f32 = jnp.bfloat16, jnp.float32
    dma = pltpu.SemaphoreType.DMA
    vmem = pl.BlockSpec(memory_space=pltpu.VMEM)
    smem = pl.BlockSpec(memory_space=pltpu.SMEM)
    anywhere = pl.BlockSpec(memory_space=pl.ANY)
    scratch = [
        pltpu.VMEM((group, feature, feature), bf16),
        pltpu.VMEM((2 * strips, width, feature), bf16),
        pltpu.VMEM((group, inner, feature), bf16),
        pltpu.VMEM((count, tokens, feature), f32),
        pltpu.VMEM((tokens, feature), f32),
        pltpu.VMEM((tokens, feature), f32),
        pltpu.VMEM((2, chunks, 2, chips, size, feature), bf16),
        pltpu.VMEM((2, chunks, chips, size, feature), bf16),
        pltpu.VMEM((2, chunks, size, feature), bf16),
        pltpu.VMEM((2, chunks, size, feature), bf16),
        pltpu.VMEM((2, chunks, size, feature), bf16),
        pltpu.VMEM((chunks, group, 8, size), f32),
        pltpu.VMEM((chunks, size, 8), f32),
        pltpu.VMEM((tokens, feature), bf16),
        pltpu.VMEM((tokens, width), bf16),
        pltpu.VMEM((size, inner), bf16),
        dma((3, max(group, 2 * strips))),
        dma((chunks,)),
        dma((2, chunks, 4)), dma((2, chunks, 4)),
        dma((2, chunks, 3)), dma((2, chunks, 3)),
        dma((chunks, group)), dma((chunks, group)),
        dma((chunks, 4)), dma((chunks, 4)),
        dma((chunks, 3)), dma((chunks, 3)),
    ]
    return pl.pallas_call(
        functools.partial(layer_kernel, chips, chunks),
        out_shape=(
            jax.ShapeDtypeStruct((count, tokens, feature), bf16),
            jax.ShapeDtypeStruct((accepted.shape[0] * repeats, feature), f32),
        ),
        in_specs=[smem] * 4 + [vmem, vmem, anywhere, anywhere, anywhere],
        out_specs=(vmem, vmem),
        scratch_shapes=scratch,
        compiler_params=pltpu.CompilerParams(
            collective_id=1, has_side_effects=True, vmem_limit_bytes=60 << 20
        ),
    )(
        hc_in,
        hc_mix,
        hc_out,
        accepted,
        attended,
        streams,
        out_weight,
        gate_up,
        down_weight,
    )


def draft_kernel(
    chips,
    final_ref,
    weight_hbm,
    vocab_hbm,
    logits_ref,
    final_all,
    weight_buf,
    vocab_buf,
    gathered,
    total,
    load_sem,
    sum_send,
    sum_recv,
    draft_send,
    draft_recv,
    copy_send,
    copy_recv,
    pass_send,
    pass_recv,
):
    rows, feature = final_ref.shape
    group = 2 * chips
    width = group * feature
    devices = gathered.shape[1] // rows
    me = lax.axis_index("head")
    home = lax.axis_index("req")
    chip = me // 2
    core = lax.rem(me, 2)
    turn = 1 - 2 * core
    sibling = chip * 2 + 1 - core

    def peer(delta):
        return lax.rem(chip + chips + delta, chips) * 2 + core

    def send_to(source, target, send_sem, recv_sem, device):
        return pltpu.make_async_remote_copy(
            src_ref=source,
            dst_ref=target,
            send_sem=send_sem,
            recv_sem=recv_sem,
            device_id=device,
            device_id_type=MESH,
        )

    loads = [pltpu.make_async_copy(weight_hbm, weight_buf, load_sem.at[0])]
    for index in range(group):
        loads.append(
            pltpu.make_async_copy(
                vocab_hbm.at[:, pl.ds(index * feature, feature)],
                vocab_buf.at[index],
                load_sem.at[1 + index],
            )
        )
    for load in loads:
        load.start()
    barrier = pltpu.get_barrier_semaphore()
    for step in range(1, group):
        pl.semaphore_signal(
            barrier, inc=1, device_id={"head": lax.rem(me + step, group)}, device_id_type=MESH
        )
    for step in range(1, devices):
        pl.semaphore_signal(
            barrier, inc=1, device_id={"req": lax.rem(home + step, devices)}, device_id_type=MESH
        )
    pl.semaphore_wait(barrier, group + devices - 2)

    sends = []

    def go(copy):
        copy.start()
        sends.append(copy)
        return copy

    sums = []
    for step in range(1, group):
        sums.append(
            go(send_to(final_ref, final_all.at[me], sum_send.at[step], sum_recv.at[step],
                       {"head": lax.rem(me + step, group)}))
        )
    final_all[me] = final_ref[...]
    loads[0].wait()
    for copy in sums:
        copy.wait_recv()
    center = jnp.zeros((rows, 1), jnp.float32)
    square = jnp.zeros((rows, 1), jnp.float32)
    for index in range(group):
        values = final_all[index]
        center = center + jnp.sum(values, axis=1, keepdims=True)
        square = square + jnp.sum(values * values, axis=1, keepdims=True)
    center = center / width
    scale = lax.rsqrt(square / width - center * center + 1e-05)
    branches = []
    for kind in range(2):
        branch = jnp.zeros((rows, feature), jnp.float32)
        for index in range(group):
            values = ((final_all[index] - center) * scale).astype(jnp.bfloat16)
            branch = branch + jnp.dot(
                values,
                weight_buf[kind, index * feature : (index + 1) * feature],
                preferred_element_type=jnp.float32,
            )
        branches.append(branch)
    odd = (lax.broadcasted_iota(jnp.int32, (rows, feature), 0) & 1) == 1
    branch = jnp.where(odd, branches[1], branches[0])
    drafted = (final_ref[...] - center) * scale + branch * lax.logistic(branch)
    mine = gathered.at[me, pl.ds(pl.multiple_of(home * rows, rows), rows)]
    mine[...] = drafted.astype(gathered.dtype)
    drafts = []
    for step in range(1, devices):
        drafts.append(
            go(send_to(mine, mine, draft_send.at[step], draft_recv.at[step],
                       {"req": lax.rem(home + step, devices)}))
        )
    for copy in drafts:
        copy.wait_recv()

    def shard(head):
        return gathered.at[head]

    def ring(index, delta, source):
        return go(send_to(shard(source), shard(source), pass_send.at[index], pass_recv.at[index],
                          {"head": peer(delta)}))

    def hand_over(index, source):
        return go(send_to(shard(source), shard(source), copy_send.at[index], copy_recv.at[index],
                          {"head": sibling}))

    fwd = ring(0, turn, me)
    bwd = ring(1, -turn, me)
    hands = [hand_over(0, me)]
    for load in loads[1:]:
        load.wait()

    def add(head, first=False):
        value = lax.dot_general(
            gathered[head],
            vocab_buf[head],
            (((1,), (1,)), ((), ())),
            preferred_element_type=jnp.float32,
        )
        total[...] = value if first else total[...] + value

    add(me, True)
    fwd.wait_recv()
    opp = ring(2, turn, peer(-turn))
    hands.append(hand_over(1, peer(-turn)))
    bwd.wait_recv()
    hands.append(hand_over(2, peer(turn)))
    add(peer(-turn))
    hands[0].wait_recv()
    add(sibling)
    add(peer(turn))
    opp.wait_recv()
    hands.append(hand_over(3, peer(2)))
    hands[1].wait_recv()

    def across(delta):
        return lax.rem(chip + chips + delta, chips) * 2 + 1 - core

    add(across(turn))
    hands[2].wait_recv()
    add(across(-turn))
    add(peer(2))
    hands[3].wait_recv()
    add(across(2))
    logits_ref[...] = total[...].astype(logits_ref.dtype)
    for copy in sends:
        copy.wait_send()


def draft_logits(final_rows, draft_weight, lm_head):
    rows, feature = final_rows.shape
    group = lax.axis_size("head")
    devices = lax.axis_size("req")
    width, vocab = lm_head.shape
    bf16, f32 = jnp.bfloat16, jnp.float32
    dma = pltpu.SemaphoreType.DMA
    vmem = pl.BlockSpec(memory_space=pltpu.VMEM)
    anywhere = pl.BlockSpec(memory_space=pl.ANY)
    return pl.pallas_call(
        functools.partial(draft_kernel, group // 2),
        out_shape=jax.ShapeDtypeStruct((devices * rows, vocab), bf16),
        in_specs=[vmem, anywhere, anywhere],
        out_specs=vmem,
        scratch_shapes=[
            pltpu.VMEM((group, rows, feature), f32),
            pltpu.VMEM(draft_weight.shape, bf16),
            pltpu.VMEM((group, vocab, feature), bf16),
            pltpu.VMEM((group, devices * rows, feature), bf16),
            pltpu.VMEM((devices * rows, vocab), f32),
            dma((1 + group,)),
            dma((group,)), dma((group,)),
            dma((devices,)), dma((devices,)),
            dma((4,)), dma((4,)),
            dma((3,)), dma((3,)),
        ],
        compiler_params=pltpu.CompilerParams(
            collective_id=2, has_side_effects=True, vmem_limit_bytes=40 << 20
        ),
    )(final_rows, draft_weight, jnp.transpose(lm_head))


def on_device(
    streams,
    hc_in,
    hc_mix,
    hc_out,
    qkv_weight,
    out_weight,
    up_gate,
    down_weight,
    draft_weight,
    lm_head,
    k_pages,
    v_pages,
    page_owner,
    page_fill,
    cache_len,
    tree_parent,
    accepted_index,
):
    tokens_local = streams.shape[0]
    req_local = cache_len.shape[0]
    tree_size = tree_parent.shape[1]
    heads_local = k_pages.shape[2]
    head_dim = k_pages.shape[3]
    draft_count = draft_weight.shape[0]
    all_requests = req_local * lax.axis_size("req")
    reach = ancestors(tree_parent)
    depth = (jnp.sum(reach.astype(jnp.float32), axis=1) - 1.0).astype(jnp.int32)
    positions = (cache_len[:, None] + depth).reshape(tokens_local)
    cosine, sine = turns(positions, head_dim)
    same_head = jnp.eye(heads_local, dtype=jnp.bfloat16)
    tree_mask = (same_head[None, :, None, :, None] * reach[:, None, :, None, :]).reshape(
        req_local, heads_local * tree_size, heads_local * tree_size
    )
    by_stream = jnp.transpose(streams, (1, 0, 2))
    width, kinds, inner = up_gate.shape
    up_rows = jnp.transpose(up_gate.reshape(width, kinds, inner // 128, 128), (0, 2, 1, 3)).reshape(
        -1, 128
    )
    attended, gate_up = cache_attention(
        by_stream,
        hc_in,
        jnp.transpose(qkv_weight, (1, 0, 2)),
        up_rows,
        cosine,
        sine,
        tree_mask,
        k_pages,
        v_pages,
        page_owner,
        page_fill,
    )
    fresh, final_local = layer(
        attended,
        by_stream,
        hc_in,
        hc_mix,
        hc_out,
        out_weight,
        gate_up,
        down_weight,
        accepted_index,
        draft_count,
    )
    new_streams = jnp.transpose(fresh, (1, 0, 2))
    logits_local = draft_logits(final_local, draft_weight, lm_head)
    logits_local = logits_local.reshape(all_requests, draft_count, -1)
    logits = lax.all_to_all(
        logits_local, ("req", "head"), split_axis=0, concat_axis=2, tiled=True
    ).astype(jnp.float32)
    return (new_streams, logits)


def solution(mesh):
    in_specs = (
        P("req", None, "head"),
        P(),
        P(),
        P(),
        P(None, None, "head"),
        P("head", None),
        P(None, None, "head"),
        P("head", None),
        P(None, None, "head"),
        P(None, ("req", "head")),
        P("req", None, "head", None),
        P("req", None, "head", None),
        P("req"),
        P("req"),
        P("req"),
        P("req", None),
        P("req"),
    )
    out_specs = (P("req", None, "head"), P(("req", "head"), None, None))
    return jax.shard_map(
        on_device, mesh=mesh, in_specs=in_specs, out_specs=out_specs, check_vma=False
    )
```

```python
import functools
import math

import jax
import jax.numpy as jnp
from jax import lax
from jax.experimental import pallas as pl
from jax.experimental.pallas import tpu as pltpu
from jax.sharding import PartitionSpec as P

NEG_FILL = -1e30


def ancestors(parents):
    length = parents.shape[1]
    places = jnp.arange(length, dtype=jnp.int32)
    linked = (places[None, :, None] == parents[:, None, :]) | (places[:, None] == places[None, :])[
        None
    ]
    reach = linked.astype(jnp.bfloat16)
    for repeat in range(max(1, (length - 1).bit_length())):
        counts = jnp.einsum("jki,jil->jkl", reach, reach, preferred_element_type=jnp.float32)
        reach = jnp.minimum(counts, 1.0).astype(jnp.bfloat16)
    return reach


def turns(positions, head_dim):
    half = head_dim // 2
    freqs = jnp.exp(
        jnp.arange(half, dtype=jnp.float32) * (-2.0 * math.log(10000.0) / head_dim)
    )
    angles = positions.astype(jnp.float32)[:, None] * freqs[None, :]
    cosine = jnp.cos(angles)
    sine = jnp.sin(angles)
    return jnp.concatenate([cosine, cosine], axis=1), jnp.concatenate([-sine, sine], axis=1)


MESH = pl.DeviceIdType.MESH
SLOT_BITS = 6
FILL_BITS = 8


def remote(source, target, send_sem, recv_sem, req):
    return pltpu.make_async_remote_copy(
        src_ref=source,
        dst_ref=target,
        send_sem=send_sem,
        recv_sem=recv_sem,
        device_id={"req": req},
        device_id_type=MESH,
    )


def weigh(tops, totals):
    top = functools.reduce(jnp.maximum, tops)
    factors = [jnp.exp(value - top) for value in tops]
    total = functools.reduce(lambda a, b: a + b, [f * t for f, t in zip(factors, totals)])
    return top, total, factors


def cache_kernel(
    side,
    chips,
    table,
    last,
    hc_in,
    streams,
    cosine,
    sine,
    mask_ref,
    weight_hbm,
    up_hbm,
    k_hbm,
    v_hbm,
    out_ref,
    gate_ref,
    q_ref,
    key_ref,
    value_ref,
    weight_buf,
    mixed_buf,
    stat_all,
    columns,
    normed,
    gathered,
    up_in,
    up_out,
    front_sem,
    own_sem,
    front_send,
    front_recv,
    copy_send,
    copy_recv,
    pass_send,
    pass_recv,
    up_in_sem,
    up_out_sem,
    tree_acc,
    tree_stat,
    q_all,
    k_buf,
    v_buf,
    scores,
    seg_acc,
    seg_top,
    seg_den,
    parts,
    stats,
    relay,
    merged,
    single,
    relay_s,
    merged_s,
    single_s,
    outgoing_s,
    factors,
    small,
    small_s,
    hop,
    hop_s,
    gather_send,
    gather_recv,
    spread_send,
    spread_recv,
    load_sem,
    far_send,
    far_recv,
    near_send,
    near_recv,
    join_send,
    join_recv,
    stat_send,
    stat_recv,
    last_send,
    last_recv,
    last_stat_send,
    last_stat_recv,
):
    block = q_ref.shape[0] // 2
    rows = q_ref.shape[1]
    slots = k_buf.shape[0]
    half_rows = rows // 2
    me = lax.axis_index("req")
    place = (me // side, lax.rem(me, side))
    turn = 1 - 2 * lax.rem(lax.axis_index("head"), 2)

    def shifted(axis, delta):
        moved = lax.rem(place[axis] + side + delta, side)
        return moved * side + place[1] if axis == 0 else place[0] * side + moved

    def at(axis, delta):
        return lax.rem(place[axis] + side + delta, side)

    first = (0, 1)
    second = (1, 0)

    def spot(half, p2, p1):
        return pl.ds(((half * side + p2) * side + p1) * block, block)

    loads = [
        pltpu.make_async_copy(k_hbm, k_buf, load_sem.at[0]),
        pltpu.make_async_copy(v_hbm, v_buf, load_sem.at[1]),
    ]
    weight_load = pltpu.make_async_copy(weight_hbm, weight_buf, front_sem)
    weight_load.start()
    barrier = pltpu.get_barrier_semaphore()
    for axis in (0, 1):
        for delta in (1, -1):
            pl.semaphore_signal(
                barrier, inc=1, device_id={"req": shifted(axis, delta)}, device_id_type=MESH
            )
    head_index = lax.axis_index("head")
    for step in range(1, 2 * chips):
        pl.semaphore_signal(
            barrier,
            inc=1,
            device_id={"head": lax.rem(head_index + step, 2 * chips)},
            device_id_type=MESH,
        )

    def enter():
        pl.semaphore_wait(barrier, 4 + 2 * chips - 1)

    pieces = gate_ref.shape[1] // up_out.shape[2]
    span = up_out.shape[2]
    tall = up_in.shape[1]

    def up_load(c):
        return pltpu.make_async_copy(
            up_hbm.at[pl.ds(c * tall, tall)], up_in.at[c % 2], up_in_sem.at[c]
        )

    def up_store(c):
        return pltpu.make_async_copy(
            up_out.at[c % 2], gate_ref.at[:, pl.ds(c * span, span)], up_out_sem.at[c]
        )

    strips = gate_ref.shape[2] // 128
    unit = 2 * strips * 16

    def untangle(c):
        if c + 1 < pieces:
            up_load(c + 1).start()
        up_load(c).wait()
        if c >= 2:
            up_store(c - 2).wait()
        out_row = lax.broadcasted_iota(jnp.int32, (unit, unit), 0)
        in_row = lax.broadcasted_iota(jnp.int32, (unit, unit), 1)
        kind = out_row // (unit // 2)
        strip = (out_row // 16) & (strips - 1)
        pick = (out_row & 15) * (2 * strips) + strip * 2 + kind
        chosen = jnp.where(in_row == pick, 1.0, 0.0).astype(jnp.bfloat16)

        def step(index, carry):
            sorted_rows = jnp.dot(
                chosen,
                up_in[c % 2, pl.ds(index * unit, unit)],
                preferred_element_type=jnp.float32,
            ).astype(up_out.dtype)
            place = pl.ds(index * 16, 16)
            for kind in (0, 1):
                for strip in range(strips):
                    row = (kind * strips + strip) * 16
                    up_out[c % 2, kind, place, strip * 128 : (strip + 1) * 128] = sorted_rows[
                        row : row + 16
                    ]
            return carry

        lax.fori_loop(0, span // 16, step, 0)
        up_store(c).start()

    up_load(0).start()

    sends = []

    def go(copy):
        copy.start()
        sends.append(copy)
        return copy

    def pass_block(half, axis, delta, p2, p1, send, recv, own=False):
        view = q_all.at[spot(half, p2, p1)]
        source = q_ref.at[pl.ds(half * block, block)] if own else view
        return go(remote(source, view, send, recv, shifted(axis, delta)))

    lines = {}
    crosses = {}

    def line(half, index, delta, p1, own=False):
        lines[half, index] = pass_block(
            half, first[half], delta, at(second[half], 0), p1,
            gather_send.at[half, index], gather_recv.at[half, index], own,
        )

    def cross(half, piece, index, delta, p2, p1, own=False):
        crosses[half, piece, index] = pass_block(
            half, second[half], delta, p2, p1,
            spread_send.at[half, piece, index], spread_recv.at[half, piece, index], own,
        )

    chunks = 2

    def front_part():
        count, tokens, feature = streams.shape
        size = tokens // chunks
        group = 2 * chips
        width = group * feature
        head_dim = q_ref.shape[2]
        rows = q_ref.shape[1]
        heads = feature // head_dim
        tree = rows // heads
        me = lax.axis_index("head")
        chip = me // 2
        core = lax.rem(me, 2)
        turn = 1 - 2 * core
        sibling = chip * 2 + 1 - core

        def peer(delta):
            return lax.rem(chip + chips + delta, chips) * 2 + core

        def send_to(source, target, send_sem, recv_sem, head):
            return pltpu.make_async_remote_copy(
                src_ref=source,
                dst_ref=target,
                send_sem=send_sem,
                recv_sem=recv_sem,
                device_id={"head": head},
                device_id_type=MESH,
            )

        block = 32
        for t in range(chunks):

            def mix(index, carry, t=t):
                here = pl.ds(t * size + index * block, block)
                mixed = None
                for s in range(count):
                    term = hc_in[0, s] * streams[s, here].astype(jnp.float32)
                    mixed = term if mixed is None else mixed + term
                mixed_buf[here] = mixed
                return carry

            lax.fori_loop(0, size // block, mix, 0)
            mixed = mixed_buf[t * size : (t + 1) * size]
            stat_all[t, me, 0:1] = transpose_sum(mixed)
            stat_all[t, me, 1:2] = transpose_sum(mixed * mixed)
            stat_all[t, me, 2:8] = jnp.zeros((6, size), jnp.float32)
        enter()
        waits = {}

        def chunk_rows(t):
            return pl.ds(t * size, size)

        def lanes(head):
            return pl.ds(pl.multiple_of(head * feature, feature), feature)

        for t in range(chunks):
            for step in range(1, group):
                waits["stat", t, step] = go(
                    send_to(stat_all.at[t, me], stat_all.at[t, me], front_send.at[t, step],
                            front_recv.at[t, step], lax.rem(me + step, group)))

        def normalized(t):
            for step in range(1, group):
                waits["stat", t, step].wait_recv()
            total = stat_all[t, 0]
            for index in range(1, group):
                total = total + stat_all[t, index]
            center = total[0:1] / width
            scale = lax.rsqrt(total[1:2] / width - center * center + 1e-05)
            row = lax.broadcasted_iota(jnp.int32, total.shape, 0)
            packed = jnp.where(row == 0, center, jnp.where(row == 1, scale, 0.0))
            columns[t] = jnp.transpose(packed)

            def step(index, carry):
                inside = pl.ds(index * block, block)
                here = pl.ds(t * size + index * block, block)
                column = columns[t, inside]
                value = (mixed_buf[here] - column[:, 0:1]) * column[:, 1:2]
                normed[here] = value.astype(normed.dtype)
                return carry

            lax.fori_loop(0, size // block, step, 0)
            mine = normed.at[chunk_rows(t)]
            view = gathered.at[chunk_rows(t), lanes(me)]
            waits["fwd", t] = go(send_to(mine, view, pass_send.at[t, 0], pass_recv.at[t, 0], peer(turn)))
            waits["bwd", t] = go(send_to(mine, view, pass_send.at[t, 1], pass_recv.at[t, 1], peer(-turn)))
            waits["own", t] = go(send_to(mine, view, copy_send.at[t, 0], copy_recv.at[t, 0], sibling))
            local = pltpu.make_async_copy(mine, view, own_sem.at[t])
            local.start()
            waits["local", t] = local

        def hand_over(t, index, delta):
            view = gathered.at[chunk_rows(t), lanes(peer(delta))]
            waits["copy", t, index] = go(
                send_to(view, view, copy_send.at[t, index], copy_recv.at[t, index], sibling))

        def pass_on(t):
            waits["fwd", t].wait_recv()
            view = gathered.at[chunk_rows(t), lanes(peer(-turn))]
            waits["opp", t] = go(send_to(view, view, pass_send.at[t, 2], pass_recv.at[t, 2], peer(turn)))
            hand_over(t, 1, -turn)
            waits["bwd", t].wait_recv()
            hand_over(t, 2, turn)

        def pass_last(t):
            waits["opp", t].wait_recv()
            hand_over(t, 3, 2)

        def project(t):
            if t == 0:
                weight_load.wait()
            waits["own", t].wait_recv()
            waits["local", t].wait()
            for index in (1, 2, 3):
                waits["copy", t, index].wait_recv()
            here = slice(t * size, (t + 1) * size)
            for kind, target in enumerate((q_ref, key_ref, value_ref)):
                product = jnp.dot(gathered[here], weight_buf[kind], preferred_element_type=jnp.float32)
                for head in range(heads):
                    value = product[:, head * head_dim : (head + 1) * head_dim]
                    if kind < 2:
                        turned = pltpu.roll(value, head_dim // 2, 1)
                        value = value * cosine[here] + turned * sine[here]
                    if kind == 0:
                        value = value * head_dim ** (-0.5)
                    value = value.astype(target.dtype)
                    for item in range(size // tree):
                        target[t * (size // tree) + item, head * tree : (head + 1) * tree] = value[
                            item * tree : (item + 1) * tree
                        ]
            launch(t)

        phases = (normalized, pass_on, pass_last, project)
        for step in range(len(phases) + chunks - 1):
            for t in range(chunks):
                if 0 <= step - t < len(phases):
                    phases[step - t](t)

    halves = (0, 1)

    def launch(half):
        line(half, 0, turn, at(first[half], 0), True)
        line(half, 1, -turn, at(first[half], 0), True)
        cross(half, 0, 0, turn, at(second[half], 0), at(first[half], 0), True)
        cross(half, 0, 1, -turn, at(second[half], 0), at(first[half], 0), True)

    front_part()
    for load in loads:
        load.start()
    for half in halves:
        q_all[spot(half, at(second[half], 0), at(first[half], 0))] = q_ref[
            half * block : (half + 1) * block
        ]
    seg_top[...] = jnp.full(seg_top.shape, NEG_FILL, jnp.float32)
    seg_den[...] = jnp.zeros(seg_den.shape, jnp.float32)
    seg_acc[slots] = jnp.zeros(seg_acc.shape[1:], seg_acc.dtype)
    tree_stat[...] = jnp.zeros(tree_stat.shape, jnp.float32)

    def tree_step(item, carry):
        found = lax.dot_general(
            key_ref[item],
            q_ref[item],
            (((1,), (1,)), ((), ())),
            preferred_element_type=jnp.float32,
        )
        found = jnp.where(mask_ref[item].astype(jnp.float32) > 0.0, found, NEG_FILL)
        top = jnp.max(found, axis=0, keepdims=True)
        weight = jnp.exp(found - top)
        tree_acc[item] = lax.dot_general(
            weight.astype(jnp.bfloat16),
            value_ref[item],
            (((0,), (0,)), ((), ())),
            preferred_element_type=jnp.float32,
        )
        tree_stat[0, item, :, 0:rows] = top
        tree_stat[1, item, :, 0:rows] = jnp.sum(weight, axis=0, keepdims=True)
        return carry

    lax.fori_loop(0, 2 * block, tree_step, 0)
    for half in halves:
        lines[half, 0].wait_recv()
        line(half, 2, turn, at(first[half], -turn))
        cross(half, 1, 0, turn, at(second[half], 0), at(first[half], -turn))
        cross(half, 1, 1, -turn, at(second[half], 0), at(first[half], -turn))
    untangle(0)
    untangle(1)
    for half in halves:
        lines[half, 1].wait_recv()
        cross(half, 2, 0, turn, at(second[half], 0), at(first[half], turn))
        cross(half, 2, 1, -turn, at(second[half], 0), at(first[half], turn))
    untangle(2)
    for half in halves:
        crosses[half, 0, 0].wait_recv()
        cross(half, 0, 2, turn, at(second[half], -turn), at(first[half], 0))
    untangle(3)
    for half in halves:
        lines[half, 2].wait_recv()
        cross(half, 3, 0, turn, at(second[half], 0), at(first[half], 2))
        cross(half, 3, 1, -turn, at(second[half], 0), at(first[half], 2))
    for piece, delta in ((1, -turn), (2, turn), (3, 2)):
        untangle(3 + piece)
        for half in halves:
            crosses[half, piece, 0].wait_recv()
            cross(half, piece, 2, turn, at(second[half], -turn), at(first[half], delta))
    untangle(7)
    for piece in range(4):
        for half in halves:
            crosses[half, piece, 1].wait_recv()
            crosses[half, piece, 2].wait_recv()
    for load in loads:
        load.wait()

    slot_mask = (1 << SLOT_BITS) - 1
    fill_mask = (1 << FILL_BITS) - 1
    requests = 2 * block * side * side

    def owner_at(index):
        return table[index] >> (SLOT_BITS + FILL_BITS)

    def starts_new(index):
        before = owner_at(jnp.maximum(index - 1, 0))
        return jnp.logical_or(index == 0, before != owner_at(index))

    shape = (k_buf.shape[1], rows)
    row_ids = lax.broadcasted_iota(jnp.int32, shape, 0)
    col_head = (lax.broadcasted_iota(jnp.int32, shape, 1) >= half_rows).astype(jnp.int32)
    matched = (row_ids & 1) == col_head
    key_ids = row_ids >> 1
    unroll = 4

    def score_step(group, carry):
        for offset in range(unroll):
            index = group * unroll + offset
            entry = table[index]
            fill = (entry >> SLOT_BITS) & fill_mask
            owner = jnp.minimum(entry >> (SLOT_BITS + FILL_BITS), requests - 1)
            home = owner // (2 * block)
            within = lax.rem(owner, 2 * block)
            half = within // block
            hx = home // side
            hy = lax.rem(home, side)
            outer = jnp.where(half == 0, hy, hx)
            inner = jnp.where(half == 0, hx, hy)
            row = ((half * side + outer) * side + inner) * block + lax.rem(within, block)
            found = lax.dot_general(
                k_buf[entry & slot_mask],
                q_all[row],
                (((1,), (1,)), ((), ())),
                preferred_element_type=jnp.float32,
            )
            found = jnp.where(jnp.logical_and(matched, key_ids < fill), found, NEG_FILL)
            scores[index] = found
            seg_top[index, :, 0:rows] = jnp.max(found, axis=0, keepdims=True)
        return carry

    lax.fori_loop(0, slots // unroll, score_step, 0)

    def forward(index, run):
        here = seg_top[index]
        run = jnp.where(starts_new(index), here, jnp.maximum(run, here))
        seg_top[index] = run
        return run

    lax.fori_loop(0, slots, forward, jnp.full(seg_top.shape[1:], NEG_FILL, jnp.float32))

    def backward(step, run):
        index = slots - 1 - step
        follow = jnp.minimum(index + 1, slots - 1)
        ends = jnp.logical_or(step == 0, owner_at(follow) != owner_at(index))
        run = jnp.where(ends, seg_top[index], run)
        seg_top[index] = run
        return run

    lax.fori_loop(0, slots, backward, jnp.full(seg_top.shape[1:], NEG_FILL, jnp.float32))

    def value_step(group, carry):
        acc_run, den_run = carry
        for offset in range(unroll):
            index = group * unroll + offset
            fresh = starts_new(index)
            top = seg_top[index][:, 0:rows]
            top = jnp.where(top < 0.5 * NEG_FILL, 0.0, top)
            weight = jnp.exp(scores[index] - top)
            den = jnp.sum(weight, axis=0, keepdims=True)
            acc = lax.dot_general(
                weight.astype(jnp.bfloat16),
                v_buf[table[index] & slot_mask],
                (((0,), (0,)), ((), ())),
                preferred_element_type=jnp.float32,
            )
            acc_run = acc + jnp.where(fresh, 0.0, acc_run)
            den_run = den + jnp.where(fresh, 0.0, den_run)
            seg_acc[index] = acc_run.astype(seg_acc.dtype)
            seg_den[index, :, 0:rows] = den_run
        return acc_run, den_run

    lax.fori_loop(
        0,
        slots // unroll,
        value_step,
        (jnp.zeros(seg_acc.shape[1:], jnp.float32), jnp.zeros((1, rows), jnp.float32)),
    )

    def place_step(group, carry):
        for piece in range(side):
            tops, dens = [], []
            for offset in range(block):
                spot_index = (group * side + piece) * block + offset
                found = last[spot_index]
                parts[spot_index] = seg_acc[found]
                tops.append(seg_top[found])
                dens.append(seg_den[found])
            stats[group, 0, piece * block : (piece + 1) * block] = jnp.concatenate(tops, axis=0)
            stats[group, 1, piece * block : (piece + 1) * block] = jnp.concatenate(dens, axis=0)
        return carry

    for half in halves:
        for delta in (2, -turn):
            place_step(half * side + at(second[half], delta), 0)

    def part(half, p2, p1):
        return parts.at[spot(half, p2, p1)]

    def stat(half, p2):
        return stats.at[half * side + p2]

    def combine(put, terms, weights):
        columns = [jnp.transpose(weight) for weight in weights]
        for item in range(block):
            total = None
            for term, column in zip(terms, columns):
                value = term[item].astype(jnp.float32) * column[0:rows, item : item + 1]
                total = value if total is None else total + value
            put(item, total)

    stat_copies = {}
    far, near = {}, {}
    for half in halves:
        up, down = shifted(second[half], turn), shifted(second[half], -turn)
        stat_copies[half, 0] = go(
            remote(stat(half, at(second[half], 2)), relay_s.at[half],
                   stat_send.at[half, 0], stat_recv.at[half, 0], up))
        stat_copies[half, 1] = go(
            remote(stat(half, at(second[half], -turn)), single_s.at[half],
                   stat_send.at[half, 1], stat_recv.at[half, 1], down))
    for order in range(4):
        for half in halves:
            up, down = shifted(second[half], turn), shifted(second[half], -turn)
            p1 = at(first[half], 2 - turn * order)
            far[half, order] = go(
                remote(part(half, at(second[half], 2), p1), relay.at[half, p1],
                       far_send.at[half, order], far_recv.at[half, order], up))
            near[half, order] = go(
                remote(part(half, at(second[half], -turn), p1), single.at[half, p1],
                       near_send.at[half, order], near_recv.at[half, order], down))

    for half in halves:
        for delta in (turn, 0):
            place_step(half * side + at(second[half], delta), 0)

    for half in halves:
        stat_copies[half, 0].wait_recv()
        mine = stat(half, at(second[half], turn))
        top, den, weights = weigh([mine[0], relay_s[half, 0]], [mine[1], relay_s[half, 1]])
        outgoing_s[half, 0] = top
        outgoing_s[half, 1] = den
        factors[half, 0] = weights[0]
        factors[half, 1] = weights[1]
        stat_copies[half, 2] = go(
            remote(outgoing_s.at[half], merged_s.at[half],
                   stat_send.at[half, 2], stat_recv.at[half, 2], shifted(second[half], turn)))

    def join_copy(half, order):
        p1 = at(first[half], 2 - turn * order)
        return remote(relay.at[half, p1], merged.at[half, p1],
                      join_send.at[half, order], join_recv.at[half, order],
                      shifted(second[half], turn))

    def far_copy(half, order):
        p1 = at(first[half], 2 - turn * order)
        return remote(part(half, at(second[half], 2), p1), relay.at[half, p1],
                      far_send.at[half, order], far_recv.at[half, order],
                      shifted(second[half], turn))

    def near_copy(half, order):
        p1 = at(first[half], 2 - turn * order)
        return remote(part(half, at(second[half], -turn), p1), single.at[half, p1],
                      near_send.at[half, order], near_recv.at[half, order],
                      shifted(second[half], -turn))

    def relay_step(order, carry):
        for half in halves:
            p1 = at(first[half], 2 + side - turn * order)
            far_copy(half, order).wait_recv()
            lanes = pl.ds(p1 * block, block)
            target = relay.at[half, p1]

            def put(item, value):
                target[item] = value.astype(target.dtype)

            combine(
                put,
                [part(half, at(second[half], turn), p1), target],
                [factors[half, 0, lanes], factors[half, 1, lanes]],
            )
            join_copy(half, order).start()
        return carry

    lax.fori_loop(0, 4, relay_step, 0)

    for half in halves:
        stat_copies[half, 1].wait_recv()
        stat_copies[half, 2].wait_recv()
        mine = stat(half, at(second[half], 0))
        top, den, weights = weigh(
            [mine[0], merged_s[half, 0], single_s[half, 0]],
            [mine[1], merged_s[half, 1], single_s[half, 1]],
        )
        for index in range(3):
            factors[half, index] = weights[index]
        for p1 in range(side):
            small_s[half, p1, 0] = top[p1 * block : (p1 + 1) * block]
            small_s[half, p1, 1] = den[p1 * block : (p1 + 1) * block]

    def gather_piece(half, order):
        p1 = at(first[half], 2 + side - turn * order)
        near_copy(half, order).wait_recv()
        join_copy(half, order).wait_recv()
        lanes = pl.ds(p1 * block, block)
        target = small.at[half, p1]

        def put(item, value):
            target[item] = value.astype(target.dtype)

        combine(
            put,
            [part(half, at(second[half], 0), p1), merged.at[half, p1], single.at[half, p1]],
            [factors[half, index, lanes] for index in range(3)],
        )

    def piece_step(order, carry):
        for half in halves:
            gather_piece(half, order)
        return carry

    tails = {}

    def tail(half, index, source, source_s, delta):
        peer = shifted(first[half], delta)
        tails[half, index] = (
            go(remote(source_s, hop_s.at[half, index],
                      last_stat_send.at[half, index], last_stat_recv.at[half, index], peer)),
            go(remote(source, hop.at[half, index],
                      last_send.at[half, index], last_recv.at[half, index], peer)),
        )

    lax.fori_loop(0, 1, piece_step, 0)
    for half in halves:
        p1 = at(first[half], 2)
        tail(half, 0, small.at[half, p1], small_s.at[half, p1], turn)
    lax.fori_loop(1, 2, piece_step, 0)
    lax.fori_loop(2, 4, piece_step, 0)
    for half in halves:
        p1 = at(first[half], -turn)
        tail(half, 1, small.at[half, p1], small_s.at[half, p1], -turn)
    for half in halves:
        p1 = at(first[half], turn)
        for copy in tails[half, 0]:
            copy.wait_recv()
        target = small.at[half, p1]
        top, den, weights = weigh(
            [small_s[half, p1, 0], hop_s[half, 0, 0]], [small_s[half, p1, 1], hop_s[half, 0, 1]]
        )
        small_s[half, p1, 0] = top
        small_s[half, p1, 1] = den

        def put(item, value, target=target):
            target[item] = value.astype(target.dtype)

        combine(put, [target, hop.at[half, 0]], weights)
        tail(half, 2, target, small_s.at[half, p1], turn)
    for half in halves:
        p1 = at(first[half], 0)
        for index in (1, 2):
            for copy in tails[half, index]:
                copy.wait_recv()
        tree = [
            jnp.concatenate(
                [tree_stat[kind, half * block + item] for item in range(block)], axis=0
            )
            for kind in (0, 1)
        ]
        top, den, weights = weigh(
            [small_s[half, p1, 0], hop_s[half, 1, 0], hop_s[half, 2, 0], tree[0]],
            [small_s[half, p1, 1], hop_s[half, 1, 1], hop_s[half, 2, 1], tree[1]],
        )
        lane = lax.broadcasted_iota(jnp.int32, den.shape, 1)
        inverse = 1.0 / jnp.where(lane < rows, den, 1.0)

        def put(item, value, half=half):
            start = (half * block + item) * half_rows
            value = value.astype(out_ref.dtype)
            width = value.shape[1]
            for head in (0, 1):
                out_ref[start : start + half_rows, head * width : (head + 1) * width] = value[
                    head * half_rows : (head + 1) * half_rows
                ]

        combine(
            put,
            [
                small.at[half, p1],
                hop.at[half, 1],
                hop.at[half, 2],
                tree_acc.at[pl.ds(half * block, block)],
            ],
            [weight * inverse for weight in weights],
        )
    for copy in sends:
        copy.wait_send()
    for half in halves:
        for order in range(4):
            join_copy(half, order).wait_send()
    for c in (pieces - 2, pieces - 1):
        up_store(c).wait()


def cache_attention(
    streams, hc_in, qkv, up_rows, cosine, sine, tree_mask, k_pages, v_pages, page_owner, page_fill
):
    req_local, rows = tree_mask.shape[0:2]
    head_dim = k_pages.shape[3]
    tokens, feature = streams.shape[1:3]
    group = lax.axis_size("head")
    width = qkv.shape[1]
    hidden_units = up_rows.shape[0] * 128 // (2 * width)
    pieces = 8
    half_tokens = tokens // 2
    slots, keys = k_pages.shape[0], k_pages.shape[1] * k_pages.shape[2]
    devices = lax.axis_size("req")
    side = math.isqrt(devices)
    block = req_local // 2
    requests = req_local * devices
    owner_key = jnp.where(page_owner < 0, requests, page_owner)
    packed = (
        (owner_key << (SLOT_BITS + FILL_BITS))
        | (jnp.where(page_owner < 0, 0, page_fill) << SLOT_BITS)
        | jnp.arange(slots, dtype=jnp.int32)
    )
    rank = jnp.sum((packed[None, :] < packed[:, None]).astype(jnp.int32), axis=1)
    places = jnp.arange(slots, dtype=jnp.int32)
    table = jnp.sum(jnp.where(rank[None, :] == places[:, None], packed[None, :], 0), axis=1)
    spots = jnp.arange(requests, dtype=jnp.int32)
    half = spots // (requests // 2)
    outer = (spots // (block * side)) % side
    inner = (spots // block) % side
    home = jnp.where(half == 0, inner * side + outer, outer * side + inner)
    request = home * req_local + half * block + spots % block
    below = jnp.sum((owner_key[None, :] <= request[:, None]).astype(jnp.int32), axis=1)
    exact = jnp.sum((owner_key[None, :] == request[:, None]).astype(jnp.int32), axis=1)
    last = jnp.where(exact > 0, below - 1, slots)
    bf16, f32 = jnp.bfloat16, jnp.float32
    unit = (2, side, block, rows, head_dim)
    dma = pltpu.SemaphoreType.DMA
    scratch = [
        pltpu.VMEM((req_local, rows, head_dim), bf16),
        pltpu.VMEM((req_local, rows, head_dim), bf16),
        pltpu.VMEM((req_local, rows, head_dim), bf16),
        pltpu.VMEM(qkv.shape, bf16),
        pltpu.VMEM((tokens, feature), f32),
        pltpu.VMEM((2, group, 8, half_tokens), f32),
        pltpu.VMEM((2, half_tokens, 8), f32),
        pltpu.VMEM((tokens, feature), bf16),
        pltpu.VMEM((tokens, width), bf16),
        pltpu.VMEM((2, up_rows.shape[0] // pieces, 128), bf16),
        pltpu.VMEM((2, 2, width // pieces, hidden_units), bf16),
        dma,
        dma((2,)),
        dma((2, group)), dma((2, group)),
        dma((2, 4)), dma((2, 4)),
        dma((2, 3)), dma((2, 3)),
        dma((pieces,)), dma((pieces,)),
        pltpu.VMEM((req_local, rows, head_dim), f32),
        pltpu.VMEM((2, req_local, 1, 128), f32),
        pltpu.VMEM((requests, rows, head_dim), bf16),
        pltpu.VMEM((slots, keys, head_dim), bf16),
        pltpu.VMEM((slots, keys, head_dim), bf16),
        pltpu.VMEM((slots, keys, rows), f32),
        pltpu.VMEM((slots + 1, rows, head_dim), bf16),
        pltpu.VMEM((slots + 1, 1, 128), f32),
        pltpu.VMEM((slots + 1, 1, 128), f32),
        pltpu.VMEM((requests, rows, head_dim), bf16),
        pltpu.VMEM((2 * side, 2, side * block, 128), f32),
        pltpu.VMEM(unit, bf16),
        pltpu.VMEM(unit, bf16),
        pltpu.VMEM(unit, bf16),
        pltpu.VMEM((2, 2, side * block, 128), f32),
        pltpu.VMEM((2, 2, side * block, 128), f32),
        pltpu.VMEM((2, 2, side * block, 128), f32),
        pltpu.VMEM((2, 2, side * block, 128), f32),
        pltpu.VMEM((2, 3, side * block, 128), f32),
        pltpu.VMEM(unit, bf16),
        pltpu.VMEM((2, side, 2, block, 128), f32),
        pltpu.VMEM((2, 3, block, rows, head_dim), bf16),
        pltpu.VMEM((2, 3, 2, block, 128), f32),
        dma((2, 3)), dma((2, 3)),
        dma((2, 4, 3)), dma((2, 4, 3)),
        dma((2,)),
        dma((2, 4)), dma((2, 4)),
        dma((2, 4)), dma((2, 4)),
        dma((2, 4)), dma((2, 4)),
        dma((2, 3)), dma((2, 3)),
        dma((2, 3)), dma((2, 3)),
        dma((2, 3)), dma((2, 3)),
    ]
    vmem = pl.BlockSpec(memory_space=pltpu.VMEM)
    smem = pl.BlockSpec(memory_space=pltpu.SMEM)
    anywhere = pl.BlockSpec(memory_space=pl.ANY)
    return pl.pallas_call(
        functools.partial(cache_kernel, side, group // 2),
        out_shape=(
            jax.ShapeDtypeStruct((req_local * rows // 2, 2 * head_dim), bf16),
            jax.ShapeDtypeStruct((2, width, hidden_units), bf16),
        ),
        in_specs=[smem] * 3 + [vmem] * 4 + [anywhere] * 4,
        out_specs=(vmem, anywhere),
        scratch_shapes=scratch,
        compiler_params=pltpu.CompilerParams(
            collective_id=0, has_side_effects=True, vmem_limit_bytes=56 << 20
        ),
    )(
        table,
        last,
        hc_in,
        streams,
        cosine,
        sine,
        tree_mask,
        qkv,
        up_rows,
        k_pages.reshape(slots, keys, head_dim),
        v_pages.reshape(slots, keys, head_dim),
    )


def transpose_sum(values):
    half = values.shape[1] // 2
    return jnp.sum(jnp.transpose(values[:, 0:half] + values[:, half:]), axis=0, keepdims=True)


def layer_kernel(
    chips,
    chunks,
    hc_in,
    hc_mix,
    hc_out,
    accepted,
    attended,
    streams,
    out_hbm,
    gate_hbm,
    down_hbm,
    weight_hbm,
    vocab_hbm,
    fresh_ref,
    logits_ref,
    final_ref,
    final_all,
    weight_buf,
    vocab_buf,
    shards,
    logits_acc,
    draft_sem,
    sum_send,
    sum_recv,
    draft_send,
    draft_recv,
    hand_send,
    hand_recv,
    loop_send,
    loop_recv,
    out_buf,
    gate_buf,
    down_buf,
    first_buf,
    mixed_buf,
    total_buf,
    share,
    twin,
    relay,
    joined,
    single,
    stat_all,
    columns,
    normed,
    gathered,
    hidden,
    load_sem,
    own_sem,
    twin_send,
    twin_recv,
    ring_send,
    ring_recv,
    stat_send,
    stat_recv,
    copy_send,
    copy_recv,
    pass_send,
    pass_recv,
):
    tokens, feature = attended.shape
    size = tokens // chunks
    group = 2 * chips
    width = group * feature
    count = streams.shape[0]
    inner = hidden.shape[1]
    strips = inner // feature
    me = lax.axis_index("head")
    chip = me // 2
    core = lax.rem(me, 2)
    turn = 1 - 2 * core

    def at(delta):
        return lax.rem(chip + chips + delta, chips)

    def peer(delta):
        return at(delta) * 2 + core

    sibling = chip * 2 + 1 - core

    def send_to(source, target, send_sem, recv_sem, head):
        return pltpu.make_async_remote_copy(
            src_ref=source,
            dst_ref=target,
            send_sem=send_sem,
            recv_sem=recv_sem,
            device_id={"head": head},
            device_id_type=MESH,
        )

    loads = []
    for index in range(group):
        loads.append(
            pltpu.make_async_copy(
                out_hbm.at[:, pl.ds(index * feature, feature)], out_buf.at[index], load_sem.at[0, index]
            )
        )
    for index in range(2 * strips):
        kind, strip = index // strips, index % strips
        loads.append(
            pltpu.make_async_copy(
                gate_hbm.at[kind, :, pl.ds(strip * feature, feature)],
                gate_buf.at[index],
                load_sem.at[1, index],
            )
        )
    for index in range(group):
        loads.append(
            pltpu.make_async_copy(
                down_hbm.at[:, pl.ds(index * feature, feature)], down_buf.at[index], load_sem.at[2, index]
            )
        )
    draft_loads = [pltpu.make_async_copy(weight_hbm, weight_buf, draft_sem.at[0])]
    for index in range(group):
        draft_loads.append(
            pltpu.make_async_copy(
                vocab_hbm.at[:, pl.ds(index * feature, feature)],
                vocab_buf.at[index],
                draft_sem.at[1 + index],
            )
        )
    for load in loads + draft_loads:
        load.start()
    barrier = pltpu.get_barrier_semaphore()
    home_index = lax.axis_index("req")
    peers = shards.shape[1] // final_ref.shape[0]
    for step in range(1, group):
        pl.semaphore_signal(
            barrier, inc=1, device_id={"head": lax.rem(me + step, group)}, device_id_type=MESH
        )
    for step in range(1, peers):
        pl.semaphore_signal(
            barrier, inc=1, device_id={"req": lax.rem(home_index + step, peers)}, device_id_type=MESH
        )
    pl.semaphore_wait(barrier, group + peers - 2)

    sends = []

    def go(copy):
        copy.start()
        sends.append(copy)
        return copy

    offsets = (2, 1, 3, 0)
    waits = {}

    def chunk_rows(t):
        return pl.ds(t * size, size)

    def lanes(head):
        return pl.ds(pl.multiple_of(head * feature, feature), feature)

    def scatter(which, t, product):
        for k, offset in enumerate(offsets):
            target = at(offset)
            piece = share.at[which, t, 1 - core, target]
            piece[...] = product(target * 2 + 1 - core).astype(piece.dtype)
            waits["twin", which, t, k] = go(
                send_to(piece, twin.at[which, t, target], twin_send.at[which, t, k],
                        twin_recv.at[which, t, k], sibling))
        for offset in offsets:
            target = at(offset)
            piece = share.at[which, t, core, target]
            piece[...] = product(target * 2 + core).astype(piece.dtype)

    def widen(ref):
        return ref[...].astype(jnp.float32)

    def chip_sum(which, t):
        def fold(k):
            waits["twin", which, t, k].wait_recv()
            target = at(offsets[k])
            piece = share.at[which, t, core, target]
            piece[...] = (widen(piece) + widen(twin.at[which, t, target])).astype(piece.dtype)

        fold(0)
        waits["far", which, t] = go(
            send_to(share.at[which, t, core, at(2)], relay.at[which, t],
                    ring_send.at[which, t, 0], ring_recv.at[which, t, 0], peer(turn)))
        fold(1)
        fold(2)
        waits["near", which, t] = go(
            send_to(share.at[which, t, core, at(-turn)], single.at[which, t],
                    ring_send.at[which, t, 1], ring_recv.at[which, t, 1], peer(-turn)))
        fold(3)

    def chip_relay(which, t):
        waits["far", which, t].wait_recv()
        piece = relay.at[which, t]
        piece[...] = (widen(piece) + widen(share.at[which, t, core, at(turn)])).astype(piece.dtype)
        waits["join", which, t] = go(
            send_to(piece, joined.at[which, t],
                    ring_send.at[which, t, 2], ring_recv.at[which, t, 2], peer(turn)))

    def finish(which, t):
        waits["near", which, t].wait_recv()
        waits["join", which, t].wait_recv()

    block = 32

    def delta_of(which, t, rows):
        return (
            share[which, t, core, at(0), rows].astype(jnp.float32)
            + joined[which, t, rows].astype(jnp.float32)
            + single[which, t, rows].astype(jnp.float32)
        )

    def remixed(layer, values, delta):
        result = []
        for target in range(count):
            total = hc_out[layer, target] * delta
            for source in range(count):
                weight = hc_mix[layer, source, target]
                if source == target:
                    weight = weight + 1.0
                total = total + weight * values[source]
            result.append(total)
        return result

    def project(t):
        if t == 0:
            for load in loads[:group]:
                load.wait()
        values = attended[t * size : (t + 1) * size]
        scatter(0, t, lambda head: jnp.dot(
            values, out_buf[head], preferred_element_type=jnp.float32))

    def middle(t):
        finish(0, t)

        def step(index, carry):
            inside = pl.ds(index * block, block)
            rows = pl.ds(t * size + index * block, block)
            values = [streams[s, rows].astype(jnp.float32) for s in range(count)]
            result = remixed(0, values, delta_of(0, t, inside))
            mixed = None
            for s in range(count):
                first_buf[s, rows] = result[s]
                term = hc_in[1, s] * result[s]
                mixed = term if mixed is None else mixed + term
            mixed_buf[rows] = mixed
            return carry

        lax.fori_loop(0, size // block, step, 0)
        mixed = mixed_buf[t * size : (t + 1) * size]
        stat_all[t, me, 0:1] = transpose_sum(mixed)
        stat_all[t, me, 1:2] = transpose_sum(mixed * mixed)
        stat_all[t, me, 2:8] = jnp.zeros((6, size), jnp.float32)
        for step in range(1, group):
            waits["stat", t, step] = go(
                send_to(stat_all.at[t, me], stat_all.at[t, me], stat_send.at[t, step],
                        stat_recv.at[t, step], lax.rem(me + step, group)))

    def normalized(t):
        for step in range(1, group):
            waits["stat", t, step].wait_recv()
        total = stat_all[t, 0]
        for index in range(1, group):
            total = total + stat_all[t, index]
        center = total[0:1] / width
        scale = lax.rsqrt(total[1:2] / width - center * center + 1e-05)
        row = lax.broadcasted_iota(jnp.int32, total.shape, 0)
        packed = jnp.where(row == 0, center, jnp.where(row == 1, scale, 0.0))
        columns[t] = jnp.transpose(packed)

        def step(index, carry):
            inside = pl.ds(index * block, block)
            rows = pl.ds(t * size + index * block, block)
            column = columns[t, inside]
            value = (mixed_buf[rows] - column[:, 0:1]) * column[:, 1:2]
            normed[rows] = value.astype(normed.dtype)
            return carry

        lax.fori_loop(0, size // block, step, 0)
        mine = normed.at[chunk_rows(t)]
        view = gathered.at[chunk_rows(t), lanes(me)]
        waits["fwd", t] = go(send_to(mine, view, pass_send.at[t, 0], pass_recv.at[t, 0], peer(turn)))
        waits["bwd", t] = go(send_to(mine, view, pass_send.at[t, 1], pass_recv.at[t, 1], peer(-turn)))
        waits["own", t] = go(send_to(mine, view, copy_send.at[t, 0], copy_recv.at[t, 0], sibling))
        local = pltpu.make_async_copy(mine, view, own_sem.at[t])
        local.start()
        waits["local", t] = local

    def hand_over(t, index, delta):
        view = gathered.at[chunk_rows(t), lanes(peer(delta))]
        waits["copy", t, index] = go(
            send_to(view, view, copy_send.at[t, index], copy_recv.at[t, index], sibling))

    def pass_on(t):
        waits["fwd", t].wait_recv()
        view = gathered.at[chunk_rows(t), lanes(peer(-turn))]
        waits["opp", t] = go(send_to(view, view, pass_send.at[t, 2], pass_recv.at[t, 2], peer(turn)))
        hand_over(t, 1, -turn)
        waits["bwd", t].wait_recv()
        hand_over(t, 2, turn)

    def pass_last(t):
        waits["opp", t].wait_recv()
        hand_over(t, 3, 2)

    def feed_forward(t):
        if t == 0:
            for load in loads[group:]:
                load.wait()
        waits["own", t].wait_recv()
        waits["local", t].wait()
        for index in (1, 2, 3):
            waits["copy", t, index].wait_recv()
        values = gathered.at[chunk_rows(t)]
        for strip in range(strips):
            gate = jnp.dot(values[...], gate_buf[strip], preferred_element_type=jnp.float32)
            up = jnp.dot(values[...], gate_buf[strips + strip], preferred_element_type=jnp.float32)
            hidden[:, strip * feature : (strip + 1) * feature] = (
                gate * lax.logistic(gate) * up
            ).astype(hidden.dtype)
        scatter(1, t, lambda head: jnp.dot(
            hidden[...], down_buf[head], preferred_element_type=jnp.float32))

    def last(t):
        finish(1, t)

        def step(index, carry):
            inside = pl.ds(index * block, block)
            rows = pl.ds(t * size + index * block, block)
            values = [first_buf[s, rows] for s in range(count)]
            result = remixed(1, values, delta_of(1, t, inside))
            total = result[0]
            for s in range(count):
                fresh_ref[s, rows] = result[s].astype(fresh_ref.dtype)
                if s > 0:
                    total = total + result[s]
            total_buf[rows] = total
            return carry

        lax.fori_loop(0, size // block, step, 0)

    phases = (
        project,
        lambda t: chip_sum(0, t),
        lambda t: chip_relay(0, t),
        middle,
        normalized,
        pass_on,
        pass_last,
        feed_forward,
        lambda t: chip_sum(1, t),
        lambda t: chip_relay(1, t),
        last,
    )
    for step in range(len(phases) + chunks - 1):
        for t in range(chunks):
            if 0 <= step - t < len(phases):
                phases[step - t](t)
    requests = accepted.shape[0]
    repeats = final_ref.shape[0] // requests
    tree = tokens // requests
    for item in range(requests):
        row = total_buf[pl.ds(item * tree + accepted[item], 1)]
        for copy_index in range(repeats):
            place = item * repeats + copy_index
            final_ref[place : place + 1] = row

    def draft_part():
        rows, feature = final_ref.shape
        group = 2 * chips
        width = group * feature
        devices = shards.shape[1] // rows
        me = lax.axis_index("head")
        home = lax.axis_index("req")
        chip = me // 2
        core = lax.rem(me, 2)
        turn = 1 - 2 * core
        sibling = chip * 2 + 1 - core

        def peer(delta):
            return lax.rem(chip + chips + delta, chips) * 2 + core

        def send_to(source, target, send_sem, recv_sem, device):
            return pltpu.make_async_remote_copy(
                src_ref=source,
                dst_ref=target,
                send_sem=send_sem,
                recv_sem=recv_sem,
                device_id=device,
                device_id_type=MESH,
            )

        sums = []
        for step in range(1, group):
            sums.append(
                go(send_to(final_ref, final_all.at[me], sum_send.at[step], sum_recv.at[step],
                           {"head": lax.rem(me + step, group)}))
            )
        final_all[me] = final_ref[...]
        draft_loads[0].wait()
        for copy in sums:
            copy.wait_recv()
        center = jnp.zeros((rows, 1), jnp.float32)
        square = jnp.zeros((rows, 1), jnp.float32)
        for index in range(group):
            values = final_all[index]
            center = center + jnp.sum(values, axis=1, keepdims=True)
            square = square + jnp.sum(values * values, axis=1, keepdims=True)
        center = center / width
        scale = lax.rsqrt(square / width - center * center + 1e-05)
        branches = []
        for kind in range(2):
            branch = jnp.zeros((rows, feature), jnp.float32)
            for index in range(group):
                values = ((final_all[index] - center) * scale).astype(jnp.bfloat16)
                branch = branch + jnp.dot(
                    values,
                    weight_buf[kind, index * feature : (index + 1) * feature],
                    preferred_element_type=jnp.float32,
                )
            branches.append(branch)
        odd = (lax.broadcasted_iota(jnp.int32, (rows, feature), 0) & 1) == 1
        branch = jnp.where(odd, branches[1], branches[0])
        drafted = (final_ref[...] - center) * scale + branch * lax.logistic(branch)
        mine = shards.at[me, pl.ds(pl.multiple_of(home * rows, rows), rows)]
        mine[...] = drafted.astype(shards.dtype)
        drafts = []
        for step in range(1, devices):
            drafts.append(
                go(send_to(mine, mine, draft_send.at[step], draft_recv.at[step],
                           {"req": lax.rem(home + step, devices)}))
            )
        for copy in drafts:
            copy.wait_recv()

        def shard(head):
            return shards.at[head]

        def ring(index, delta, source):
            return go(send_to(shard(source), shard(source), loop_send.at[index], loop_recv.at[index],
                              {"head": peer(delta)}))

        def hand_over(index, source):
            return go(send_to(shard(source), shard(source), hand_send.at[index], hand_recv.at[index],
                              {"head": sibling}))

        fwd = ring(0, turn, me)
        bwd = ring(1, -turn, me)
        hands = [hand_over(0, me)]
        for load in draft_loads[1:]:
            load.wait()

        def add(head, first=False):
            value = lax.dot_general(
                shards[head],
                vocab_buf[head],
                (((1,), (1,)), ((), ())),
                preferred_element_type=jnp.float32,
            )
            logits_acc[...] = value if first else logits_acc[...] + value

        add(me, True)
        fwd.wait_recv()
        opp = ring(2, turn, peer(-turn))
        hands.append(hand_over(1, peer(-turn)))
        bwd.wait_recv()
        hands.append(hand_over(2, peer(turn)))
        add(peer(-turn))
        hands[0].wait_recv()
        add(sibling)
        add(peer(turn))
        opp.wait_recv()
        hands.append(hand_over(3, peer(2)))
        hands[1].wait_recv()

        def across(delta):
            return lax.rem(chip + chips + delta, chips) * 2 + 1 - core

        add(across(turn))
        hands[2].wait_recv()
        add(across(-turn))
        add(peer(2))
        hands[3].wait_recv()
        add(across(2))
        logits_ref[...] = logits_acc[...].astype(logits_ref.dtype)

    draft_part()
    for copy in sends:
        copy.wait_send()


def layer(
    attended,
    streams,
    hc_in,
    hc_mix,
    hc_out,
    out_weight,
    gate_up,
    down_weight,
    accepted,
    draft_weight,
    lm_head,
):
    repeats = draft_weight.shape[0]
    rows = accepted.shape[0] * repeats
    devices = lax.axis_size("req")
    vocab = lm_head.shape[1]
    tokens, feature = attended.shape
    count = streams.shape[0]
    group = lax.axis_size("head")
    chips = group // 2
    width = out_weight.shape[1]
    inner = down_weight.shape[0]
    strips = inner // feature
    chunks = 3
    size = tokens // chunks
    bf16, f32 = jnp.bfloat16, jnp.float32
    dma = pltpu.SemaphoreType.DMA
    vmem = pl.BlockSpec(memory_space=pltpu.VMEM)
    smem = pl.BlockSpec(memory_space=pltpu.SMEM)
    anywhere = pl.BlockSpec(memory_space=pl.ANY)
    scratch = [
        pltpu.VMEM((rows, feature), f32),
        pltpu.VMEM((group, rows, feature), f32),
        pltpu.VMEM(draft_weight.shape, bf16),
        pltpu.VMEM((group, vocab, feature), bf16),
        pltpu.VMEM((group, devices * rows, feature), bf16),
        pltpu.VMEM((devices * rows, vocab), f32),
        dma((1 + group,)),
        dma((group,)), dma((group,)),
        dma((devices,)), dma((devices,)),
        dma((4,)), dma((4,)),
        dma((3,)), dma((3,)),
        pltpu.VMEM((group, feature, feature), bf16),
        pltpu.VMEM((2 * strips, width, feature), bf16),
        pltpu.VMEM((group, inner, feature), bf16),
        pltpu.VMEM((count, tokens, feature), f32),
        pltpu.VMEM((tokens, feature), f32),
        pltpu.VMEM((tokens, feature), f32),
        pltpu.VMEM((2, chunks, 2, chips, size, feature), bf16),
        pltpu.VMEM((2, chunks, chips, size, feature), bf16),
        pltpu.VMEM((2, chunks, size, feature), bf16),
        pltpu.VMEM((2, chunks, size, feature), bf16),
        pltpu.VMEM((2, chunks, size, feature), bf16),
        pltpu.VMEM((chunks, group, 8, size), f32),
        pltpu.VMEM((chunks, size, 8), f32),
        pltpu.VMEM((tokens, feature), bf16),
        pltpu.VMEM((tokens, width), bf16),
        pltpu.VMEM((size, inner), bf16),
        dma((3, max(group, 2 * strips))),
        dma((chunks,)),
        dma((2, chunks, 4)), dma((2, chunks, 4)),
        dma((2, chunks, 3)), dma((2, chunks, 3)),
        dma((chunks, group)), dma((chunks, group)),
        dma((chunks, 4)), dma((chunks, 4)),
        dma((chunks, 3)), dma((chunks, 3)),
    ]
    return pl.pallas_call(
        functools.partial(layer_kernel, chips, chunks),
        out_shape=(
            jax.ShapeDtypeStruct((count, tokens, feature), bf16),
            jax.ShapeDtypeStruct((devices * rows, vocab), bf16),
        ),
        in_specs=[smem] * 4 + [vmem, vmem] + [anywhere] * 5,
        out_specs=(vmem, vmem),
        scratch_shapes=scratch,
        compiler_params=pltpu.CompilerParams(
            collective_id=1, has_side_effects=True, vmem_limit_bytes=60 << 20
        ),
    )(
        hc_in,
        hc_mix,
        hc_out,
        accepted,
        attended,
        streams,
        out_weight,
        gate_up,
        down_weight,
        draft_weight,
        jnp.transpose(lm_head),
    )


def on_device(
    streams,
    hc_in,
    hc_mix,
    hc_out,
    qkv_weight,
    out_weight,
    up_gate,
    down_weight,
    draft_weight,
    lm_head,
    k_pages,
    v_pages,
    page_owner,
    page_fill,
    cache_len,
    tree_parent,
    accepted_index,
):
    tokens_local = streams.shape[0]
    req_local = cache_len.shape[0]
    tree_size = tree_parent.shape[1]
    heads_local = k_pages.shape[2]
    head_dim = k_pages.shape[3]
    draft_count = draft_weight.shape[0]
    all_requests = req_local * lax.axis_size("req")
    reach = ancestors(tree_parent)
    depth = (jnp.sum(reach.astype(jnp.float32), axis=1) - 1.0).astype(jnp.int32)
    positions = (cache_len[:, None] + depth).reshape(tokens_local)
    cosine, sine = turns(positions, head_dim)
    same_head = jnp.eye(heads_local, dtype=jnp.bfloat16)
    tree_mask = (same_head[None, :, None, :, None] * reach[:, None, :, None, :]).reshape(
        req_local, heads_local * tree_size, heads_local * tree_size
    )
    by_stream = jnp.transpose(streams, (1, 0, 2))
    width, kinds, inner = up_gate.shape
    up_rows = jnp.transpose(up_gate.reshape(width, kinds, inner // 128, 128), (0, 2, 1, 3)).reshape(
        -1, 128
    )
    attended, gate_up = cache_attention(
        by_stream,
        hc_in,
        jnp.transpose(qkv_weight, (1, 0, 2)),
        up_rows,
        cosine,
        sine,
        tree_mask,
        k_pages,
        v_pages,
        page_owner,
        page_fill,
    )
    fresh, logits_local = layer(
        attended,
        by_stream,
        hc_in,
        hc_mix,
        hc_out,
        out_weight,
        gate_up,
        down_weight,
        accepted_index,
        draft_weight,
        lm_head,
    )
    new_streams = jnp.transpose(fresh, (1, 0, 2))
    logits_local = logits_local.reshape(all_requests, draft_count, -1)
    logits = lax.all_to_all(
        logits_local, ("req", "head"), split_axis=0, concat_axis=2, tiled=True
    ).astype(jnp.float32)
    return (new_streams, logits)


def solution(mesh):
    in_specs = (
        P("req", None, "head"),
        P(),
        P(),
        P(),
        P(None, None, "head"),
        P("head", None),
        P(None, None, "head"),
        P("head", None),
        P(None, None, "head"),
        P(None, ("req", "head")),
        P("req", None, "head", None),
        P("req", None, "head", None),
        P("req"),
        P("req"),
        P("req"),
        P("req", None),
        P("req"),
    )
    out_specs = (P("req", None, "head"), P(("req", "head"), None, None))
    return jax.shard_map(
        on_device, mesh=mesh, in_specs=in_specs, out_specs=out_specs, check_vma=False
    )
```

```python
import functools
import math

import jax
import jax.numpy as jnp
from jax import lax
from jax.experimental import pallas as pl
from jax.experimental.pallas import tpu as pltpu
from jax.sharding import PartitionSpec as P

NEG_FILL = -1e30


def ancestors(parents):
    length = parents.shape[1]
    places = jnp.arange(length, dtype=jnp.int32)
    linked = (places[None, :, None] == parents[:, None, :]) | (places[:, None] == places[None, :])[
        None
    ]
    reach = linked.astype(jnp.bfloat16)
    for repeat in range(max(1, (length - 1).bit_length())):
        counts = jnp.einsum("jki,jil->jkl", reach, reach, preferred_element_type=jnp.float32)
        reach = jnp.minimum(counts, 1.0).astype(jnp.bfloat16)
    return reach


def turns(positions, head_dim):
    half = head_dim // 2
    freqs = jnp.exp(
        jnp.arange(half, dtype=jnp.float32) * (-2.0 * math.log(10000.0) / head_dim)
    )
    angles = positions.astype(jnp.float32)[:, None] * freqs[None, :]
    cosine = jnp.cos(angles)
    sine = jnp.sin(angles)
    return jnp.concatenate([cosine, cosine], axis=1), jnp.concatenate([-sine, sine], axis=1)


MESH = pl.DeviceIdType.MESH
SLOT_BITS = 6
FILL_BITS = 8


def remote(source, target, send_sem, recv_sem, req):
    return pltpu.make_async_remote_copy(
        src_ref=source,
        dst_ref=target,
        send_sem=send_sem,
        recv_sem=recv_sem,
        device_id={"req": req},
        device_id_type=MESH,
    )


def weigh(tops, totals):
    top = functools.reduce(jnp.maximum, tops)
    factors = [jnp.exp(value - top) for value in tops]
    total = functools.reduce(lambda a, b: a + b, [f * t for f, t in zip(factors, totals)])
    return top, total, factors


def cache_kernel(
    side,
    chips,
    table,
    last,
    hc_in,
    streams,
    cosine,
    sine,
    mask_ref,
    weight_hbm,
    up_hbm,
    k_hbm,
    v_hbm,
    out_ref,
    gate_ref,
    q_ref,
    key_ref,
    value_ref,
    weight_buf,
    mixed_buf,
    stat_all,
    columns,
    normed,
    gathered,
    up_in,
    up_out,
    front_sem,
    own_sem,
    front_send,
    front_recv,
    copy_send,
    copy_recv,
    pass_send,
    pass_recv,
    up_in_sem,
    up_out_sem,
    tree_acc,
    tree_stat,
    q_all,
    k_buf,
    v_buf,
    scores,
    seg_acc,
    seg_top,
    seg_den,
    parts,
    stats,
    relay,
    merged,
    single,
    relay_s,
    merged_s,
    single_s,
    outgoing_s,
    factors,
    small,
    small_s,
    hop,
    hop_s,
    gather_send,
    gather_recv,
    spread_send,
    spread_recv,
    load_sem,
    far_send,
    far_recv,
    near_send,
    near_recv,
    join_send,
    join_recv,
    stat_send,
    stat_recv,
    last_send,
    last_recv,
    last_stat_send,
    last_stat_recv,
):
    block = q_ref.shape[0] // 2
    rows = q_ref.shape[1]
    slots = k_buf.shape[0]
    half_rows = rows // 2
    me = lax.axis_index("req")
    place = (me // side, lax.rem(me, side))
    turn = 1 - 2 * lax.rem(lax.axis_index("head"), 2)

    def shifted(axis, delta):
        moved = lax.rem(place[axis] + side + delta, side)
        return moved * side + place[1] if axis == 0 else place[0] * side + moved

    def at(axis, delta):
        return lax.rem(place[axis] + side + delta, side)

    first = (0, 1)
    second = (1, 0)

    def spot(half, p2, p1):
        return pl.ds(((half * side + p2) * side + p1) * block, block)

    loads = [
        pltpu.make_async_copy(k_hbm, k_buf, load_sem.at[0]),
        pltpu.make_async_copy(v_hbm, v_buf, load_sem.at[1]),
    ]
    weight_load = pltpu.make_async_copy(weight_hbm, weight_buf, front_sem)
    weight_load.start()
    barrier = pltpu.get_barrier_semaphore()
    for axis in (0, 1):
        for delta in (1, -1):
            pl.semaphore_signal(
                barrier, inc=1, device_id={"req": shifted(axis, delta)}, device_id_type=MESH
            )
    head_index = lax.axis_index("head")
    for step in range(1, 2 * chips):
        pl.semaphore_signal(
            barrier,
            inc=1,
            device_id={"head": lax.rem(head_index + step, 2 * chips)},
            device_id_type=MESH,
        )

    def enter():
        pl.semaphore_wait(barrier, 4 + 2 * chips - 1)

    pieces = gate_ref.shape[1] // up_out.shape[2]
    span = up_out.shape[2]
    tall = up_in.shape[1]

    def up_load(c):
        return pltpu.make_async_copy(
            up_hbm.at[pl.ds(c * tall, tall)], up_in.at[c % 2], up_in_sem.at[c]
        )

    def up_store(c):
        return pltpu.make_async_copy(
            up_out.at[c % 2], gate_ref.at[:, pl.ds(c * span, span)], up_out_sem.at[c]
        )

    strips = gate_ref.shape[2] // 128
    unit = 2 * strips * 16

    def untangle(c):
        if c + 1 < pieces:
            up_load(c + 1).start()
        up_load(c).wait()
        if c >= 2:
            up_store(c - 2).wait()
        out_row = lax.broadcasted_iota(jnp.int32, (unit, unit), 0)
        in_row = lax.broadcasted_iota(jnp.int32, (unit, unit), 1)
        kind = out_row // (unit // 2)
        strip = (out_row // 16) & (strips - 1)
        pick = (out_row & 15) * (2 * strips) + strip * 2 + kind
        chosen = jnp.where(in_row == pick, 1.0, 0.0).astype(jnp.bfloat16)

        def step(index, carry):
            sorted_rows = jnp.dot(
                chosen,
                up_in[c % 2, pl.ds(index * unit, unit)],
                preferred_element_type=jnp.float32,
            ).astype(up_out.dtype)
            place = pl.ds(index * 16, 16)
            for kind in (0, 1):
                for strip in range(strips):
                    row = (kind * strips + strip) * 16
                    up_out[c % 2, kind, place, strip * 128 : (strip + 1) * 128] = sorted_rows[
                        row : row + 16
                    ]
            return carry

        lax.fori_loop(0, span // 16, step, 0)
        up_store(c).start()

    up_load(0).start()

    sends = []

    def go(copy):
        copy.start()
        sends.append(copy)
        return copy

    def pass_block(half, axis, delta, p2, p1, send, recv, own=False):
        view = q_all.at[spot(half, p2, p1)]
        source = q_ref.at[pl.ds(half * block, block)] if own else view
        return go(remote(source, view, send, recv, shifted(axis, delta)))

    lines = {}
    crosses = {}

    def line(half, index, delta, p1, own=False):
        lines[half, index] = pass_block(
            half, first[half], delta, at(second[half], 0), p1,
            gather_send.at[half, index], gather_recv.at[half, index], own,
        )

    def cross(half, piece, index, delta, p2, p1, own=False):
        crosses[half, piece, index] = pass_block(
            half, second[half], delta, p2, p1,
            spread_send.at[half, piece, index], spread_recv.at[half, piece, index], own,
        )

    chunks = 2

    def front_part():
        count, tokens, feature = streams.shape
        size = tokens // chunks
        group = 2 * chips
        width = group * feature
        head_dim = q_ref.shape[2]
        rows = q_ref.shape[1]
        heads = feature // head_dim
        tree = rows // heads
        me = lax.axis_index("head")
        chip = me // 2
        core = lax.rem(me, 2)
        turn = 1 - 2 * core
        sibling = chip * 2 + 1 - core

        def peer(delta):
            return lax.rem(chip + chips + delta, chips) * 2 + core

        def send_to(source, target, send_sem, recv_sem, head):
            return pltpu.make_async_remote_copy(
                src_ref=source,
                dst_ref=target,
                send_sem=send_sem,
                recv_sem=recv_sem,
                device_id={"head": head},
                device_id_type=MESH,
            )

        block = 32
        for t in range(chunks):

            def mix(index, carry, t=t):
                here = pl.ds(t * size + index * block, block)
                mixed = None
                for s in range(count):
                    term = hc_in[0, s] * streams[s, here].astype(jnp.float32)
                    mixed = term if mixed is None else mixed + term
                mixed_buf[here] = mixed
                return carry

            lax.fori_loop(0, size // block, mix, 0)
            mixed = mixed_buf[t * size : (t + 1) * size]
            stat_all[t, me, 0:1] = transpose_sum(mixed)
            stat_all[t, me, 1:2] = transpose_sum(mixed * mixed)
            stat_all[t, me, 2:8] = jnp.zeros((6, size), jnp.float32)
        enter()
        waits = {}

        def chunk_rows(t):
            return pl.ds(t * size, size)

        def lanes(head):
            return pl.ds(pl.multiple_of(head * feature, feature), feature)

        for t in range(chunks):
            for step in range(1, group):
                waits["stat", t, step] = go(
                    send_to(stat_all.at[t, me], stat_all.at[t, me], front_send.at[t, step],
                            front_recv.at[t, step], lax.rem(me + step, group)))

        def normalized(t):
            for step in range(1, group):
                waits["stat", t, step].wait_recv()
            total = stat_all[t, 0]
            for index in range(1, group):
                total = total + stat_all[t, index]
            center = total[0:1] / width
            scale = lax.rsqrt(total[1:2] / width - center * center + 1e-05)
            row = lax.broadcasted_iota(jnp.int32, total.shape, 0)
            packed = jnp.where(row == 0, center, jnp.where(row == 1, scale, 0.0))
            columns[t] = jnp.transpose(packed)

            def step(index, carry):
                inside = pl.ds(index * block, block)
                here = pl.ds(t * size + index * block, block)
                column = columns[t, inside]
                value = (mixed_buf[here] - column[:, 0:1]) * column[:, 1:2]
                normed[here] = value.astype(normed.dtype)
                return carry

            lax.fori_loop(0, size // block, step, 0)
            mine = normed.at[chunk_rows(t)]
            view = gathered.at[chunk_rows(t), lanes(me)]
            waits["fwd", t] = go(send_to(mine, view, pass_send.at[t, 0], pass_recv.at[t, 0], peer(turn)))
            waits["bwd", t] = go(send_to(mine, view, pass_send.at[t, 1], pass_recv.at[t, 1], peer(-turn)))
            waits["own", t] = go(send_to(mine, view, copy_send.at[t, 0], copy_recv.at[t, 0], sibling))
            local = pltpu.make_async_copy(mine, view, own_sem.at[t])
            local.start()
            waits["local", t] = local

        def hand_over(t, index, delta):
            view = gathered.at[chunk_rows(t), lanes(peer(delta))]
            waits["copy", t, index] = go(
                send_to(view, view, copy_send.at[t, index], copy_recv.at[t, index], sibling))

        def pass_on(t):
            waits["fwd", t].wait_recv()
            view = gathered.at[chunk_rows(t), lanes(peer(-turn))]
            waits["opp", t] = go(send_to(view, view, pass_send.at[t, 2], pass_recv.at[t, 2], peer(turn)))
            hand_over(t, 1, -turn)
            waits["bwd", t].wait_recv()
            hand_over(t, 2, turn)

        def pass_last(t):
            waits["opp", t].wait_recv()
            hand_over(t, 3, 2)

        def project(t):
            if t == 0:
                weight_load.wait()
            waits["own", t].wait_recv()
            waits["local", t].wait()
            for index in (1, 2, 3):
                waits["copy", t, index].wait_recv()
            here = slice(t * size, (t + 1) * size)
            for kind, target in enumerate((q_ref, key_ref, value_ref)):
                product = jnp.dot(gathered[here], weight_buf[kind], preferred_element_type=jnp.float32)
                for head in range(heads):
                    value = product[:, head * head_dim : (head + 1) * head_dim]
                    if kind < 2:
                        turned = pltpu.roll(value, head_dim // 2, 1)
                        value = value * cosine[here] + turned * sine[here]
                    if kind == 0:
                        value = value * head_dim ** (-0.5)
                    value = value.astype(target.dtype)
                    for item in range(size // tree):
                        target[t * (size // tree) + item, head * tree : (head + 1) * tree] = value[
                            item * tree : (item + 1) * tree
                        ]
            launch(t)

        phases = (normalized, pass_on, pass_last, project)
        for step in range(len(phases) + chunks - 1):
            for t in range(chunks):
                if 0 <= step - t < len(phases):
                    phases[step - t](t)

    halves = (0, 1)

    def launch(half):
        line(half, 0, turn, at(first[half], 0), True)
        line(half, 1, -turn, at(first[half], 0), True)
        cross(half, 0, 0, turn, at(second[half], 0), at(first[half], 0), True)
        cross(half, 0, 1, -turn, at(second[half], 0), at(first[half], 0), True)

    front_part()
    for load in loads:
        load.start()
    for half in halves:
        q_all[spot(half, at(second[half], 0), at(first[half], 0))] = q_ref[
            half * block : (half + 1) * block
        ]
    seg_top[...] = jnp.full(seg_top.shape, NEG_FILL, jnp.float32)
    seg_den[...] = jnp.zeros(seg_den.shape, jnp.float32)
    seg_acc[slots] = jnp.zeros(seg_acc.shape[1:], seg_acc.dtype)
    tree_stat[...] = jnp.zeros(tree_stat.shape, jnp.float32)

    def tree_step(item, carry):
        found = lax.dot_general(
            key_ref[item],
            q_ref[item],
            (((1,), (1,)), ((), ())),
            preferred_element_type=jnp.float32,
        )
        found = jnp.where(mask_ref[item].astype(jnp.float32) > 0.0, found, NEG_FILL)
        top = jnp.max(found, axis=0, keepdims=True)
        weight = jnp.exp(found - top)
        tree_acc[item] = lax.dot_general(
            weight.astype(jnp.bfloat16),
            value_ref[item],
            (((0,), (0,)), ((), ())),
            preferred_element_type=jnp.float32,
        )
        tree_stat[0, item, :, 0:rows] = top
        tree_stat[1, item, :, 0:rows] = jnp.sum(weight, axis=0, keepdims=True)
        return carry

    lax.fori_loop(0, 2 * block, tree_step, 0)
    for half in halves:
        lines[half, 0].wait_recv()
        line(half, 2, turn, at(first[half], -turn))
        cross(half, 1, 0, turn, at(second[half], 0), at(first[half], -turn))
        cross(half, 1, 1, -turn, at(second[half], 0), at(first[half], -turn))
    untangle(0)
    untangle(1)
    for half in halves:
        lines[half, 1].wait_recv()
        cross(half, 2, 0, turn, at(second[half], 0), at(first[half], turn))
        cross(half, 2, 1, -turn, at(second[half], 0), at(first[half], turn))
    untangle(2)
    for half in halves:
        crosses[half, 0, 0].wait_recv()
        cross(half, 0, 2, turn, at(second[half], -turn), at(first[half], 0))
    untangle(3)
    for half in halves:
        lines[half, 2].wait_recv()
        cross(half, 3, 0, turn, at(second[half], 0), at(first[half], 2))
        cross(half, 3, 1, -turn, at(second[half], 0), at(first[half], 2))
    for piece, delta in ((1, -turn), (2, turn), (3, 2)):
        untangle(3 + piece)
        for half in halves:
            crosses[half, piece, 0].wait_recv()
            cross(half, piece, 2, turn, at(second[half], -turn), at(first[half], delta))
    untangle(7)
    for piece in range(4):
        for half in halves:
            crosses[half, piece, 1].wait_recv()
            crosses[half, piece, 2].wait_recv()
    for load in loads:
        load.wait()

    slot_mask = (1 << SLOT_BITS) - 1
    fill_mask = (1 << FILL_BITS) - 1
    requests = 2 * block * side * side

    def owner_at(index):
        return table[index] >> (SLOT_BITS + FILL_BITS)

    def starts_new(index):
        before = owner_at(jnp.maximum(index - 1, 0))
        return jnp.logical_or(index == 0, before != owner_at(index))

    shape = (k_buf.shape[1], rows)
    row_ids = lax.broadcasted_iota(jnp.int32, shape, 0)
    col_head = (lax.broadcasted_iota(jnp.int32, shape, 1) >= half_rows).astype(jnp.int32)
    matched = (row_ids & 1) == col_head
    key_ids = row_ids >> 1
    unroll = 4

    def score_step(group, carry):
        for offset in range(unroll):
            index = group * unroll + offset
            entry = table[index]
            fill = (entry >> SLOT_BITS) & fill_mask
            owner = jnp.minimum(entry >> (SLOT_BITS + FILL_BITS), requests - 1)
            home = owner // (2 * block)
            within = lax.rem(owner, 2 * block)
            half = within // block
            hx = home // side
            hy = lax.rem(home, side)
            outer = jnp.where(half == 0, hy, hx)
            inner = jnp.where(half == 0, hx, hy)
            row = ((half * side + outer) * side + inner) * block + lax.rem(within, block)
            found = lax.dot_general(
                k_buf[entry & slot_mask],
                q_all[row],
                (((1,), (1,)), ((), ())),
                preferred_element_type=jnp.float32,
            )
            found = jnp.where(jnp.logical_and(matched, key_ids < fill), found, NEG_FILL)
            scores[index] = found
            seg_top[index, :, 0:rows] = jnp.max(found, axis=0, keepdims=True)
        return carry

    lax.fori_loop(0, slots // unroll, score_step, 0)

    def forward(index, run):
        here = seg_top[index]
        run = jnp.where(starts_new(index), here, jnp.maximum(run, here))
        seg_top[index] = run
        return run

    lax.fori_loop(0, slots, forward, jnp.full(seg_top.shape[1:], NEG_FILL, jnp.float32))

    def backward(step, run):
        index = slots - 1 - step
        follow = jnp.minimum(index + 1, slots - 1)
        ends = jnp.logical_or(step == 0, owner_at(follow) != owner_at(index))
        run = jnp.where(ends, seg_top[index], run)
        seg_top[index] = run
        return run

    lax.fori_loop(0, slots, backward, jnp.full(seg_top.shape[1:], NEG_FILL, jnp.float32))

    def value_step(group, carry):
        acc_run, den_run = carry
        for offset in range(unroll):
            index = group * unroll + offset
            fresh = starts_new(index)
            top = seg_top[index][:, 0:rows]
            top = jnp.where(top < 0.5 * NEG_FILL, 0.0, top)
            weight = jnp.exp(scores[index] - top)
            den = jnp.sum(weight, axis=0, keepdims=True)
            acc = lax.dot_general(
                weight.astype(jnp.bfloat16),
                v_buf[table[index] & slot_mask],
                (((0,), (0,)), ((), ())),
                preferred_element_type=jnp.float32,
            )
            acc_run = acc + jnp.where(fresh, 0.0, acc_run)
            den_run = den + jnp.where(fresh, 0.0, den_run)
            seg_acc[index] = acc_run.astype(seg_acc.dtype)
            seg_den[index, :, 0:rows] = den_run
        return acc_run, den_run

    lax.fori_loop(
        0,
        slots // unroll,
        value_step,
        (jnp.zeros(seg_acc.shape[1:], jnp.float32), jnp.zeros((1, rows), jnp.float32)),
    )

    def place_step(group, carry):
        for piece in range(side):
            tops, dens = [], []
            for offset in range(block):
                spot_index = (group * side + piece) * block + offset
                found = last[spot_index]
                parts[spot_index] = seg_acc[found]
                tops.append(seg_top[found])
                dens.append(seg_den[found])
            stats[group, 0, piece * block : (piece + 1) * block] = jnp.concatenate(tops, axis=0)
            stats[group, 1, piece * block : (piece + 1) * block] = jnp.concatenate(dens, axis=0)
        return carry

    for half in halves:
        for delta in (2, -turn):
            place_step(half * side + at(second[half], delta), 0)

    def part(half, p2, p1):
        return parts.at[spot(half, p2, p1)]

    def stat(half, p2):
        return stats.at[half * side + p2]

    def combine(put, terms, weights):
        columns = [jnp.transpose(weight) for weight in weights]
        for item in range(block):
            total = None
            for term, column in zip(terms, columns):
                value = term[item].astype(jnp.float32) * column[0:rows, item : item + 1]
                total = value if total is None else total + value
            put(item, total)

    def offset(order):
        if isinstance(order, int):
            swapped = order + order // 2 - 2 * (order // 3)
        else:
            swapped = order + lax.div(order, 2) - 2 * lax.div(order, 3)
        return 2 + side - turn * swapped

    stat_copies = {}
    far, near = {}, {}
    for half in halves:
        up, down = shifted(second[half], turn), shifted(second[half], -turn)
        stat_copies[half, 0] = go(
            remote(stat(half, at(second[half], 2)), relay_s.at[half],
                   stat_send.at[half, 0], stat_recv.at[half, 0], up))
        stat_copies[half, 1] = go(
            remote(stat(half, at(second[half], -turn)), single_s.at[half],
                   stat_send.at[half, 1], stat_recv.at[half, 1], down))
    for order in range(4):
        for half in halves:
            up, down = shifted(second[half], turn), shifted(second[half], -turn)
            p1 = at(first[half], offset(order))
            far[half, order] = go(
                remote(part(half, at(second[half], 2), p1), relay.at[half, p1],
                       far_send.at[half, order], far_recv.at[half, order], up))
            near[half, order] = go(
                remote(part(half, at(second[half], -turn), p1), single.at[half, p1],
                       near_send.at[half, order], near_recv.at[half, order], down))

    for half in halves:
        for delta in (turn, 0):
            place_step(half * side + at(second[half], delta), 0)

    for half in halves:
        stat_copies[half, 0].wait_recv()
        mine = stat(half, at(second[half], turn))
        top, den, weights = weigh([mine[0], relay_s[half, 0]], [mine[1], relay_s[half, 1]])
        outgoing_s[half, 0] = top
        outgoing_s[half, 1] = den
        factors[half, 0] = weights[0]
        factors[half, 1] = weights[1]
        stat_copies[half, 2] = go(
            remote(outgoing_s.at[half], merged_s.at[half],
                   stat_send.at[half, 2], stat_recv.at[half, 2], shifted(second[half], turn)))

    def join_copy(half, order):
        p1 = at(first[half], offset(order))
        return remote(relay.at[half, p1], merged.at[half, p1],
                      join_send.at[half, order], join_recv.at[half, order],
                      shifted(second[half], turn))

    def far_copy(half, order):
        p1 = at(first[half], offset(order))
        return remote(part(half, at(second[half], 2), p1), relay.at[half, p1],
                      far_send.at[half, order], far_recv.at[half, order],
                      shifted(second[half], turn))

    def near_copy(half, order):
        p1 = at(first[half], offset(order))
        return remote(part(half, at(second[half], -turn), p1), single.at[half, p1],
                      near_send.at[half, order], near_recv.at[half, order],
                      shifted(second[half], -turn))

    def relay_step(order, carry):
        for half in halves:
            p1 = at(first[half], offset(order))
            far_copy(half, order).wait_recv()
            lanes = pl.ds(p1 * block, block)
            target = relay.at[half, p1]

            def put(item, value):
                target[item] = value.astype(target.dtype)

            combine(
                put,
                [part(half, at(second[half], turn), p1), target],
                [factors[half, 0, lanes], factors[half, 1, lanes]],
            )
            join_copy(half, order).start()
        return carry

    lax.fori_loop(0, 4, relay_step, 0)

    for half in halves:
        stat_copies[half, 1].wait_recv()
        stat_copies[half, 2].wait_recv()
        mine = stat(half, at(second[half], 0))
        top, den, weights = weigh(
            [mine[0], merged_s[half, 0], single_s[half, 0]],
            [mine[1], merged_s[half, 1], single_s[half, 1]],
        )
        for index in range(3):
            factors[half, index] = weights[index]
        for p1 in range(side):
            small_s[half, p1, 0] = top[p1 * block : (p1 + 1) * block]
            small_s[half, p1, 1] = den[p1 * block : (p1 + 1) * block]

    def gather_piece(half, order):
        p1 = at(first[half], offset(order))
        near_copy(half, order).wait_recv()
        join_copy(half, order).wait_recv()
        lanes = pl.ds(p1 * block, block)
        target = small.at[half, p1]

        def put(item, value):
            target[item] = value.astype(target.dtype)

        combine(
            put,
            [part(half, at(second[half], 0), p1), merged.at[half, p1], single.at[half, p1]],
            [factors[half, index, lanes] for index in range(3)],
        )

    def piece_step(order, carry):
        for half in halves:
            gather_piece(half, order)
        return carry

    tails = {}

    def tail(half, index, source, source_s, delta):
        peer = shifted(first[half], delta)
        tails[half, index] = (
            go(remote(source_s, hop_s.at[half, index],
                      last_stat_send.at[half, index], last_stat_recv.at[half, index], peer)),
            go(remote(source, hop.at[half, index],
                      last_send.at[half, index], last_recv.at[half, index], peer)),
        )

    lax.fori_loop(0, 1, piece_step, 0)
    for half in halves:
        p1 = at(first[half], 2)
        tail(half, 0, small.at[half, p1], small_s.at[half, p1], turn)
    lax.fori_loop(1, 3, piece_step, 0)
    for half in halves:
        p1 = at(first[half], -turn)
        tail(half, 1, small.at[half, p1], small_s.at[half, p1], -turn)
    for half in halves:
        p1 = at(first[half], turn)
        for copy in tails[half, 0]:
            copy.wait_recv()
        target = small.at[half, p1]
        top, den, weights = weigh(
            [small_s[half, p1, 0], hop_s[half, 0, 0]], [small_s[half, p1, 1], hop_s[half, 0, 1]]
        )
        small_s[half, p1, 0] = top
        small_s[half, p1, 1] = den

        def put(item, value, target=target):
            target[item] = value.astype(target.dtype)

        combine(put, [target, hop.at[half, 0]], weights)
        tail(half, 2, target, small_s.at[half, p1], turn)
    lax.fori_loop(3, 4, piece_step, 0)
    for half in halves:
        p1 = at(first[half], 0)
        for index in (1, 2):
            for copy in tails[half, index]:
                copy.wait_recv()
        tree = [
            jnp.concatenate(
                [tree_stat[kind, half * block + item] for item in range(block)], axis=0
            )
            for kind in (0, 1)
        ]
        top, den, weights = weigh(
            [small_s[half, p1, 0], hop_s[half, 1, 0], hop_s[half, 2, 0], tree[0]],
            [small_s[half, p1, 1], hop_s[half, 1, 1], hop_s[half, 2, 1], tree[1]],
        )
        lane = lax.broadcasted_iota(jnp.int32, den.shape, 1)
        inverse = 1.0 / jnp.where(lane < rows, den, 1.0)

        def put(item, value, half=half):
            start = (half * block + item) * half_rows
            value = value.astype(out_ref.dtype)
            width = value.shape[1]
            for head in (0, 1):
                out_ref[start : start + half_rows, head * width : (head + 1) * width] = value[
                    head * half_rows : (head + 1) * half_rows
                ]

        combine(
            put,
            [
                small.at[half, p1],
                hop.at[half, 1],
                hop.at[half, 2],
                tree_acc.at[pl.ds(half * block, block)],
            ],
            [weight * inverse for weight in weights],
        )
    for copy in sends:
        copy.wait_send()
    for half in halves:
        for order in range(4):
            join_copy(half, order).wait_send()
    for c in (pieces - 2, pieces - 1):
        up_store(c).wait()


def cache_attention(
    streams, hc_in, qkv, up_rows, cosine, sine, tree_mask, k_pages, v_pages, page_owner, page_fill
):
    req_local, rows = tree_mask.shape[0:2]
    head_dim = k_pages.shape[3]
    tokens, feature = streams.shape[1:3]
    group = lax.axis_size("head")
    width = qkv.shape[1]
    hidden_units = up_rows.shape[0] * 128 // (2 * width)
    pieces = 8
    half_tokens = tokens // 2
    slots, keys = k_pages.shape[0], k_pages.shape[1] * k_pages.shape[2]
    devices = lax.axis_size("req")
    side = math.isqrt(devices)
    block = req_local // 2
    requests = req_local * devices
    owner_key = jnp.where(page_owner < 0, requests, page_owner)
    packed = (
        (owner_key << (SLOT_BITS + FILL_BITS))
        | (jnp.where(page_owner < 0, 0, page_fill) << SLOT_BITS)
        | jnp.arange(slots, dtype=jnp.int32)
    )
    rank = jnp.sum((packed[None, :] < packed[:, None]).astype(jnp.int32), axis=1)
    places = jnp.arange(slots, dtype=jnp.int32)
    table = jnp.sum(jnp.where(rank[None, :] == places[:, None], packed[None, :], 0), axis=1)
    spots = jnp.arange(requests, dtype=jnp.int32)
    half = spots // (requests // 2)
    outer = (spots // (block * side)) % side
    inner = (spots // block) % side
    home = jnp.where(half == 0, inner * side + outer, outer * side + inner)
    request = home * req_local + half * block + spots % block
    below = jnp.sum((owner_key[None, :] <= request[:, None]).astype(jnp.int32), axis=1)
    exact = jnp.sum((owner_key[None, :] == request[:, None]).astype(jnp.int32), axis=1)
    last = jnp.where(exact > 0, below - 1, slots)
    bf16, f32 = jnp.bfloat16, jnp.float32
    unit = (2, side, block, rows, head_dim)
    dma = pltpu.SemaphoreType.DMA
    scratch = [
        pltpu.VMEM((req_local, rows, head_dim), bf16),
        pltpu.VMEM((req_local, rows, head_dim), bf16),
        pltpu.VMEM((req_local, rows, head_dim), bf16),
        pltpu.VMEM(qkv.shape, bf16),
        pltpu.VMEM((tokens, feature), f32),
        pltpu.VMEM((2, group, 8, half_tokens), f32),
        pltpu.VMEM((2, half_tokens, 8), f32),
        pltpu.VMEM((tokens, feature), bf16),
        pltpu.VMEM((tokens, width), bf16),
        pltpu.VMEM((2, up_rows.shape[0] // pieces, 128), bf16),
        pltpu.VMEM((2, 2, width // pieces, hidden_units), bf16),
        dma,
        dma((2,)),
        dma((2, group)), dma((2, group)),
        dma((2, 4)), dma((2, 4)),
        dma((2, 3)), dma((2, 3)),
        dma((pieces,)), dma((pieces,)),
        pltpu.VMEM((req_local, rows, head_dim), f32),
        pltpu.VMEM((2, req_local, 1, 128), f32),
        pltpu.VMEM((requests, rows, head_dim), bf16),
        pltpu.VMEM((slots, keys, head_dim), bf16),
        pltpu.VMEM((slots, keys, head_dim), bf16),
        pltpu.VMEM((slots, keys, rows), f32),
        pltpu.VMEM((slots + 1, rows, head_dim), bf16),
        pltpu.VMEM((slots + 1, 1, 128), f32),
        pltpu.VMEM((slots + 1, 1, 128), f32),
        pltpu.VMEM((requests, rows, head_dim), bf16),
        pltpu.VMEM((2 * side, 2, side * block, 128), f32),
        pltpu.VMEM(unit, bf16),
        pltpu.VMEM(unit, bf16),
        pltpu.VMEM(unit, bf16),
        pltpu.VMEM((2, 2, side * block, 128), f32),
        pltpu.VMEM((2, 2, side * block, 128), f32),
        pltpu.VMEM((2, 2, side * block, 128), f32),
        pltpu.VMEM((2, 2, side * block, 128), f32),
        pltpu.VMEM((2, 3, side * block, 128), f32),
        pltpu.VMEM(unit, bf16),
        pltpu.VMEM((2, side, 2, block, 128), f32),
        pltpu.VMEM((2, 3, block, rows, head_dim), bf16),
        pltpu.VMEM((2, 3, 2, block, 128), f32),
        dma((2, 3)), dma((2, 3)),
        dma((2, 4, 3)), dma((2, 4, 3)),
        dma((2,)),
        dma((2, 4)), dma((2, 4)),
        dma((2, 4)), dma((2, 4)),
        dma((2, 4)), dma((2, 4)),
        dma((2, 3)), dma((2, 3)),
        dma((2, 3)), dma((2, 3)),
        dma((2, 3)), dma((2, 3)),
    ]
    vmem = pl.BlockSpec(memory_space=pltpu.VMEM)
    smem = pl.BlockSpec(memory_space=pltpu.SMEM)
    anywhere = pl.BlockSpec(memory_space=pl.ANY)
    return pl.pallas_call(
        functools.partial(cache_kernel, side, group // 2),
        out_shape=(
            jax.ShapeDtypeStruct((req_local * rows // 2, 2 * head_dim), bf16),
            jax.ShapeDtypeStruct((2, width, hidden_units), bf16),
        ),
        in_specs=[smem] * 3 + [vmem] * 4 + [anywhere] * 4,
        out_specs=(vmem, anywhere),
        scratch_shapes=scratch,
        compiler_params=pltpu.CompilerParams(
            collective_id=0, has_side_effects=True, vmem_limit_bytes=56 << 20
        ),
    )(
        table,
        last,
        hc_in,
        streams,
        cosine,
        sine,
        tree_mask,
        qkv,
        up_rows,
        k_pages.reshape(slots, keys, head_dim),
        v_pages.reshape(slots, keys, head_dim),
    )


def transpose_sum(values):
    half = values.shape[1] // 2
    return jnp.sum(jnp.transpose(values[:, 0:half] + values[:, half:]), axis=0, keepdims=True)


def layer_kernel(
    chips,
    chunks,
    hc_in,
    hc_mix,
    hc_out,
    accepted,
    attended,
    streams,
    out_hbm,
    gate_hbm,
    down_hbm,
    weight_hbm,
    vocab_hbm,
    fresh_ref,
    logits_ref,
    final_ref,
    final_all,
    weight_buf,
    vocab_buf,
    shards,
    logits_acc,
    draft_sem,
    sum_send,
    sum_recv,
    draft_send,
    draft_recv,
    hand_send,
    hand_recv,
    loop_send,
    loop_recv,
    out_buf,
    gate_buf,
    down_buf,
    first_buf,
    mixed_buf,
    total_buf,
    share,
    twin,
    relay,
    joined,
    single,
    stat_all,
    columns,
    normed,
    gathered,
    hidden,
    load_sem,
    own_sem,
    twin_send,
    twin_recv,
    ring_send,
    ring_recv,
    stat_send,
    stat_recv,
    copy_send,
    copy_recv,
    pass_send,
    pass_recv,
):
    tokens, feature = attended.shape
    size = tokens // chunks
    group = 2 * chips
    width = group * feature
    count = streams.shape[0]
    inner = hidden.shape[1]
    strips = inner // feature
    me = lax.axis_index("head")
    chip = me // 2
    core = lax.rem(me, 2)
    turn = 1 - 2 * core

    def at(delta):
        return lax.rem(chip + chips + delta, chips)

    def peer(delta):
        return at(delta) * 2 + core

    sibling = chip * 2 + 1 - core

    def send_to(source, target, send_sem, recv_sem, head):
        return pltpu.make_async_remote_copy(
            src_ref=source,
            dst_ref=target,
            send_sem=send_sem,
            recv_sem=recv_sem,
            device_id={"head": head},
            device_id_type=MESH,
        )

    loads = []
    for index in range(group):
        loads.append(
            pltpu.make_async_copy(
                out_hbm.at[:, pl.ds(index * feature, feature)], out_buf.at[index], load_sem.at[0, index]
            )
        )
    for index in range(2 * strips):
        kind, strip = index // strips, index % strips
        loads.append(
            pltpu.make_async_copy(
                gate_hbm.at[kind, :, pl.ds(strip * feature, feature)],
                gate_buf.at[index],
                load_sem.at[1, index],
            )
        )
    for index in range(group):
        loads.append(
            pltpu.make_async_copy(
                down_hbm.at[:, pl.ds(index * feature, feature)], down_buf.at[index], load_sem.at[2, index]
            )
        )
    draft_loads = [pltpu.make_async_copy(weight_hbm, weight_buf, draft_sem.at[0])]
    for index in range(group):
        draft_loads.append(
            pltpu.make_async_copy(
                vocab_hbm.at[:, pl.ds(index * feature, feature)],
                vocab_buf.at[index],
                draft_sem.at[1 + index],
            )
        )
    for load in loads + draft_loads:
        load.start()
    barrier = pltpu.get_barrier_semaphore()
    home_index = lax.axis_index("req")
    peers = shards.shape[1] // final_ref.shape[0]
    for step in range(1, group):
        pl.semaphore_signal(
            barrier, inc=1, device_id={"head": lax.rem(me + step, group)}, device_id_type=MESH
        )
    for step in range(1, peers):
        pl.semaphore_signal(
            barrier, inc=1, device_id={"req": lax.rem(home_index + step, peers)}, device_id_type=MESH
        )
    pl.semaphore_wait(barrier, group + peers - 2)

    sends = []

    def go(copy):
        copy.start()
        sends.append(copy)
        return copy

    offsets = (2, 1, 3, 0)
    waits = {}

    def chunk_rows(t):
        return pl.ds(t * size, size)

    def lanes(head):
        return pl.ds(pl.multiple_of(head * feature, feature), feature)

    def scatter(which, t, product):
        for k, offset in enumerate(offsets):
            target = at(offset)
            piece = share.at[which, t, 1 - core, target]
            piece[...] = product(target * 2 + 1 - core).astype(piece.dtype)
            waits["twin", which, t, k] = go(
                send_to(piece, twin.at[which, t, target], twin_send.at[which, t, k],
                        twin_recv.at[which, t, k], sibling))
        for offset in offsets:
            target = at(offset)
            piece = share.at[which, t, core, target]
            piece[...] = product(target * 2 + core).astype(piece.dtype)

    def widen(ref):
        return ref[...].astype(jnp.float32)

    def chip_sum(which, t):
        def fold(k):
            waits["twin", which, t, k].wait_recv()
            target = at(offsets[k])
            piece = share.at[which, t, core, target]
            piece[...] = (widen(piece) + widen(twin.at[which, t, target])).astype(piece.dtype)

        fold(0)
        waits["far", which, t] = go(
            send_to(share.at[which, t, core, at(2)], relay.at[which, t],
                    ring_send.at[which, t, 0], ring_recv.at[which, t, 0], peer(turn)))
        fold(1)
        fold(2)
        waits["near", which, t] = go(
            send_to(share.at[which, t, core, at(-turn)], single.at[which, t],
                    ring_send.at[which, t, 1], ring_recv.at[which, t, 1], peer(-turn)))
        fold(3)

    def chip_relay(which, t):
        waits["far", which, t].wait_recv()
        piece = relay.at[which, t]
        piece[...] = (widen(piece) + widen(share.at[which, t, core, at(turn)])).astype(piece.dtype)
        waits["join", which, t] = go(
            send_to(piece, joined.at[which, t],
                    ring_send.at[which, t, 2], ring_recv.at[which, t, 2], peer(turn)))

    def finish(which, t):
        waits["near", which, t].wait_recv()
        waits["join", which, t].wait_recv()

    block = 32

    def delta_of(which, t, rows):
        return (
            share[which, t, core, at(0), rows].astype(jnp.float32)
            + joined[which, t, rows].astype(jnp.float32)
            + single[which, t, rows].astype(jnp.float32)
        )

    def remixed(layer, values, delta):
        result = []
        for target in range(count):
            total = hc_out[layer, target] * delta
            for source in range(count):
                weight = hc_mix[layer, source, target]
                if source == target:
                    weight = weight + 1.0
                total = total + weight * values[source]
            result.append(total)
        return result

    def project(t):
        if t == 0:
            for load in loads[:group]:
                load.wait()
        values = attended[t * size : (t + 1) * size]
        scatter(0, t, lambda head: jnp.dot(
            values, out_buf[head], preferred_element_type=jnp.float32))

    def middle(t):
        finish(0, t)

        def step(index, carry):
            inside = pl.ds(index * block, block)
            rows = pl.ds(t * size + index * block, block)
            values = [streams[s, rows].astype(jnp.float32) for s in range(count)]
            result = remixed(0, values, delta_of(0, t, inside))
            mixed = None
            for s in range(count):
                first_buf[s, rows] = result[s]
                term = hc_in[1, s] * result[s]
                mixed = term if mixed is None else mixed + term
            mixed_buf[rows] = mixed
            return carry

        lax.fori_loop(0, size // block, step, 0)
        mixed = mixed_buf[t * size : (t + 1) * size]
        stat_all[t, me, 0:1] = transpose_sum(mixed)
        stat_all[t, me, 1:2] = transpose_sum(mixed * mixed)
        stat_all[t, me, 2:8] = jnp.zeros((6, size), jnp.float32)
        for step in range(1, group):
            waits["stat", t, step] = go(
                send_to(stat_all.at[t, me], stat_all.at[t, me], stat_send.at[t, step],
                        stat_recv.at[t, step], lax.rem(me + step, group)))

    def normalized(t):
        for step in range(1, group):
            waits["stat", t, step].wait_recv()
        total = stat_all[t, 0]
        for index in range(1, group):
            total = total + stat_all[t, index]
        center = total[0:1] / width
        scale = lax.rsqrt(total[1:2] / width - center * center + 1e-05)
        row = lax.broadcasted_iota(jnp.int32, total.shape, 0)
        packed = jnp.where(row == 0, center, jnp.where(row == 1, scale, 0.0))
        columns[t] = jnp.transpose(packed)

        def step(index, carry):
            inside = pl.ds(index * block, block)
            rows = pl.ds(t * size + index * block, block)
            column = columns[t, inside]
            value = (mixed_buf[rows] - column[:, 0:1]) * column[:, 1:2]
            normed[rows] = value.astype(normed.dtype)
            return carry

        lax.fori_loop(0, size // block, step, 0)
        mine = normed.at[chunk_rows(t)]
        view = gathered.at[chunk_rows(t), lanes(me)]
        waits["fwd", t] = go(send_to(mine, view, pass_send.at[t, 0], pass_recv.at[t, 0], peer(turn)))
        waits["bwd", t] = go(send_to(mine, view, pass_send.at[t, 1], pass_recv.at[t, 1], peer(-turn)))
        waits["own", t] = go(send_to(mine, view, copy_send.at[t, 0], copy_recv.at[t, 0], sibling))
        local = pltpu.make_async_copy(mine, view, own_sem.at[t])
        local.start()
        waits["local", t] = local

    def hand_over(t, index, delta):
        view = gathered.at[chunk_rows(t), lanes(peer(delta))]
        waits["copy", t, index] = go(
            send_to(view, view, copy_send.at[t, index], copy_recv.at[t, index], sibling))

    def pass_on(t):
        waits["fwd", t].wait_recv()
        view = gathered.at[chunk_rows(t), lanes(peer(-turn))]
        waits["opp", t] = go(send_to(view, view, pass_send.at[t, 2], pass_recv.at[t, 2], peer(turn)))
        hand_over(t, 1, -turn)
        waits["bwd", t].wait_recv()
        hand_over(t, 2, turn)

    def pass_last(t):
        waits["opp", t].wait_recv()
        hand_over(t, 3, 2)

    def feed_forward(t):
        if t == 0:
            for load in loads[group:]:
                load.wait()
        waits["own", t].wait_recv()
        waits["local", t].wait()
        for index in (1, 2, 3):
            waits["copy", t, index].wait_recv()
        values = gathered.at[chunk_rows(t)]
        for strip in range(strips):
            gate = jnp.dot(values[...], gate_buf[strip], preferred_element_type=jnp.float32)
            up = jnp.dot(values[...], gate_buf[strips + strip], preferred_element_type=jnp.float32)
            hidden[:, strip * feature : (strip + 1) * feature] = (
                gate * lax.logistic(gate) * up
            ).astype(hidden.dtype)
        scatter(1, t, lambda head: jnp.dot(
            hidden[...], down_buf[head], preferred_element_type=jnp.float32))

    def last(t):
        finish(1, t)

        def step(index, carry):
            inside = pl.ds(index * block, block)
            rows = pl.ds(t * size + index * block, block)
            values = [first_buf[s, rows] for s in range(count)]
            result = remixed(1, values, delta_of(1, t, inside))
            total = result[0]
            for s in range(count):
                fresh_ref[s, rows] = result[s].astype(fresh_ref.dtype)
                if s > 0:
                    total = total + result[s]
            total_buf[rows] = total
            return carry

        lax.fori_loop(0, size // block, step, 0)

    phases = (
        project,
        lambda t: chip_sum(0, t),
        lambda t: chip_relay(0, t),
        middle,
        normalized,
        pass_on,
        pass_last,
        feed_forward,
        lambda t: chip_sum(1, t),
        lambda t: chip_relay(1, t),
        last,
    )
    for step in range(len(phases) + chunks - 1):
        for t in range(chunks):
            if 0 <= step - t < len(phases):
                phases[step - t](t)
    requests = accepted.shape[0]
    repeats = final_ref.shape[0] // requests
    tree = tokens // requests
    for item in range(requests):
        row = total_buf[pl.ds(item * tree + accepted[item], 1)]
        for copy_index in range(repeats):
            place = item * repeats + copy_index
            final_ref[place : place + 1] = row

    def draft_part():
        rows, feature = final_ref.shape
        group = 2 * chips
        width = group * feature
        devices = shards.shape[1] // rows
        me = lax.axis_index("head")
        home = lax.axis_index("req")
        chip = me // 2
        core = lax.rem(me, 2)
        turn = 1 - 2 * core
        sibling = chip * 2 + 1 - core

        def peer(delta):
            return lax.rem(chip + chips + delta, chips) * 2 + core

        def send_to(source, target, send_sem, recv_sem, device):
            return pltpu.make_async_remote_copy(
                src_ref=source,
                dst_ref=target,
                send_sem=send_sem,
                recv_sem=recv_sem,
                device_id=device,
                device_id_type=MESH,
            )

        sums = []
        for step in range(1, group):
            sums.append(
                go(send_to(final_ref, final_all.at[me], sum_send.at[step], sum_recv.at[step],
                           {"head": lax.rem(me + step, group)}))
            )
        final_all[me] = final_ref[...]
        draft_loads[0].wait()
        for copy in sums:
            copy.wait_recv()
        center = jnp.zeros((rows, 1), jnp.float32)
        square = jnp.zeros((rows, 1), jnp.float32)
        for index in range(group):
            values = final_all[index]
            center = center + jnp.sum(values, axis=1, keepdims=True)
            square = square + jnp.sum(values * values, axis=1, keepdims=True)
        center = center / width
        scale = lax.rsqrt(square / width - center * center + 1e-05)
        branches = []
        for kind in range(2):
            branch = jnp.zeros((rows, feature), jnp.float32)
            for index in range(group):
                values = ((final_all[index] - center) * scale).astype(jnp.bfloat16)
                branch = branch + jnp.dot(
                    values,
                    weight_buf[kind, index * feature : (index + 1) * feature],
                    preferred_element_type=jnp.float32,
                )
            branches.append(branch)
        odd = (lax.broadcasted_iota(jnp.int32, (rows, feature), 0) & 1) == 1
        branch = jnp.where(odd, branches[1], branches[0])
        drafted = (final_ref[...] - center) * scale + branch * lax.logistic(branch)
        mine = shards.at[me, pl.ds(pl.multiple_of(home * rows, rows), rows)]
        mine[...] = drafted.astype(shards.dtype)
        drafts = []
        for step in range(1, devices):
            drafts.append(
                go(send_to(mine, mine, draft_send.at[step], draft_recv.at[step],
                           {"req": lax.rem(home + step, devices)}))
            )
        for copy in drafts:
            copy.wait_recv()

        def shard(head):
            return shards.at[head]

        def ring(index, delta, source):
            return go(send_to(shard(source), shard(source), loop_send.at[index], loop_recv.at[index],
                              {"head": peer(delta)}))

        def hand_over(index, source):
            return go(send_to(shard(source), shard(source), hand_send.at[index], hand_recv.at[index],
                              {"head": sibling}))

        fwd = ring(0, turn, me)
        bwd = ring(1, -turn, me)
        hands = [hand_over(0, me)]
        for load in draft_loads[1:]:
            load.wait()

        def add(head, first=False):
            value = lax.dot_general(
                shards[head],
                vocab_buf[head],
                (((1,), (1,)), ((), ())),
                preferred_element_type=jnp.float32,
            )
            logits_acc[...] = value if first else logits_acc[...] + value

        add(me, True)
        fwd.wait_recv()
        opp = ring(2, turn, peer(-turn))
        hands.append(hand_over(1, peer(-turn)))
        bwd.wait_recv()
        hands.append(hand_over(2, peer(turn)))
        add(peer(-turn))
        hands[0].wait_recv()
        add(sibling)
        add(peer(turn))
        opp.wait_recv()
        hands.append(hand_over(3, peer(2)))
        hands[1].wait_recv()

        def across(delta):
            return lax.rem(chip + chips + delta, chips) * 2 + 1 - core

        add(across(turn))
        hands[2].wait_recv()
        add(across(-turn))
        add(peer(2))
        hands[3].wait_recv()
        add(across(2))
        logits_ref[...] = logits_acc[...].astype(logits_ref.dtype)

    draft_part()
    for copy in sends:
        copy.wait_send()


def layer(
    attended,
    streams,
    hc_in,
    hc_mix,
    hc_out,
    out_weight,
    gate_up,
    down_weight,
    accepted,
    draft_weight,
    lm_head,
):
    repeats = draft_weight.shape[0]
    rows = accepted.shape[0] * repeats
    devices = lax.axis_size("req")
    vocab = lm_head.shape[1]
    tokens, feature = attended.shape
    count = streams.shape[0]
    group = lax.axis_size("head")
    chips = group // 2
    width = out_weight.shape[1]
    inner = down_weight.shape[0]
    strips = inner // feature
    chunks = 3
    size = tokens // chunks
    bf16, f32 = jnp.bfloat16, jnp.float32
    dma = pltpu.SemaphoreType.DMA
    vmem = pl.BlockSpec(memory_space=pltpu.VMEM)
    smem = pl.BlockSpec(memory_space=pltpu.SMEM)
    anywhere = pl.BlockSpec(memory_space=pl.ANY)
    scratch = [
        pltpu.VMEM((rows, feature), f32),
        pltpu.VMEM((group, rows, feature), f32),
        pltpu.VMEM(draft_weight.shape, bf16),
        pltpu.VMEM((group, vocab, feature), bf16),
        pltpu.VMEM((group, devices * rows, feature), bf16),
        pltpu.VMEM((devices * rows, vocab), f32),
        dma((1 + group,)),
        dma((group,)), dma((group,)),
        dma((devices,)), dma((devices,)),
        dma((4,)), dma((4,)),
        dma((3,)), dma((3,)),
        pltpu.VMEM((group, feature, feature), bf16),
        pltpu.VMEM((2 * strips, width, feature), bf16),
        pltpu.VMEM((group, inner, feature), bf16),
        pltpu.VMEM((count, tokens, feature), f32),
        pltpu.VMEM((tokens, feature), f32),
        pltpu.VMEM((tokens, feature), f32),
        pltpu.VMEM((2, chunks, 2, chips, size, feature), bf16),
        pltpu.VMEM((2, chunks, chips, size, feature), bf16),
        pltpu.VMEM((2, chunks, size, feature), bf16),
        pltpu.VMEM((2, chunks, size, feature), bf16),
        pltpu.VMEM((2, chunks, size, feature), bf16),
        pltpu.VMEM((chunks, group, 8, size), f32),
        pltpu.VMEM((chunks, size, 8), f32),
        pltpu.VMEM((tokens, feature), bf16),
        pltpu.VMEM((tokens, width), bf16),
        pltpu.VMEM((size, inner), bf16),
        dma((3, max(group, 2 * strips))),
        dma((chunks,)),
        dma((2, chunks, 4)), dma((2, chunks, 4)),
        dma((2, chunks, 3)), dma((2, chunks, 3)),
        dma((chunks, group)), dma((chunks, group)),
        dma((chunks, 4)), dma((chunks, 4)),
        dma((chunks, 3)), dma((chunks, 3)),
    ]
    return pl.pallas_call(
        functools.partial(layer_kernel, chips, chunks),
        out_shape=(
            jax.ShapeDtypeStruct((count, tokens, feature), bf16),
            jax.ShapeDtypeStruct((devices * rows, vocab), bf16),
        ),
        in_specs=[smem] * 4 + [vmem, vmem] + [anywhere] * 5,
        out_specs=(vmem, vmem),
        scratch_shapes=scratch,
        compiler_params=pltpu.CompilerParams(
            collective_id=1, has_side_effects=True, vmem_limit_bytes=60 << 20
        ),
    )(
        hc_in,
        hc_mix,
        hc_out,
        accepted,
        attended,
        streams,
        out_weight,
        gate_up,
        down_weight,
        draft_weight,
        jnp.transpose(lm_head),
    )


def on_device(
    streams,
    hc_in,
    hc_mix,
    hc_out,
    qkv_weight,
    out_weight,
    up_gate,
    down_weight,
    draft_weight,
    lm_head,
    k_pages,
    v_pages,
    page_owner,
    page_fill,
    cache_len,
    tree_parent,
    accepted_index,
):
    tokens_local = streams.shape[0]
    req_local = cache_len.shape[0]
    tree_size = tree_parent.shape[1]
    heads_local = k_pages.shape[2]
    head_dim = k_pages.shape[3]
    draft_count = draft_weight.shape[0]
    all_requests = req_local * lax.axis_size("req")
    reach = ancestors(tree_parent)
    depth = (jnp.sum(reach.astype(jnp.float32), axis=1) - 1.0).astype(jnp.int32)
    positions = (cache_len[:, None] + depth).reshape(tokens_local)
    cosine, sine = turns(positions, head_dim)
    same_head = jnp.eye(heads_local, dtype=jnp.bfloat16)
    tree_mask = (same_head[None, :, None, :, None] * reach[:, None, :, None, :]).reshape(
        req_local, heads_local * tree_size, heads_local * tree_size
    )
    by_stream = jnp.transpose(streams, (1, 0, 2))
    width, kinds, inner = up_gate.shape
    up_rows = jnp.transpose(up_gate.reshape(width, kinds, inner // 128, 128), (0, 2, 1, 3)).reshape(
        -1, 128
    )
    attended, gate_up = cache_attention(
        by_stream,
        hc_in,
        jnp.transpose(qkv_weight, (1, 0, 2)),
        up_rows,
        cosine,
        sine,
        tree_mask,
        k_pages,
        v_pages,
        page_owner,
        page_fill,
    )
    fresh, logits_local = layer(
        attended,
        by_stream,
        hc_in,
        hc_mix,
        hc_out,
        out_weight,
        gate_up,
        down_weight,
        accepted_index,
        draft_weight,
        lm_head,
    )
    new_streams = jnp.transpose(fresh, (1, 0, 2))
    logits_local = logits_local.reshape(all_requests, draft_count, -1)
    logits = lax.all_to_all(
        logits_local, ("req", "head"), split_axis=0, concat_axis=2, tiled=True
    ).astype(jnp.float32)
    return (new_streams, logits)


def solution(mesh):
    in_specs = (
        P("req", None, "head"),
        P(),
        P(),
        P(),
        P(None, None, "head"),
        P("head", None),
        P(None, None, "head"),
        P("head", None),
        P(None, None, "head"),
        P(None, ("req", "head")),
        P("req", None, "head", None),
        P("req", None, "head", None),
        P("req"),
        P("req"),
        P("req"),
        P("req", None),
        P("req"),
    )
    out_specs = (P("req", None, "head"), P(("req", "head"), None, None))
    return jax.shard_map(
        on_device, mesh=mesh, in_specs=in_specs, out_specs=out_specs, check_vma=False
    )
```

```python
import functools
import math

import jax
import jax.numpy as jnp
from jax import lax
from jax.experimental import pallas as pl
from jax.experimental.pallas import tpu as pltpu
from jax.sharding import PartitionSpec as P

NEG_FILL = -1e30


def ancestors(parents):
    length = parents.shape[1]
    places = jnp.arange(length, dtype=jnp.int32)
    linked = (places[None, :, None] == parents[:, None, :]) | (places[:, None] == places[None, :])[
        None
    ]
    reach = linked.astype(jnp.bfloat16)
    for repeat in range(max(1, (length - 1).bit_length())):
        counts = jnp.einsum("jki,jil->jkl", reach, reach, preferred_element_type=jnp.float32)
        reach = jnp.minimum(counts, 1.0).astype(jnp.bfloat16)
    return reach


def turns(positions, head_dim):
    half = head_dim // 2
    freqs = jnp.exp(
        jnp.arange(half, dtype=jnp.float32) * (-2.0 * math.log(10000.0) / head_dim)
    )
    angles = positions.astype(jnp.float32)[:, None] * freqs[None, :]
    cosine = jnp.cos(angles)
    sine = jnp.sin(angles)
    return jnp.concatenate([cosine, cosine], axis=1), jnp.concatenate([-sine, sine], axis=1)


MESH = pl.DeviceIdType.MESH
SLOT_BITS = 6
FILL_BITS = 8


def remote(source, target, send_sem, recv_sem, req):
    return pltpu.make_async_remote_copy(
        src_ref=source,
        dst_ref=target,
        send_sem=send_sem,
        recv_sem=recv_sem,
        device_id={"req": req},
        device_id_type=MESH,
    )


def weigh(tops, totals):
    top = functools.reduce(jnp.maximum, tops)
    factors = [jnp.exp(value - top) for value in tops]
    total = functools.reduce(lambda a, b: a + b, [f * t for f, t in zip(factors, totals)])
    return top, total, factors


def cache_kernel(
    side,
    chips,
    table,
    last,
    hc_in,
    streams,
    cosine,
    sine,
    mask_ref,
    weight_hbm,
    up_hbm,
    k_hbm,
    v_hbm,
    out_ref,
    gate_ref,
    q_ref,
    key_ref,
    value_ref,
    weight_buf,
    mixed_buf,
    stat_all,
    columns,
    normed,
    gathered,
    up_in,
    up_out,
    front_sem,
    own_sem,
    front_send,
    front_recv,
    copy_send,
    copy_recv,
    pass_send,
    pass_recv,
    up_in_sem,
    up_out_sem,
    tree_acc,
    tree_stat,
    q_all,
    k_buf,
    v_buf,
    scores,
    seg_acc,
    seg_top,
    seg_den,
    parts,
    stats,
    relay,
    merged,
    single,
    relay_s,
    merged_s,
    single_s,
    outgoing_s,
    factors,
    small,
    small_s,
    hop,
    hop_s,
    gather_send,
    gather_recv,
    spread_send,
    spread_recv,
    load_sem,
    far_send,
    far_recv,
    near_send,
    near_recv,
    join_send,
    join_recv,
    stat_send,
    stat_recv,
    last_send,
    last_recv,
    last_stat_send,
    last_stat_recv,
):
    block = q_ref.shape[0] // 2
    rows = q_ref.shape[1]
    slots = k_buf.shape[0]
    half_rows = rows // 2
    me = lax.axis_index("req")
    place = (me // side, lax.rem(me, side))
    turn = 1 - 2 * lax.rem(lax.axis_index("head"), 2)

    def shifted(axis, delta):
        moved = lax.rem(place[axis] + side + delta, side)
        return moved * side + place[1] if axis == 0 else place[0] * side + moved

    def at(axis, delta):
        return lax.rem(place[axis] + side + delta, side)

    first = (0, 1)
    second = (1, 0)

    def spot(half, p2, p1):
        return pl.ds(((half * side + p2) * side + p1) * block, block)

    loads = [
        pltpu.make_async_copy(k_hbm, k_buf, load_sem.at[0]),
        pltpu.make_async_copy(v_hbm, v_buf, load_sem.at[1]),
    ]
    weight_load = pltpu.make_async_copy(weight_hbm, weight_buf, front_sem)
    weight_load.start()
    barrier = pltpu.get_barrier_semaphore()
    for axis in (0, 1):
        for delta in (1, -1):
            pl.semaphore_signal(
                barrier, inc=1, device_id={"req": shifted(axis, delta)}, device_id_type=MESH
            )
    head_index = lax.axis_index("head")
    for step in range(1, 2 * chips):
        pl.semaphore_signal(
            barrier,
            inc=1,
            device_id={"head": lax.rem(head_index + step, 2 * chips)},
            device_id_type=MESH,
        )

    def enter():
        pl.semaphore_wait(barrier, 4 + 2 * chips - 1)

    pieces = gate_ref.shape[1] // up_out.shape[2]
    span = up_out.shape[2]
    tall = up_in.shape[1]

    def up_load(c):
        return pltpu.make_async_copy(
            up_hbm.at[pl.ds(c * tall, tall)], up_in.at[c % 2], up_in_sem.at[c]
        )

    def up_store(c):
        return pltpu.make_async_copy(
            up_out.at[c % 2], gate_ref.at[:, pl.ds(c * span, span)], up_out_sem.at[c]
        )

    strips = gate_ref.shape[2] // 128
    unit = 2 * strips * 16

    def untangle(c):
        if c + 1 < pieces:
            up_load(c + 1).start()
        up_load(c).wait()
        if c >= 2:
            up_store(c - 2).wait()
        out_row = lax.broadcasted_iota(jnp.int32, (unit, unit), 0)
        in_row = lax.broadcasted_iota(jnp.int32, (unit, unit), 1)
        kind = out_row // (unit // 2)
        strip = (out_row // 16) & (strips - 1)
        pick = (out_row & 15) * (2 * strips) + strip * 2 + kind
        chosen = jnp.where(in_row == pick, 1.0, 0.0).astype(jnp.bfloat16)

        def step(index, carry):
            sorted_rows = jnp.dot(
                chosen,
                up_in[c % 2, pl.ds(index * unit, unit)],
                preferred_element_type=jnp.float32,
            ).astype(up_out.dtype)
            place = pl.ds(index * 16, 16)
            for kind in (0, 1):
                for strip in range(strips):
                    row = (kind * strips + strip) * 16
                    up_out[c % 2, kind, place, strip * 128 : (strip + 1) * 128] = sorted_rows[
                        row : row + 16
                    ]
            return carry

        lax.fori_loop(0, span // 16, step, 0)
        up_store(c).start()

    up_load(0).start()

    sends = []

    def go(copy):
        copy.start()
        sends.append(copy)
        return copy

    def pass_block(half, axis, delta, p2, p1, send, recv, own=False):
        view = q_all.at[spot(half, p2, p1)]
        source = q_ref.at[pl.ds(half * block, block)] if own else view
        return go(remote(source, view, send, recv, shifted(axis, delta)))

    lines = {}
    crosses = {}

    def line(half, index, delta, p1, own=False):
        lines[half, index] = pass_block(
            half, first[half], delta, at(second[half], 0), p1,
            gather_send.at[half, index], gather_recv.at[half, index], own,
        )

    def cross(half, piece, index, delta, p2, p1, own=False):
        crosses[half, piece, index] = pass_block(
            half, second[half], delta, p2, p1,
            spread_send.at[half, piece, index], spread_recv.at[half, piece, index], own,
        )

    chunks = 2

    def front_part():
        count, tokens, feature = streams.shape
        size = tokens // chunks
        group = 2 * chips
        width = group * feature
        head_dim = q_ref.shape[2]
        rows = q_ref.shape[1]
        heads = feature // head_dim
        tree = rows // heads
        me = lax.axis_index("head")
        chip = me // 2
        core = lax.rem(me, 2)
        turn = 1 - 2 * core
        sibling = chip * 2 + 1 - core

        def peer(delta):
            return lax.rem(chip + chips + delta, chips) * 2 + core

        def send_to(source, target, send_sem, recv_sem, head):
            return pltpu.make_async_remote_copy(
                src_ref=source,
                dst_ref=target,
                send_sem=send_sem,
                recv_sem=recv_sem,
                device_id={"head": head},
                device_id_type=MESH,
            )

        block = 32
        for t in range(chunks):

            def mix(index, carry, t=t):
                here = pl.ds(t * size + index * block, block)
                mixed = None
                for s in range(count):
                    term = hc_in[0, s] * streams[s, here].astype(jnp.float32)
                    mixed = term if mixed is None else mixed + term
                mixed_buf[here] = mixed
                return carry

            lax.fori_loop(0, size // block, mix, 0)
            mixed = mixed_buf[t * size : (t + 1) * size]
            stat_all[t, me, 0:1] = transpose_sum(mixed)
            stat_all[t, me, 1:2] = transpose_sum(mixed * mixed)
            stat_all[t, me, 2:8] = jnp.zeros((6, size), jnp.float32)
        enter()
        waits = {}

        def chunk_rows(t):
            return pl.ds(t * size, size)

        def lanes(head):
            return pl.ds(pl.multiple_of(head * feature, feature), feature)

        for t in range(chunks):
            for step in range(1, group):
                waits["stat", t, step] = go(
                    send_to(stat_all.at[t, me], stat_all.at[t, me], front_send.at[t, step],
                            front_recv.at[t, step], lax.rem(me + step, group)))

        def normalized(t):
            for step in range(1, group):
                waits["stat", t, step].wait_recv()
            total = stat_all[t, 0]
            for index in range(1, group):
                total = total + stat_all[t, index]
            center = total[0:1] / width
            scale = lax.rsqrt(total[1:2] / width - center * center + 1e-05)
            row = lax.broadcasted_iota(jnp.int32, total.shape, 0)
            packed = jnp.where(row == 0, center, jnp.where(row == 1, scale, 0.0))
            columns[t] = jnp.transpose(packed)

            def step(index, carry):
                inside = pl.ds(index * block, block)
                here = pl.ds(t * size + index * block, block)
                column = columns[t, inside]
                value = (mixed_buf[here] - column[:, 0:1]) * column[:, 1:2]
                normed[here] = value.astype(normed.dtype)
                return carry

            lax.fori_loop(0, size // block, step, 0)
            mine = normed.at[chunk_rows(t)]
            view = gathered.at[chunk_rows(t), lanes(me)]
            waits["fwd", t] = go(send_to(mine, view, pass_send.at[t, 0], pass_recv.at[t, 0], peer(turn)))
            waits["bwd", t] = go(send_to(mine, view, pass_send.at[t, 1], pass_recv.at[t, 1], peer(-turn)))
            waits["own", t] = go(send_to(mine, view, copy_send.at[t, 0], copy_recv.at[t, 0], sibling))
            local = pltpu.make_async_copy(mine, view, own_sem.at[t])
            local.start()
            waits["local", t] = local

        def hand_over(t, index, delta):
            view = gathered.at[chunk_rows(t), lanes(peer(delta))]
            waits["copy", t, index] = go(
                send_to(view, view, copy_send.at[t, index], copy_recv.at[t, index], sibling))

        def pass_on(t):
            waits["fwd", t].wait_recv()
            view = gathered.at[chunk_rows(t), lanes(peer(-turn))]
            waits["opp", t] = go(send_to(view, view, pass_send.at[t, 2], pass_recv.at[t, 2], peer(turn)))
            hand_over(t, 1, -turn)
            waits["bwd", t].wait_recv()
            hand_over(t, 2, turn)

        def pass_last(t):
            waits["opp", t].wait_recv()
            hand_over(t, 3, 2)

        def project(t):
            if t == 0:
                weight_load.wait()
            waits["own", t].wait_recv()
            waits["local", t].wait()
            for index in (1, 2, 3):
                waits["copy", t, index].wait_recv()
            here = slice(t * size, (t + 1) * size)
            for kind, target in enumerate((q_ref, key_ref, value_ref)):
                product = jnp.dot(gathered[here], weight_buf[kind], preferred_element_type=jnp.float32)
                for head in range(heads):
                    value = product[:, head * head_dim : (head + 1) * head_dim]
                    if kind < 2:
                        turned = pltpu.roll(value, head_dim // 2, 1)
                        value = value * cosine[here] + turned * sine[here]
                    if kind == 0:
                        value = value * head_dim ** (-0.5)
                    value = value.astype(target.dtype)
                    for item in range(size // tree):
                        target[t * (size // tree) + item, head * tree : (head + 1) * tree] = value[
                            item * tree : (item + 1) * tree
                        ]
            launch(t)

        phases = (normalized, pass_on, pass_last, project)
        for step in range(len(phases) + chunks - 1):
            for t in range(chunks):
                if 0 <= step - t < len(phases):
                    phases[step - t](t)

    halves = (0, 1)

    def launch(half):
        line(half, 0, turn, at(first[half], 0), True)
        line(half, 1, -turn, at(first[half], 0), True)
        cross(half, 0, 0, turn, at(second[half], 0), at(first[half], 0), True)
        cross(half, 0, 1, -turn, at(second[half], 0), at(first[half], 0), True)

    front_part()
    for load in loads:
        load.start()
    for half in halves:
        q_all[spot(half, at(second[half], 0), at(first[half], 0))] = q_ref[
            half * block : (half + 1) * block
        ]
    seg_top[...] = jnp.full(seg_top.shape, NEG_FILL, jnp.float32)
    seg_den[...] = jnp.zeros(seg_den.shape, jnp.float32)
    seg_acc[slots] = jnp.zeros(seg_acc.shape[1:], seg_acc.dtype)
    tree_stat[...] = jnp.zeros(tree_stat.shape, jnp.float32)

    spread_row = lax.broadcasted_iota(jnp.int32, (half_rows, rows), 0)
    spread_col = lax.broadcasted_iota(jnp.int32, (half_rows, rows), 1)
    spread = jnp.where(
        jnp.logical_or(spread_col == spread_row, spread_col == spread_row + half_rows), 1.0, 0.0
    ).astype(jnp.bfloat16)
    key_head = lax.broadcasted_iota(jnp.int32, (rows, rows), 0) >= half_rows
    query_head = lax.broadcasted_iota(jnp.int32, (rows, rows), 1) >= half_rows
    same_head = key_head.astype(jnp.int32) == query_head.astype(jnp.int32)

    def tree_step(item, carry):
        found = lax.dot_general(
            key_ref[item],
            q_ref[item],
            (((1,), (1,)), ((), ())),
            preferred_element_type=jnp.float32,
        )
        wide = lax.dot_general(
            mask_ref[item], spread, (((1,), (0,)), ((), ())), preferred_element_type=jnp.float32
        ).astype(jnp.bfloat16)
        reached = lax.dot_general(
            spread, wide, (((0,), (0,)), ((), ())), preferred_element_type=jnp.float32
        )
        found = jnp.where(jnp.logical_and(same_head, reached > 0.0), found, NEG_FILL)
        top = jnp.max(found, axis=0, keepdims=True)
        weight = jnp.exp(found - top)
        tree_acc[item] = lax.dot_general(
            weight.astype(jnp.bfloat16),
            value_ref[item],
            (((0,), (0,)), ((), ())),
            preferred_element_type=jnp.float32,
        )
        tree_stat[0, item, :, 0:rows] = top
        tree_stat[1, item, :, 0:rows] = jnp.sum(weight, axis=0, keepdims=True)
        return carry

    lax.fori_loop(0, 2 * block, tree_step, 0)
    for half in halves:
        lines[half, 0].wait_recv()
        line(half, 2, turn, at(first[half], -turn))
        cross(half, 1, 0, turn, at(second[half], 0), at(first[half], -turn))
        cross(half, 1, 1, -turn, at(second[half], 0), at(first[half], -turn))
    untangle(0)
    untangle(1)
    for half in halves:
        lines[half, 1].wait_recv()
        cross(half, 2, 0, turn, at(second[half], 0), at(first[half], turn))
        cross(half, 2, 1, -turn, at(second[half], 0), at(first[half], turn))
    untangle(2)
    for half in halves:
        crosses[half, 0, 0].wait_recv()
        cross(half, 0, 2, turn, at(second[half], -turn), at(first[half], 0))
    untangle(3)
    for half in halves:
        lines[half, 2].wait_recv()
        cross(half, 3, 0, turn, at(second[half], 0), at(first[half], 2))
        cross(half, 3, 1, -turn, at(second[half], 0), at(first[half], 2))
    for piece, delta in ((1, -turn), (2, turn), (3, 2)):
        untangle(3 + piece)
        for half in halves:
            crosses[half, piece, 0].wait_recv()
            cross(half, piece, 2, turn, at(second[half], -turn), at(first[half], delta))
    untangle(7)
    for piece in range(4):
        for half in halves:
            crosses[half, piece, 1].wait_recv()
            crosses[half, piece, 2].wait_recv()
    for load in loads:
        load.wait()

    slot_mask = (1 << SLOT_BITS) - 1
    fill_mask = (1 << FILL_BITS) - 1
    requests = 2 * block * side * side

    def owner_at(index):
        return table[index] >> (SLOT_BITS + FILL_BITS)

    def starts_new(index):
        before = owner_at(jnp.maximum(index - 1, 0))
        return jnp.logical_or(index == 0, before != owner_at(index))

    shape = (k_buf.shape[1], rows)
    row_ids = lax.broadcasted_iota(jnp.int32, shape, 0)
    col_head = (lax.broadcasted_iota(jnp.int32, shape, 1) >= half_rows).astype(jnp.int32)
    matched = (row_ids & 1) == col_head
    key_ids = row_ids >> 1
    unroll = 4

    def score_step(group, carry):
        for offset in range(unroll):
            index = group * unroll + offset
            entry = table[index]
            fill = (entry >> SLOT_BITS) & fill_mask
            owner = jnp.minimum(entry >> (SLOT_BITS + FILL_BITS), requests - 1)
            home = owner // (2 * block)
            within = lax.rem(owner, 2 * block)
            half = within // block
            hx = home // side
            hy = lax.rem(home, side)
            outer = jnp.where(half == 0, hy, hx)
            inner = jnp.where(half == 0, hx, hy)
            row = ((half * side + outer) * side + inner) * block + lax.rem(within, block)
            found = lax.dot_general(
                k_buf[entry & slot_mask],
                q_all[row],
                (((1,), (1,)), ((), ())),
                preferred_element_type=jnp.float32,
            )
            found = jnp.where(jnp.logical_and(matched, key_ids < fill), found, NEG_FILL)
            scores[index] = found
            seg_top[index, :, 0:rows] = jnp.max(found, axis=0, keepdims=True)
        return carry

    lax.fori_loop(0, slots // unroll, score_step, 0)

    def forward(index, run):
        here = seg_top[index]
        run = jnp.where(starts_new(index), here, jnp.maximum(run, here))
        seg_top[index] = run
        return run

    lax.fori_loop(0, slots, forward, jnp.full(seg_top.shape[1:], NEG_FILL, jnp.float32))

    def backward(step, run):
        index = slots - 1 - step
        follow = jnp.minimum(index + 1, slots - 1)
        ends = jnp.logical_or(step == 0, owner_at(follow) != owner_at(index))
        run = jnp.where(ends, seg_top[index], run)
        seg_top[index] = run
        return run

    lax.fori_loop(0, slots, backward, jnp.full(seg_top.shape[1:], NEG_FILL, jnp.float32))

    def value_step(group, carry):
        acc_run, den_run = carry
        for offset in range(unroll):
            index = group * unroll + offset
            fresh = starts_new(index)
            top = seg_top[index][:, 0:rows]
            top = jnp.where(top < 0.5 * NEG_FILL, 0.0, top)
            weight = jnp.exp(scores[index] - top)
            den = jnp.sum(weight, axis=0, keepdims=True)
            acc = lax.dot_general(
                weight.astype(jnp.bfloat16),
                v_buf[table[index] & slot_mask],
                (((0,), (0,)), ((), ())),
                preferred_element_type=jnp.float32,
            )
            acc_run = acc + jnp.where(fresh, 0.0, acc_run)
            den_run = den + jnp.where(fresh, 0.0, den_run)
            seg_acc[index] = acc_run.astype(seg_acc.dtype)
            seg_den[index, :, 0:rows] = den_run
        return acc_run, den_run

    lax.fori_loop(
        0,
        slots // unroll,
        value_step,
        (jnp.zeros(seg_acc.shape[1:], jnp.float32), jnp.zeros((1, rows), jnp.float32)),
    )

    def place_step(group, carry):
        for piece in range(side):
            tops, dens = [], []
            for offset in range(block):
                spot_index = (group * side + piece) * block + offset
                found = last[spot_index]
                parts[spot_index] = seg_acc[found]
                tops.append(seg_top[found])
                dens.append(seg_den[found])
            stats[group, 0, piece * block : (piece + 1) * block] = jnp.concatenate(tops, axis=0)
            stats[group, 1, piece * block : (piece + 1) * block] = jnp.concatenate(dens, axis=0)
        return carry

    for half in halves:
        for delta in (2, -turn):
            place_step(half * side + at(second[half], delta), 0)

    def part(half, p2, p1):
        return parts.at[spot(half, p2, p1)]

    def stat(half, p2):
        return stats.at[half * side + p2]

    def combine(put, terms, weights):
        columns = [jnp.transpose(weight) for weight in weights]
        for item in range(block):
            total = None
            for term, column in zip(terms, columns):
                value = term[item].astype(jnp.float32) * column[0:rows, item : item + 1]
                total = value if total is None else total + value
            put(item, total)

    def offset(order):
        if isinstance(order, int):
            swapped = order + order // 2 - 2 * (order // 3)
        else:
            swapped = order + lax.div(order, 2) - 2 * lax.div(order, 3)
        return 2 + side - turn * swapped

    stat_copies = {}
    far, near = {}, {}
    for half in halves:
        up, down = shifted(second[half], turn), shifted(second[half], -turn)
        stat_copies[half, 0] = go(
            remote(stat(half, at(second[half], 2)), relay_s.at[half],
                   stat_send.at[half, 0], stat_recv.at[half, 0], up))
        stat_copies[half, 1] = go(
            remote(stat(half, at(second[half], -turn)), single_s.at[half],
                   stat_send.at[half, 1], stat_recv.at[half, 1], down))
    for order in range(4):
        for half in halves:
            up, down = shifted(second[half], turn), shifted(second[half], -turn)
            p1 = at(first[half], offset(order))
            far[half, order] = go(
                remote(part(half, at(second[half], 2), p1), relay.at[half, p1],
                       far_send.at[half, order], far_recv.at[half, order], up))
            near[half, order] = go(
                remote(part(half, at(second[half], -turn), p1), single.at[half, p1],
                       near_send.at[half, order], near_recv.at[half, order], down))

    for half in halves:
        for delta in (turn, 0):
            place_step(half * side + at(second[half], delta), 0)

    for half in halves:
        stat_copies[half, 0].wait_recv()
        mine = stat(half, at(second[half], turn))
        top, den, weights = weigh([mine[0], relay_s[half, 0]], [mine[1], relay_s[half, 1]])
        outgoing_s[half, 0] = top
        outgoing_s[half, 1] = den
        factors[half, 0] = weights[0]
        factors[half, 1] = weights[1]
        stat_copies[half, 2] = go(
            remote(outgoing_s.at[half], merged_s.at[half],
                   stat_send.at[half, 2], stat_recv.at[half, 2], shifted(second[half], turn)))

    def join_copy(half, order):
        p1 = at(first[half], offset(order))
        return remote(relay.at[half, p1], merged.at[half, p1],
                      join_send.at[half, order], join_recv.at[half, order],
                      shifted(second[half], turn))

    def far_copy(half, order):
        p1 = at(first[half], offset(order))
        return remote(part(half, at(second[half], 2), p1), relay.at[half, p1],
                      far_send.at[half, order], far_recv.at[half, order],
                      shifted(second[half], turn))

    def near_copy(half, order):
        p1 = at(first[half], offset(order))
        return remote(part(half, at(second[half], -turn), p1), single.at[half, p1],
                      near_send.at[half, order], near_recv.at[half, order],
                      shifted(second[half], -turn))

    def relay_step(order, carry):
        for half in halves:
            p1 = at(first[half], offset(order))
            far_copy(half, order).wait_recv()
            lanes = pl.ds(p1 * block, block)
            target = relay.at[half, p1]

            def put(item, value):
                target[item] = value.astype(target.dtype)

            combine(
                put,
                [part(half, at(second[half], turn), p1), target],
                [factors[half, 0, lanes], factors[half, 1, lanes]],
            )
            join_copy(half, order).start()
        return carry

    lax.fori_loop(0, 4, relay_step, 0)

    for half in halves:
        stat_copies[half, 1].wait_recv()
        stat_copies[half, 2].wait_recv()
        mine = stat(half, at(second[half], 0))
        top, den, weights = weigh(
            [mine[0], merged_s[half, 0], single_s[half, 0]],
            [mine[1], merged_s[half, 1], single_s[half, 1]],
        )
        for index in range(3):
            factors[half, index] = weights[index]
        for p1 in range(side):
            small_s[half, p1, 0] = top[p1 * block : (p1 + 1) * block]
            small_s[half, p1, 1] = den[p1 * block : (p1 + 1) * block]

    def gather_piece(half, order):
        p1 = at(first[half], offset(order))
        near_copy(half, order).wait_recv()
        join_copy(half, order).wait_recv()
        lanes = pl.ds(p1 * block, block)
        target = small.at[half, p1]

        def put(item, value):
            target[item] = value.astype(target.dtype)

        combine(
            put,
            [part(half, at(second[half], 0), p1), merged.at[half, p1], single.at[half, p1]],
            [factors[half, index, lanes] for index in range(3)],
        )

    def piece_step(order, carry):
        for half in halves:
            gather_piece(half, order)
        return carry

    tails = {}

    def tail(half, index, source, source_s, delta):
        peer = shifted(first[half], delta)
        tails[half, index] = (
            go(remote(source_s, hop_s.at[half, index],
                      last_stat_send.at[half, index], last_stat_recv.at[half, index], peer)),
            go(remote(source, hop.at[half, index],
                      last_send.at[half, index], last_recv.at[half, index], peer)),
        )

    lax.fori_loop(0, 1, piece_step, 0)
    for half in halves:
        p1 = at(first[half], 2)
        tail(half, 0, small.at[half, p1], small_s.at[half, p1], turn)
    lax.fori_loop(1, 3, piece_step, 0)
    for half in halves:
        p1 = at(first[half], -turn)
        tail(half, 1, small.at[half, p1], small_s.at[half, p1], -turn)
    for half in halves:
        p1 = at(first[half], turn)
        for copy in tails[half, 0]:
            copy.wait_recv()
        target = small.at[half, p1]
        top, den, weights = weigh(
            [small_s[half, p1, 0], hop_s[half, 0, 0]], [small_s[half, p1, 1], hop_s[half, 0, 1]]
        )
        small_s[half, p1, 0] = top
        small_s[half, p1, 1] = den

        def put(item, value, target=target):
            target[item] = value.astype(target.dtype)

        combine(put, [target, hop.at[half, 0]], weights)
        tail(half, 2, target, small_s.at[half, p1], turn)
    lax.fori_loop(3, 4, piece_step, 0)
    for half in halves:
        p1 = at(first[half], 0)
        for index in (1, 2):
            for copy in tails[half, index]:
                copy.wait_recv()
        tree = [
            jnp.concatenate(
                [tree_stat[kind, half * block + item] for item in range(block)], axis=0
            )
            for kind in (0, 1)
        ]
        top, den, weights = weigh(
            [small_s[half, p1, 0], hop_s[half, 1, 0], hop_s[half, 2, 0], tree[0]],
            [small_s[half, p1, 1], hop_s[half, 1, 1], hop_s[half, 2, 1], tree[1]],
        )
        lane = lax.broadcasted_iota(jnp.int32, den.shape, 1)
        inverse = 1.0 / jnp.where(lane < rows, den, 1.0)

        def put(item, value, half=half):
            start = (half * block + item) * half_rows
            value = value.astype(out_ref.dtype)
            width = value.shape[1]
            for head in (0, 1):
                out_ref[start : start + half_rows, head * width : (head + 1) * width] = value[
                    head * half_rows : (head + 1) * half_rows
                ]

        combine(
            put,
            [
                small.at[half, p1],
                hop.at[half, 1],
                hop.at[half, 2],
                tree_acc.at[pl.ds(half * block, block)],
            ],
            [weight * inverse for weight in weights],
        )
    for copy in sends:
        copy.wait_send()
    for half in halves:
        for order in range(4):
            join_copy(half, order).wait_send()
    for c in (pieces - 2, pieces - 1):
        up_store(c).wait()


def cache_attention(
    streams, hc_in, qkv, up_rows, cosine, sine, tree_mask, k_pages, v_pages, page_owner, page_fill
):
    req_local = tree_mask.shape[0]
    rows = k_pages.shape[2] * tree_mask.shape[1]
    head_dim = k_pages.shape[3]
    tokens, feature = streams.shape[1:3]
    group = lax.axis_size("head")
    width = qkv.shape[1]
    hidden_units = up_rows.shape[0] * 128 // (2 * width)
    pieces = 8
    half_tokens = tokens // 2
    slots, keys = k_pages.shape[0], k_pages.shape[1] * k_pages.shape[2]
    devices = lax.axis_size("req")
    side = math.isqrt(devices)
    block = req_local // 2
    requests = req_local * devices
    owner_key = jnp.where(page_owner < 0, requests, page_owner)
    packed = (
        (owner_key << (SLOT_BITS + FILL_BITS))
        | (jnp.where(page_owner < 0, 0, page_fill) << SLOT_BITS)
        | jnp.arange(slots, dtype=jnp.int32)
    )
    rank = jnp.sum((packed[None, :] < packed[:, None]).astype(jnp.int32), axis=1)
    places = jnp.arange(slots, dtype=jnp.int32)
    table = jnp.sum(jnp.where(rank[None, :] == places[:, None], packed[None, :], 0), axis=1)
    spots = jnp.arange(requests, dtype=jnp.int32)
    half = spots // (requests // 2)
    outer = (spots // (block * side)) % side
    inner = (spots // block) % side
    home = jnp.where(half == 0, inner * side + outer, outer * side + inner)
    request = home * req_local + half * block + spots % block
    below = jnp.sum((owner_key[None, :] <= request[:, None]).astype(jnp.int32), axis=1)
    exact = jnp.sum((owner_key[None, :] == request[:, None]).astype(jnp.int32), axis=1)
    last = jnp.where(exact > 0, below - 1, slots)
    bf16, f32 = jnp.bfloat16, jnp.float32
    unit = (2, side, block, rows, head_dim)
    dma = pltpu.SemaphoreType.DMA
    scratch = [
        pltpu.VMEM((req_local, rows, head_dim), bf16),
        pltpu.VMEM((req_local, rows, head_dim), bf16),
        pltpu.VMEM((req_local, rows, head_dim), bf16),
        pltpu.VMEM(qkv.shape, bf16),
        pltpu.VMEM((tokens, feature), f32),
        pltpu.VMEM((2, group, 8, half_tokens), f32),
        pltpu.VMEM((2, half_tokens, 8), f32),
        pltpu.VMEM((tokens, feature), bf16),
        pltpu.VMEM((tokens, width), bf16),
        pltpu.VMEM((2, up_rows.shape[0] // pieces, 128), bf16),
        pltpu.VMEM((2, 2, width // pieces, hidden_units), bf16),
        dma,
        dma((2,)),
        dma((2, group)), dma((2, group)),
        dma((2, 4)), dma((2, 4)),
        dma((2, 3)), dma((2, 3)),
        dma((pieces,)), dma((pieces,)),
        pltpu.VMEM((req_local, rows, head_dim), f32),
        pltpu.VMEM((2, req_local, 1, 128), f32),
        pltpu.VMEM((requests, rows, head_dim), bf16),
        pltpu.VMEM((slots, keys, head_dim), bf16),
        pltpu.VMEM((slots, keys, head_dim), bf16),
        pltpu.VMEM((slots, keys, rows), f32),
        pltpu.VMEM((slots + 1, rows, head_dim), bf16),
        pltpu.VMEM((slots + 1, 1, 128), f32),
        pltpu.VMEM((slots + 1, 1, 128), f32),
        pltpu.VMEM((requests, rows, head_dim), bf16),
        pltpu.VMEM((2 * side, 2, side * block, 128), f32),
        pltpu.VMEM(unit, bf16),
        pltpu.VMEM(unit, bf16),
        pltpu.VMEM(unit, bf16),
        pltpu.VMEM((2, 2, side * block, 128), f32),
        pltpu.VMEM((2, 2, side * block, 128), f32),
        pltpu.VMEM((2, 2, side * block, 128), f32),
        pltpu.VMEM((2, 2, side * block, 128), f32),
        pltpu.VMEM((2, 3, side * block, 128), f32),
        pltpu.VMEM(unit, bf16),
        pltpu.VMEM((2, side, 2, block, 128), f32),
        pltpu.VMEM((2, 3, block, rows, head_dim), bf16),
        pltpu.VMEM((2, 3, 2, block, 128), f32),
        dma((2, 3)), dma((2, 3)),
        dma((2, 4, 3)), dma((2, 4, 3)),
        dma((2,)),
        dma((2, 4)), dma((2, 4)),
        dma((2, 4)), dma((2, 4)),
        dma((2, 4)), dma((2, 4)),
        dma((2, 3)), dma((2, 3)),
        dma((2, 3)), dma((2, 3)),
        dma((2, 3)), dma((2, 3)),
    ]
    vmem = pl.BlockSpec(memory_space=pltpu.VMEM)
    smem = pl.BlockSpec(memory_space=pltpu.SMEM)
    anywhere = pl.BlockSpec(memory_space=pl.ANY)
    return pl.pallas_call(
        functools.partial(cache_kernel, side, group // 2),
        out_shape=(
            jax.ShapeDtypeStruct((req_local * rows // 2, 2 * head_dim), bf16),
            jax.ShapeDtypeStruct((2, width, hidden_units), bf16),
        ),
        in_specs=[smem] * 3 + [vmem] * 4 + [anywhere] * 4,
        out_specs=(vmem, anywhere),
        scratch_shapes=scratch,
        compiler_params=pltpu.CompilerParams(
            collective_id=0, has_side_effects=True, vmem_limit_bytes=56 << 20
        ),
    )(
        table,
        last,
        hc_in,
        streams,
        cosine,
        sine,
        tree_mask,
        qkv,
        up_rows,
        k_pages.reshape(slots, keys, head_dim),
        v_pages.reshape(slots, keys, head_dim),
    )


def transpose_sum(values):
    half = values.shape[1] // 2
    return jnp.sum(jnp.transpose(values[:, 0:half] + values[:, half:]), axis=0, keepdims=True)


def layer_kernel(
    chips,
    chunks,
    hc_in,
    hc_mix,
    hc_out,
    accepted,
    attended,
    streams,
    out_hbm,
    gate_hbm,
    down_hbm,
    weight_hbm,
    vocab_hbm,
    fresh_ref,
    logits_ref,
    final_ref,
    final_all,
    weight_buf,
    vocab_buf,
    shards,
    logits_acc,
    draft_sem,
    sum_send,
    sum_recv,
    draft_send,
    draft_recv,
    hand_send,
    hand_recv,
    loop_send,
    loop_recv,
    out_buf,
    gate_buf,
    down_buf,
    first_buf,
    mixed_buf,
    total_buf,
    share,
    twin,
    relay,
    joined,
    single,
    stat_all,
    columns,
    normed,
    gathered,
    hidden,
    load_sem,
    own_sem,
    twin_send,
    twin_recv,
    ring_send,
    ring_recv,
    stat_send,
    stat_recv,
    copy_send,
    copy_recv,
    pass_send,
    pass_recv,
):
    tokens, feature = attended.shape
    size = tokens // chunks
    group = 2 * chips
    width = group * feature
    count = streams.shape[0]
    inner = hidden.shape[1]
    strips = inner // feature
    me = lax.axis_index("head")
    chip = me // 2
    core = lax.rem(me, 2)
    turn = 1 - 2 * core

    def at(delta):
        return lax.rem(chip + chips + delta, chips)

    def peer(delta):
        return at(delta) * 2 + core

    sibling = chip * 2 + 1 - core

    def send_to(source, target, send_sem, recv_sem, head):
        return pltpu.make_async_remote_copy(
            src_ref=source,
            dst_ref=target,
            send_sem=send_sem,
            recv_sem=recv_sem,
            device_id={"head": head},
            device_id_type=MESH,
        )

    loads = []
    for index in range(group):
        loads.append(
            pltpu.make_async_copy(
                out_hbm.at[:, pl.ds(index * feature, feature)], out_buf.at[index], load_sem.at[0, index]
            )
        )
    for index in range(2 * strips):
        kind, strip = index // strips, index % strips
        loads.append(
            pltpu.make_async_copy(
                gate_hbm.at[kind, :, pl.ds(strip * feature, feature)],
                gate_buf.at[index],
                load_sem.at[1, index],
            )
        )
    for index in range(group):
        loads.append(
            pltpu.make_async_copy(
                down_hbm.at[:, pl.ds(index * feature, feature)], down_buf.at[index], load_sem.at[2, index]
            )
        )
    draft_loads = [pltpu.make_async_copy(weight_hbm, weight_buf, draft_sem.at[0])]
    for index in range(group):
        draft_loads.append(
            pltpu.make_async_copy(
                vocab_hbm.at[:, pl.ds(index * feature, feature)],
                vocab_buf.at[index],
                draft_sem.at[1 + index],
            )
        )
    for load in loads + draft_loads:
        load.start()
    barrier = pltpu.get_barrier_semaphore()
    home_index = lax.axis_index("req")
    peers = shards.shape[1] // final_ref.shape[0]
    for step in range(1, group):
        pl.semaphore_signal(
            barrier, inc=1, device_id={"head": lax.rem(me + step, group)}, device_id_type=MESH
        )
    for step in range(1, peers):
        pl.semaphore_signal(
            barrier, inc=1, device_id={"req": lax.rem(home_index + step, peers)}, device_id_type=MESH
        )
    pl.semaphore_wait(barrier, group + peers - 2)

    sends = []

    def go(copy):
        copy.start()
        sends.append(copy)
        return copy

    offsets = (2, 1, 3, 0)
    waits = {}

    def chunk_rows(t):
        return pl.ds(t * size, size)

    def lanes(head):
        return pl.ds(pl.multiple_of(head * feature, feature), feature)

    def scatter(which, t, product):
        for k, offset in enumerate(offsets):
            target = at(offset)
            piece = share.at[which, t, 1 - core, target]
            piece[...] = product(target * 2 + 1 - core).astype(piece.dtype)
            waits["twin", which, t, k] = go(
                send_to(piece, twin.at[which, t, target], twin_send.at[which, t, k],
                        twin_recv.at[which, t, k], sibling))
        for offset in offsets:
            target = at(offset)
            piece = share.at[which, t, core, target]
            piece[...] = product(target * 2 + core).astype(piece.dtype)

    def widen(ref):
        return ref[...].astype(jnp.float32)

    def chip_sum(which, t):
        def fold(k):
            waits["twin", which, t, k].wait_recv()
            target = at(offsets[k])
            piece = share.at[which, t, core, target]
            piece[...] = (widen(piece) + widen(twin.at[which, t, target])).astype(piece.dtype)

        fold(0)
        waits["far", which, t] = go(
            send_to(share.at[which, t, core, at(2)], relay.at[which, t],
                    ring_send.at[which, t, 0], ring_recv.at[which, t, 0], peer(turn)))
        fold(1)
        fold(2)
        waits["near", which, t] = go(
            send_to(share.at[which, t, core, at(-turn)], single.at[which, t],
                    ring_send.at[which, t, 1], ring_recv.at[which, t, 1], peer(-turn)))
        fold(3)

    def chip_relay(which, t):
        waits["far", which, t].wait_recv()
        piece = relay.at[which, t]
        piece[...] = (widen(piece) + widen(share.at[which, t, core, at(turn)])).astype(piece.dtype)
        waits["join", which, t] = go(
            send_to(piece, joined.at[which, t],
                    ring_send.at[which, t, 2], ring_recv.at[which, t, 2], peer(turn)))

    def finish(which, t):
        waits["near", which, t].wait_recv()
        waits["join", which, t].wait_recv()

    block = 32

    def delta_of(which, t, rows):
        return (
            share[which, t, core, at(0), rows].astype(jnp.float32)
            + joined[which, t, rows].astype(jnp.float32)
            + single[which, t, rows].astype(jnp.float32)
        )

    def remixed(layer, values, delta):
        result = []
        for target in range(count):
            total = hc_out[layer, target] * delta
            for source in range(count):
                weight = hc_mix[layer, source, target]
                if source == target:
                    weight = weight + 1.0
                total = total + weight * values[source]
            result.append(total)
        return result

    def project(t):
        if t == 0:
            for load in loads[:group]:
                load.wait()
        values = attended[t * size : (t + 1) * size]
        scatter(0, t, lambda head: jnp.dot(
            values, out_buf[head], preferred_element_type=jnp.float32))

    def middle(t):
        finish(0, t)

        def step(index, carry):
            inside = pl.ds(index * block, block)
            rows = pl.ds(t * size + index * block, block)
            values = [streams[s, rows].astype(jnp.float32) for s in range(count)]
            result = remixed(0, values, delta_of(0, t, inside))
            mixed = None
            for s in range(count):
                first_buf[s, rows] = result[s]
                term = hc_in[1, s] * result[s]
                mixed = term if mixed is None else mixed + term
            mixed_buf[rows] = mixed
            return carry

        lax.fori_loop(0, size // block, step, 0)
        mixed = mixed_buf[t * size : (t + 1) * size]
        stat_all[t, me, 0:1] = transpose_sum(mixed)
        stat_all[t, me, 1:2] = transpose_sum(mixed * mixed)
        stat_all[t, me, 2:8] = jnp.zeros((6, size), jnp.float32)
        for step in range(1, group):
            waits["stat", t, step] = go(
                send_to(stat_all.at[t, me], stat_all.at[t, me], stat_send.at[t, step],
                        stat_recv.at[t, step], lax.rem(me + step, group)))

    def normalized(t):
        for step in range(1, group):
            waits["stat", t, step].wait_recv()
        total = stat_all[t, 0]
        for index in range(1, group):
            total = total + stat_all[t, index]
        center = total[0:1] / width
        scale = lax.rsqrt(total[1:2] / width - center * center + 1e-05)
        row = lax.broadcasted_iota(jnp.int32, total.shape, 0)
        packed = jnp.where(row == 0, center, jnp.where(row == 1, scale, 0.0))
        columns[t] = jnp.transpose(packed)

        def step(index, carry):
            inside = pl.ds(index * block, block)
            rows = pl.ds(t * size + index * block, block)
            column = columns[t, inside]
            value = (mixed_buf[rows] - column[:, 0:1]) * column[:, 1:2]
            normed[rows] = value.astype(normed.dtype)
            return carry

        lax.fori_loop(0, size // block, step, 0)
        mine = normed.at[chunk_rows(t)]
        view = gathered.at[chunk_rows(t), lanes(me)]
        waits["fwd", t] = go(send_to(mine, view, pass_send.at[t, 0], pass_recv.at[t, 0], peer(turn)))
        waits["bwd", t] = go(send_to(mine, view, pass_send.at[t, 1], pass_recv.at[t, 1], peer(-turn)))
        waits["own", t] = go(send_to(mine, view, copy_send.at[t, 0], copy_recv.at[t, 0], sibling))
        local = pltpu.make_async_copy(mine, view, own_sem.at[t])
        local.start()
        waits["local", t] = local

    def hand_over(t, index, delta):
        view = gathered.at[chunk_rows(t), lanes(peer(delta))]
        waits["copy", t, index] = go(
            send_to(view, view, copy_send.at[t, index], copy_recv.at[t, index], sibling))

    def pass_on(t):
        waits["fwd", t].wait_recv()
        view = gathered.at[chunk_rows(t), lanes(peer(-turn))]
        waits["opp", t] = go(send_to(view, view, pass_send.at[t, 2], pass_recv.at[t, 2], peer(turn)))
        hand_over(t, 1, -turn)
        waits["bwd", t].wait_recv()
        hand_over(t, 2, turn)

    def pass_last(t):
        waits["opp", t].wait_recv()
        hand_over(t, 3, 2)

    def feed_forward(t):
        if t == 0:
            for load in loads[group:]:
                load.wait()
        waits["own", t].wait_recv()
        waits["local", t].wait()
        for index in (1, 2, 3):
            waits["copy", t, index].wait_recv()
        values = gathered.at[chunk_rows(t)]
        for strip in range(strips):
            gate = jnp.dot(values[...], gate_buf[strip], preferred_element_type=jnp.float32)
            up = jnp.dot(values[...], gate_buf[strips + strip], preferred_element_type=jnp.float32)
            hidden[:, strip * feature : (strip + 1) * feature] = (
                gate * lax.logistic(gate) * up
            ).astype(hidden.dtype)
        scatter(1, t, lambda head: jnp.dot(
            hidden[...], down_buf[head], preferred_element_type=jnp.float32))

    def last(t):
        finish(1, t)

        def step(index, carry):
            inside = pl.ds(index * block, block)
            rows = pl.ds(t * size + index * block, block)
            values = [first_buf[s, rows] for s in range(count)]
            result = remixed(1, values, delta_of(1, t, inside))
            total = result[0]
            for s in range(count):
                fresh_ref[s, rows] = result[s].astype(fresh_ref.dtype)
                if s > 0:
                    total = total + result[s]
            total_buf[rows] = total
            return carry

        lax.fori_loop(0, size // block, step, 0)

    phases = (
        project,
        lambda t: chip_sum(0, t),
        lambda t: chip_relay(0, t),
        middle,
        normalized,
        pass_on,
        pass_last,
        feed_forward,
        lambda t: chip_sum(1, t),
        lambda t: chip_relay(1, t),
        last,
    )
    for step in range(len(phases) + chunks - 1):
        for t in range(chunks):
            if 0 <= step - t < len(phases):
                phases[step - t](t)
    requests = accepted.shape[0]
    repeats = final_ref.shape[0] // requests
    tree = tokens // requests
    for item in range(requests):
        row = total_buf[pl.ds(item * tree + accepted[item], 1)]
        for copy_index in range(repeats):
            place = item * repeats + copy_index
            final_ref[place : place + 1] = row

    def draft_part():
        rows, feature = final_ref.shape
        group = 2 * chips
        width = group * feature
        devices = shards.shape[1] // rows
        me = lax.axis_index("head")
        home = lax.axis_index("req")
        chip = me // 2
        core = lax.rem(me, 2)
        turn = 1 - 2 * core
        sibling = chip * 2 + 1 - core

        def peer(delta):
            return lax.rem(chip + chips + delta, chips) * 2 + core

        def send_to(source, target, send_sem, recv_sem, device):
            return pltpu.make_async_remote_copy(
                src_ref=source,
                dst_ref=target,
                send_sem=send_sem,
                recv_sem=recv_sem,
                device_id=device,
                device_id_type=MESH,
            )

        sums = []
        for step in range(1, group):
            sums.append(
                go(send_to(final_ref, final_all.at[me], sum_send.at[step], sum_recv.at[step],
                           {"head": lax.rem(me + step, group)}))
            )
        final_all[me] = final_ref[...]
        draft_loads[0].wait()
        for copy in sums:
            copy.wait_recv()
        center = jnp.zeros((rows, 1), jnp.float32)
        square = jnp.zeros((rows, 1), jnp.float32)
        for index in range(group):
            values = final_all[index]
            center = center + jnp.sum(values, axis=1, keepdims=True)
            square = square + jnp.sum(values * values, axis=1, keepdims=True)
        center = center / width
        scale = lax.rsqrt(square / width - center * center + 1e-05)
        branches = []
        for kind in range(2):
            branch = jnp.zeros((rows, feature), jnp.float32)
            for index in range(group):
                values = ((final_all[index] - center) * scale).astype(jnp.bfloat16)
                branch = branch + jnp.dot(
                    values,
                    weight_buf[kind, index * feature : (index + 1) * feature],
                    preferred_element_type=jnp.float32,
                )
            branches.append(branch)
        odd = (lax.broadcasted_iota(jnp.int32, (rows, feature), 0) & 1) == 1
        branch = jnp.where(odd, branches[1], branches[0])
        drafted = (final_ref[...] - center) * scale + branch * lax.logistic(branch)
        mine = shards.at[me, pl.ds(pl.multiple_of(home * rows, rows), rows)]
        mine[...] = drafted.astype(shards.dtype)
        drafts = []
        for step in range(1, devices):
            drafts.append(
                go(send_to(mine, mine, draft_send.at[step], draft_recv.at[step],
                           {"req": lax.rem(home + step, devices)}))
            )
        for copy in drafts:
            copy.wait_recv()

        def shard(head):
            return shards.at[head]

        def ring(index, delta, source):
            return go(send_to(shard(source), shard(source), loop_send.at[index], loop_recv.at[index],
                              {"head": peer(delta)}))

        def hand_over(index, source):
            return go(send_to(shard(source), shard(source), hand_send.at[index], hand_recv.at[index],
                              {"head": sibling}))

        fwd = ring(0, turn, me)
        bwd = ring(1, -turn, me)
        hands = [hand_over(0, me)]
        for load in draft_loads[1:]:
            load.wait()

        def add(head, first=False):
            value = lax.dot_general(
                shards[head],
                vocab_buf[head],
                (((1,), (1,)), ((), ())),
                preferred_element_type=jnp.float32,
            )
            logits_acc[...] = value if first else logits_acc[...] + value

        add(me, True)
        fwd.wait_recv()
        opp = ring(2, turn, peer(-turn))
        hands.append(hand_over(1, peer(-turn)))
        bwd.wait_recv()
        hands.append(hand_over(2, peer(turn)))
        add(peer(-turn))
        hands[0].wait_recv()
        add(sibling)
        add(peer(turn))
        opp.wait_recv()
        hands.append(hand_over(3, peer(2)))
        hands[1].wait_recv()

        def across(delta):
            return lax.rem(chip + chips + delta, chips) * 2 + 1 - core

        add(across(turn))
        hands[2].wait_recv()
        add(across(-turn))
        add(peer(2))
        hands[3].wait_recv()
        add(across(2))
        logits_ref[...] = logits_acc[...].astype(logits_ref.dtype)

    draft_part()
    for copy in sends:
        copy.wait_send()


def layer(
    attended,
    streams,
    hc_in,
    hc_mix,
    hc_out,
    out_weight,
    gate_up,
    down_weight,
    accepted,
    draft_weight,
    lm_head,
):
    repeats = draft_weight.shape[0]
    rows = accepted.shape[0] * repeats
    devices = lax.axis_size("req")
    vocab = lm_head.shape[1]
    tokens, feature = attended.shape
    count = streams.shape[0]
    group = lax.axis_size("head")
    chips = group // 2
    width = out_weight.shape[1]
    inner = down_weight.shape[0]
    strips = inner // feature
    chunks = 3
    size = tokens // chunks
    bf16, f32 = jnp.bfloat16, jnp.float32
    dma = pltpu.SemaphoreType.DMA
    vmem = pl.BlockSpec(memory_space=pltpu.VMEM)
    smem = pl.BlockSpec(memory_space=pltpu.SMEM)
    anywhere = pl.BlockSpec(memory_space=pl.ANY)
    scratch = [
        pltpu.VMEM((rows, feature), f32),
        pltpu.VMEM((group, rows, feature), f32),
        pltpu.VMEM(draft_weight.shape, bf16),
        pltpu.VMEM((group, vocab, feature), bf16),
        pltpu.VMEM((group, devices * rows, feature), bf16),
        pltpu.VMEM((devices * rows, vocab), f32),
        dma((1 + group,)),
        dma((group,)), dma((group,)),
        dma((devices,)), dma((devices,)),
        dma((4,)), dma((4,)),
        dma((3,)), dma((3,)),
        pltpu.VMEM((group, feature, feature), bf16),
        pltpu.VMEM((2 * strips, width, feature), bf16),
        pltpu.VMEM((group, inner, feature), bf16),
        pltpu.VMEM((count, tokens, feature), f32),
        pltpu.VMEM((tokens, feature), f32),
        pltpu.VMEM((tokens, feature), f32),
        pltpu.VMEM((2, chunks, 2, chips, size, feature), bf16),
        pltpu.VMEM((2, chunks, chips, size, feature), bf16),
        pltpu.VMEM((2, chunks, size, feature), bf16),
        pltpu.VMEM((2, chunks, size, feature), bf16),
        pltpu.VMEM((2, chunks, size, feature), bf16),
        pltpu.VMEM((chunks, group, 8, size), f32),
        pltpu.VMEM((chunks, size, 8), f32),
        pltpu.VMEM((tokens, feature), bf16),
        pltpu.VMEM((tokens, width), bf16),
        pltpu.VMEM((size, inner), bf16),
        dma((3, max(group, 2 * strips))),
        dma((chunks,)),
        dma((2, chunks, 4)), dma((2, chunks, 4)),
        dma((2, chunks, 3)), dma((2, chunks, 3)),
        dma((chunks, group)), dma((chunks, group)),
        dma((chunks, 4)), dma((chunks, 4)),
        dma((chunks, 3)), dma((chunks, 3)),
    ]
    return pl.pallas_call(
        functools.partial(layer_kernel, chips, chunks),
        out_shape=(
            jax.ShapeDtypeStruct((count, tokens, feature), bf16),
            jax.ShapeDtypeStruct((devices * rows, vocab), bf16),
        ),
        in_specs=[smem] * 4 + [vmem, vmem] + [anywhere] * 5,
        out_specs=(vmem, vmem),
        scratch_shapes=scratch,
        compiler_params=pltpu.CompilerParams(
            collective_id=1, has_side_effects=True, vmem_limit_bytes=60 << 20
        ),
    )(
        hc_in,
        hc_mix,
        hc_out,
        accepted,
        attended,
        streams,
        out_weight,
        gate_up,
        down_weight,
        draft_weight,
        jnp.transpose(lm_head),
    )


def on_device(
    streams,
    hc_in,
    hc_mix,
    hc_out,
    qkv_weight,
    out_weight,
    up_gate,
    down_weight,
    draft_weight,
    lm_head,
    k_pages,
    v_pages,
    page_owner,
    page_fill,
    cache_len,
    tree_parent,
    accepted_index,
):
    tokens_local = streams.shape[0]
    req_local = cache_len.shape[0]
    tree_size = tree_parent.shape[1]
    heads_local = k_pages.shape[2]
    head_dim = k_pages.shape[3]
    draft_count = draft_weight.shape[0]
    all_requests = req_local * lax.axis_size("req")
    reach = ancestors(tree_parent)
    depth = (jnp.sum(reach.astype(jnp.float32), axis=1) - 1.0).astype(jnp.int32)
    positions = (cache_len[:, None] + depth).reshape(tokens_local)
    cosine, sine = turns(positions, head_dim)
    by_stream = jnp.transpose(streams, (1, 0, 2))
    width, kinds, inner = up_gate.shape
    up_rows = jnp.transpose(up_gate.reshape(width, kinds, inner // 128, 128), (0, 2, 1, 3)).reshape(
        -1, 128
    )
    attended, gate_up = cache_attention(
        by_stream,
        hc_in,
        jnp.transpose(qkv_weight, (1, 0, 2)),
        up_rows,
        cosine,
        sine,
        reach,
        k_pages,
        v_pages,
        page_owner,
        page_fill,
    )
    fresh, logits_local = layer(
        attended,
        by_stream,
        hc_in,
        hc_mix,
        hc_out,
        out_weight,
        gate_up,
        down_weight,
        accepted_index,
        draft_weight,
        lm_head,
    )
    new_streams = jnp.transpose(fresh, (1, 0, 2))
    logits_local = logits_local.reshape(all_requests, draft_count, -1)
    logits = lax.all_to_all(
        logits_local, ("req", "head"), split_axis=0, concat_axis=2, tiled=True
    ).astype(jnp.float32)
    return (new_streams, logits)


def solution(mesh):
    in_specs = (
        P("req", None, "head"),
        P(),
        P(),
        P(),
        P(None, None, "head"),
        P("head", None),
        P(None, None, "head"),
        P("head", None),
        P(None, None, "head"),
        P(None, ("req", "head")),
        P("req", None, "head", None),
        P("req", None, "head", None),
        P("req"),
        P("req"),
        P("req"),
        P("req", None),
        P("req"),
    )
    out_specs = (P("req", None, "head"), P(("req", "head"), None, None))
    return jax.shard_map(
        on_device, mesh=mesh, in_specs=in_specs, out_specs=out_specs, check_vma=False
    )
```
